32 devices in a mesh: dp: 8 (over y, x, core), tensor: 4 (over z).
Axes of the slice: x: 2, y: 2, z: 4, core: 2. Of those that a mesh axis runs over, the one named last changes fastest.
Arguments:
- tokens: bfloat16 [8192, 2048], P(('dp', 'tensor')), may hold values from -6 to 6
- lengths: int32 [8], P('dp'), may hold values from 513 to 1024, as said below
- routes: int32 [8192, 4], P('dp'), may hold values from 0 to 7, all different within a row; in each aligned block of 1024 rows (0 to 1023, 1024 to 2047, ...) at most 768 rows name the same one
- cotangent: bfloat16 [8192, 2048], P(('dp', 'tensor')), may hold values from -6 to 6
- norm_one: bfloat16 [2048], replicated, may hold values from 0.5 to 1.5
- qkv_weight: bfloat16 [2048, 3, 2048], P(None, None, 'tensor'), may hold values from -0.125 to 0.125
- qkv_bias: bfloat16 [3, 2048], P(None, 'tensor'), may hold values from -0.59765625 to 0.59765625
- out_weight: bfloat16 [2048, 2048], P('tensor'), may hold values from -1.5 to 1.5
- norm_two: bfloat16 [2048], replicated, may hold values from 0.5 to 1.5
- router_weight: bfloat16 [2048, 8], replicated, may hold values from -0.0625 to 0.0625
- expert_in: bfloat16 [8, 2048, 2, 1408], P(None, None, None, 'tensor'), may hold values from -0.125 to 0.125
- expert_out: bfloat16 [8, 1408, 2048], P(None, 'tensor'), may hold values from -0.625 to 0.625
- shared_in: bfloat16 [2048, 2, 5632], P(None, None, 'tensor'), may hold values from -0.125 to 0.125
- shared_out: bfloat16 [5632, 2048], P('tensor'), may hold values from -0.15625 to 0.15625
- shared_gate: bfloat16 [2048], replicated, may hold values from -0.125 to 0.125
Outputs:
- output: bfloat16 [8192, 2048], P(('dp', 'tensor'))
- input_grad: float32 [8192, 2048], P(('dp', 'tensor'))
- norm_one_grad: float32 [2048], replicated
- qkv_weight_grad: float32 [2048, 3, 2048], P('dp', None, 'tensor')
- qkv_bias_grad: float32 [3, 2048], P(None, 'tensor')
- out_weight_grad: float32 [2048, 2048], P('tensor', 'dp')
- norm_two_grad: float32 [2048], replicated
- router_grad: float32 [2048, 8], replicated
- expert_in_grad: float32 [8, 2048, 2, 1408], P(None, 'dp', None, 'tensor')
- expert_out_grad: float32 [8, 1408, 2048], P(None, 'tensor', 'dp')
- shared_in_grad: float32 [2048, 2, 5632], P('dp', None, 'tensor')
- shared_out_grad: float32 [5632, 2048], P('tensor', 'dp')
- shared_gate_grad: float32 [2048], replicated
The draws below stay inside these ranges and needn't reach their ends.
Inputs may be any that keep to these rules, and one draw needn't show every extreme that they name: Row r holds one sequence in its first lengths[r] slots; the other slots are padding. In every draw some row is full. `routes`: the 4 experts of a slot are all different. Within each packed row (aligned blocks of 1024 slots) no expert is named more than 768 times; in some row some expert is named exactly 768 times.
All inputs are finite; a program needn't handle non-finite values.
Results may differ from the reference program's by a relative error of at most 0.018.
The reference program's roundings to bfloat16 on the way count: a program that leaves them out, or rounds other values in their place, can miss the bound.
Values may be sent and summed in bfloat16 or wider, within the bound.
A program may use at most 384 MiB of HBM per device.

```python
import math
import jax
import jax.numpy as jnp
import numpy as np
from jax import lax

D = 2048
HEADS = 16
HEAD_DIM = 128
EFF = 1408
SFF = 5632
TOP = 4
EXPERTS = 8
SLOTS = 1024
CAP = 768
ROWS = 8
TOKENS = 8192


def draw_lengths(key, part):
    row_lengths = jax.random.randint(key, (ROWS,), SLOTS // 2 + 1, SLOTS + 1)
    full_row = jax.random.randint(jax.random.fold_in(key, 7), (), 0, ROWS)
    return jnp.where(jnp.arange(ROWS) == full_row, SLOTS, row_lengths).astype(jnp.int32)


def strengthened(drawn, stream_key, source, target, parts, factor):
    owner, partner = [(jnp.arange(drawn.shape[position]) // (drawn.shape[position] // parts)).reshape([-1 if axis == position else 1 for axis in range(drawn.ndim)]) for position in (source, target)]
    chosen = jax.random.permutation(stream_key, parts)[partner]
    strong = (owner == chosen) | (owner == (partner + parts // 2) % parts)
    return jnp.where(strong, factor * drawn, drawn)


def block_scale(rng, shape, cuts, low, largest):
    def one(axis_at, parts):
        draws = jax.random.uniform(jax.random.fold_in(jax.random.fold_in(rng, 6), axis_at), (parts,), jnp.float32, low / len(cuts), largest / len(cuts))
        return jnp.repeat(jnp.exp(draws), shape[axis_at] // parts).reshape((-1,) + (1,) * (len(shape) - axis_at - 1))

    loudness = one(*cuts[0])
    for cut in cuts[1:]:
        loudness = loudness * one(*cut)
    return loudness


def deal_out(stream_key, own, number, rows, number_of, top, limit, skew):
    sequence = jax.random.permutation(stream_key, number_of)
    packed, usual = shares(number_of, rows * top, limit, skew, True), shares(number_of, rows * top, limit, skew, False)
    places = jnp.arange(number_of)

    def named(sizes, turn):
        used = int((sizes > 0).sum())
        fixed = max(1, used // 4)
        passed = fixed + (places - fixed + turn * (used - fixed)) % max(1, number_of - fixed)
        return jnp.zeros((number_of,), jnp.int32).at[sequence[jnp.where(places < fixed, places, passed)]].set(jnp.asarray(sizes, jnp.int32))

    sizes = jnp.where(number % 4 == 0, named(packed, number // 4), named(usual, number - number // 4 - 1))
    mixed = jax.random.permutation(jax.random.fold_in(own, 3), number_of)
    source_of, taker = mixed[0:number_of // 2 * 2:2], mixed[1:number_of // 2 * 2:2]
    slack = jnp.minimum(sizes[source_of] - 1, limit - sizes[taker]) // 2
    slack = jnp.where((source_of == sequence[0]) | (taker == sequence[0]) | (sizes[taker] == 0), 0, jnp.maximum(slack, 0))
    passed = jax.random.randint(jax.random.fold_in(own, 4), (number_of // 2,), 0, 1 << 20) % (slack + 1)
    sizes = sizes.at[source_of].add(-passed).at[taker].add(passed)
    items = jnp.searchsorted(jnp.cumsum(sizes), jnp.arange(rows * top), side="right").astype(jnp.int32)
    listing = items.reshape(top, rows).T
    listing = listing[jax.random.permutation(jax.random.fold_in(own, 1), rows)]
    turn = jax.random.randint(jax.random.fold_in(own, 2), (rows, 1), 0, top)
    return jnp.take_along_axis(listing, (jnp.arange(top)[None, :] + turn) % top, axis=1)


def shares(amount, total, reach, lean, full):
    loads = [(1 << 20) // math.isqrt(standing ** lean) + 1 for standing in range(1, amount + 1)]
    largest = reach if full else min(reach, max(-(-total // amount), total * loads[0] // sum(loads)))
    least = 1 if total - largest >= amount - 1 else 0
    counts, surplus = [largest] + [least] * (amount - 1), total - largest - least * (amount - 1)
    while surplus > 0:
        candidates = [i for i in range(1, amount) if counts[i] < largest] or [i for i in range(1, amount) if counts[i] < reach]
        mass, left = sum([loads[i] for i in candidates]), surplus
        for i in candidates:
            addition = min(reach - counts[i], max(1, left * loads[i] // mass), surplus)
            counts[i] = counts[i] + addition
            surplus = surplus - addition
    return np.array(counts)


def gaussian(stream_key, shape, deviation, reach, shards=(), kind=jnp.bfloat16):
    entries = jax.random.normal(stream_key, shape, jnp.float32) * deviation
    if len(shards) > 0:
        entries = block_scale(stream_key, shape, shards, -0.22, 0.18) * entries
    return jnp.clip(entries, min=-reach, max=reach).astype(kind)


def gaussian_with(own_key, shape, deviation, bound, split, heavy, kind=jnp.bfloat16):
    array = deviation * jax.random.normal(own_key, shape, jnp.float32)
    if split:
        array = array * block_scale(own_key, shape, split, -0.22, 0.18)
    return jnp.clip(strengthened(array, jax.random.fold_in(own_key, 3), *heavy), -bound, bound).astype(kind)


def setup_inputs(seed: int = 0) -> dict:
    key_list = jax.random.split(jax.random.key(seed), 16)
    tokens = gaussian(key_list[0], (TOKENS, D), 1.0, 6.0, ((0, 32),))
    lengths = draw_lengths(jax.random.fold_in(key_list[15], 71), 0)
    routes_keys = jax.random.split(jax.random.fold_in(key_list[2], 1), TOKENS // SLOTS)
    routes_turns = jax.random.permutation(jax.random.fold_in(key_list[2], 3), TOKENS // SLOTS)
    routes = jax.vmap(lambda own, number: deal_out(jax.random.fold_in(key_list[2], 2), own, number, SLOTS, EXPERTS, TOP, CAP, 1))(routes_keys, routes_turns).reshape((TOKENS, TOP))
    cotangent = gaussian_with(key_list[3], (TOKENS, D), 1.0, 6.0, ((0, 32),), (0, 1, 32, 2.75))
    norm_one = jnp.clip(1.0 + 0.1 * jax.random.normal(key_list[4], (D,), jnp.float32), 0.5, 1.5).astype(jnp.bfloat16)
    qkv_weight = gaussian(key_list[5], (D, 3, HEADS * HEAD_DIM), D ** -0.5, 0.125, ((2, 4),))
    qkv_bias = gaussian(key_list[6], (3, HEADS * HEAD_DIM), 0.1, 0.59765625, ((1, 4),))
    out_weight = gaussian(key_list[7], (HEADS * HEAD_DIM, D), HEADS ** -0.5, 1.5, ((0, 4),))
    norm_two = jnp.clip(1.0 + 0.1 * jax.random.normal(key_list[8], (D,), jnp.float32), 0.5, 1.5).astype(jnp.bfloat16)
    router_weight = gaussian(key_list[9], (D, EXPERTS), (4 * D) ** -0.5, 0.0625)
    expert_in = gaussian(key_list[10], (EXPERTS, D, 2, EFF), D ** -0.5, 0.125, ((3, 4),))
    expert_out = gaussian(key_list[11], (EXPERTS, EFF, D), (EFF // 16) ** -0.5, 0.625, ((1, 4),))
    shared_in = gaussian(key_list[12], (D, 2, SFF), D ** -0.5, 0.125, ((2, 4),))
    shared_out = gaussian(key_list[13], (SFF, D), (SFF // 4) ** -0.5, 0.15625, ((0, 4),))
    shared_gate = gaussian(key_list[14], (D,), D ** -0.5, 0.125)
    return {"tokens": tokens, "lengths": lengths, "routes": routes, "cotangent": cotangent, "norm_one": norm_one, "qkv_weight": qkv_weight, "qkv_bias": qkv_bias, "out_weight": out_weight, "norm_two": norm_two, "router_weight": router_weight, "expert_in": expert_in, "expert_out": expert_out, "shared_in": shared_in, "shared_out": shared_out, "shared_gate": shared_gate}


epsilon = 1e-06
theta_base = 1000000.0
precise = lax.Precision.HIGHEST

@jax.custom_vjp
def low(v):
    return lax.optimization_barrier(v.astype(jnp.bfloat16)).astype(jnp.float32)

@jax.custom_vjp
def low_back(v):
    return v

def low_keep(v):
    return (low(v), None)

def low_pass(kept, grad):
    return (grad,)

def back_keep(v):
    return (v, None)

def back_low(kept, grad):
    return (low(grad),)
low.defvjp(low_keep, low_pass)
low_back.defvjp(back_keep, back_low)

def rotary_tables(row_count, head_width):
    half_index = jnp.arange(head_width // 2).astype(jnp.float32)
    frequency = theta_base ** (-2.0 * half_index / head_width)
    angles = jnp.arange(row_count).astype(jnp.float32)[:, None] * frequency[None, :]
    angles = jnp.concatenate([angles, angles], axis=-1)
    return (jnp.cos(angles)[:, None, :], jnp.sin(angles)[:, None, :])

def rotary(values, cos_table, sine_table):
    half_width = values.shape[-1] // 2
    turned = jnp.concatenate([-values[..., half_width:], values[..., :half_width]], axis=-1)
    return values * cos_table + turned * sine_table

def rms_norm(values, gain_vector):
    return values * lax.rsqrt(lax.optimization_barrier(jnp.mean(values * values, axis=-1, keepdims=True)) + epsilon) * gain_vector

def layer(tokens_in, length, chosen, params):
    norm_one, qkv_weight, qkv_bias, out_weight, norm_two, router_weight, expert_in, expert_out, shared_in, shared_out, shared_gate = params
    row_count = tokens_in.shape[0]
    slot_index = jnp.arange(row_count)
    live_mask = (slot_index < length).astype(tokens_in.dtype)[:, None]
    normed_one = low(rms_norm(tokens_in, norm_one))
    qkv_all = jnp.dot(normed_one, qkv_weight.reshape(D, 3 * HEADS * HEAD_DIM), precision=precise)
    qkv_all = low_back(qkv_all.reshape(row_count, 3, HEADS * HEAD_DIM) + qkv_bias)
    cos_table, sine_table = rotary_tables(row_count, HEAD_DIM)
    query_heads = low(rotary(qkv_all[:, 0].reshape(row_count, HEADS, HEAD_DIM), cos_table, sine_table))
    key_heads = low(rotary(qkv_all[:, 1].reshape(row_count, HEADS, HEAD_DIM), cos_table, sine_table))
    value_heads = low(qkv_all[:, 2].reshape(row_count, HEADS, HEAD_DIM))
    scores = jnp.einsum('qhd,khd->hqk', query_heads, key_heads, precision=precise) * HEAD_DIM ** (-0.5)
    scores = low_back(scores)
    allowed = (slot_index[None, :] <= slot_index[:, None]) & (slot_index[None, :] < length)
    scores = jnp.where(allowed[None], scores, -1000000000.0)
    attn_probs = low(jax.nn.softmax(scores, axis=-1))
    mixed_heads = jnp.einsum('hqk,khd->qhd', attn_probs, value_heads, precision=precise)
    mixed_heads = low(low_back(mixed_heads.reshape(row_count, HEADS * HEAD_DIM)))
    branch_one = low_back(jnp.dot(mixed_heads, out_weight, precision=precise))
    hidden = tokens_in + live_mask * branch_one
    normed_two = low(rms_norm(hidden, norm_two))
    router_probs = jax.nn.softmax(jnp.dot(normed_two, router_weight, precision=precise), axis=-1)
    picked = lax.optimization_barrier(jnp.sum((chosen[:, :, None] == jnp.arange(EXPERTS)[None, None, :]).astype(tokens_in.dtype), axis=1))
    weights = router_probs * picked
    combined = jnp.zeros_like(tokens_in)
    for expert in range(EXPERTS):
        gate_up = low_back(jnp.dot(normed_two, expert_in[expert].reshape(D, 2 * EFF), precision=precise))
        gate_up = gate_up.reshape(row_count, 2, EFF)
        inner_act = low(jax.nn.silu(gate_up[:, 0]) * gate_up[:, 1])
        result = low_back(jnp.dot(inner_act, expert_out[expert], precision=precise))
        combined = combined + weights[:, expert:expert + 1] * result
    shared_up = low_back(jnp.dot(normed_two, shared_in.reshape(D, 2 * SFF), precision=precise))
    shared_up = shared_up.reshape(row_count, 2, SFF)
    shared_act = low(jax.nn.silu(shared_up[:, 0]) * shared_up[:, 1])
    shared_result = low_back(jnp.dot(shared_act, shared_out, precision=precise))
    gate_value = jax.nn.sigmoid(jnp.dot(normed_two, shared_gate, precision=precise))
    combined = combined + gate_value[:, None] * shared_result
    branch_two = low_back(combined)
    return hidden + live_mask * branch_two

def reference(tokens, lengths, routes, cotangent, norm_one, qkv_weight, qkv_bias, out_weight, norm_two, router_weight, expert_in, expert_out, shared_in, shared_out, shared_gate):
    params = tuple((item.astype(jnp.float32) for item in (norm_one, qkv_weight, qkv_bias, out_weight, norm_two, router_weight, expert_in, expert_out, shared_in, shared_out, shared_gate)))
    row_tokens = tokens.astype(jnp.float32).reshape(ROWS, SLOTS, D)
    row_cot = cotangent.astype(jnp.float32).reshape(ROWS, SLOTS, D)
    row_routes = routes.reshape(ROWS, SLOTS, TOP)

    def one_row(grad_sums, row_data):
        tokens_in, length, chosen, cot_in = row_data
        live_mask = (jnp.arange(SLOTS) < length).astype(jnp.float32)[:, None]

        def forward(tokens_arg, params_arg):
            return layer(tokens_arg, length, chosen, params_arg)
        output, pullback = jax.vjp(forward, tokens_in, params)
        grad_tokens, grad_params = pullback(cot_in * live_mask)
        grad_sums = jax.tree.map(lambda left, right: left + right, grad_sums, grad_params)
        return (grad_sums, (output.astype(jnp.bfloat16), grad_tokens))
    zero_grads = jax.tree.map(jnp.zeros_like, params)
    grad_total, (outputs, token_grads) = lax.scan(one_row, zero_grads, (row_tokens, lengths, row_routes, row_cot))
    return (outputs.reshape(TOKENS, D), token_grads.reshape(TOKENS, D), grad_total[0], grad_total[1], grad_total[2], grad_total[3], grad_total[4], grad_total[5], grad_total[6], grad_total[7], grad_total[8], grad_total[9], grad_total[10])
```

```python
import functools

import jax
import jax.numpy as jnp
from jax import lax
from jax.experimental import pallas as pl
from jax.experimental.pallas import tpu as pltpu
from jax.sharding import PartitionSpec as P

HEAD_DIM = 128
MESH = pl.DeviceIdType.MESH
LA, LB, LC = 1, 2, 2
MIB = 2**20


epsilon = 1e-06
theta_base = 1000000.0
NT = (((1,), (1,)), ((), ()))
TN = (((0,), (0,)), ((), ()))


def rotary_tables(row_count, head_width):
    half_index = jnp.arange(head_width // 2).astype(jnp.float32)
    frequency = theta_base ** (-2.0 * half_index / head_width)
    angles = jnp.arange(row_count).astype(jnp.float32)[:, None] * frequency[None, :]
    angles = jnp.concatenate([angles, angles], axis=-1)
    return (jnp.cos(angles)[:, None, :], jnp.sin(angles)[:, None, :])


def rotary(values, cos_table, sine_table):
    half_width = values.shape[-1] // 2
    turned = jnp.concatenate([-values[..., half_width:], values[..., :half_width]], axis=-1)
    return values * cos_table + turned * sine_table


def rotary_back(grads_in, cos_table, sine_table):
    half_width = grads_in.shape[-1] // 2
    scaled = grads_in * sine_table
    return grads_in * cos_table + jnp.concatenate(
        [scaled[..., half_width:], -scaled[..., :half_width]], axis=-1
    )


def norm_back(d_normed, unit_rows, inverse, gain_vector):
    d_unit = d_normed * gain_vector
    return inverse * (d_unit - unit_rows * jnp.mean(d_unit * unit_rows, axis=-1, keepdims=True))


def rs_body(nc, a_ref, b_ref, o_ref, own, sa, ra, kt, s1, r1, ku, s2, r2, sem_sa, sem_ra, sem_s1, sem_r1, sem_s2, sem_r2):
    i = pl.program_id(0)
    r, w = o_ref.shape
    hr = r // 2
    dp = lax.axis_index("dp")
    k = dp % 2
    x = (dp // 2) % 2
    y = dp // 4
    core_peer = y * 4 + x * 2 + (1 - k)
    x_peer = y * 4 + (1 - x) * 2 + k
    y_peer = (1 - y) * 4 + x * 2 + k

    def copy_a(c):
        return pltpu.make_async_remote_copy(
            src_ref=sa.at[c % 2], dst_ref=ra.at[c % 3], send_sem=sem_sa.at[c % 2], recv_sem=sem_ra.at[c % 3],
            device_id={"dp": core_peer}, device_id_type=MESH)

    def copy_1(c, half):
        return pltpu.make_async_remote_copy(
            src_ref=s1.at[c % 3, half], dst_ref=r1.at[c % 6, half], send_sem=sem_s1.at[c % 3, half],
            recv_sem=sem_r1.at[c % 6, half], device_id={"dp": y_peer if half else x_peer}, device_id_type=MESH)

    def copy_2(c, half):
        return pltpu.make_async_remote_copy(
            src_ref=s2.at[c % 2, half], dst_ref=r2.at[c % 6, half], send_sem=sem_s2.at[c % 2, half],
            recv_sem=sem_r2.at[c % 6, half], device_id={"dp": x_peer if half else y_peer}, device_id_type=MESH)

    @pl.when(i == 0)
    def _():
        barrier = pltpu.get_barrier_semaphore()
        for peer in (core_peer, x_peer, y_peer):
            pl.semaphore_signal(barrier, inc=1, device_id={"dp": peer}, device_id_type=MESH)
        pl.semaphore_wait(barrier, 3)

    @pl.when(jnp.logical_and(i >= LA + 3, i < nc + LA + 3))
    def _():
        copy_1(i - LA - 3, 0).wait_send()
        copy_1(i - LA - 3, 1).wait_send()

    @pl.when(jnp.logical_and(i >= LA, i < nc + LA))
    def _():
        c = i - LA
        copy_a(c).wait_recv()
        for half in range(2):
            rows = slice(half * hr, half * hr + hr)
            keep, other = (1, 2) if half else (2, 1)
            def total(role):
                return own[c % 2, role, rows, :] + ra[c % 3, role, rows, :].astype(jnp.float32)
            s1[c % 3, half, 0] = total(other).astype(jnp.bfloat16)
            s1[c % 3, half, 1] = total(3).astype(jnp.bfloat16)
            copy_1(c, half).start()
            kt[c % 3, half, 0] = total(0)
            kt[c % 3, half, 1] = total(keep)

    @pl.when(jnp.logical_and(i >= LA + LB, i < nc + LA + LB))
    def _():
        c = i - LA - LB
        @pl.when(c >= 2)
        def _():
            copy_2(c - 2, 0).wait_send()
            copy_2(c - 2, 1).wait_send()
        for half in range(2):
            copy_1(c, half).wait_recv()
            s2[c % 2, half] = (kt[c % 3, half, 1] + r1[c % 6, half, 1].astype(jnp.float32)).astype(jnp.bfloat16)
            copy_2(c, half).start()
            ku[c % 3, half] = kt[c % 3, half, 0] + r1[c % 6, half, 0].astype(jnp.float32)

    @pl.when(i >= LA + LB + LC)
    def _():
        c = i - LA - LB - LC
        for half in range(2):
            copy_2(c, half).wait_recv()
            o_ref[half * hr:half * hr + hr, :] = ku[c % 3, half] + r2[c % 6, half].astype(jnp.float32)
        @pl.when(c >= nc - 2)
        def _():
            copy_2(c, 0).wait_send()
            copy_2(c, 1).wait_send()

    @pl.when(jnp.logical_and(i >= 2, i < nc + 2))
    def _():
        copy_a(i - 2).wait_send()

    @pl.when(i < nc)
    def _():
        a = a_ref[...]
        targets = (y * 4 + x * 2, y * 4 + (1 - x) * 2, (1 - y) * 4 + x * 2, (1 - y) * 4 + (1 - x) * 2)
        for role in range(4):
            cols = pl.ds(pl.multiple_of((targets[role] + 1 - k) * w, w), w)
            sa[i % 2, role] = jnp.dot(a, b_ref[:, cols], preferred_element_type=jnp.float32).astype(jnp.bfloat16)
        copy_a(i).start()
        for role in range(4):
            cols = pl.ds(pl.multiple_of((targets[role] + k) * w, w), w)
            own[i % 2, role] = jnp.dot(a, b_ref[:, cols], preferred_element_type=jnp.float32)

def weight_grad_scatter_kernel(a, b, r, cid, name):
    R, T = a.shape
    D = b.shape[1]
    w = D // 8
    nc = R // r
    L = LA + LB + LC
    f32, bf = jnp.float32, jnp.bfloat16
    dma = pltpu.SemaphoreType.DMA
    return pl.pallas_call(
        functools.partial(rs_body, nc),
        grid=(nc + L,),
        in_specs=[pl.BlockSpec((r, T), lambda i: (jnp.minimum(i, nc - 1), 0)),
                  pl.BlockSpec((T, D), lambda i: (0, 0), pipeline_mode=pl.Buffered(1))],
        out_specs=pl.BlockSpec((r, w), lambda i: (jnp.maximum(i - L, 0), 0)),
        out_shape=jax.ShapeDtypeStruct((R, w), f32),
        scratch_shapes=[
            pltpu.VMEM((2, 4, r, w), f32), pltpu.VMEM((2, 4, r, w), bf), pltpu.VMEM((3, 4, r, w), bf),
            pltpu.VMEM((3, 2, 2, r // 2, w), f32), pltpu.VMEM((3, 2, 2, r // 2, w), bf), pltpu.VMEM((6, 2, 2, r // 2, w), bf),
            pltpu.VMEM((3, 2, r // 2, w), f32), pltpu.VMEM((2, 2, r // 2, w), bf), pltpu.VMEM((6, 2, r // 2, w), bf),
            dma((2,)), dma((3,)), dma((3, 2)), dma((6, 2)), dma((2, 2)), dma((6, 2))],
        compiler_params=pltpu.CompilerParams(vmem_limit_bytes=48 * 2**20, collective_id=cid, has_side_effects=True),
        cost_estimate=pl.CostEstimate(flops=2 * R * T * D, bytes_accessed=2 * R * T + 2 * T * D + 4 * R * w, transcendentals=0),
        name=name)(a, b)


def ffn_body(
    experts, x_ref, d_ref, routes_ref, rw_ref, wi_ref, wd_ref,
    dgu_ref, s_ref, dn_ref, bt_ref, rg_ref,
    dn_acc, bt_acc, probs_ref, w_ref, ds_ref,
):
    c = pl.program_id(0)
    chunks = pl.num_programs(0)
    h = wd_ref.shape[1]
    slots, width = x_ref.shape
    wi = wi_ref.at[0]
    wd = wd_ref.at[0]

    def picked():
        expert = lax.broadcasted_iota(jnp.int32, (experts, slots), 0)
        hit = jnp.zeros((experts, slots), jnp.float32)
        for j in range(routes_ref.shape[0]):
            hit = hit + jnp.where(routes_ref[j : j + 1, :] == expert, 1.0, 0.0)
        return hit

    @pl.when(c == 0)
    def _():
        logits = lax.dot_general(rw_ref[...], x_ref[...], NT, preferred_element_type=jnp.float32)
        raised = jnp.exp(logits[:experts] - jnp.max(logits[:experts], axis=0, keepdims=True))
        probs = raised / jnp.sum(raised, axis=0, keepdims=True)
        gate = 1.0 / (1.0 + jnp.exp(-logits[experts:]))
        probs_ref[...] = probs
        w_ref[:experts, :] = probs * picked()
        w_ref[experts:, :] = gate
        ds_ref[...] = jnp.zeros_like(ds_ref)
        dn_acc[...] = jnp.zeros_like(dn_acc)
        bt_acc[...] = jnp.zeros_like(bt_acc)

    row = pl.ds(jnp.minimum(c, experts), 1)
    x = x_ref[...]
    g = lax.dot_general(wi[:h], x, NT, preferred_element_type=jnp.float32)
    u = lax.dot_general(wi[h:], x, NT, preferred_element_type=jnp.float32)
    p = lax.dot_general(wd[...], d_ref[...], NT, preferred_element_type=jnp.float32)
    w = w_ref[row, :]
    sg = 1.0 / (1.0 + jnp.exp(-g))
    si = g * sg
    inner = (si * u).astype(jnp.bfloat16).astype(jnp.float32)
    s = (w * inner).astype(jnp.bfloat16)
    s_ref[0] = s
    ds_ref[row, :] += jnp.sum(p * inner, axis=0, keepdims=True)
    di = w * p
    dg = (di * u * sg * (1.0 + g * (1.0 - sg))).astype(jnp.bfloat16)
    du = (di * si).astype(jnp.bfloat16)
    dgu_ref[0, :h] = dg
    dgu_ref[0, h:] = du
    dgu = jnp.concatenate([dg, du], axis=0)
    block = 512
    for n in range(0, width, block):
        cols = slice(n, n + block)
        dn_acc[:, cols] += lax.dot_general(dgu, wi[:, cols], TN, preferred_element_type=jnp.float32)
        bt_acc[:, cols] += lax.dot_general(s, wd[:, cols], TN, preferred_element_type=jnp.float32)

    @pl.when(c == chunks - 1)
    def _():
        probs = probs_ref[...]
        d_probs = ds_ref[:experts, :] * picked()
        d_logits = probs * (d_probs - jnp.sum(probs * d_probs, axis=0, keepdims=True))
        gate = w_ref[experts:, :]
        d_gate = ds_ref[experts:, :] * gate * (1.0 - gate)
        small = jnp.concatenate([d_logits, d_gate], axis=0)
        high = small.astype(jnp.bfloat16)
        low = (small - high.astype(jnp.float32)).astype(jnp.bfloat16)
        rg_ref[...] = jnp.dot(high, x_ref[...], preferred_element_type=jnp.float32) + jnp.dot(
            low, x_ref[...], preferred_element_type=jnp.float32
        )
        for n in range(0, width, block):
            cols = slice(n, n + block)
            extra = lax.dot_general(high, rw_ref[:, cols], TN, preferred_element_type=jnp.float32)
            extra += lax.dot_general(low, rw_ref[:, cols], TN, preferred_element_type=jnp.float32)
            dn_ref[:, cols] = (dn_acc[:, cols] + extra).astype(dn_ref.dtype)
        bt_ref[...] = bt_acc[...].astype(bt_ref.dtype)


def ffn(x, d_two, routes_t, router_rows, wi, wd, experts):
    chunks, h2, width = wi.shape
    h = h2 // 2
    slots = x.shape[0]
    rows = router_rows.shape[0]
    bf, f32 = jnp.bfloat16, jnp.float32

    def whole(shape):
        return pl.BlockSpec(shape, lambda c: (0,) * len(shape), pipeline_mode=pl.Buffered(1))

    def chunk(shape):
        return pl.BlockSpec((1, *shape), lambda c: (c, 0, 0))

    return pl.pallas_call(
        functools.partial(ffn_body, experts),
        grid=(chunks,),
        in_specs=[
            whole((slots, width)), whole((slots, width)), whole(routes_t.shape), whole((rows, width)),
            chunk((h2, width)), chunk((h, width)),
        ],
        out_specs=[
            chunk((h2, slots)), chunk((h, slots)), whole((slots, width)), whole((slots, width)), whole((rows, width)),
        ],
        out_shape=[
            jax.ShapeDtypeStruct((chunks, h2, slots), bf), jax.ShapeDtypeStruct((chunks, h, slots), bf),
            jax.ShapeDtypeStruct((slots, width), bf), jax.ShapeDtypeStruct((slots, width), bf),
            jax.ShapeDtypeStruct((rows, width), f32),
        ],
        scratch_shapes=[
            pltpu.VMEM((slots, width), f32), pltpu.VMEM((slots, width), f32),
            pltpu.VMEM((experts, slots), f32), pltpu.VMEM((rows, slots), f32), pltpu.VMEM((rows, slots), f32),
        ],
        compiler_params=pltpu.CompilerParams(vmem_limit_bytes=62 * MIB),
        cost_estimate=pl.CostEstimate(
            flops=12 * chunks * h * slots * width, bytes_accessed=10 * chunks * h * width + 16 * slots * width,
            transcendentals=chunks * h * slots,
        ),
        name="ffn",
    )(x, d_two, routes_t, router_rows, wi, wd)


def weight_grad_scatter(a, b, r, cid, name):
    if lax.axis_size("dp") == 8:
        return weight_grad_scatter_kernel(a, b, r, cid, name)
    product = jnp.dot(a, b, preferred_element_type=jnp.float32)
    return lax.psum_scatter(
        product.astype(jnp.bfloat16), "dp", scatter_dimension=1, tiled=True
    ).astype(jnp.float32)


def gather_body(own_ref, out_ref, local_sem, send_sem, recv_sem):
    me = lax.axis_index("tensor")
    size = lax.axis_size("tensor")
    rows = own_ref.shape[0]
    barrier = pltpu.get_barrier_semaphore()
    for step in range(1, size):
        pl.semaphore_signal(
            barrier, inc=1, device_id={"tensor": lax.rem(me + step, size)}, device_id_type=MESH
        )
    pl.semaphore_wait(barrier, size - 1)
    place = pl.ds(pl.multiple_of(me * rows, rows), rows)
    local = pltpu.make_async_copy(own_ref, out_ref.at[place], local_sem)
    local.start()
    copies = []
    for step in range(1, size):
        copies.append(
            pltpu.make_async_remote_copy(
                src_ref=own_ref, dst_ref=out_ref.at[place], send_sem=send_sem.at[step], recv_sem=recv_sem.at[step],
                device_id={"tensor": lax.rem(me + step, size)}, device_id_type=MESH,
            )
        )
        copies[-1].start()
    local.wait()
    for copy in copies:
        copy.wait()


def gather_rows(own, cid):
    size = lax.axis_size("tensor")
    rows, width = own.shape
    return pl.pallas_call(
        gather_body,
        in_specs=[pl.BlockSpec(memory_space=pl.ANY)],
        out_specs=pl.BlockSpec(memory_space=pl.ANY),
        out_shape=jax.ShapeDtypeStruct((rows * size, width), own.dtype),
        scratch_shapes=[
            pltpu.SemaphoreType.DMA, pltpu.SemaphoreType.DMA((size,)), pltpu.SemaphoreType.DMA((size,)),
        ],
        compiler_params=pltpu.CompilerParams(collective_id=cid, has_side_effects=True),
        cost_estimate=pl.CostEstimate(flops=0, bytes_accessed=2 * rows * size * width * 2, transcendentals=0),
        name="gather_rows",
    )(own)


def sums_body(part_ref, dp_ref, all_ref, from_dp, from_tensor, send_dp, recv_dp, send_t, recv_t):
    size_dp = lax.axis_size("dp")
    size_t = lax.axis_size("tensor")
    me_dp = lax.axis_index("dp")
    me_t = lax.axis_index("tensor")
    barrier = pltpu.get_barrier_semaphore()
    for step in range(1, size_dp):
        pl.semaphore_signal(
            barrier, inc=1, device_id={"dp": lax.rem(me_dp + step, size_dp)}, device_id_type=MESH
        )
    for step in range(1, size_t):
        pl.semaphore_signal(
            barrier, inc=1, device_id={"tensor": lax.rem(me_t + step, size_t)}, device_id_type=MESH
        )
    pl.semaphore_wait(barrier, size_dp + size_t - 2)

    def exchange(axis, me, size, source, slots, send, recv):
        copies = []
        for step in range(1, size):
            copies.append(
                pltpu.make_async_remote_copy(
                    src_ref=source, dst_ref=slots.at[step], send_sem=send.at[step], recv_sem=recv.at[step],
                    device_id={axis: lax.rem(me + step, size)}, device_id_type=MESH,
                )
            )
            copies[-1].start()
        total = source[...]
        for step in range(1, size):
            copies[step - 1].wait_recv()
            total = total + slots[step]
        for copy in copies:
            copy.wait_send()
        return total

    dp_ref[...] = exchange("dp", me_dp, size_dp, part_ref, from_dp, send_dp, recv_dp)
    all_ref[...] = exchange("tensor", me_t, size_t, dp_ref, from_tensor, send_t, recv_t)


def small_sums(part, cid):
    size_dp, size_t = lax.axis_size("dp"), lax.axis_size("tensor")
    vmem = pl.BlockSpec(memory_space=pltpu.VMEM)
    dma = pltpu.SemaphoreType.DMA
    return pl.pallas_call(
        sums_body,
        in_specs=[vmem],
        out_specs=[vmem, vmem],
        out_shape=[jax.ShapeDtypeStruct(part.shape, part.dtype)] * 2,
        scratch_shapes=[
            pltpu.VMEM((size_dp, *part.shape), part.dtype), pltpu.VMEM((size_t, *part.shape), part.dtype),
            dma((size_dp,)), dma((size_dp,)), dma((size_t,)), dma((size_t,)),
        ],
        compiler_params=pltpu.CompilerParams(collective_id=cid, has_side_effects=True),
        name="small_sums",
    )(part)


def on_device(
    tokens,
    lengths,
    routes,
    cotangent,
    norm_one,
    qkv_weight,
    qkv_bias,
    out_weight,
    norm_two,
    router_weight,
    expert_in,
    expert_out,
    shared_in,
    shared_out,
    shared_gate,
):
    own_rows = tokens.shape[0]
    slot_count = routes.shape[0]
    model_width = tokens.shape[1]
    qkv_cols = qkv_weight.shape[2]
    local_heads = qkv_cols // HEAD_DIM
    experts_total = router_weight.shape[1]
    eff = expert_in.shape[3]
    shared_chunks = shared_out.shape[0] // eff
    length = lengths[0]
    tensor_index = lax.axis_index("tensor")
    first_row = tensor_index * own_rows
    slot_index = jnp.arange(slot_count)
    live_own = (first_row + jnp.arange(own_rows) < length).astype(jnp.float32)[:, None]
    block_rows = min(512, slot_count)
    scale = HEAD_DIM ** (-0.5)
    tokens_f = tokens.astype(jnp.float32)
    gain_one = norm_one.astype(jnp.float32)
    gain_two = norm_two.astype(jnp.float32)
    inv_one = lax.rsqrt(jnp.mean(tokens_f * tokens_f, axis=-1, keepdims=True) + epsilon)
    unit_one = tokens_f * inv_one
    normed_one = lax.all_gather(
        (unit_one * gain_one).astype(jnp.bfloat16), "tensor", axis=0, tiled=True
    )
    shared_in_t = shared_in.reshape(model_width, 2, shared_chunks, eff).transpose(2, 1, 3, 0)
    wi = jnp.concatenate(
        [
            expert_in.transpose(0, 2, 3, 1).reshape(experts_total, 2 * eff, model_width),
            shared_in_t.reshape(shared_chunks, 2 * eff, model_width),
        ],
        axis=0,
    )
    wd = jnp.concatenate([expert_out, shared_out.reshape(shared_chunks, eff, model_width)], axis=0)
    router_rows = jnp.concatenate(
        [
            router_weight.T,
            shared_gate[None],
            jnp.zeros((16 - (experts_total + 1) % 16, model_width), jnp.bfloat16),
        ],
        axis=0,
    )
    normed_one, wi, wd = lax.optimization_barrier((normed_one, wi, wd))
    qkv_flat_weight = qkv_weight.reshape(model_width, 3 * qkv_cols)
    qkv_all = jnp.dot(normed_one, qkv_flat_weight, preferred_element_type=jnp.float32)
    qkv_all = qkv_all.reshape(slot_count, 3, qkv_cols) + qkv_bias.astype(jnp.float32)
    cos_table, sine_table = rotary_tables(slot_count, HEAD_DIM)
    query_heads = rotary(
        qkv_all[:, 0].reshape(slot_count, local_heads, HEAD_DIM), cos_table, sine_table
    ).astype(jnp.bfloat16)
    key_heads = rotary(
        qkv_all[:, 1].reshape(slot_count, local_heads, HEAD_DIM), cos_table, sine_table
    ).astype(jnp.bfloat16)
    value_heads = qkv_all[:, 2].reshape(slot_count, local_heads, HEAD_DIM).astype(jnp.bfloat16)

    def block_scores(block_start, block_end):
        raw_scores = (
            jnp.einsum(
                "qhd,khd->hqk",
                query_heads[block_start:block_end],
                key_heads[:block_end],
                preferred_element_type=jnp.float32,
            )
            * scale
        )
        allowed = (slot_index[None, :block_end] <= slot_index[block_start:block_end, None]) & (
            slot_index[None, :block_end] < length
        )
        return jnp.where(allowed[None], raw_scores, -1000000000.0)

    mixed_parts = []
    lse_parts = []
    for block_start in range(0, slot_count, block_rows):
        block_end = block_start + block_rows
        raw_scores = block_scores(block_start, block_end)
        row_peak = jnp.max(raw_scores, axis=-1, keepdims=True)
        exp_terms = jnp.exp(raw_scores - row_peak)
        summed = jnp.sum(exp_terms, axis=-1, keepdims=True)
        probs_low = (exp_terms / summed).astype(jnp.bfloat16)
        mixed_parts.append(
            jnp.einsum(
                "hqk,khd->qhd",
                probs_low,
                value_heads[:block_end],
                preferred_element_type=jnp.float32,
            )
        )
        lse_parts.append(row_peak + jnp.log(summed))
    mixed = jnp.concatenate(mixed_parts, axis=0).reshape(slot_count, qkv_cols).astype(jnp.bfloat16)
    branch_partial = jnp.dot(mixed, out_weight, preferred_element_type=jnp.float32)
    branch_one = lax.psum_scatter(
        branch_partial.astype(jnp.bfloat16), "tensor", scatter_dimension=0, tiled=True
    ).astype(jnp.float32)
    grad_out = cotangent.astype(jnp.float32) * live_own
    d_two_own = (live_own * grad_out).astype(jnp.bfloat16)
    d_two_own, _ = lax.optimization_barrier((d_two_own, mixed))
    d_two = gather_rows(d_two_own, 1)
    hidden = tokens_f + live_own * branch_one
    inv_two = lax.rsqrt(jnp.mean(hidden * hidden, axis=-1, keepdims=True) + epsilon)
    unit_two = hidden * inv_two
    normed_two = lax.all_gather(
        (unit_two * gain_two).astype(jnp.bfloat16), "tensor", axis=0, tiled=True
    )
    d_gate_up, scaled_inner, d_normed, combined, router_part = ffn(
        normed_two, d_two, routes.T, router_rows, wi, wd, experts_total
    )
    chunks = experts_total + shared_chunks
    grad_two = lax.psum_scatter(
        d_normed, "tensor", scatter_dimension=0, tiled=True
    ).astype(jnp.float32)
    out_grads = weight_grad_scatter(
        scaled_inner.reshape(chunks * eff, slot_count), d_two, eff, 2, "down_grads"
    )
    norm_two_part = jnp.sum(grad_two * unit_two, axis=0)
    grad_hidden = grad_out + norm_back(grad_two, unit_two, inv_two, gain_two)
    d_one_own, out_grads = lax.optimization_barrier(
        ((live_own * grad_hidden).astype(jnp.bfloat16), out_grads)
    )
    d_one = lax.all_gather(d_one_own, "tensor", axis=0, tiled=True)
    half = chunks // 2
    d_gate_up_a, _ = lax.optimization_barrier((d_gate_up[:half], d_one_own))
    in_grads_a = weight_grad_scatter(
        d_gate_up_a.reshape(half * 2 * eff, slot_count), normed_two, eff, 3, "in_grads_a"
    )
    d_one, in_grads_a, combined = lax.optimization_barrier((d_one, in_grads_a, combined))
    branch_two = lax.psum_scatter(combined, "tensor", scatter_dimension=0, tiled=True).astype(
        jnp.float32
    )
    output = (hidden + live_own * branch_two).astype(jnp.bfloat16)
    d_mixed = jnp.einsum("sd,cd->sc", d_one, out_weight, preferred_element_type=jnp.float32)
    d_mixed = d_mixed.astype(jnp.bfloat16).reshape(slot_count, local_heads, HEAD_DIM)
    d_query_parts = []
    d_key = jnp.zeros((slot_count, local_heads, HEAD_DIM), jnp.float32)
    d_value = jnp.zeros((slot_count, local_heads, HEAD_DIM), jnp.float32)
    for block_number, block_start in enumerate(range(0, slot_count, block_rows)):
        block_end = block_start + block_rows
        raw_scores = block_scores(block_start, block_end)
        probs_full = jnp.exp(raw_scores - lse_parts[block_number])
        probs_low = probs_full.astype(jnp.bfloat16)
        d_grad_block = d_mixed[block_start:block_end]
        d_probs_att = jnp.einsum(
            "qhd,khd->hqk",
            d_grad_block,
            value_heads[:block_end],
            preferred_element_type=jnp.float32,
        )
        delta_sum = jnp.sum(probs_full * d_probs_att, axis=-1, keepdims=True)
        d_scores = (probs_full * (d_probs_att - delta_sum)).astype(jnp.bfloat16)
        d_query_parts.append(
            jnp.einsum(
                "hqk,khd->qhd", d_scores, key_heads[:block_end], preferred_element_type=jnp.float32
            )
            * scale
        )
        d_key = d_key.at[:block_end].add(
            jnp.einsum(
                "hqk,qhd->khd",
                d_scores,
                query_heads[block_start:block_end],
                preferred_element_type=jnp.float32,
            )
            * scale
        )
        d_value = d_value.at[:block_end].add(
            jnp.einsum("hqk,qhd->khd", probs_low, d_grad_block, preferred_element_type=jnp.float32)
        )
    d_query = jnp.concatenate(d_query_parts, axis=0)
    d_qkv = jnp.stack(
        [
            rotary_back(d_query, cos_table, sine_table).reshape(slot_count, qkv_cols),
            rotary_back(d_key, cos_table, sine_table).reshape(slot_count, qkv_cols),
            d_value.reshape(slot_count, qkv_cols),
        ],
        axis=1,
    ).astype(jnp.bfloat16)
    d_qkv_flat = d_qkv.reshape(slot_count, 3 * qkv_cols)
    bias_part = jnp.sum(d_qkv.astype(jnp.float32), axis=0)
    grad_one = jnp.einsum(
        "sc,dc->sd", d_qkv_flat, qkv_flat_weight, preferred_element_type=jnp.float32
    ).astype(jnp.bfloat16)
    grad_one_own = lax.psum_scatter(grad_one, "tensor", scatter_dimension=0, tiled=True)
    d_gate_up_b, _ = lax.optimization_barrier((d_gate_up[half:], grad_one))
    in_grads_b = weight_grad_scatter(
        d_gate_up_b.reshape((chunks - half) * 2 * eff, slot_count), normed_two, eff, 4, "in_grads_b"
    )
    qkv_sum = weight_grad_scatter(d_qkv_flat.T, normed_one, 3 * qkv_cols // 4, 5, "qkv_grads")
    out_sum = weight_grad_scatter(mixed.T, d_one, qkv_cols // 2, 6, "mix_grads")
    grad_one = grad_one_own.astype(jnp.float32)
    norm_one_part = jnp.sum(grad_one * unit_one, axis=0)
    input_grad = grad_hidden + norm_back(grad_one, unit_one, inv_one, gain_one)
    part = jnp.concatenate(
        [
            router_part[: experts_total + 1],
            norm_one_part[None],
            norm_two_part[None],
            jnp.pad(bias_part.reshape(1, 3 * qkv_cols), ((0, 0), (0, model_width - 3 * qkv_cols))),
        ],
        axis=0,
    )
    dp_sums, all_sums = small_sums(part, 7)
    qkv_bias_grad = dp_sums[experts_total + 3, : 3 * qkv_cols].reshape(3, qkv_cols)
    router_grad = all_sums[:experts_total].T
    shared_gate_grad = all_sums[experts_total]
    norm_one_grad = all_sums[experts_total + 1]
    norm_two_grad = all_sums[experts_total + 2]
    own_cols = out_grads.shape[1]
    in_grads = jnp.concatenate([in_grads_a, in_grads_b], axis=0).reshape(chunks, 2, eff, own_cols)
    expert_in_grad = in_grads[:experts_total].transpose(0, 3, 1, 2)
    shared_in_grad = (
        in_grads[experts_total:].transpose(3, 1, 0, 2).reshape(own_cols, 2, shared_chunks * eff)
    )
    expert_out_grad = out_grads[: experts_total * eff].reshape(experts_total, eff, own_cols)
    shared_out_grad = out_grads[experts_total * eff :]
    return (
        output,
        input_grad,
        norm_one_grad,
        qkv_sum.reshape(3, qkv_cols, own_cols).transpose(2, 0, 1),
        qkv_bias_grad,
        out_sum,
        norm_two_grad,
        router_grad,
        expert_in_grad,
        expert_out_grad,
        shared_in_grad,
        shared_out_grad,
        shared_gate_grad,
    )


def solution(mesh):
    in_specs = (
        P(("dp", "tensor"), None),
        P("dp"),
        P("dp", None),
        P(("dp", "tensor"), None),
        P(),
        P(None, None, "tensor"),
        P(None, "tensor"),
        P("tensor", None),
        P(),
        P(),
        P(None, None, None, "tensor"),
        P(None, "tensor", None),
        P(None, None, "tensor"),
        P("tensor", None),
        P(),
    )
    out_specs = (
        P(("dp", "tensor"), None),
        P(("dp", "tensor"), None),
        P(),
        P("dp", None, "tensor"),
        P(None, "tensor"),
        P("tensor", "dp"),
        P(),
        P(),
        P(None, "dp", None, "tensor"),
        P(None, "tensor", "dp"),
        P("dp", None, "tensor"),
        P("tensor", "dp"),
        P(),
    )
    return jax.shard_map(
        on_device, mesh=mesh, in_specs=in_specs, out_specs=out_specs, check_vma=False
    )
```

```python
import functools

import jax
import jax.numpy as jnp
from jax import lax
from jax.experimental import pallas as pl
from jax.experimental.pallas import tpu as pltpu
from jax.sharding import PartitionSpec as P

HEAD_DIM = 128
MESH = pl.DeviceIdType.MESH
LA, LB, LC = 1, 2, 2
MIB = 2**20


epsilon = 1e-06
theta_base = 1000000.0
NT = (((1,), (1,)), ((), ()))
TN = (((0,), (0,)), ((), ()))


def rotary_tables(row_count, head_width):
    half_index = jnp.arange(head_width // 2).astype(jnp.float32)
    frequency = theta_base ** (-2.0 * half_index / head_width)
    angles = jnp.arange(row_count).astype(jnp.float32)[:, None] * frequency[None, :]
    sines = jnp.sin(angles)
    cosines = jnp.cos(angles)
    return (
        jnp.concatenate([cosines, cosines], axis=-1),
        jnp.concatenate([-sines, sines], axis=-1),
    )


def norm_back(d_normed, unit_rows, inverse, gain_vector):
    d_unit = d_normed * gain_vector
    return inverse * (d_unit - unit_rows * jnp.mean(d_unit * unit_rows, axis=-1, keepdims=True))


def rs_body(nc, cut, a_ref, b_ref, o_ref, o2_ref, own, sa, ra, kt, s1, r1, ku, s2, r2, sem_sa, sem_ra, sem_s1, sem_r1, sem_s2, sem_r2):
    i = pl.program_id(0)
    r, w = o_ref.shape
    hr = r // 2
    dp = lax.axis_index("dp")
    k = dp % 2
    x = (dp // 2) % 2
    y = dp // 4
    core_peer = y * 4 + x * 2 + (1 - k)
    x_peer = y * 4 + (1 - x) * 2 + k
    y_peer = (1 - y) * 4 + x * 2 + k

    def copy_a(c):
        return pltpu.make_async_remote_copy(
            src_ref=sa.at[c % 2], dst_ref=ra.at[c % 3], send_sem=sem_sa.at[c % 2], recv_sem=sem_ra.at[c % 3],
            device_id={"dp": core_peer}, device_id_type=MESH)

    def copy_1(c, half):
        return pltpu.make_async_remote_copy(
            src_ref=s1.at[c % 3, half], dst_ref=r1.at[c % 6, half], send_sem=sem_s1.at[c % 3, half],
            recv_sem=sem_r1.at[c % 6, half], device_id={"dp": y_peer if half else x_peer}, device_id_type=MESH)

    def copy_2(c, half):
        return pltpu.make_async_remote_copy(
            src_ref=s2.at[c % 2, half], dst_ref=r2.at[c % 6, half], send_sem=sem_s2.at[c % 2, half],
            recv_sem=sem_r2.at[c % 6, half], device_id={"dp": x_peer if half else y_peer}, device_id_type=MESH)

    @pl.when(i == 0)
    def _():
        barrier = pltpu.get_barrier_semaphore()
        for peer in (core_peer, x_peer, y_peer):
            pl.semaphore_signal(barrier, inc=1, device_id={"dp": peer}, device_id_type=MESH)
        pl.semaphore_wait(barrier, 3)

    @pl.when(jnp.logical_and(i >= LA + 3, i < nc + LA + 3))
    def _():
        copy_1(i - LA - 3, 0).wait_send()
        copy_1(i - LA - 3, 1).wait_send()

    @pl.when(jnp.logical_and(i >= LA, i < nc + LA))
    def _():
        c = i - LA
        copy_a(c).wait_recv()
        for half in range(2):
            rows = slice(half * hr, half * hr + hr)
            keep, other = (1, 2) if half else (2, 1)
            def total(role):
                return own[c % 2, role, rows, :] + ra[c % 3, role, rows, :].astype(jnp.float32)
            s1[c % 3, half, 0] = total(other).astype(jnp.bfloat16)
            s1[c % 3, half, 1] = total(3).astype(jnp.bfloat16)
            copy_1(c, half).start()
            kt[c % 3, half, 0] = total(0)
            kt[c % 3, half, 1] = total(keep)

    @pl.when(jnp.logical_and(i >= LA + LB, i < nc + LA + LB))
    def _():
        c = i - LA - LB
        @pl.when(c >= 2)
        def _():
            copy_2(c - 2, 0).wait_send()
            copy_2(c - 2, 1).wait_send()
        for half in range(2):
            copy_1(c, half).wait_recv()
            s2[c % 2, half] = (kt[c % 3, half, 1] + r1[c % 6, half, 1].astype(jnp.float32)).astype(jnp.bfloat16)
            copy_2(c, half).start()
            ku[c % 3, half] = kt[c % 3, half, 0] + r1[c % 6, half, 0].astype(jnp.float32)

    @pl.when(i >= LA + LB + LC)
    def _():
        c = i - LA - LB - LC
        for half in range(2):
            rows = slice(half * hr, half * hr + hr)
            copy_2(c, half).wait_recv()
            result = ku[c % 3, half] + r2[c % 6, half].astype(jnp.float32)

            @pl.when(c < cut)
            def _():
                o_ref[rows, :] = result

            @pl.when(c >= cut)
            def _():
                o2_ref[rows, :] = result

        @pl.when(c >= nc - 2)
        def _():
            copy_2(c, 0).wait_send()
            copy_2(c, 1).wait_send()

    @pl.when(jnp.logical_and(i >= 2, i < nc + 2))
    def _():
        copy_a(i - 2).wait_send()

    @pl.when(i < nc)
    def _():
        a = a_ref[...]
        targets = (y * 4 + x * 2, y * 4 + (1 - x) * 2, (1 - y) * 4 + x * 2, (1 - y) * 4 + (1 - x) * 2)
        for role in range(4):
            cols = pl.ds(pl.multiple_of((targets[role] + 1 - k) * w, w), w)
            sa[i % 2, role] = jnp.dot(a, b_ref[:, cols], preferred_element_type=jnp.float32).astype(jnp.bfloat16)
        copy_a(i).start()
        for role in range(4):
            cols = pl.ds(pl.multiple_of((targets[role] + k) * w, w), w)
            own[i % 2, role] = jnp.dot(a, b_ref[:, cols], preferred_element_type=jnp.float32)

def weight_grad_scatter_kernel(a, b, r, cid, name, first, count, cut):
    T = a.shape[1]
    R = count * r
    D = b.shape[1]
    w = D // 8
    nc = count
    L = LA + LB + LC
    f32, bf = jnp.float32, jnp.bfloat16
    dma = pltpu.SemaphoreType.DMA
    return pl.pallas_call(
        functools.partial(rs_body, nc, cut),
        grid=(nc + L,),
        in_specs=[pl.BlockSpec((r, T), lambda i: (jnp.minimum(i, nc - 1) + first, 0)),
                  pl.BlockSpec((T, D), lambda i: (0, 0), pipeline_mode=pl.Buffered(1))],
        out_specs=[
            pl.BlockSpec((r, w), lambda i: (jnp.clip(i - L, 0, cut - 1), 0)),
            pl.BlockSpec((r, w), lambda i: (jnp.clip(i - L - cut, 0, max(nc - cut, 1) - 1), 0)),
        ],
        out_shape=[
            jax.ShapeDtypeStruct((cut * r, w), f32),
            jax.ShapeDtypeStruct((max(nc - cut, 1) * r, w), f32),
        ],
        scratch_shapes=[
            pltpu.VMEM((2, 4, r, w), f32), pltpu.VMEM((2, 4, r, w), bf), pltpu.VMEM((3, 4, r, w), bf),
            pltpu.VMEM((3, 2, 2, r // 2, w), f32), pltpu.VMEM((3, 2, 2, r // 2, w), bf), pltpu.VMEM((6, 2, 2, r // 2, w), bf),
            pltpu.VMEM((3, 2, r // 2, w), f32), pltpu.VMEM((2, 2, r // 2, w), bf), pltpu.VMEM((6, 2, r // 2, w), bf),
            dma((2,)), dma((3,)), dma((3, 2)), dma((6, 2)), dma((2, 2)), dma((6, 2))],
        compiler_params=pltpu.CompilerParams(vmem_limit_bytes=48 * 2**20, collective_id=cid, has_side_effects=True),
        cost_estimate=pl.CostEstimate(flops=2 * R * T * D, bytes_accessed=2 * R * T + 2 * T * D + 4 * R * w, transcendentals=0),
        name=name)(a, b)


def ffn_body(
    experts, x_ref, d_ref, routes_ref, rw_ref, ei_ref, si_ref, eo_ref, so_ref,
    dgu_ref, s_ref, dn_ref, bt_ref, rg_ref, np_ref,
    dn_acc, bt_acc, probs_ref, w_ref, ds_ref, wi_buf, wd_buf, sem,
):
    c = pl.program_id(0)
    chunks = pl.num_programs(0)
    h = eo_ref.shape[1]
    slots, width = x_ref.shape

    def fetch(step):
        slot = step % 2

        @pl.when(step < experts)
        def _():
            pltpu.make_async_copy(ei_ref.at[step], wi_buf.at[slot], sem.at[0, slot]).start()
            pltpu.make_async_copy(eo_ref.at[step], wd_buf.at[slot], sem.at[1, slot]).start()

        @pl.when(step >= experts)
        def _():
            pltpu.make_async_copy(si_ref.at[step - experts], wi_buf.at[slot], sem.at[0, slot]).start()
            pltpu.make_async_copy(so_ref.at[step - experts], wd_buf.at[slot], sem.at[1, slot]).start()

    @pl.when(c == 0)
    def _():
        fetch(c)

    @pl.when(c + 1 < chunks)
    def _():
        fetch(c + 1)

    def picked():
        expert = lax.broadcasted_iota(jnp.int32, (experts, slots), 0)
        hit = jnp.zeros((experts, slots), jnp.float32)
        for j in range(routes_ref.shape[0]):
            hit = hit + jnp.where(routes_ref[j : j + 1, :] == expert, 1.0, 0.0)
        return hit

    @pl.when(c == 0)
    def _():
        logits = lax.dot_general(rw_ref[...], x_ref[...], NT, preferred_element_type=jnp.float32)
        raised = jnp.exp(logits[:experts] - jnp.max(logits[:experts], axis=0, keepdims=True))
        probs = raised / jnp.sum(raised, axis=0, keepdims=True)
        gate = 1.0 / (1.0 + jnp.exp(-logits[experts:]))
        probs_ref[...] = probs
        w_ref[:experts, :] = probs * picked()
        w_ref[experts:, :] = gate
        ds_ref[...] = jnp.zeros_like(ds_ref)
        dn_acc[...] = jnp.zeros_like(dn_acc)
        bt_acc[...] = jnp.zeros_like(bt_acc)

    row = pl.ds(jnp.minimum(c, experts), 1)
    slot = c % 2
    pltpu.make_async_copy(ei_ref.at[0], wi_buf.at[slot], sem.at[0, slot]).wait()
    pltpu.make_async_copy(eo_ref.at[0], wd_buf.at[slot], sem.at[1, slot]).wait()
    wi = wi_buf.at[slot]
    wd = wd_buf.at[slot]
    x = x_ref[...]
    g = lax.dot_general(wi[:h], x, NT, preferred_element_type=jnp.float32)
    u = lax.dot_general(wi[h:], x, NT, preferred_element_type=jnp.float32)
    p = lax.dot_general(wd[...], d_ref[...], NT, preferred_element_type=jnp.float32)
    w = w_ref[row, :]
    sg = 1.0 / (1.0 + jnp.exp(-g))
    si = g * sg
    inner = (si * u).astype(jnp.bfloat16).astype(jnp.float32)
    s = (w * inner).astype(jnp.bfloat16)
    s_ref[0] = s
    ds_ref[row, :] += jnp.sum(p * inner, axis=0, keepdims=True)
    di = w * p
    dg = (di * u * sg * (1.0 + g * (1.0 - sg))).astype(jnp.bfloat16)
    du = (di * si).astype(jnp.bfloat16)
    dgu_ref[0, :h] = dg
    dgu_ref[0, h:] = du
    dgu = jnp.concatenate([dg, du], axis=0)
    block = 512
    for n in range(0, width, block):
        cols = slice(n, n + block)
        dn_acc[:, cols] += lax.dot_general(dgu, wi[:, cols], TN, preferred_element_type=jnp.float32)
        bt_acc[:, cols] += lax.dot_general(s, wd[:, cols], TN, preferred_element_type=jnp.float32)

    @pl.when(c == chunks - 1)
    def _():
        probs = probs_ref[...]
        d_probs = ds_ref[:experts, :] * picked()
        d_logits = probs * (d_probs - jnp.sum(probs * d_probs, axis=0, keepdims=True))
        gate = w_ref[experts:, :]
        d_gate = ds_ref[experts:, :] * gate * (1.0 - gate)
        small = jnp.concatenate([d_logits, d_gate], axis=0)
        high = small.astype(jnp.bfloat16)
        low = (small - high.astype(jnp.float32)).astype(jnp.bfloat16)
        rg_ref[...] = jnp.dot(high, x_ref[...], preferred_element_type=jnp.float32) + jnp.dot(
            low, x_ref[...], preferred_element_type=jnp.float32
        )
        for n in range(0, width, block):
            cols = slice(n, n + block)
            extra = lax.dot_general(high, rw_ref[:, cols], TN, preferred_element_type=jnp.float32)
            extra += lax.dot_general(low, rw_ref[:, cols], TN, preferred_element_type=jnp.float32)
            total = dn_acc[:, cols] + extra
            dn_ref[:, cols] = total.astype(dn_ref.dtype)
            np_ref[:, cols] = jnp.sum(total * x_ref[:, cols].astype(jnp.float32), axis=0, keepdims=True)
        bt_ref[...] = bt_acc[...].astype(bt_ref.dtype)


def ffn(x, d_two, routes_t, router_rows, ei, si, eo, so):
    experts, h2, width = ei.shape
    chunks = experts + si.shape[0]
    h = h2 // 2
    slots = x.shape[0]
    rows = router_rows.shape[0]
    bf, f32 = jnp.bfloat16, jnp.float32
    anywhere = pl.BlockSpec(memory_space=pl.ANY)

    def whole(shape):
        return pl.BlockSpec(shape, lambda c: (0,) * len(shape), pipeline_mode=pl.Buffered(1))

    def chunk(shape):
        return pl.BlockSpec((1, *shape), lambda c: (c, 0, 0))

    return pl.pallas_call(
        functools.partial(ffn_body, experts),
        grid=(chunks,),
        in_specs=[
            whole((slots, width)), whole((slots, width)), whole(routes_t.shape), whole((rows, width)),
            anywhere, anywhere, anywhere, anywhere,
        ],
        out_specs=[
            chunk((h2, slots)), chunk((h, slots)), whole((slots, width)), whole((slots, width)), whole((rows, width)),
            whole((1, width)),
        ],
        out_shape=[
            jax.ShapeDtypeStruct((chunks, h2, slots), bf), jax.ShapeDtypeStruct((chunks, h, slots), bf),
            jax.ShapeDtypeStruct((slots, width), bf), jax.ShapeDtypeStruct((slots, width), bf),
            jax.ShapeDtypeStruct((rows, width), f32), jax.ShapeDtypeStruct((1, width), f32),
        ],
        scratch_shapes=[
            pltpu.VMEM((slots, width), f32), pltpu.VMEM((slots, width), f32),
            pltpu.VMEM((experts, slots), f32), pltpu.VMEM((rows, slots), f32), pltpu.VMEM((rows, slots), f32),
            pltpu.VMEM((2, h2, width), bf), pltpu.VMEM((2, h, width), bf), pltpu.SemaphoreType.DMA((2, 2)),
        ],
        compiler_params=pltpu.CompilerParams(vmem_limit_bytes=62 * MIB),
        cost_estimate=pl.CostEstimate(
            flops=12 * chunks * h * slots * width, bytes_accessed=10 * chunks * h * width + 16 * slots * width,
            transcendentals=chunks * h * slots,
        ),
        name="ffn",
    )(x, d_two, routes_t, router_rows, ei, si, eo, so)


def turn(v):
    half = v.shape[1] // 2
    return jnp.concatenate([v[:, half:], v[:, :half]], axis=1)


def qkv_body(x_ref, w_ref, bias_ref, cos_ref, sin_ref, out_ref):
    j = pl.program_id(0)
    cols = w_ref.shape[2]
    y = jnp.dot(x_ref[...], w_ref[0], preferred_element_type=jnp.float32)
    y = y + bias_ref[0].astype(jnp.float32)

    @pl.when(j < 2)
    def _():
        for head in range(cols // HEAD_DIM):
            place = slice(head * HEAD_DIM, (head + 1) * HEAD_DIM)
            v = y[:, place]
            out_ref[0, :, place] = (v * cos_ref[...] + turn(v) * sin_ref[...]).astype(out_ref.dtype)

    @pl.when(j == 2)
    def _():
        out_ref[0] = y.astype(out_ref.dtype)


def project_qkv(x, w, bias, cos_table, sin_table):
    slots, width = x.shape
    cols = w.shape[2]
    table = pl.BlockSpec((slots, HEAD_DIM), lambda j: (0, 0), pipeline_mode=pl.Buffered(1))
    return pl.pallas_call(
        qkv_body,
        grid=(3,),
        in_specs=[
            pl.BlockSpec((slots, width), lambda j: (0, 0), pipeline_mode=pl.Buffered(1)),
            pl.BlockSpec((1, width, cols), lambda j: (j, 0, 0)),
            pl.BlockSpec((1, 1, cols), lambda j: (j, 0, 0)),
            table, table,
        ],
        out_specs=pl.BlockSpec((1, slots, cols), lambda j: (j, 0, 0)),
        out_shape=jax.ShapeDtypeStruct((3, slots, cols), jnp.bfloat16),
        compiler_params=pltpu.CompilerParams(vmem_limit_bytes=48 * MIB),
        cost_estimate=pl.CostEstimate(
            flops=6 * slots * width * cols, bytes_accessed=2 * slots * width + 6 * width * cols, transcendentals=0
        ),
        name="project_qkv",
    )(x, w, bias, cos_table, sin_table)


def block_probs(length_ref, q, k, start):
    s = lax.dot_general(q, k, NT, preferred_element_type=jnp.float32) * (HEAD_DIM**-0.5)
    row = lax.broadcasted_iota(jnp.int32, s.shape, 0) + start
    col = lax.broadcasted_iota(jnp.int32, s.shape, 1)
    s = jnp.where((col <= row) & (col < length_ref[0]), s, -1000000000.0)
    e = jnp.exp(s - jnp.max(s, axis=1, keepdims=True))
    return e * (1.0 / jnp.sum(e, axis=1, keepdims=True))


def attend_body(rows, length_ref, q_ref, k_ref, v_ref, mixed_ref, mixed_t_ref):
    for start in range(0, q_ref.shape[1], rows):
        here, end = slice(start, start + rows), start + rows
        p = block_probs(length_ref, q_ref[0, here, :], k_ref[0, :end, :], start)
        mixed = jnp.dot(p.astype(jnp.bfloat16), v_ref[0, :end, :], preferred_element_type=jnp.float32)
        mixed_ref[here, :] = mixed.astype(mixed_ref.dtype)
        mixed_t_ref[:, here] = mixed.T.astype(mixed_ref.dtype)


def attend(lengths, qkv):
    _, slots, cols = qkv.shape
    rows = min(256, slots)

    def part(j):
        return pl.BlockSpec((1, slots, HEAD_DIM), lambda h: (j, 0, h))

    return pl.pallas_call(
        functools.partial(attend_body, rows),
        grid=(cols // HEAD_DIM,),
        in_specs=[pl.BlockSpec(memory_space=pltpu.SMEM), part(0), part(1), part(2)],
        out_specs=[
            pl.BlockSpec((slots, HEAD_DIM), lambda h: (0, h)), pl.BlockSpec((HEAD_DIM, slots), lambda h: (h, 0)),
        ],
        out_shape=[
            jax.ShapeDtypeStruct((slots, cols), jnp.bfloat16), jax.ShapeDtypeStruct((cols, slots), jnp.bfloat16),
        ],
        compiler_params=pltpu.CompilerParams(vmem_limit_bytes=32 * MIB),
        cost_estimate=pl.CostEstimate(
            flops=4 * slots * slots * cols, bytes_accessed=10 * slots * cols, transcendentals=slots * slots * cols // HEAD_DIM
        ),
        name="attend",
    )(lengths, qkv, qkv, qkv)


def attend_back_body(
    rows, length_ref, q_ref, k_ref, v_ref, dm_ref, cos_ref, sin_ref, out_ref, out_t_ref, bias_ref, dk_acc, dv_acc
):
    slots = q_ref.shape[1]
    scale = HEAD_DIM**-0.5
    bf, f32 = jnp.bfloat16, jnp.float32

    def finish(j, here, grad):
        if j < 2:
            grad = grad * cos_ref[here, :] - turn(grad) * sin_ref[here, :]
        low = grad.astype(bf)
        out_ref[j, here, :] = low
        out_t_ref[j, :, here] = grad.T.astype(bf)
        return jnp.sum(low.astype(f32), axis=0, keepdims=True)

    dq_sum = jnp.zeros((1, HEAD_DIM), f32)
    starts = list(range(0, slots, rows))[::-1]
    for start in starts:
        here, end = slice(start, start + rows), start + rows
        q, k, v, dm = q_ref[0, here, :], k_ref[0, :end, :], v_ref[0, :end, :], dm_ref[here, :]
        p = block_probs(length_ref, q, k, start)
        dp = lax.dot_general(dm, v, NT, preferred_element_type=f32)
        ds = (p * (dp - jnp.sum(p * dp, axis=1, keepdims=True))).astype(bf)
        dq_sum += finish(0, here, jnp.dot(ds, k, preferred_element_type=f32) * scale)
        dk = lax.dot_general(ds, q, TN, preferred_element_type=f32) * scale
        dv = lax.dot_general(p.astype(bf), dm, TN, preferred_element_type=f32)
        if start == starts[0]:
            dk_acc[...] = dk
            dv_acc[...] = dv
        else:
            dk_acc[:end, :] += dk
            dv_acc[:end, :] += dv
    every = slice(0, slots)
    bias_ref[0] = dq_sum
    bias_ref[1] = finish(1, every, dk_acc[...])
    bias_ref[2] = finish(2, every, dv_acc[...])


def attend_back(lengths, qkv, d_mixed, cos_table, sin_table):
    _, slots, cols = qkv.shape
    rows = min(256, slots)
    bf, f32 = jnp.bfloat16, jnp.float32

    def part(j):
        return pl.BlockSpec((1, slots, HEAD_DIM), lambda h: (j, 0, h))

    table = pl.BlockSpec((slots, HEAD_DIM), lambda h: (0, 0), pipeline_mode=pl.Buffered(1))
    return pl.pallas_call(
        functools.partial(attend_back_body, rows),
        grid=(cols // HEAD_DIM,),
        in_specs=[
            pl.BlockSpec(memory_space=pltpu.SMEM), part(0), part(1), part(2),
            pl.BlockSpec((slots, HEAD_DIM), lambda h: (0, h)), table, table,
        ],
        out_specs=[
            pl.BlockSpec((3, slots, HEAD_DIM), lambda h: (0, 0, h)), pl.BlockSpec((3, HEAD_DIM, slots), lambda h: (0, h, 0)),
            pl.BlockSpec((3, 1, HEAD_DIM), lambda h: (0, 0, h)),
        ],
        out_shape=[
            jax.ShapeDtypeStruct((3, slots, cols), bf), jax.ShapeDtypeStruct((3, cols, slots), bf),
            jax.ShapeDtypeStruct((3, 1, cols), f32),
        ],
        scratch_shapes=[pltpu.VMEM((slots, HEAD_DIM), f32), pltpu.VMEM((slots, HEAD_DIM), f32)],
        compiler_params=pltpu.CompilerParams(vmem_limit_bytes=40 * MIB),
        cost_estimate=pl.CostEstimate(
            flops=10 * slots * slots * cols, bytes_accessed=20 * slots * cols, transcendentals=slots * slots * cols // HEAD_DIM
        ),
        name="attend_back",
    )(lengths, qkv, qkv, qkv, d_mixed, cos_table, sin_table)


def qkv_back_body(d_ref, w_ref, x_ref, out_ref, np_ref):
    total = lax.dot_general(d_ref[0], w_ref[0], NT, preferred_element_type=jnp.float32)
    for j in range(1, 3):
        total += lax.dot_general(d_ref[j], w_ref[j], NT, preferred_element_type=jnp.float32)
    out_ref[...] = total.astype(out_ref.dtype)
    np_ref[...] = jnp.sum(total * x_ref[...].astype(jnp.float32), axis=0, keepdims=True)


def qkv_back(d_qkv, w, x):
    _, slots, cols = d_qkv.shape
    width = w.shape[1]
    block = 512
    return pl.pallas_call(
        qkv_back_body,
        grid=(width // block,),
        in_specs=[
            pl.BlockSpec((3, slots, cols), lambda n: (0, 0, 0), pipeline_mode=pl.Buffered(1)),
            pl.BlockSpec((3, block, cols), lambda n: (0, n, 0)),
            pl.BlockSpec((slots, block), lambda n: (0, n)),
        ],
        out_specs=[pl.BlockSpec((slots, block), lambda n: (0, n)), pl.BlockSpec((1, block), lambda n: (0, n))],
        out_shape=[
            jax.ShapeDtypeStruct((slots, width), jnp.bfloat16), jax.ShapeDtypeStruct((1, width), jnp.float32),
        ],
        compiler_params=pltpu.CompilerParams(vmem_limit_bytes=48 * MIB),
        cost_estimate=pl.CostEstimate(
            flops=6 * slots * width * cols, bytes_accessed=4 * slots * width + 6 * width * cols, transcendentals=0
        ),
        name="qkv_back",
    )(d_qkv, w, x)


def weight_grad_scatter(a, b, r, cid, name, first=0, count=None, cut=None):
    count = a.shape[0] // r if count is None else count
    cut = count if cut is None else cut
    if lax.axis_size("dp") == 8:
        return weight_grad_scatter_kernel(a, b, r, cid, name, first, count, cut)
    product = jnp.dot(a[first * r : (first + count) * r], b, preferred_element_type=jnp.float32)
    result = lax.psum_scatter(
        product.astype(jnp.bfloat16), "dp", scatter_dimension=1, tiled=True
    ).astype(jnp.float32)
    return result[: cut * r], result[cut * r :]


def gather_body(own_ref, out_ref, local_sem, send_left, recv_left, send_right, recv_right):
    me = lax.axis_index("tensor")
    size = lax.axis_size("tensor")
    rows = own_ref.shape[0]
    has_left, has_right = me > 0, me < size - 1

    def block(owner):
        return out_ref.at[pl.ds(pl.multiple_of(owner * rows, rows), rows)]

    def to_left(step):
        source = own_ref if step == 0 else block(me + step)
        return pltpu.make_async_remote_copy(
            src_ref=source, dst_ref=block(me + step), send_sem=send_left.at[step], recv_sem=recv_left.at[step],
            device_id={"tensor": me - 1}, device_id_type=MESH,
        )

    def from_right(step):
        return pltpu.make_async_remote_copy(
            src_ref=own_ref, dst_ref=block(me + 1 + step), send_sem=send_left.at[step], recv_sem=recv_left.at[step],
            device_id={"tensor": me + 1}, device_id_type=MESH,
        )

    def to_right(step):
        source = own_ref if step == 0 else block(me - step)
        return pltpu.make_async_remote_copy(
            src_ref=source, dst_ref=block(me - step), send_sem=send_right.at[step], recv_sem=recv_right.at[step],
            device_id={"tensor": me + 1}, device_id_type=MESH,
        )

    def from_left(step):
        return pltpu.make_async_remote_copy(
            src_ref=own_ref, dst_ref=block(me - 1 - step), send_sem=send_right.at[step], recv_sem=recv_right.at[step],
            device_id={"tensor": me - 1}, device_id_type=MESH,
        )

    barrier = pltpu.get_barrier_semaphore()

    @pl.when(has_left)
    def _():
        pl.semaphore_signal(barrier, inc=1, device_id={"tensor": me - 1}, device_id_type=MESH)

    @pl.when(has_right)
    def _():
        pl.semaphore_signal(barrier, inc=1, device_id={"tensor": me + 1}, device_id_type=MESH)

    pl.semaphore_wait(barrier, has_left.astype(jnp.int32) + has_right.astype(jnp.int32))
    local = pltpu.make_async_copy(own_ref, block(me), local_sem)
    local.start()
    for step in range(size):
        if step > 0:
            @pl.when(me + step < size)
            def _():
                from_right(step - 1).wait_recv()

        @pl.when(has_left & (me + step < size))
        def _():
            to_left(step).start()

        if step > 0:
            @pl.when(me - step >= 0)
            def _():
                from_left(step - 1).wait_recv()

        @pl.when(has_right & (me - step >= 0))
        def _():
            to_right(step).start()

    for step in range(size):
        @pl.when(has_left & (me + step < size))
        def _():
            to_left(step).wait_send()

        @pl.when(has_right & (me - step >= 0))
        def _():
            to_right(step).wait_send()

    local.wait()


def gather_rows(own, cid):
    size = lax.axis_size("tensor")
    rows, width = own.shape
    return pl.pallas_call(
        gather_body,
        in_specs=[pl.BlockSpec(memory_space=pl.ANY)],
        out_specs=pl.BlockSpec(memory_space=pl.ANY),
        out_shape=jax.ShapeDtypeStruct((rows * size, width), own.dtype),
        scratch_shapes=[
            pltpu.SemaphoreType.DMA, *[pltpu.SemaphoreType.DMA((size,))] * 4,
        ],
        compiler_params=pltpu.CompilerParams(collective_id=cid, has_side_effects=True),
        cost_estimate=pl.CostEstimate(flops=0, bytes_accessed=2 * rows * size * width * 2, transcendentals=0),
        name="gather_rows",
    )(own)


def sums_body(
    local_rows, part_ref, out_ref, from_dp, mine, from_tensor, send_dp, recv_dp, send_t, recv_t, send_out, recv_out
):
    size_dp, size_t = lax.axis_size("dp"), lax.axis_size("tensor")
    me_dp, me_t = lax.axis_index("dp"), lax.axis_index("tensor")
    width = mine.shape[1]

    def piece(ref, owner):
        return ref.at[:, pl.ds(pl.multiple_of(owner * width, width), width)]

    barrier = pltpu.get_barrier_semaphore()
    for step in range(1, size_dp):
        peer = lax.rem(me_dp + step, size_dp)
        pl.semaphore_signal(barrier, inc=1, device_id={"dp": peer}, device_id_type=MESH)
    for step in range(1, size_t):
        peer = lax.rem(me_t + step, size_t)
        pl.semaphore_signal(barrier, inc=1, device_id={"tensor": peer}, device_id_type=MESH)
    pl.semaphore_wait(barrier, size_dp + size_t - 2)

    def send(source, target, axis, step, send_sem, recv_sem):
        me, size = (me_dp, size_dp) if axis == "dp" else (me_t, size_t)
        copy = pltpu.make_async_remote_copy(
            src_ref=source, dst_ref=target, send_sem=send_sem.at[step], recv_sem=recv_sem.at[step],
            device_id={axis: lax.rem(me + step, size)}, device_id_type=MESH,
        )
        copy.start()
        return copy

    first = [
        send(piece(part_ref, lax.rem(me_dp + step, size_dp)), from_dp.at[step], "dp", step, send_dp, recv_dp)
        for step in range(1, size_dp)
    ]
    total = piece(part_ref, me_dp)[...]
    for step, copy in enumerate(first, 1):
        copy.wait_recv()
        total = total + from_dp[step]
    mine[...] = total
    second = [send(mine, from_tensor.at[step], "tensor", step, send_t, recv_t) for step in range(1, size_t)]
    for step, copy in enumerate(second, 1):
        copy.wait_recv()
        total = total + from_tensor[step]
    here = piece(out_ref, me_dp)
    here[...] = total
    piece(out_ref.at[local_rows:], me_dp)[...] = mine[local_rows:, :]
    third = [send(here, here, "dp", step, send_out, recv_out) for step in range(1, size_dp)]
    for copy in third:
        copy.wait_recv()
    for copy in first + second + third:
        copy.wait_send()


def small_sums(part, local_rows, cid):
    size_dp, size_t = lax.axis_size("dp"), lax.axis_size("tensor")
    rows, width = part.shape[0], part.shape[1] // size_dp
    vmem = pl.BlockSpec(memory_space=pltpu.VMEM)
    dma = pltpu.SemaphoreType.DMA
    f32 = jnp.float32
    return pl.pallas_call(
        functools.partial(sums_body, local_rows),
        in_specs=[vmem],
        out_specs=vmem,
        out_shape=jax.ShapeDtypeStruct(part.shape, f32),
        scratch_shapes=[
            pltpu.VMEM((size_dp, rows, width), f32), pltpu.VMEM((rows, width), f32), pltpu.VMEM((size_t, rows, width), f32),
            dma((size_dp,)), dma((size_dp,)), dma((size_t,)), dma((size_t,)), dma((size_dp,)), dma((size_dp,)),
        ],
        compiler_params=pltpu.CompilerParams(collective_id=cid, has_side_effects=True),
        name="small_sums",
    )(part)


def on_device(
    tokens,
    lengths,
    routes,
    cotangent,
    norm_one,
    qkv_weight,
    qkv_bias,
    out_weight,
    norm_two,
    router_weight,
    expert_in,
    expert_out,
    shared_in,
    shared_out,
    shared_gate,
):
    own_rows = tokens.shape[0]
    slot_count = routes.shape[0]
    model_width = tokens.shape[1]
    qkv_cols = qkv_weight.shape[2]
    local_heads = qkv_cols // HEAD_DIM
    experts = router_weight.shape[1]
    eff = expert_in.shape[3]
    shared_chunks = shared_out.shape[0] // eff
    chunks = experts + shared_chunks
    bf = jnp.bfloat16
    qkv_cols = qkv_weight.shape[2]
    length = lengths[0]
    tensor_index = lax.axis_index("tensor")
    first_row = tensor_index * own_rows
    live_own = (first_row + jnp.arange(own_rows) < length).astype(jnp.float32)[:, None]
    tokens_f = tokens.astype(jnp.float32)
    gain_one = norm_one.astype(jnp.float32)
    gain_two = norm_two.astype(jnp.float32)
    inv_one = lax.rsqrt(jnp.mean(tokens_f * tokens_f, axis=-1, keepdims=True) + epsilon)
    unit_one = tokens_f * inv_one
    normed_one = lax.all_gather((unit_one * gain_one).astype(bf), "tensor", axis=0, tiled=True)
    cos_table, sin_table = rotary_tables(slot_count, HEAD_DIM)
    qkv_w = qkv_weight.transpose(1, 0, 2)
    ei = expert_in.transpose(0, 2, 3, 1).reshape(experts, 2 * eff, model_width)
    eo = expert_out
    si = (
        shared_in.reshape(model_width, 2, shared_chunks, eff)
        .transpose(2, 1, 3, 0)
        .reshape(shared_chunks, 2 * eff, model_width)
    )
    so = shared_out.reshape(shared_chunks, eff, model_width)
    router_rows = jnp.concatenate(
        [
            router_weight.T,
            shared_gate[None],
            jnp.zeros((-(experts + 1) % 16, model_width), bf),
        ],
        axis=0,
    )
    grad_out = cotangent.astype(jnp.float32) * live_own
    d_two_own = (live_own * grad_out).astype(bf)
    normed_one, si, router_rows, cos_table, sin_table, d_two_own = lax.optimization_barrier(
        (normed_one, si, router_rows, cos_table, sin_table, d_two_own)
    )
    qkv = project_qkv(normed_one, qkv_w, qkv_bias[:, None, :], cos_table, sin_table)
    mixed, mixed_t = attend(lengths, qkv)
    branch_partial = jnp.dot(mixed, out_weight, preferred_element_type=jnp.float32).astype(bf)
    d_two_own, branch_partial = lax.optimization_barrier((d_two_own, branch_partial))
    branch_one = lax.psum_scatter(branch_partial, "tensor", scatter_dimension=0, tiled=True)
    d_two = gather_rows(d_two_own, 1)
    branch_one, d_two = lax.optimization_barrier((branch_one, d_two))
    hidden = tokens_f + live_own * branch_one.astype(jnp.float32)
    inv_two = lax.rsqrt(jnp.mean(hidden * hidden, axis=-1, keepdims=True) + epsilon)
    unit_two = hidden * inv_two
    normed_two = lax.all_gather((unit_two * gain_two).astype(bf), "tensor", axis=0, tiled=True)
    d_gate_up, scaled_inner, d_normed, combined, router_part, norm_two_part = ffn(
        normed_two, d_two, routes.T, router_rows, ei, si, eo, so
    )
    d_gate_up = d_gate_up.reshape(chunks * 2 * eff, slot_count)
    scaled_inner = scaled_inner.reshape(chunks * eff, slot_count)
    grad_two = lax.psum_scatter(d_normed, "tensor", scatter_dimension=0, tiled=True)
    out_grads, shared_out_grad = weight_grad_scatter(
        scaled_inner, d_two, eff, 2, "down_grads", cut=experts
    )
    grad_two = grad_two.astype(jnp.float32)
    grad_hidden = grad_out + norm_back(grad_two, unit_two, inv_two, gain_two)
    d_one_own, out_grads = lax.optimization_barrier(
        ((live_own * grad_hidden).astype(bf), out_grads)
    )
    d_one = lax.all_gather(d_one_own, "tensor", axis=0, tiled=True)
    d_gate_up, _ = lax.optimization_barrier((d_gate_up, d_one_own))
    in_grads_a, _ = weight_grad_scatter(
        d_gate_up, normed_two, eff, 3, "expert_in_grads", 0, 2 * experts
    )
    d_one, in_grads_a, combined, d_gate_up = lax.optimization_barrier(
        (d_one, in_grads_a, combined, d_gate_up)
    )
    branch_two = lax.psum_scatter(combined, "tensor", scatter_dimension=0, tiled=True)
    d_mixed = lax.dot_general(d_one, out_weight, NT, preferred_element_type=jnp.float32).astype(bf)
    d_qkv, d_qkv_t, bias_part = attend_back(lengths, qkv, d_mixed, cos_table, sin_table)
    grad_one, norm_one_part = qkv_back(d_qkv, qkv_w, normed_one)
    grad_one, d_gate_up, d_qkv_t, mixed_t = lax.optimization_barrier(
        (grad_one, d_gate_up, d_qkv_t, mixed_t)
    )
    grad_one_own = lax.psum_scatter(grad_one, "tensor", scatter_dimension=0, tiled=True)
    part = jnp.concatenate(
        [
            router_part[: experts + 1],
            norm_one_part / gain_one[None],
            norm_two_part / gain_two[None],
            jnp.pad(bias_part.reshape(1, 3 * qkv_cols), ((0, 0), (0, model_width - 3 * qkv_cols))),
        ],
        axis=0,
    )
    sums = small_sums(part, experts + 3, 7)
    in_grads_b, _ = weight_grad_scatter(
        d_gate_up, normed_two, eff, 4, "shared_in_grads", 2 * experts, 2 * shared_chunks
    )
    qkv_sum, _ = weight_grad_scatter(
        d_qkv_t.reshape(3 * qkv_cols, slot_count), normed_one, 3 * qkv_cols // 4, 5, "qkv_grads"
    )
    out_sum, _ = weight_grad_scatter(mixed_t, d_one, qkv_cols // 2, 6, "mix_grads")
    output = (hidden + live_own * branch_two.astype(jnp.float32)).astype(bf)
    grad_one = grad_one_own.astype(jnp.float32)
    input_grad = grad_hidden + norm_back(grad_one, unit_one, inv_one, gain_one)
    qkv_bias_grad = sums[experts + 3, : 3 * qkv_cols].reshape(3, qkv_cols)
    own_cols = out_grads.shape[1]
    expert_in_grad = in_grads_a.reshape(experts, 2, eff, own_cols).transpose(0, 3, 1, 2)
    shared_in_grad = (
        in_grads_b.reshape(shared_chunks, 2, eff, own_cols)
        .transpose(3, 1, 0, 2)
        .reshape(own_cols, 2, shared_chunks * eff)
    )
    return (
        output,
        input_grad,
        sums[experts + 1],
        qkv_sum.reshape(3, qkv_cols, own_cols).transpose(2, 0, 1),
        qkv_bias_grad,
        out_sum,
        sums[experts + 2],
        sums[:experts].T,
        expert_in_grad,
        out_grads.reshape(experts, eff, own_cols),
        shared_in_grad,
        shared_out_grad,
        sums[experts],
    )


def solution(mesh):
    in_specs = (
        P(("dp", "tensor"), None),
        P("dp"),
        P("dp", None),
        P(("dp", "tensor"), None),
        P(),
        P(None, None, "tensor"),
        P(None, "tensor"),
        P("tensor", None),
        P(),
        P(),
        P(None, None, None, "tensor"),
        P(None, "tensor", None),
        P(None, None, "tensor"),
        P("tensor", None),
        P(),
    )
    out_specs = (
        P(("dp", "tensor"), None),
        P(("dp", "tensor"), None),
        P(),
        P("dp", None, "tensor"),
        P(None, "tensor"),
        P("tensor", "dp"),
        P(),
        P(),
        P(None, "dp", None, "tensor"),
        P(None, "tensor", "dp"),
        P("dp", None, "tensor"),
        P("tensor", "dp"),
        P(),
    )
    return jax.shard_map(
        on_device, mesh=mesh, in_specs=in_specs, out_specs=out_specs, check_vma=False
    )
```

```python
import functools

import jax
import jax.numpy as jnp
from jax import lax
from jax.experimental import pallas as pl
from jax.experimental.pallas import tpu as pltpu
from jax.sharding import PartitionSpec as P

HEAD_DIM = 128
MESH = pl.DeviceIdType.MESH
LA, LB, LC = 1, 2, 2
FFN_LAGS = (1, 1, 1)
MIB = 2**20


epsilon = 1e-06
theta_base = 1000000.0
NT = (((1,), (1,)), ((), ()))
TN = (((0,), (0,)), ((), ()))


def rotary_tables(row_count, head_width):
    half_index = jnp.arange(head_width // 2).astype(jnp.float32)
    frequency = theta_base ** (-2.0 * half_index / head_width)
    angles = jnp.arange(row_count).astype(jnp.float32)[:, None] * frequency[None, :]
    sines = jnp.sin(angles)
    cosines = jnp.cos(angles)
    return (
        jnp.concatenate([cosines, cosines], axis=-1),
        jnp.concatenate([-sines, sines], axis=-1),
    )


def norm_back(d_normed, unit_rows, inverse, gain_vector):
    d_unit = d_normed * gain_vector
    return inverse * (d_unit - unit_rows * jnp.mean(d_unit * unit_rows, axis=-1, keepdims=True))


def scatter_scratch(r, w):
    f32, bf = jnp.float32, jnp.bfloat16
    dma = pltpu.SemaphoreType.DMA
    h = r // 2
    return [
        pltpu.VMEM((2, 4, r, w), f32), pltpu.VMEM((2, 4, r, w), bf), pltpu.VMEM((3, 4, r, w), bf),
        pltpu.VMEM((3, 2, 2, h, w), f32), pltpu.VMEM((3, 2, 2, h, w), bf), pltpu.VMEM((6, 2, 2, h, w), bf),
        pltpu.VMEM((3, 2, h, w), f32), pltpu.VMEM((2, 2, h, w), bf), pltpu.VMEM((6, 2, h, w), bf),
        dma((2,)), dma((3,)), dma((3, 2)), dma((6, 2)), dma((2, 2)), dma((6, 2)),
    ]


def scatter_steps(i, nc, lags, w, scratch, store):
    own, sa, ra, kt, s1, r1, ku, s2, r2, sem_sa, sem_ra, sem_s1, sem_r1, sem_s2, sem_r2 = scratch
    la, lb, lc = lags
    keep_1 = min(3, lb + lc)
    hr = own.shape[2] // 2
    dp = lax.axis_index("dp")
    k = dp % 2
    x = (dp // 2) % 2
    y = dp // 4
    core_peer = y * 4 + x * 2 + (1 - k)
    x_peer = y * 4 + (1 - x) * 2 + k
    y_peer = (1 - y) * 4 + x * 2 + k

    def copy_a(c):
        return pltpu.make_async_remote_copy(
            src_ref=sa.at[c % 2], dst_ref=ra.at[c % 3], send_sem=sem_sa.at[c % 2], recv_sem=sem_ra.at[c % 3],
            device_id={"dp": core_peer}, device_id_type=MESH,
        )

    def copy_1(c, half):
        return pltpu.make_async_remote_copy(
            src_ref=s1.at[c % 3, half], dst_ref=r1.at[c % 6, half], send_sem=sem_s1.at[c % 3, half],
            recv_sem=sem_r1.at[c % 6, half], device_id={"dp": y_peer if half else x_peer}, device_id_type=MESH,
        )

    def copy_2(c, half):
        return pltpu.make_async_remote_copy(
            src_ref=s2.at[c % 2, half], dst_ref=r2.at[c % 6, half], send_sem=sem_s2.at[c % 2, half],
            recv_sem=sem_r2.at[c % 6, half], device_id={"dp": x_peer if half else y_peer}, device_id_type=MESH,
        )

    @pl.when(i == 0)
    def _():
        barrier = pltpu.get_barrier_semaphore()
        for peer in (core_peer, x_peer, y_peer):
            pl.semaphore_signal(barrier, inc=1, device_id={"dp": peer}, device_id_type=MESH)
        pl.semaphore_wait(barrier, 3)

    @pl.when((i >= la + keep_1) & (i < nc + la + keep_1))
    def _():
        copy_1(i - la - keep_1, 0).wait_send()
        copy_1(i - la - keep_1, 1).wait_send()

    @pl.when((i >= la) & (i < nc + la))
    def _():
        c = i - la
        copy_a(c).wait_recv()
        for half in range(2):
            rows = slice(half * hr, half * hr + hr)
            keep, other = (1, 2) if half else (2, 1)

            def total(role):
                return own[c % 2, role, rows, :] + ra[c % 3, role, rows, :].astype(jnp.float32)

            s1[c % 3, half, 0] = total(other).astype(jnp.bfloat16)
            s1[c % 3, half, 1] = total(3).astype(jnp.bfloat16)
            copy_1(c, half).start()
            kt[c % 3, half, 0] = total(0)
            kt[c % 3, half, 1] = total(keep)

    @pl.when((i >= la + lb) & (i < nc + la + lb))
    def _():
        c = i - la - lb

        @pl.when(c >= 2)
        def _():
            copy_2(c - 2, 0).wait_send()
            copy_2(c - 2, 1).wait_send()

        for half in range(2):
            copy_1(c, half).wait_recv()
            s2[c % 2, half] = (kt[c % 3, half, 1] + r1[c % 6, half, 1].astype(jnp.float32)).astype(jnp.bfloat16)
            copy_2(c, half).start()
            ku[c % 3, half] = kt[c % 3, half, 0] + r1[c % 6, half, 0].astype(jnp.float32)

    @pl.when(i >= la + lb + lc)
    def _():
        c = i - la - lb - lc
        for half in range(2):
            copy_2(c, half).wait_recv()
            store(c, slice(half * hr, half * hr + hr), ku[c % 3, half] + r2[c % 6, half].astype(jnp.float32))

        @pl.when(c >= nc - 2)
        def _():
            copy_2(c, 0).wait_send()
            copy_2(c, 1).wait_send()

    @pl.when((i >= 2) & (i < nc + 2))
    def _():
        copy_a(i - 2).wait_send()

    def send(product):
        targets = (y * 4 + x * 2, y * 4 + (1 - x) * 2, (1 - y) * 4 + x * 2, (1 - y) * 4 + (1 - x) * 2)

        def cols(role, core):
            return pl.ds(pl.multiple_of((targets[role] + core) * w, w), w)

        for role in range(4):
            sa[i % 2, role] = product(cols(role, 1 - k)).astype(jnp.bfloat16)
        copy_a(i).start()
        for role in range(4):
            own[i % 2, role] = product(cols(role, k))

    return send


def rs_body(nc, cut, pairs, *refs):
    a_refs, b_refs = refs[:pairs], refs[pairs : 2 * pairs]
    o_ref, o2_ref = refs[2 * pairs : 2 * pairs + 2]
    i = pl.program_id(0)

    def store(c, rows, result):
        @pl.when(c < cut)
        def _():
            o_ref[rows, :] = result

        @pl.when(c >= cut)
        def _():
            o2_ref[rows, :] = result

    send = scatter_steps(i, nc, (LA, LB, LC), o_ref.shape[1], refs[2 * pairs + 2 :], store)

    @pl.when(i < nc)
    def _():
        def product(cols):
            total = jnp.dot(a_refs[0][...], b_refs[0][:, cols], preferred_element_type=jnp.float32)
            for a_ref, b_ref in zip(a_refs[1:], b_refs[1:]):
                total += jnp.dot(a_ref[...], b_ref[:, cols], preferred_element_type=jnp.float32)
            return total

        send(product)


def scatter_outs(nc, cut, lag, r, w):
    rest = max(nc - cut, 1)
    specs = [
        pl.BlockSpec((r, w), lambda i: (jnp.clip(i - lag, 0, cut - 1), 0)),
        pl.BlockSpec((r, w), lambda i: (jnp.clip(i - lag - cut, 0, rest - 1), 0)),
    ]
    return specs, [jax.ShapeDtypeStruct((n * r, w), jnp.float32) for n in (cut, rest)]


def weight_grad_scatter_kernel(a_list, b_list, r, cid, name, first, count, cut):
    D = b_list[0].shape[1]
    T = sum(b.shape[0] for b in b_list)
    w = D // 8
    lag = LA + LB + LC
    out_specs, out_shape = scatter_outs(count, cut, lag, r, w)
    return pl.pallas_call(
        functools.partial(rs_body, count, cut, len(a_list)),
        grid=(count + lag,),
        in_specs=[
            *[pl.BlockSpec((r, a.shape[1]), lambda i: (jnp.minimum(i, count - 1) + first, 0)) for a in a_list],
            *[pl.BlockSpec(b.shape, lambda i: (0, 0), pipeline_mode=pl.Buffered(1)) for b in b_list],
        ],
        out_specs=out_specs,
        out_shape=out_shape,
        scratch_shapes=scatter_scratch(r, w),
        compiler_params=pltpu.CompilerParams(vmem_limit_bytes=48 * MIB, collective_id=cid, has_side_effects=True),
        cost_estimate=pl.CostEstimate(
            flops=2 * count * r * T * D, bytes_accessed=2 * count * r * T + 2 * T * D + 4 * count * r * w, transcendentals=0
        ),
        name=name,
    )(*a_list, *b_list)


def ffn_body(
    experts, chunks, scatter,
    x_ref, d_ref, routes_ref, rw_ref, ei_ref, si_ref, eo_ref, so_ref, *refs,
):
    if scatter:
        s_other_ref, d_other_ref, dgu_ref, dn_ref, bt_ref, rg_ref, np_ref, og_ref, og2_ref, *refs = refs
    else:
        dgu_ref, dn_ref, bt_ref, rg_ref, np_ref, s_ref, *refs = refs
    dn_acc, bt_acc, probs_ref, w_ref, ds_ref, wi_buf, wd_buf, sem, *scratch = refs
    c = pl.program_id(0)
    h = eo_ref.shape[1]
    slots, width = x_ref.shape

    def fetch(step):
        slot = step % 2

        @pl.when(step < experts)
        def _():
            pltpu.make_async_copy(ei_ref.at[step], wi_buf.at[slot], sem.at[0, slot]).start()
            pltpu.make_async_copy(eo_ref.at[step], wd_buf.at[slot], sem.at[1, slot]).start()

        @pl.when(step >= experts)
        def _():
            pltpu.make_async_copy(si_ref.at[step - experts], wi_buf.at[slot], sem.at[0, slot]).start()
            pltpu.make_async_copy(so_ref.at[step - experts], wd_buf.at[slot], sem.at[1, slot]).start()

    @pl.when(c == 0)
    def _():
        fetch(c)

    @pl.when(c + 1 < chunks)
    def _():
        fetch(c + 1)

    def picked():
        expert = lax.broadcasted_iota(jnp.int32, (experts, slots), 0)
        hit = jnp.zeros((experts, slots), jnp.float32)
        for j in range(routes_ref.shape[0]):
            hit = hit + jnp.where(routes_ref[j : j + 1, :] == expert, 1.0, 0.0)
        return hit

    @pl.when(c == 0)
    def _():
        logits = lax.dot_general(rw_ref[...], x_ref[...], NT, preferred_element_type=jnp.float32)
        raised = jnp.exp(logits[:experts] - jnp.max(logits[:experts], axis=0, keepdims=True))
        probs = raised / jnp.sum(raised, axis=0, keepdims=True)
        gate = 1.0 / (1.0 + jnp.exp(-logits[experts:]))
        probs_ref[...] = probs
        w_ref[:experts, :] = probs * picked()
        w_ref[experts:, :] = gate
        ds_ref[...] = jnp.zeros_like(ds_ref)
        dn_acc[...] = jnp.zeros_like(dn_acc)
        bt_acc[...] = jnp.zeros_like(bt_acc)

    if scatter:
        def store(chunk, rows, result):
            @pl.when(chunk < experts)
            def _():
                og_ref[rows, :] = result

            @pl.when(chunk >= experts)
            def _():
                og2_ref[rows, :] = result

        send = scatter_steps(c, chunks, FFN_LAGS, og_ref.shape[1], scratch, store)

    block = 512

    @pl.when(c < chunks)
    def _():
        row = pl.ds(jnp.minimum(c, experts), 1)
        slot = c % 2
        pltpu.make_async_copy(ei_ref.at[0], wi_buf.at[slot], sem.at[0, slot]).wait()
        pltpu.make_async_copy(eo_ref.at[0], wd_buf.at[slot], sem.at[1, slot]).wait()
        wi = wi_buf.at[slot]
        wd = wd_buf.at[slot]
        x = x_ref[...]
        g = lax.dot_general(wi[:h], x, NT, preferred_element_type=jnp.float32)
        u = lax.dot_general(wi[h:], x, NT, preferred_element_type=jnp.float32)
        p = lax.dot_general(wd[...], d_ref[...], NT, preferred_element_type=jnp.float32)
        w = w_ref[row, :]
        sg = 1.0 / (1.0 + jnp.exp(-g))
        si = g * sg
        inner = (si * u).astype(jnp.bfloat16).astype(jnp.float32)
        s = (w * inner).astype(jnp.bfloat16)
        ds_ref[row, :] += jnp.sum(p * inner, axis=0, keepdims=True)
        di = w * p
        dg = (di * u * sg * (1.0 + g * (1.0 - sg))).astype(jnp.bfloat16)
        du = (di * si).astype(jnp.bfloat16)
        dgu_ref[0, :h] = dg
        dgu_ref[0, h:] = du
        dgu = jnp.concatenate([dg, du], axis=0)
        if scatter:
            def product(cols):
                return jnp.dot(s, d_ref[:, cols], preferred_element_type=jnp.float32) + jnp.dot(
                    s_other_ref[0], d_other_ref[:, cols], preferred_element_type=jnp.float32
                )

            send(product)
        else:
            s_ref[0] = s
        for n in range(0, width, block):
            cols = slice(n, n + block)
            dn_acc[:, cols] += lax.dot_general(dgu, wi[:, cols], TN, preferred_element_type=jnp.float32)
            bt_acc[:, cols] += lax.dot_general(s, wd[:, cols], TN, preferred_element_type=jnp.float32)

    @pl.when(c == chunks - 1)
    def _():
        probs = probs_ref[...]
        d_probs = ds_ref[:experts, :] * picked()
        d_logits = probs * (d_probs - jnp.sum(probs * d_probs, axis=0, keepdims=True))
        gate = w_ref[experts:, :]
        d_gate = ds_ref[experts:, :] * gate * (1.0 - gate)
        small = jnp.concatenate([d_logits, d_gate], axis=0)
        high = small.astype(jnp.bfloat16)
        low = (small - high.astype(jnp.float32)).astype(jnp.bfloat16)
        rg_ref[...] = jnp.dot(high, x_ref[...], preferred_element_type=jnp.float32) + jnp.dot(
            low, x_ref[...], preferred_element_type=jnp.float32
        )
        for n in range(0, width, block):
            cols = slice(n, n + block)
            extra = lax.dot_general(high, rw_ref[:, cols], TN, preferred_element_type=jnp.float32)
            extra += lax.dot_general(low, rw_ref[:, cols], TN, preferred_element_type=jnp.float32)
            total = dn_acc[:, cols] + extra
            dn_ref[:, cols] = total.astype(dn_ref.dtype)
            np_ref[:, cols] = jnp.sum(total * x_ref[:, cols].astype(jnp.float32), axis=0, keepdims=True)
        bt_ref[...] = bt_acc[...].astype(bt_ref.dtype)


def ffn(x, d_two, routes_t, router_rows, ei, si, eo, so, other=None):
    experts, h2, width = ei.shape
    chunks = experts + si.shape[0]
    h = h2 // 2
    slots = x.shape[0]
    rows = router_rows.shape[0]
    bf, f32 = jnp.bfloat16, jnp.float32
    anywhere = pl.BlockSpec(memory_space=pl.ANY)
    scatter = other is not None

    def whole(shape):
        return pl.BlockSpec(shape, lambda c: (0,) * len(shape), pipeline_mode=pl.Buffered(1))

    def chunk(shape):
        return pl.BlockSpec((1, *shape), lambda c: (jnp.minimum(c, chunks - 1), 0, 0))

    in_specs = [
        whole((slots, width)), whole((slots, width)), whole(routes_t.shape), whole((rows, width)),
        anywhere, anywhere, anywhere, anywhere,
    ]
    out_specs = [chunk((h2, slots)), whole((slots, width)), whole((slots, width)), whole((rows, width)), whole((1, width))]
    out_shape = [
        jax.ShapeDtypeStruct((chunks, h2, slots), bf), jax.ShapeDtypeStruct((slots, width), bf),
        jax.ShapeDtypeStruct((slots, width), bf), jax.ShapeDtypeStruct((rows, width), f32),
        jax.ShapeDtypeStruct((1, width), f32),
    ]
    scratch = [
        pltpu.VMEM((slots, width), f32), pltpu.VMEM((slots, width), f32),
        pltpu.VMEM((experts, slots), f32), pltpu.VMEM((rows, slots), f32), pltpu.VMEM((rows, slots), f32),
        pltpu.VMEM((2, h2, width), bf), pltpu.VMEM((2, h, width), bf), pltpu.SemaphoreType.DMA((2, 2)),
    ]
    args = [x, d_two, routes_t, router_rows, ei, si, eo, so]
    if scatter:
        s_other, d_other = other
        in_specs += [chunk((h, s_other.shape[2])), whole(d_other.shape)]
        args += [s_other, d_other]
        w = width // 8
        lag = sum(FFN_LAGS)
        specs, shapes = scatter_outs(chunks, experts, lag, h, w)
        out_specs += specs
        out_shape += shapes
        scratch += scatter_scratch(h, w)
        grid = (chunks + lag,)
        params = pltpu.CompilerParams(vmem_limit_bytes=62 * MIB, collective_id=2, has_side_effects=True)
    else:
        out_specs.append(chunk((h, slots)))
        out_shape.append(jax.ShapeDtypeStruct((chunks, h, slots), bf))
        grid = (chunks,)
        params = pltpu.CompilerParams(vmem_limit_bytes=62 * MIB)
    return pl.pallas_call(
        functools.partial(ffn_body, experts, chunks, scatter),
        grid=grid,
        in_specs=in_specs,
        out_specs=out_specs,
        out_shape=out_shape,
        scratch_shapes=scratch,
        compiler_params=params,
        cost_estimate=pl.CostEstimate(
            flops=12 * chunks * h * slots * width, bytes_accessed=10 * chunks * h * width + 16 * slots * width,
            transcendentals=chunks * h * slots,
        ),
        name="ffn_scatter" if scatter else "ffn",
    )(*args)


def turn(v):
    half = v.shape[1] // 2
    return jnp.concatenate([v[:, half:], v[:, :half]], axis=1)


def qkv_body(x_ref, w_ref, bias_ref, cos_ref, sin_ref, out_ref):
    j = pl.program_id(0)
    cols = w_ref.shape[2]
    y = jnp.dot(x_ref[...], w_ref[0], preferred_element_type=jnp.float32)
    y = y + bias_ref[0].astype(jnp.float32)

    @pl.when(j < 2)
    def _():
        for head in range(cols // HEAD_DIM):
            place = slice(head * HEAD_DIM, (head + 1) * HEAD_DIM)
            v = y[:, place]
            out_ref[0, :, place] = (v * cos_ref[...] + turn(v) * sin_ref[...]).astype(out_ref.dtype)

    @pl.when(j == 2)
    def _():
        out_ref[0] = y.astype(out_ref.dtype)


def project_qkv(x, w, bias, cos_table, sin_table):
    slots, width = x.shape
    cols = w.shape[2]
    table = pl.BlockSpec((slots, HEAD_DIM), lambda j: (0, 0), pipeline_mode=pl.Buffered(1))
    return pl.pallas_call(
        qkv_body,
        grid=(3,),
        in_specs=[
            pl.BlockSpec((slots, width), lambda j: (0, 0), pipeline_mode=pl.Buffered(1)),
            pl.BlockSpec((1, width, cols), lambda j: (j, 0, 0)),
            pl.BlockSpec((1, 1, cols), lambda j: (j, 0, 0)),
            table, table,
        ],
        out_specs=pl.BlockSpec((1, slots, cols), lambda j: (j, 0, 0)),
        out_shape=jax.ShapeDtypeStruct((3, slots, cols), jnp.bfloat16),
        compiler_params=pltpu.CompilerParams(vmem_limit_bytes=48 * MIB),
        cost_estimate=pl.CostEstimate(
            flops=6 * slots * width * cols, bytes_accessed=2 * slots * width + 6 * width * cols, transcendentals=0
        ),
        name="project_qkv",
    )(x, w, bias, cos_table, sin_table)


def block_probs(length_ref, q, k, start):
    s = lax.dot_general(q, k, NT, preferred_element_type=jnp.float32) * (HEAD_DIM**-0.5)
    row = lax.broadcasted_iota(jnp.int32, s.shape, 0) + start
    col = lax.broadcasted_iota(jnp.int32, s.shape, 1)
    s = jnp.where((col <= row) & (col < length_ref[0]), s, -1000000000.0)
    e = jnp.exp(s - jnp.max(s, axis=1, keepdims=True))
    return e * (1.0 / jnp.sum(e, axis=1, keepdims=True))


def attend_body(rows, length_ref, q_ref, k_ref, v_ref, mixed_ref, mixed_t_ref):
    for start in range(0, q_ref.shape[1], rows):
        here, end = slice(start, start + rows), start + rows
        p = block_probs(length_ref, q_ref[0, here, :], k_ref[0, :end, :], start)
        mixed = jnp.dot(p.astype(jnp.bfloat16), v_ref[0, :end, :], preferred_element_type=jnp.float32)
        mixed_ref[here, :] = mixed.astype(mixed_ref.dtype)
        mixed_t_ref[:, here] = mixed.T.astype(mixed_ref.dtype)


def attend(lengths, qkv):
    _, slots, cols = qkv.shape
    rows = min(256, slots)

    def part(j):
        return pl.BlockSpec((1, slots, HEAD_DIM), lambda h: (j, 0, h))

    return pl.pallas_call(
        functools.partial(attend_body, rows),
        grid=(cols // HEAD_DIM,),
        in_specs=[pl.BlockSpec(memory_space=pltpu.SMEM), part(0), part(1), part(2)],
        out_specs=[
            pl.BlockSpec((slots, HEAD_DIM), lambda h: (0, h)), pl.BlockSpec((HEAD_DIM, slots), lambda h: (h, 0)),
        ],
        out_shape=[
            jax.ShapeDtypeStruct((slots, cols), jnp.bfloat16), jax.ShapeDtypeStruct((cols, slots), jnp.bfloat16),
        ],
        compiler_params=pltpu.CompilerParams(vmem_limit_bytes=32 * MIB),
        cost_estimate=pl.CostEstimate(
            flops=4 * slots * slots * cols, bytes_accessed=10 * slots * cols, transcendentals=slots * slots * cols // HEAD_DIM
        ),
        name="attend",
    )(lengths, qkv, qkv, qkv)


def attend_back_body(
    rows, length_ref, q_ref, k_ref, v_ref, dm_ref, cos_ref, sin_ref, out_ref, out_t_ref, bias_ref, dk_acc, dv_acc
):
    slots = q_ref.shape[1]
    scale = HEAD_DIM**-0.5
    bf, f32 = jnp.bfloat16, jnp.float32

    def finish(j, here, grad):
        if j < 2:
            grad = grad * cos_ref[here, :] - turn(grad) * sin_ref[here, :]
        low = grad.astype(bf)
        out_ref[j, here, :] = low
        out_t_ref[j, :, here] = grad.T.astype(bf)
        return jnp.sum(low.astype(f32), axis=0, keepdims=True)

    dq_sum = jnp.zeros((1, HEAD_DIM), f32)
    starts = list(range(0, slots, rows))[::-1]
    for start in starts:
        here, end = slice(start, start + rows), start + rows
        q, k, v, dm = q_ref[0, here, :], k_ref[0, :end, :], v_ref[0, :end, :], dm_ref[here, :]
        p = block_probs(length_ref, q, k, start)
        dp = lax.dot_general(dm, v, NT, preferred_element_type=f32)
        ds = (p * (dp - jnp.sum(p * dp, axis=1, keepdims=True))).astype(bf)
        dq_sum += finish(0, here, jnp.dot(ds, k, preferred_element_type=f32) * scale)
        dk = lax.dot_general(ds, q, TN, preferred_element_type=f32) * scale
        dv = lax.dot_general(p.astype(bf), dm, TN, preferred_element_type=f32)
        if start == starts[0]:
            dk_acc[...] = dk
            dv_acc[...] = dv
        else:
            dk_acc[:end, :] += dk
            dv_acc[:end, :] += dv
    every = slice(0, slots)
    bias_ref[0] = dq_sum
    bias_ref[1] = finish(1, every, dk_acc[...])
    bias_ref[2] = finish(2, every, dv_acc[...])


def attend_back(lengths, qkv, d_mixed, cos_table, sin_table):
    _, slots, cols = qkv.shape
    rows = min(256, slots)
    bf, f32 = jnp.bfloat16, jnp.float32

    def part(j):
        return pl.BlockSpec((1, slots, HEAD_DIM), lambda h: (j, 0, h))

    table = pl.BlockSpec((slots, HEAD_DIM), lambda h: (0, 0), pipeline_mode=pl.Buffered(1))
    return pl.pallas_call(
        functools.partial(attend_back_body, rows),
        grid=(cols // HEAD_DIM,),
        in_specs=[
            pl.BlockSpec(memory_space=pltpu.SMEM), part(0), part(1), part(2),
            pl.BlockSpec((slots, HEAD_DIM), lambda h: (0, h)), table, table,
        ],
        out_specs=[
            pl.BlockSpec((3, slots, HEAD_DIM), lambda h: (0, 0, h)), pl.BlockSpec((3, HEAD_DIM, slots), lambda h: (0, h, 0)),
            pl.BlockSpec((3, 1, HEAD_DIM), lambda h: (0, 0, h)),
        ],
        out_shape=[
            jax.ShapeDtypeStruct((3, slots, cols), bf), jax.ShapeDtypeStruct((3, cols, slots), bf),
            jax.ShapeDtypeStruct((3, 1, cols), f32),
        ],
        scratch_shapes=[pltpu.VMEM((slots, HEAD_DIM), f32), pltpu.VMEM((slots, HEAD_DIM), f32)],
        compiler_params=pltpu.CompilerParams(vmem_limit_bytes=40 * MIB),
        cost_estimate=pl.CostEstimate(
            flops=10 * slots * slots * cols, bytes_accessed=20 * slots * cols, transcendentals=slots * slots * cols // HEAD_DIM
        ),
        name="attend_back",
    )(lengths, qkv, qkv, qkv, d_mixed, cos_table, sin_table)


def qkv_back_body(d_ref, w_ref, x_ref, out_ref, np_ref):
    total = lax.dot_general(d_ref[0], w_ref[0], NT, preferred_element_type=jnp.float32)
    for j in range(1, 3):
        total += lax.dot_general(d_ref[j], w_ref[j], NT, preferred_element_type=jnp.float32)
    out_ref[...] = total.astype(out_ref.dtype)
    np_ref[...] = jnp.sum(total * x_ref[...].astype(jnp.float32), axis=0, keepdims=True)


def qkv_back(d_qkv, w, x):
    _, slots, cols = d_qkv.shape
    width = w.shape[1]
    block = 512
    return pl.pallas_call(
        qkv_back_body,
        grid=(width // block,),
        in_specs=[
            pl.BlockSpec((3, slots, cols), lambda n: (0, 0, 0), pipeline_mode=pl.Buffered(1)),
            pl.BlockSpec((3, block, cols), lambda n: (0, n, 0)),
            pl.BlockSpec((slots, block), lambda n: (0, n)),
        ],
        out_specs=[pl.BlockSpec((slots, block), lambda n: (0, n)), pl.BlockSpec((1, block), lambda n: (0, n))],
        out_shape=[
            jax.ShapeDtypeStruct((slots, width), jnp.bfloat16), jax.ShapeDtypeStruct((1, width), jnp.float32),
        ],
        compiler_params=pltpu.CompilerParams(vmem_limit_bytes=48 * MIB),
        cost_estimate=pl.CostEstimate(
            flops=6 * slots * width * cols, bytes_accessed=4 * slots * width + 6 * width * cols, transcendentals=0
        ),
        name="qkv_back",
    )(d_qkv, w, x)


def weight_grad_scatter(a_list, b_list, r, cid, name, first=0, count=None, cut=None):
    count = a_list[0].shape[0] // r if count is None else count
    cut = count if cut is None else cut
    if lax.axis_size("dp") == 8:
        return weight_grad_scatter_kernel(a_list, b_list, r, cid, name, first, count, cut)
    product = sum(
        jnp.dot(a[first * r : (first + count) * r], b, preferred_element_type=jnp.float32)
        for a, b in zip(a_list, b_list)
    )
    result = lax.psum_scatter(
        product.astype(jnp.bfloat16), "dp", scatter_dimension=1, tiled=True
    ).astype(jnp.float32)
    return result[: cut * r], result[cut * r :]


def gather_body(own_ref, out_ref, local_sem, send_left, recv_left, send_right, recv_right):
    me = lax.axis_index("tensor")
    size = lax.axis_size("tensor")
    rows = own_ref.shape[0]
    has_left, has_right = me > 0, me < size - 1

    def block(owner):
        return out_ref.at[pl.ds(pl.multiple_of(owner * rows, rows), rows)]

    def to_left(step):
        source = own_ref if step == 0 else block(me + step)
        return pltpu.make_async_remote_copy(
            src_ref=source, dst_ref=block(me + step), send_sem=send_left.at[step], recv_sem=recv_left.at[step],
            device_id={"tensor": me - 1}, device_id_type=MESH,
        )

    def from_right(step):
        return pltpu.make_async_remote_copy(
            src_ref=own_ref, dst_ref=block(me + 1 + step), send_sem=send_left.at[step], recv_sem=recv_left.at[step],
            device_id={"tensor": me + 1}, device_id_type=MESH,
        )

    def to_right(step):
        source = own_ref if step == 0 else block(me - step)
        return pltpu.make_async_remote_copy(
            src_ref=source, dst_ref=block(me - step), send_sem=send_right.at[step], recv_sem=recv_right.at[step],
            device_id={"tensor": me + 1}, device_id_type=MESH,
        )

    def from_left(step):
        return pltpu.make_async_remote_copy(
            src_ref=own_ref, dst_ref=block(me - 1 - step), send_sem=send_right.at[step], recv_sem=recv_right.at[step],
            device_id={"tensor": me - 1}, device_id_type=MESH,
        )

    barrier = pltpu.get_barrier_semaphore()

    @pl.when(has_left)
    def _():
        pl.semaphore_signal(barrier, inc=1, device_id={"tensor": me - 1}, device_id_type=MESH)

    @pl.when(has_right)
    def _():
        pl.semaphore_signal(barrier, inc=1, device_id={"tensor": me + 1}, device_id_type=MESH)

    pl.semaphore_wait(barrier, has_left.astype(jnp.int32) + has_right.astype(jnp.int32))
    local = pltpu.make_async_copy(own_ref, block(me), local_sem)
    local.start()
    for step in range(size):
        if step > 0:
            @pl.when(me + step < size)
            def _():
                from_right(step - 1).wait_recv()

        @pl.when(has_left & (me + step < size))
        def _():
            to_left(step).start()

        if step > 0:
            @pl.when(me - step >= 0)
            def _():
                from_left(step - 1).wait_recv()

        @pl.when(has_right & (me - step >= 0))
        def _():
            to_right(step).start()

    for step in range(size):
        @pl.when(has_left & (me + step < size))
        def _():
            to_left(step).wait_send()

        @pl.when(has_right & (me - step >= 0))
        def _():
            to_right(step).wait_send()

    local.wait()


def gather_rows(own, cid):
    size = lax.axis_size("tensor")
    rows, width = own.shape
    return pl.pallas_call(
        gather_body,
        in_specs=[pl.BlockSpec(memory_space=pl.ANY)],
        out_specs=pl.BlockSpec(memory_space=pl.ANY),
        out_shape=jax.ShapeDtypeStruct((rows * size, width), own.dtype),
        scratch_shapes=[
            pltpu.SemaphoreType.DMA, *[pltpu.SemaphoreType.DMA((size,))] * 4,
        ],
        compiler_params=pltpu.CompilerParams(collective_id=cid, has_side_effects=True),
        cost_estimate=pl.CostEstimate(flops=0, bytes_accessed=2 * rows * size * width * 2, transcendentals=0),
        name="gather_rows",
    )(own)


def sums_body(
    local_rows, part_ref, out_ref, from_dp, mine, from_tensor, send_dp, recv_dp, send_t, recv_t, send_out, recv_out
):
    size_dp, size_t = lax.axis_size("dp"), lax.axis_size("tensor")
    me_dp, me_t = lax.axis_index("dp"), lax.axis_index("tensor")
    width = mine.shape[1]

    def piece(ref, owner):
        return ref.at[:, pl.ds(pl.multiple_of(owner * width, width), width)]

    barrier = pltpu.get_barrier_semaphore()
    for step in range(1, size_dp):
        peer = lax.rem(me_dp + step, size_dp)
        pl.semaphore_signal(barrier, inc=1, device_id={"dp": peer}, device_id_type=MESH)
    for step in range(1, size_t):
        peer = lax.rem(me_t + step, size_t)
        pl.semaphore_signal(barrier, inc=1, device_id={"tensor": peer}, device_id_type=MESH)
    pl.semaphore_wait(barrier, size_dp + size_t - 2)

    def send(source, target, axis, step, send_sem, recv_sem):
        me, size = (me_dp, size_dp) if axis == "dp" else (me_t, size_t)
        copy = pltpu.make_async_remote_copy(
            src_ref=source, dst_ref=target, send_sem=send_sem.at[step], recv_sem=recv_sem.at[step],
            device_id={axis: lax.rem(me + step, size)}, device_id_type=MESH,
        )
        copy.start()
        return copy

    first = [
        send(piece(part_ref, lax.rem(me_dp + step, size_dp)), from_dp.at[step], "dp", step, send_dp, recv_dp)
        for step in range(1, size_dp)
    ]
    total = piece(part_ref, me_dp)[...]
    for step, copy in enumerate(first, 1):
        copy.wait_recv()
        total = total + from_dp[step]
    mine[...] = total
    second = [send(mine, from_tensor.at[step], "tensor", step, send_t, recv_t) for step in range(1, size_t)]
    for step, copy in enumerate(second, 1):
        copy.wait_recv()
        total = total + from_tensor[step]
    here = piece(out_ref, me_dp)
    here[...] = total
    piece(out_ref.at[local_rows:], me_dp)[...] = mine[local_rows:, :]
    third = [send(here, here, "dp", step, send_out, recv_out) for step in range(1, size_dp)]
    for copy in third:
        copy.wait_recv()
    for copy in first + second + third:
        copy.wait_send()


def small_sums(part, local_rows, cid):
    size_dp, size_t = lax.axis_size("dp"), lax.axis_size("tensor")
    rows, width = part.shape[0], part.shape[1] // size_dp
    vmem = pl.BlockSpec(memory_space=pltpu.VMEM)
    dma = pltpu.SemaphoreType.DMA
    f32 = jnp.float32
    return pl.pallas_call(
        functools.partial(sums_body, local_rows),
        in_specs=[vmem],
        out_specs=vmem,
        out_shape=jax.ShapeDtypeStruct(part.shape, f32),
        scratch_shapes=[
            pltpu.VMEM((size_dp, rows, width), f32), pltpu.VMEM((rows, width), f32), pltpu.VMEM((size_t, rows, width), f32),
            dma((size_dp,)), dma((size_dp,)), dma((size_t,)), dma((size_t,)), dma((size_dp,)), dma((size_dp,)),
        ],
        compiler_params=pltpu.CompilerParams(collective_id=cid, has_side_effects=True),
        name="small_sums",
    )(part)


def on_device(
    tokens,
    lengths,
    routes,
    cotangent,
    norm_one,
    qkv_weight,
    qkv_bias,
    out_weight,
    norm_two,
    router_weight,
    expert_in,
    expert_out,
    shared_in,
    shared_out,
    shared_gate,
):
    own_rows = tokens.shape[0]
    slot_count = routes.shape[0]
    model_width = tokens.shape[1]
    qkv_cols = qkv_weight.shape[2]
    local_heads = qkv_cols // HEAD_DIM
    experts = router_weight.shape[1]
    eff = expert_in.shape[3]
    shared_chunks = shared_out.shape[0] // eff
    chunks = experts + shared_chunks
    bf = jnp.bfloat16
    qkv_cols = qkv_weight.shape[2]
    length = lengths[0]
    tensor_index = lax.axis_index("tensor")
    first_row = tensor_index * own_rows
    live_own = (first_row + jnp.arange(own_rows) < length).astype(jnp.float32)[:, None]
    tokens_f = tokens.astype(jnp.float32)
    gain_one = norm_one.astype(jnp.float32)
    gain_two = norm_two.astype(jnp.float32)
    inv_one = lax.rsqrt(jnp.mean(tokens_f * tokens_f, axis=-1, keepdims=True) + epsilon)
    unit_one = tokens_f * inv_one
    normed_one = lax.all_gather((unit_one * gain_one).astype(bf), "tensor", axis=0, tiled=True)
    cos_table, sin_table = rotary_tables(slot_count, HEAD_DIM)
    qkv_w = qkv_weight.transpose(1, 0, 2)
    ei = expert_in.transpose(0, 2, 3, 1).reshape(experts, 2 * eff, model_width)
    eo = expert_out
    si = (
        shared_in.reshape(model_width, 2, shared_chunks, eff)
        .transpose(2, 1, 3, 0)
        .reshape(shared_chunks, 2 * eff, model_width)
    )
    so = shared_out.reshape(shared_chunks, eff, model_width)
    router_rows = jnp.concatenate(
        [
            router_weight.T,
            shared_gate[None],
            jnp.zeros((-(experts + 1) % 16, model_width), bf),
        ],
        axis=0,
    )
    grad_out = cotangent.astype(jnp.float32) * live_own
    d_two_own = (live_own * grad_out).astype(bf)
    normed_one, si, router_rows, cos_table, sin_table, d_two_own = lax.optimization_barrier(
        (normed_one, si, router_rows, cos_table, sin_table, d_two_own)
    )
    qkv = project_qkv(normed_one, qkv_w, qkv_bias[:, None, :], cos_table, sin_table)
    mixed, mixed_t = attend(lengths, qkv)
    branch_partial = jnp.dot(mixed, out_weight, preferred_element_type=jnp.float32).astype(bf)
    d_two_own, branch_partial = lax.optimization_barrier((d_two_own, branch_partial))
    branch_one = lax.psum_scatter(branch_partial, "tensor", scatter_dimension=0, tiled=True)
    d_two = gather_rows(d_two_own, 1)
    branch_one, d_two = lax.optimization_barrier((branch_one, d_two))
    hidden = tokens_f + live_own * branch_one.astype(jnp.float32)
    inv_two = lax.rsqrt(jnp.mean(hidden * hidden, axis=-1, keepdims=True) + epsilon)
    unit_two = hidden * inv_two
    normed_two = (unit_two * gain_two).astype(bf)
    half = own_rows // 2
    size_t = lax.axis_size("tensor")

    def halves(rows):
        return rows.reshape(size_t, 2, half, -1).transpose(1, 0, 2, 3).reshape(2, size_t * half, -1)

    d_a, d_b = halves(d_two)
    routes_a, routes_b = halves(routes)
    x_a = lax.all_gather(normed_two[:half], "tensor", axis=0, tiled=True)
    x_a, second, d_a, d_b = lax.optimization_barrier((x_a, normed_two[half:], d_a, d_b))
    x_b = lax.all_gather(second, "tensor", axis=0, tiled=True)
    weights = (router_rows, ei, si, eo, so)
    dgu_a, dn_a, bt_a, router_a, np_a, s_a = ffn(x_a, d_a, routes_a.T, *weights)
    x_b, dn_a, bt_a, s_a = lax.optimization_barrier((x_b, dn_a, bt_a, s_a))
    grad_a = lax.psum_scatter(dn_a, "tensor", scatter_dimension=0, tiled=True)
    two_a = lax.psum_scatter(bt_a, "tensor", scatter_dimension=0, tiled=True)
    if lax.axis_size("dp") == 8:
        dgu_b, dn_b, bt_b, router_b, np_b, out_grads, shared_out_grad = ffn(
            x_b, d_b, routes_b.T, *weights, other=(s_a, d_a)
        )
    else:
        dgu_b, dn_b, bt_b, router_b, np_b, s_b = ffn(x_b, d_b, routes_b.T, *weights)
        inner = [s.reshape(chunks * eff, -1) for s in (s_a, s_b)]
        out_grads, shared_out_grad = weight_grad_scatter(
            inner, [d_a, d_b], eff, 2, "down_grads", cut=experts
        )
    router_part = router_a + router_b
    norm_two_part = np_a + np_b
    d_gate_up = [d.reshape(chunks * 2 * eff, -1) for d in (dgu_a, dgu_b)]
    grad_a, two_a, dn_b = lax.optimization_barrier((grad_a, two_a, dn_b))
    grad_b = lax.psum_scatter(dn_b, "tensor", scatter_dimension=0, tiled=True)
    in_grads_b, _ = weight_grad_scatter(
        d_gate_up, [x_a, x_b], eff, 4, "shared_in_grads", 2 * experts, 2 * shared_chunks
    )
    grad_two = jnp.concatenate([grad_a, grad_b], axis=0).astype(jnp.float32)
    grad_hidden = grad_out + norm_back(grad_two, unit_two, inv_two, gain_two)
    d_one_own, in_grads_b = lax.optimization_barrier(
        ((live_own * grad_hidden).astype(bf), in_grads_b)
    )
    d_one = lax.all_gather(d_one_own, "tensor", axis=0, tiled=True)
    d_gate_up, _ = lax.optimization_barrier((d_gate_up, d_one_own))
    in_grads_a, _ = weight_grad_scatter(
        d_gate_up, [x_a, x_b], eff, 3, "expert_in_grads", 0, 2 * experts
    )
    d_one, in_grads_a, bt_b = lax.optimization_barrier((d_one, in_grads_a, bt_b))
    two_b = lax.psum_scatter(bt_b, "tensor", scatter_dimension=0, tiled=True)
    d_mixed = lax.dot_general(d_one, out_weight, NT, preferred_element_type=jnp.float32).astype(bf)
    d_qkv, d_qkv_t, bias_part = attend_back(lengths, qkv, d_mixed, cos_table, sin_table)
    grad_one, norm_one_part = qkv_back(d_qkv, qkv_w, normed_one)
    grad_one, d_qkv_t, mixed_t, two_b = lax.optimization_barrier(
        (grad_one, d_qkv_t, mixed_t, two_b)
    )
    grad_one_own = lax.psum_scatter(grad_one, "tensor", scatter_dimension=0, tiled=True)
    part = jnp.concatenate(
        [
            router_part[: experts + 1],
            norm_one_part / gain_one[None],
            norm_two_part / gain_two[None],
            jnp.pad(bias_part.reshape(1, 3 * qkv_cols), ((0, 0), (0, model_width - 3 * qkv_cols))),
        ],
        axis=0,
    )
    sums = small_sums(part, experts + 3, 7)
    qkv_sum, _ = weight_grad_scatter(
        [d_qkv_t.reshape(3 * qkv_cols, slot_count)], [normed_one], 3 * qkv_cols // 4, 5, "qkv_grads"
    )
    out_sum, _ = weight_grad_scatter([mixed_t], [d_one], qkv_cols // 2, 6, "mix_grads")
    branch_two = jnp.concatenate([two_a, two_b], axis=0).astype(jnp.float32)
    output = (hidden + live_own * branch_two).astype(bf)
    grad_one = grad_one_own.astype(jnp.float32)
    input_grad = grad_hidden + norm_back(grad_one, unit_one, inv_one, gain_one)
    qkv_bias_grad = sums[experts + 3, : 3 * qkv_cols].reshape(3, qkv_cols)
    own_cols = out_grads.shape[1]
    expert_in_grad = in_grads_a.reshape(experts, 2, eff, own_cols).transpose(0, 3, 1, 2)
    shared_in_grad = (
        in_grads_b.reshape(shared_chunks, 2, eff, own_cols)
        .transpose(3, 1, 0, 2)
        .reshape(own_cols, 2, shared_chunks * eff)
    )
    return (
        output,
        input_grad,
        sums[experts + 1],
        qkv_sum.reshape(3, qkv_cols, own_cols).transpose(2, 0, 1),
        qkv_bias_grad,
        out_sum,
        sums[experts + 2],
        sums[:experts].T,
        expert_in_grad,
        out_grads.reshape(experts, eff, own_cols),
        shared_in_grad,
        shared_out_grad,
        sums[experts],
    )


def solution(mesh):
    in_specs = (
        P(("dp", "tensor"), None),
        P("dp"),
        P("dp", None),
        P(("dp", "tensor"), None),
        P(),
        P(None, None, "tensor"),
        P(None, "tensor"),
        P("tensor", None),
        P(),
        P(),
        P(None, None, None, "tensor"),
        P(None, "tensor", None),
        P(None, None, "tensor"),
        P("tensor", None),
        P(),
    )
    out_specs = (
        P(("dp", "tensor"), None),
        P(("dp", "tensor"), None),
        P(),
        P("dp", None, "tensor"),
        P(None, "tensor"),
        P("tensor", "dp"),
        P(),
        P(),
        P(None, "dp", None, "tensor"),
        P(None, "tensor", "dp"),
        P("dp", None, "tensor"),
        P("tensor", "dp"),
        P(),
    )
    return jax.shard_map(
        on_device, mesh=mesh, in_specs=in_specs, out_specs=out_specs, check_vma=False
    )
```

```python
import functools

import jax
import jax.numpy as jnp
from jax import lax
from jax.experimental import pallas as pl
from jax.experimental.pallas import tpu as pltpu
from jax.sharding import PartitionSpec as P

HEAD_DIM = 128
MESH = pl.DeviceIdType.MESH
LA, LB, LC = 1, 2, 2
FFN_LAGS = (1, 1, 1)
MIB = 2**20


epsilon = 1e-06
theta_base = 1000000.0
NT = (((1,), (1,)), ((), ()))
TN = (((0,), (0,)), ((), ()))


def rotary_tables(row_count, head_width):
    half_index = jnp.arange(head_width // 2).astype(jnp.float32)
    frequency = theta_base ** (-2.0 * half_index / head_width)
    angles = jnp.arange(row_count).astype(jnp.float32)[:, None] * frequency[None, :]
    sines = jnp.sin(angles)
    cosines = jnp.cos(angles)
    return (
        jnp.concatenate([cosines, cosines], axis=-1),
        jnp.concatenate([-sines, sines], axis=-1),
    )


def norm_back(d_normed, unit_rows, inverse, gain_vector):
    d_unit = d_normed * gain_vector
    return inverse * (d_unit - unit_rows * jnp.mean(d_unit * unit_rows, axis=-1, keepdims=True))


def scatter_scratch(r, w):
    f32, bf = jnp.float32, jnp.bfloat16
    dma = pltpu.SemaphoreType.DMA
    h = r // 2
    return [
        pltpu.VMEM((2, 4, r, w), f32), pltpu.VMEM((2, 4, r, w), bf), pltpu.VMEM((3, 4, r, w), bf),
        pltpu.VMEM((3, 2, 2, h, w), f32), pltpu.VMEM((3, 2, 2, h, w), bf), pltpu.VMEM((6, 2, 2, h, w), bf),
        pltpu.VMEM((3, 2, h, w), f32), pltpu.VMEM((2, 2, h, w), bf), pltpu.VMEM((6, 2, h, w), bf),
        dma((2,)), dma((3,)), dma((3, 2)), dma((6, 2)), dma((2, 2)), dma((6, 2)),
    ]


def scatter_steps(i, nc, lags, w, scratch, store):
    own, sa, ra, kt, s1, r1, ku, s2, r2, sem_sa, sem_ra, sem_s1, sem_r1, sem_s2, sem_r2 = scratch
    la, lb, lc = lags
    keep_1 = min(3, lb + lc)
    hr = own.shape[2] // 2
    dp = lax.axis_index("dp")
    k = dp % 2
    x = (dp // 2) % 2
    y = dp // 4
    core_peer = y * 4 + x * 2 + (1 - k)
    x_peer = y * 4 + (1 - x) * 2 + k
    y_peer = (1 - y) * 4 + x * 2 + k

    def copy_a(c):
        return pltpu.make_async_remote_copy(
            src_ref=sa.at[c % 2], dst_ref=ra.at[c % 3], send_sem=sem_sa.at[c % 2], recv_sem=sem_ra.at[c % 3],
            device_id={"dp": core_peer}, device_id_type=MESH,
        )

    def copy_1(c, half):
        return pltpu.make_async_remote_copy(
            src_ref=s1.at[c % 3, half], dst_ref=r1.at[c % 6, half], send_sem=sem_s1.at[c % 3, half],
            recv_sem=sem_r1.at[c % 6, half], device_id={"dp": y_peer if half else x_peer}, device_id_type=MESH,
        )

    def copy_2(c, half):
        return pltpu.make_async_remote_copy(
            src_ref=s2.at[c % 2, half], dst_ref=r2.at[c % 6, half], send_sem=sem_s2.at[c % 2, half],
            recv_sem=sem_r2.at[c % 6, half], device_id={"dp": x_peer if half else y_peer}, device_id_type=MESH,
        )

    @pl.when(i == 0)
    def _():
        barrier = pltpu.get_barrier_semaphore()
        for peer in (core_peer, x_peer, y_peer):
            pl.semaphore_signal(barrier, inc=1, device_id={"dp": peer}, device_id_type=MESH)
        pl.semaphore_wait(barrier, 3)

    @pl.when((i >= la + keep_1) & (i < nc + la + keep_1))
    def _():
        copy_1(i - la - keep_1, 0).wait_send()
        copy_1(i - la - keep_1, 1).wait_send()

    @pl.when((i >= la) & (i < nc + la))
    def _():
        c = i - la
        copy_a(c).wait_recv()
        for half in range(2):
            rows = slice(half * hr, half * hr + hr)
            keep, other = (1, 2) if half else (2, 1)

            def total(role):
                return own[c % 2, role, rows, :] + ra[c % 3, role, rows, :].astype(jnp.float32)

            s1[c % 3, half, 0] = total(other).astype(jnp.bfloat16)
            s1[c % 3, half, 1] = total(3).astype(jnp.bfloat16)
            copy_1(c, half).start()
            kt[c % 3, half, 0] = total(0)
            kt[c % 3, half, 1] = total(keep)

    @pl.when((i >= la + lb) & (i < nc + la + lb))
    def _():
        c = i - la - lb

        @pl.when(c >= 2)
        def _():
            copy_2(c - 2, 0).wait_send()
            copy_2(c - 2, 1).wait_send()

        for half in range(2):
            copy_1(c, half).wait_recv()
            s2[c % 2, half] = (kt[c % 3, half, 1] + r1[c % 6, half, 1].astype(jnp.float32)).astype(jnp.bfloat16)
            copy_2(c, half).start()
            ku[c % 3, half] = kt[c % 3, half, 0] + r1[c % 6, half, 0].astype(jnp.float32)

    @pl.when(i >= la + lb + lc)
    def _():
        c = i - la - lb - lc
        for half in range(2):
            copy_2(c, half).wait_recv()
            store(c, slice(half * hr, half * hr + hr), ku[c % 3, half] + r2[c % 6, half].astype(jnp.float32))

        @pl.when(c >= nc - 2)
        def _():
            copy_2(c, 0).wait_send()
            copy_2(c, 1).wait_send()

    @pl.when((i >= 2) & (i < nc + 2))
    def _():
        copy_a(i - 2).wait_send()

    def send(product):
        targets = (y * 4 + x * 2, y * 4 + (1 - x) * 2, (1 - y) * 4 + x * 2, (1 - y) * 4 + (1 - x) * 2)

        def cols(role, core):
            return pl.ds(pl.multiple_of((targets[role] + core) * w, w), w)

        for role in range(4):
            sa[i % 2, role] = product(cols(role, 1 - k)).astype(jnp.bfloat16)
        copy_a(i).start()
        for role in range(4):
            own[i % 2, role] = product(cols(role, k))

    return send


def rs_body(nc, cut, pairs, *refs):
    a_refs, b_refs = refs[:pairs], refs[pairs : 2 * pairs]
    o_ref, o2_ref = refs[2 * pairs : 2 * pairs + 2]
    i = pl.program_id(0)

    def store(c, rows, result):
        @pl.when(c < cut)
        def _():
            o_ref[rows, :] = result

        @pl.when(c >= cut)
        def _():
            o2_ref[rows, :] = result

    send = scatter_steps(i, nc, (LA, LB, LC), o_ref.shape[1], refs[2 * pairs + 2 :], store)

    @pl.when(i < nc)
    def _():
        def product(cols):
            total = jnp.dot(a_refs[0][...], b_refs[0][:, cols], preferred_element_type=jnp.float32)
            for a_ref, b_ref in zip(a_refs[1:], b_refs[1:]):
                total += jnp.dot(a_ref[...], b_ref[:, cols], preferred_element_type=jnp.float32)
            return total

        send(product)


def scatter_outs(nc, cut, lag, r, w):
    rest = max(nc - cut, 1)
    specs = [
        pl.BlockSpec((r, w), lambda i: (jnp.clip(i - lag, 0, cut - 1), 0)),
        pl.BlockSpec((r, w), lambda i: (jnp.clip(i - lag - cut, 0, rest - 1), 0)),
    ]
    return specs, [jax.ShapeDtypeStruct((n * r, w), jnp.float32) for n in (cut, rest)]


def weight_grad_scatter_kernel(a_list, b_list, r, cid, name, first, count, cut):
    D = b_list[0].shape[1]
    T = sum(b.shape[0] for b in b_list)
    w = D // 8
    lag = LA + LB + LC
    out_specs, out_shape = scatter_outs(count, cut, lag, r, w)
    return pl.pallas_call(
        functools.partial(rs_body, count, cut, len(a_list)),
        grid=(count + lag,),
        in_specs=[
            *[pl.BlockSpec((r, a.shape[1]), lambda i: (jnp.minimum(i, count - 1) + first, 0)) for a in a_list],
            *[pl.BlockSpec(b.shape, lambda i: (0, 0), pipeline_mode=pl.Buffered(1)) for b in b_list],
        ],
        out_specs=out_specs,
        out_shape=out_shape,
        scratch_shapes=scatter_scratch(r, w),
        compiler_params=pltpu.CompilerParams(vmem_limit_bytes=48 * MIB, collective_id=cid, has_side_effects=True),
        cost_estimate=pl.CostEstimate(
            flops=2 * count * r * T * D, bytes_accessed=2 * count * r * T + 2 * T * D + 4 * count * r * w, transcendentals=0
        ),
        name=name,
    )(*a_list, *b_list)


def ffn_body(
    experts, chunks, scatter,
    x_ref, d_ref, routes_ref, rw_ref, ei_ref, si_ref, eo_ref, so_ref, *refs,
):
    if scatter:
        s_other_ref, d_other_ref, dgu_ref, dn_ref, bt_ref, rg_ref, np_ref, og_ref, og2_ref, *refs = refs
    else:
        dgu_ref, dn_ref, bt_ref, rg_ref, np_ref, s_ref, *refs = refs
    dn_acc, bt_acc, probs_ref, w_ref, ds_ref, wi_buf, wd_buf, sem, *scratch = refs
    c = pl.program_id(0)
    h = eo_ref.shape[1]
    slots, width = x_ref.shape

    def fetch(step):
        slot = step % 2

        @pl.when(step < experts)
        def _():
            pltpu.make_async_copy(ei_ref.at[step], wi_buf.at[slot], sem.at[0, slot]).start()
            pltpu.make_async_copy(eo_ref.at[step], wd_buf.at[slot], sem.at[1, slot]).start()

        @pl.when(step >= experts)
        def _():
            pltpu.make_async_copy(si_ref.at[step - experts], wi_buf.at[slot], sem.at[0, slot]).start()
            pltpu.make_async_copy(so_ref.at[step - experts], wd_buf.at[slot], sem.at[1, slot]).start()

    @pl.when(c == 0)
    def _():
        fetch(c)

    @pl.when(c + 1 < chunks)
    def _():
        fetch(c + 1)

    def picked():
        expert = lax.broadcasted_iota(jnp.int32, (experts, slots), 0)
        hit = jnp.zeros((experts, slots), jnp.float32)
        for j in range(routes_ref.shape[0]):
            hit = hit + jnp.where(routes_ref[j : j + 1, :] == expert, 1.0, 0.0)
        return hit

    @pl.when(c == 0)
    def _():
        logits = lax.dot_general(rw_ref[...], x_ref[...], NT, preferred_element_type=jnp.float32)
        raised = jnp.exp(logits[:experts] - jnp.max(logits[:experts], axis=0, keepdims=True))
        probs = raised / jnp.sum(raised, axis=0, keepdims=True)
        gate = 1.0 / (1.0 + jnp.exp(-logits[experts:]))
        probs_ref[...] = probs
        w_ref[:experts, :] = probs * picked()
        w_ref[experts:, :] = gate
        ds_ref[...] = jnp.zeros_like(ds_ref)
        dn_acc[...] = jnp.zeros_like(dn_acc)
        bt_acc[...] = jnp.zeros_like(bt_acc)

    if scatter:
        def store(chunk, rows, result):
            @pl.when(chunk < experts)
            def _():
                og_ref[rows, :] = result

            @pl.when(chunk >= experts)
            def _():
                og2_ref[rows, :] = result

        send = scatter_steps(c, chunks, FFN_LAGS, og_ref.shape[1], scratch, store)

    block = 512

    @pl.when(c < chunks)
    def _():
        row = pl.ds(jnp.minimum(c, experts), 1)
        slot = c % 2
        pltpu.make_async_copy(ei_ref.at[0], wi_buf.at[slot], sem.at[0, slot]).wait()
        pltpu.make_async_copy(eo_ref.at[0], wd_buf.at[slot], sem.at[1, slot]).wait()
        wi = wi_buf.at[slot]
        wd = wd_buf.at[slot]
        x = x_ref[...]
        g = lax.dot_general(wi[:h], x, NT, preferred_element_type=jnp.float32)
        u = lax.dot_general(wi[h:], x, NT, preferred_element_type=jnp.float32)
        p = lax.dot_general(wd[...], d_ref[...], NT, preferred_element_type=jnp.float32)
        w = w_ref[row, :]
        sg = 1.0 / (1.0 + jnp.exp(-g))
        si = g * sg
        inner = (si * u).astype(jnp.bfloat16).astype(jnp.float32)
        s = (w * inner).astype(jnp.bfloat16)
        ds_ref[row, :] += jnp.sum(p * inner, axis=0, keepdims=True)
        di = w * p
        dg = (di * u * sg * (1.0 + g * (1.0 - sg))).astype(jnp.bfloat16)
        du = (di * si).astype(jnp.bfloat16)
        dgu_ref[0, :h] = dg
        dgu_ref[0, h:] = du
        dgu = jnp.concatenate([dg, du], axis=0)
        if scatter:
            def product(cols):
                return jnp.dot(s, d_ref[:, cols], preferred_element_type=jnp.float32) + jnp.dot(
                    s_other_ref[0], d_other_ref[:, cols], preferred_element_type=jnp.float32
                )

            send(product)
        else:
            s_ref[0] = s
        for n in range(0, width, block):
            cols = slice(n, n + block)
            dn_acc[:, cols] += lax.dot_general(dgu, wi[:, cols], TN, preferred_element_type=jnp.float32)
            bt_acc[:, cols] += lax.dot_general(s, wd[:, cols], TN, preferred_element_type=jnp.float32)

    @pl.when(c == chunks - 1)
    def _():
        probs = probs_ref[...]
        d_probs = ds_ref[:experts, :] * picked()
        d_logits = probs * (d_probs - jnp.sum(probs * d_probs, axis=0, keepdims=True))
        gate = w_ref[experts:, :]
        d_gate = ds_ref[experts:, :] * gate * (1.0 - gate)
        small = jnp.concatenate([d_logits, d_gate], axis=0)
        high = small.astype(jnp.bfloat16)
        low = (small - high.astype(jnp.float32)).astype(jnp.bfloat16)
        rg_ref[...] = jnp.dot(high, x_ref[...], preferred_element_type=jnp.float32) + jnp.dot(
            low, x_ref[...], preferred_element_type=jnp.float32
        )
        for n in range(0, width, block):
            cols = slice(n, n + block)
            extra = lax.dot_general(high, rw_ref[:, cols], TN, preferred_element_type=jnp.float32)
            extra += lax.dot_general(low, rw_ref[:, cols], TN, preferred_element_type=jnp.float32)
            total = dn_acc[:, cols] + extra
            dn_ref[:, cols] = total.astype(dn_ref.dtype)
            np_ref[:, cols] = jnp.sum(total * x_ref[:, cols].astype(jnp.float32), axis=0, keepdims=True)
        bt_ref[...] = bt_acc[...].astype(bt_ref.dtype)


def ffn(x, d_two, routes_t, router_rows, ei, si, eo, so, other=None):
    experts, h2, width = ei.shape
    chunks = experts + si.shape[0]
    h = h2 // 2
    slots = x.shape[0]
    rows = router_rows.shape[0]
    bf, f32 = jnp.bfloat16, jnp.float32
    anywhere = pl.BlockSpec(memory_space=pl.ANY)
    scatter = other is not None

    def whole(shape):
        return pl.BlockSpec(shape, lambda c: (0,) * len(shape), pipeline_mode=pl.Buffered(1))

    def chunk(shape):
        return pl.BlockSpec((1, *shape), lambda c: (jnp.minimum(c, chunks - 1), 0, 0))

    in_specs = [
        whole((slots, width)), whole((slots, width)), whole(routes_t.shape), whole((rows, width)),
        anywhere, anywhere, anywhere, anywhere,
    ]
    out_specs = [chunk((h2, slots)), whole((slots, width)), whole((slots, width)), whole((rows, width)), whole((1, width))]
    out_shape = [
        jax.ShapeDtypeStruct((chunks, h2, slots), bf), jax.ShapeDtypeStruct((slots, width), bf),
        jax.ShapeDtypeStruct((slots, width), bf), jax.ShapeDtypeStruct((rows, width), f32),
        jax.ShapeDtypeStruct((1, width), f32),
    ]
    scratch = [
        pltpu.VMEM((slots, width), f32), pltpu.VMEM((slots, width), f32),
        pltpu.VMEM((experts, slots), f32), pltpu.VMEM((rows, slots), f32), pltpu.VMEM((rows, slots), f32),
        pltpu.VMEM((2, h2, width), bf), pltpu.VMEM((2, h, width), bf), pltpu.SemaphoreType.DMA((2, 2)),
    ]
    args = [x, d_two, routes_t, router_rows, ei, si, eo, so]
    if scatter:
        s_other, d_other = other
        in_specs += [chunk((h, s_other.shape[2])), whole(d_other.shape)]
        args += [s_other, d_other]
        w = width // 8
        lag = sum(FFN_LAGS)
        specs, shapes = scatter_outs(chunks, experts, lag, h, w)
        out_specs += specs
        out_shape += shapes
        scratch += scatter_scratch(h, w)
        grid = (chunks + lag,)
        params = pltpu.CompilerParams(vmem_limit_bytes=62 * MIB, collective_id=2, has_side_effects=True)
    else:
        out_specs.append(chunk((h, slots)))
        out_shape.append(jax.ShapeDtypeStruct((chunks, h, slots), bf))
        grid = (chunks,)
        params = pltpu.CompilerParams(vmem_limit_bytes=62 * MIB)
    return pl.pallas_call(
        functools.partial(ffn_body, experts, chunks, scatter),
        grid=grid,
        in_specs=in_specs,
        out_specs=out_specs,
        out_shape=out_shape,
        scratch_shapes=scratch,
        compiler_params=params,
        cost_estimate=pl.CostEstimate(
            flops=12 * chunks * h * slots * width, bytes_accessed=10 * chunks * h * width + 16 * slots * width,
            transcendentals=chunks * h * slots,
        ),
        name="ffn_scatter" if scatter else "ffn",
    )(*args)


def turn(v):
    half = v.shape[1] // 2
    return jnp.concatenate([v[:, half:], v[:, :half]], axis=1)


def qkv_body(x_ref, w_ref, bias_ref, cos_ref, sin_ref, out_ref):
    j = pl.program_id(0)
    cols = w_ref.shape[2]
    y = jnp.dot(x_ref[...], w_ref[0], preferred_element_type=jnp.float32)
    y = y + bias_ref[0].astype(jnp.float32)

    @pl.when(j < 2)
    def _():
        for head in range(cols // HEAD_DIM):
            place = slice(head * HEAD_DIM, (head + 1) * HEAD_DIM)
            v = y[:, place]
            out_ref[0, :, place] = (v * cos_ref[...] + turn(v) * sin_ref[...]).astype(out_ref.dtype)

    @pl.when(j == 2)
    def _():
        out_ref[0] = y.astype(out_ref.dtype)


def project_qkv(x, w, bias, cos_table, sin_table):
    slots, width = x.shape
    cols = w.shape[2]
    table = pl.BlockSpec((slots, HEAD_DIM), lambda j: (0, 0), pipeline_mode=pl.Buffered(1))
    return pl.pallas_call(
        qkv_body,
        grid=(3,),
        in_specs=[
            pl.BlockSpec((slots, width), lambda j: (0, 0), pipeline_mode=pl.Buffered(1)),
            pl.BlockSpec((1, width, cols), lambda j: (j, 0, 0)),
            pl.BlockSpec((1, 1, cols), lambda j: (j, 0, 0)),
            table, table,
        ],
        out_specs=pl.BlockSpec((1, slots, cols), lambda j: (j, 0, 0)),
        out_shape=jax.ShapeDtypeStruct((3, slots, cols), jnp.bfloat16),
        compiler_params=pltpu.CompilerParams(vmem_limit_bytes=48 * MIB),
        cost_estimate=pl.CostEstimate(
            flops=6 * slots * width * cols, bytes_accessed=2 * slots * width + 6 * width * cols, transcendentals=0
        ),
        name="project_qkv",
    )(x, w, bias, cos_table, sin_table)


def block_probs(length_ref, q, k, start):
    s = lax.dot_general(q, k, NT, preferred_element_type=jnp.float32) * (HEAD_DIM**-0.5)
    row = lax.broadcasted_iota(jnp.int32, s.shape, 0) + start
    col = lax.broadcasted_iota(jnp.int32, s.shape, 1)
    s = jnp.where((col <= row) & (col < length_ref[0]), s, -1000000000.0)
    e = jnp.exp(s - jnp.max(s, axis=1, keepdims=True))
    return e * (1.0 / jnp.sum(e, axis=1, keepdims=True))


def attend_body(rows, length_ref, q_ref, k_ref, v_ref, mixed_ref, mixed_t_ref):
    for start in range(0, q_ref.shape[1], rows):
        here, end = slice(start, start + rows), start + rows
        p = block_probs(length_ref, q_ref[0, here, :], k_ref[0, :end, :], start)
        mixed = jnp.dot(p.astype(jnp.bfloat16), v_ref[0, :end, :], preferred_element_type=jnp.float32)
        mixed_ref[here, :] = mixed.astype(mixed_ref.dtype)
        mixed_t_ref[:, here] = mixed.T.astype(mixed_ref.dtype)


def attend(lengths, qkv):
    _, slots, cols = qkv.shape
    rows = min(256, slots)

    def part(j):
        return pl.BlockSpec((1, slots, HEAD_DIM), lambda h: (j, 0, h))

    return pl.pallas_call(
        functools.partial(attend_body, rows),
        grid=(cols // HEAD_DIM,),
        in_specs=[pl.BlockSpec(memory_space=pltpu.SMEM), part(0), part(1), part(2)],
        out_specs=[
            pl.BlockSpec((slots, HEAD_DIM), lambda h: (0, h)), pl.BlockSpec((HEAD_DIM, slots), lambda h: (h, 0)),
        ],
        out_shape=[
            jax.ShapeDtypeStruct((slots, cols), jnp.bfloat16), jax.ShapeDtypeStruct((cols, slots), jnp.bfloat16),
        ],
        compiler_params=pltpu.CompilerParams(vmem_limit_bytes=32 * MIB),
        cost_estimate=pl.CostEstimate(
            flops=4 * slots * slots * cols, bytes_accessed=10 * slots * cols, transcendentals=slots * slots * cols // HEAD_DIM
        ),
        name="attend",
    )(lengths, qkv, qkv, qkv)


def attend_back_body(
    rows, length_ref, q_ref, k_ref, v_ref, dm_ref, cos_ref, sin_ref, out_ref, out_t_ref, bias_ref, dk_acc, dv_acc
):
    slots = q_ref.shape[1]
    scale = HEAD_DIM**-0.5
    bf, f32 = jnp.bfloat16, jnp.float32

    def finish(j, here, grad):
        if j < 2:
            grad = grad * cos_ref[here, :] - turn(grad) * sin_ref[here, :]
        low = grad.astype(bf)
        out_ref[j, here, :] = low
        out_t_ref[j, :, here] = grad.T.astype(bf)
        return jnp.sum(low.astype(f32), axis=0, keepdims=True)

    dq_sum = jnp.zeros((1, HEAD_DIM), f32)
    starts = list(range(0, slots, rows))[::-1]
    for start in starts:
        here, end = slice(start, start + rows), start + rows
        q, k, v, dm = q_ref[0, here, :], k_ref[0, :end, :], v_ref[0, :end, :], dm_ref[here, :]
        p = block_probs(length_ref, q, k, start)
        dp = lax.dot_general(dm, v, NT, preferred_element_type=f32)
        ds = (p * (dp - jnp.sum(p * dp, axis=1, keepdims=True))).astype(bf)
        dq_sum += finish(0, here, jnp.dot(ds, k, preferred_element_type=f32) * scale)
        dk = lax.dot_general(ds, q, TN, preferred_element_type=f32) * scale
        dv = lax.dot_general(p.astype(bf), dm, TN, preferred_element_type=f32)
        if start == starts[0]:
            dk_acc[...] = dk
            dv_acc[...] = dv
        else:
            dk_acc[:end, :] += dk
            dv_acc[:end, :] += dv
    every = slice(0, slots)
    bias_ref[0] = dq_sum
    bias_ref[1] = finish(1, every, dk_acc[...])
    bias_ref[2] = finish(2, every, dv_acc[...])


def attend_back(lengths, qkv, d_mixed, cos_table, sin_table):
    _, slots, cols = qkv.shape
    rows = min(256, slots)
    bf, f32 = jnp.bfloat16, jnp.float32

    def part(j):
        return pl.BlockSpec((1, slots, HEAD_DIM), lambda h: (j, 0, h))

    table = pl.BlockSpec((slots, HEAD_DIM), lambda h: (0, 0), pipeline_mode=pl.Buffered(1))
    return pl.pallas_call(
        functools.partial(attend_back_body, rows),
        grid=(cols // HEAD_DIM,),
        in_specs=[
            pl.BlockSpec(memory_space=pltpu.SMEM), part(0), part(1), part(2),
            pl.BlockSpec((slots, HEAD_DIM), lambda h: (0, h)), table, table,
        ],
        out_specs=[
            pl.BlockSpec((3, slots, HEAD_DIM), lambda h: (0, 0, h)), pl.BlockSpec((3, HEAD_DIM, slots), lambda h: (0, h, 0)),
            pl.BlockSpec((3, 1, HEAD_DIM), lambda h: (0, 0, h)),
        ],
        out_shape=[
            jax.ShapeDtypeStruct((3, slots, cols), bf), jax.ShapeDtypeStruct((3, cols, slots), bf),
            jax.ShapeDtypeStruct((3, 1, cols), f32),
        ],
        scratch_shapes=[pltpu.VMEM((slots, HEAD_DIM), f32), pltpu.VMEM((slots, HEAD_DIM), f32)],
        compiler_params=pltpu.CompilerParams(vmem_limit_bytes=40 * MIB),
        cost_estimate=pl.CostEstimate(
            flops=10 * slots * slots * cols, bytes_accessed=20 * slots * cols, transcendentals=slots * slots * cols // HEAD_DIM
        ),
        name="attend_back",
    )(lengths, qkv, qkv, qkv, d_mixed, cos_table, sin_table)


def qkv_back_body(d_ref, w_ref, x_ref, out_ref, np_ref):
    total = lax.dot_general(d_ref[0], w_ref[0], NT, preferred_element_type=jnp.float32)
    for j in range(1, 3):
        total += lax.dot_general(d_ref[j], w_ref[j], NT, preferred_element_type=jnp.float32)
    out_ref[...] = total.astype(out_ref.dtype)
    np_ref[...] = jnp.sum(total * x_ref[...].astype(jnp.float32), axis=0, keepdims=True)


def qkv_back(d_qkv, w, x):
    _, slots, cols = d_qkv.shape
    width = w.shape[1]
    block = 512
    return pl.pallas_call(
        qkv_back_body,
        grid=(width // block,),
        in_specs=[
            pl.BlockSpec((3, slots, cols), lambda n: (0, 0, 0), pipeline_mode=pl.Buffered(1)),
            pl.BlockSpec((3, block, cols), lambda n: (0, n, 0)),
            pl.BlockSpec((slots, block), lambda n: (0, n)),
        ],
        out_specs=[pl.BlockSpec((slots, block), lambda n: (0, n)), pl.BlockSpec((1, block), lambda n: (0, n))],
        out_shape=[
            jax.ShapeDtypeStruct((slots, width), jnp.bfloat16), jax.ShapeDtypeStruct((1, width), jnp.float32),
        ],
        compiler_params=pltpu.CompilerParams(vmem_limit_bytes=48 * MIB),
        cost_estimate=pl.CostEstimate(
            flops=6 * slots * width * cols, bytes_accessed=4 * slots * width + 6 * width * cols, transcendentals=0
        ),
        name="qkv_back",
    )(d_qkv, w, x)


def weight_grad_scatter(a_list, b_list, r, cid, name, first=0, count=None, cut=None):
    count = a_list[0].shape[0] // r if count is None else count
    cut = count if cut is None else cut
    if lax.axis_size("dp") == 8:
        return weight_grad_scatter_kernel(a_list, b_list, r, cid, name, first, count, cut)
    product = sum(
        jnp.dot(a[first * r : (first + count) * r], b, preferred_element_type=jnp.float32)
        for a, b in zip(a_list, b_list)
    )
    result = lax.psum_scatter(
        product.astype(jnp.bfloat16), "dp", scatter_dimension=1, tiled=True
    ).astype(jnp.float32)
    return result[: cut * r], result[cut * r :]


def line_gather(me, size, own, block, local_sem, sems):
    send_left, recv_left, send_right, recv_right = sems
    has_left, has_right = me > 0, me < size - 1

    def remote(source, owner, send, recv, step, to):
        return pltpu.make_async_remote_copy(
            src_ref=source, dst_ref=block(owner), send_sem=send.at[step], recv_sem=recv.at[step],
            device_id={"tensor": to}, device_id_type=MESH,
        )

    def to_left(step):
        return remote(own if step == 0 else block(me + step), me + step, send_left, recv_left, step, me - 1)

    def to_right(step):
        return remote(own if step == 0 else block(me - step), me - step, send_right, recv_right, step, me + 1)

    def advance(step):
        if step == 0:
            pltpu.make_async_copy(own, block(me), local_sem).start()
        else:
            @pl.when(me + step < size)
            def _():
                remote(own, me + step, send_left, recv_left, step - 1, me + 1).wait_recv()

        @pl.when(has_left & (me + step < size))
        def _():
            to_left(step).start()

        if step > 0:
            @pl.when(me - step >= 0)
            def _():
                remote(own, me - step, send_right, recv_right, step - 1, me - 1).wait_recv()

        @pl.when(has_right & (me - step >= 0))
        def _():
            to_right(step).start()

    def finish():
        for step in range(size):
            @pl.when(has_left & (me + step < size))
            def _():
                to_left(step).wait_send()

            @pl.when(has_right & (me - step >= 0))
            def _():
                to_right(step).wait_send()

        pltpu.make_async_copy(own, block(me), local_sem).wait()

    return advance, finish


def line_barrier(me, size):
    barrier = pltpu.get_barrier_semaphore()
    has_left, has_right = me > 0, me < size - 1

    @pl.when(has_left)
    def _():
        pl.semaphore_signal(barrier, inc=1, device_id={"tensor": me - 1}, device_id_type=MESH)

    @pl.when(has_right)
    def _():
        pl.semaphore_signal(barrier, inc=1, device_id={"tensor": me + 1}, device_id_type=MESH)

    pl.semaphore_wait(barrier, has_left.astype(jnp.int32) + has_right.astype(jnp.int32))


def branch_body(
    length_ref, part_ref, tokens_ref, gain_ref, cot_ref, hidden_ref, second_ref, xa_ref, da_ref, db_ref,
    from_left, from_right, normed, local_sem, send_r, recv_r, send_l, recv_l, *sems,
):
    me = lax.axis_index("tensor")
    size = lax.axis_size("tensor")
    rows = tokens_ref.shape[0]
    half = rows // 2
    bf, f32 = jnp.bfloat16, jnp.float32
    has_left, has_right = me > 0, me < size - 1
    line_barrier(me, size)

    def place(ref, owner):
        return ref.at[pl.ds(pl.multiple_of(owner * half, half), half)]

    def own_cot(h):
        return cot_ref.at[pl.ds(h * half, half)]

    def part(ref, owner, h):
        return ref.at[owner, pl.ds(h * half, half)]

    def direction(right):
        slots, send, recv = (from_left, send_r, recv_r) if right else (from_right, send_l, recv_l)
        to = me + 1 if right else me - 1
        before = me if right else size - 1 - me
        has_to = has_right if right else has_left
        has_from = has_left if right else has_right

        def copy(source, target, t):
            return pltpu.make_async_remote_copy(
                src_ref=source, dst_ref=target, send_sem=send.at[t], recv_sem=recv.at[t],
                device_id={"tensor": to}, device_id_type=MESH,
            )

        def sent(t):
            copy(part(part_ref, 0, 0), part(slots, 0, 0), t).wait_send()

        def step(t):
            s, h = t // 2, t % 2
            gathered = (da_ref, db_ref)[h]
            if t >= 2:
                @pl.when(has_to)
                def _():
                    sent(t - 2)

            @pl.when(s <= before)
            def _():
                owner = me - s if right else me + s
                if s > 0:
                    copy(own_cot(h), place(gathered, owner), t - 2).wait_recv()

                @pl.when(has_to)
                def _():
                    copy(own_cot(h) if s == 0 else place(gathered, owner), place(gathered, owner), t).start()

            @pl.when(s > before)
            def _():
                owner = size + me - s if right else me + s - size

                @pl.when(has_from)
                def _():
                    copy(part(part_ref, owner, h), part(slots, owner, h), t - 2).wait_recv()
                    both = part(slots, owner, h)
                    both[...] = (both[...].astype(f32) + part(part_ref, owner, h)[...].astype(f32)).astype(bf)
                    copy(both, part(slots, owner, h), t).start()

                @pl.when(jnp.logical_not(has_from))
                def _():
                    copy(part(part_ref, owner, h), part(slots, owner, h), t).start()

        def last():
            @pl.when(has_to)
            def _():
                sent(2 * size - 2)
                sent(2 * size - 1)

            @pl.when(has_from)
            def _():
                for h in range(2):
                    copy(part(part_ref, me, h), part(slots, me, h), 2 * size - 2 + h).wait_recv()
                hidden_ref[...] += slots[me].astype(f32)

        return step, last

    local = [
        pltpu.make_async_copy(own_cot(h), place(ref, me), local_sem.at[h]) for h, ref in enumerate((da_ref, db_ref))
    ]
    for copy in local:
        copy.start()
    step_r, last_r = direction(True)
    step_l, last_l = direction(False)
    for t in range(2 * size):
        step_r(t)
        step_l(t)
    hidden_ref[...] = part_ref[me].astype(f32)
    last_r()
    last_l()
    row = lax.broadcasted_iota(jnp.int32, (rows, 1), 0) + me * rows
    live = jnp.where(row < length_ref[0], 1.0, 0.0)
    hidden = tokens_ref[...].astype(f32) + live * hidden_ref[...]
    hidden_ref[...] = hidden
    inverse = lax.rsqrt(jnp.mean(hidden * hidden, axis=1, keepdims=True) + epsilon)
    normed[...] = (hidden * inverse * gain_ref[...].astype(f32)).astype(bf)
    step_x, finish_x = line_gather(
        me, size, normed.at[:half], lambda owner: place(xa_ref, owner), local_sem.at[2], sems
    )
    for j in range(size):
        step_x(j)
    second_ref[...] = normed[half:, :]
    for copy in local:
        copy.wait()
    finish_x()


def finish_branch(lengths, part, tokens, gain, cot, cid):
    size = lax.axis_size("tensor")
    rows, width = tokens.shape
    half = rows // 2
    bf, f32 = jnp.bfloat16, jnp.float32
    vmem = pl.BlockSpec(memory_space=pltpu.VMEM)
    anywhere = pl.BlockSpec(memory_space=pl.ANY)
    dma = pltpu.SemaphoreType.DMA
    gathered = jax.ShapeDtypeStruct((size * half, width), bf)
    return pl.pallas_call(
        branch_body,
        in_specs=[pl.BlockSpec(memory_space=pltpu.SMEM), vmem, vmem, vmem, anywhere],
        out_specs=[vmem, vmem, anywhere, anywhere, anywhere],
        out_shape=[
            jax.ShapeDtypeStruct((rows, width), f32), jax.ShapeDtypeStruct((half, width), bf), gathered, gathered, gathered,
        ],
        scratch_shapes=[
            pltpu.VMEM((size, rows, width), bf), pltpu.VMEM((size, rows, width), bf), pltpu.VMEM((rows, width), bf),
            dma((3,)), *[dma((2 * size,))] * 4, *[dma((size,))] * 4,
        ],
        compiler_params=pltpu.CompilerParams(vmem_limit_bytes=48 * MIB, collective_id=cid, has_side_effects=True),
        cost_estimate=pl.CostEstimate(flops=0, bytes_accessed=24 * rows * size * width, transcendentals=0),
        name="finish_branch",
    )(lengths, part.reshape(size, rows, width), tokens, gain[None], cot)


def sums_body(
    local_rows, part_ref, out_ref, from_dp, mine, from_tensor, send_dp, recv_dp, send_t, recv_t, send_out, recv_out
):
    size_dp, size_t = lax.axis_size("dp"), lax.axis_size("tensor")
    me_dp, me_t = lax.axis_index("dp"), lax.axis_index("tensor")
    width = mine.shape[1]

    def piece(ref, owner):
        return ref.at[:, pl.ds(pl.multiple_of(owner * width, width), width)]

    barrier = pltpu.get_barrier_semaphore()
    for step in range(1, size_dp):
        peer = lax.rem(me_dp + step, size_dp)
        pl.semaphore_signal(barrier, inc=1, device_id={"dp": peer}, device_id_type=MESH)
    for step in range(1, size_t):
        peer = lax.rem(me_t + step, size_t)
        pl.semaphore_signal(barrier, inc=1, device_id={"tensor": peer}, device_id_type=MESH)
    pl.semaphore_wait(barrier, size_dp + size_t - 2)

    def send(source, target, axis, step, send_sem, recv_sem):
        me, size = (me_dp, size_dp) if axis == "dp" else (me_t, size_t)
        copy = pltpu.make_async_remote_copy(
            src_ref=source, dst_ref=target, send_sem=send_sem.at[step], recv_sem=recv_sem.at[step],
            device_id={axis: lax.rem(me + step, size)}, device_id_type=MESH,
        )
        copy.start()
        return copy

    first = [
        send(piece(part_ref, lax.rem(me_dp + step, size_dp)), from_dp.at[step], "dp", step, send_dp, recv_dp)
        for step in range(1, size_dp)
    ]
    total = piece(part_ref, me_dp)[...]
    for step, copy in enumerate(first, 1):
        copy.wait_recv()
        total = total + from_dp[step]
    mine[...] = total
    second = [send(mine, from_tensor.at[step], "tensor", step, send_t, recv_t) for step in range(1, size_t)]
    for step, copy in enumerate(second, 1):
        copy.wait_recv()
        total = total + from_tensor[step]
    here = piece(out_ref, me_dp)
    here[...] = total
    piece(out_ref.at[local_rows:], me_dp)[...] = mine[local_rows:, :]
    third = [send(here, here, "dp", step, send_out, recv_out) for step in range(1, size_dp)]
    for copy in third:
        copy.wait_recv()
    for copy in first + second + third:
        copy.wait_send()


def small_sums(part, local_rows, cid):
    size_dp, size_t = lax.axis_size("dp"), lax.axis_size("tensor")
    rows, width = part.shape[0], part.shape[1] // size_dp
    vmem = pl.BlockSpec(memory_space=pltpu.VMEM)
    dma = pltpu.SemaphoreType.DMA
    f32 = jnp.float32
    return pl.pallas_call(
        functools.partial(sums_body, local_rows),
        in_specs=[vmem],
        out_specs=vmem,
        out_shape=jax.ShapeDtypeStruct(part.shape, f32),
        scratch_shapes=[
            pltpu.VMEM((size_dp, rows, width), f32), pltpu.VMEM((rows, width), f32), pltpu.VMEM((size_t, rows, width), f32),
            dma((size_dp,)), dma((size_dp,)), dma((size_t,)), dma((size_t,)), dma((size_dp,)), dma((size_dp,)),
        ],
        compiler_params=pltpu.CompilerParams(collective_id=cid, has_side_effects=True),
        name="small_sums",
    )(part)


def on_device(
    tokens,
    lengths,
    routes,
    cotangent,
    norm_one,
    qkv_weight,
    qkv_bias,
    out_weight,
    norm_two,
    router_weight,
    expert_in,
    expert_out,
    shared_in,
    shared_out,
    shared_gate,
):
    own_rows = tokens.shape[0]
    slot_count = routes.shape[0]
    model_width = tokens.shape[1]
    qkv_cols = qkv_weight.shape[2]
    local_heads = qkv_cols // HEAD_DIM
    experts = router_weight.shape[1]
    eff = expert_in.shape[3]
    shared_chunks = shared_out.shape[0] // eff
    chunks = experts + shared_chunks
    bf = jnp.bfloat16
    qkv_cols = qkv_weight.shape[2]
    length = lengths[0]
    tensor_index = lax.axis_index("tensor")
    first_row = tensor_index * own_rows
    live_own = (first_row + jnp.arange(own_rows) < length).astype(jnp.float32)[:, None]
    tokens_f = tokens.astype(jnp.float32)
    gain_one = norm_one.astype(jnp.float32)
    gain_two = norm_two.astype(jnp.float32)
    inv_one = lax.rsqrt(jnp.mean(tokens_f * tokens_f, axis=-1, keepdims=True) + epsilon)
    unit_one = tokens_f * inv_one
    normed_one = lax.all_gather((unit_one * gain_one).astype(bf), "tensor", axis=0, tiled=True)
    cos_table, sin_table = rotary_tables(slot_count, HEAD_DIM)
    qkv_w = qkv_weight.transpose(1, 0, 2)
    ei = expert_in.transpose(0, 2, 3, 1).reshape(experts, 2 * eff, model_width)
    eo = expert_out
    si = (
        shared_in.reshape(model_width, 2, shared_chunks, eff)
        .transpose(2, 1, 3, 0)
        .reshape(shared_chunks, 2 * eff, model_width)
    )
    so = shared_out.reshape(shared_chunks, eff, model_width)
    router_rows = jnp.concatenate(
        [
            router_weight.T,
            shared_gate[None],
            jnp.zeros((-(experts + 1) % 16, model_width), bf),
        ],
        axis=0,
    )
    grad_out = cotangent.astype(jnp.float32) * live_own
    d_two_own = (live_own * grad_out).astype(bf)
    normed_one, si, router_rows, cos_table, sin_table, d_two_own = lax.optimization_barrier(
        (normed_one, si, router_rows, cos_table, sin_table, d_two_own)
    )
    qkv = project_qkv(normed_one, qkv_w, qkv_bias[:, None, :], cos_table, sin_table)
    mixed, mixed_t = attend(lengths, qkv)
    branch_partial = jnp.dot(mixed, out_weight, preferred_element_type=jnp.float32).astype(bf)
    size_t = lax.axis_size("tensor")
    half = own_rows // 2
    hidden, second, x_a, d_a, d_b = finish_branch(
        lengths, branch_partial, tokens, norm_two, d_two_own, 1
    )
    inv_two = lax.rsqrt(jnp.mean(hidden * hidden, axis=-1, keepdims=True) + epsilon)
    unit_two = hidden * inv_two
    routes_a, routes_b = (
        routes.reshape(size_t, 2, half, -1).transpose(1, 0, 2, 3).reshape(2, size_t * half, -1)
    )
    x_b = lax.all_gather(second, "tensor", axis=0, tiled=True)
    weights = (router_rows, ei, si, eo, so)
    dgu_a, dn_a, bt_a, router_a, np_a, s_a = ffn(x_a, d_a, routes_a.T, *weights)
    x_b, dn_a, bt_a, s_a = lax.optimization_barrier((x_b, dn_a, bt_a, s_a))
    grad_a = lax.psum_scatter(dn_a, "tensor", scatter_dimension=0, tiled=True)
    two_a = lax.psum_scatter(bt_a, "tensor", scatter_dimension=0, tiled=True)
    if lax.axis_size("dp") == 8:
        dgu_b, dn_b, bt_b, router_b, np_b, out_grads, shared_out_grad = ffn(
            x_b, d_b, routes_b.T, *weights, other=(s_a, d_a)
        )
    else:
        dgu_b, dn_b, bt_b, router_b, np_b, s_b = ffn(x_b, d_b, routes_b.T, *weights)
        inner = [s.reshape(chunks * eff, -1) for s in (s_a, s_b)]
        out_grads, shared_out_grad = weight_grad_scatter(
            inner, [d_a, d_b], eff, 2, "down_grads", cut=experts
        )
    router_part = router_a + router_b
    norm_two_part = np_a + np_b
    d_gate_up = [d.reshape(chunks * 2 * eff, -1) for d in (dgu_a, dgu_b)]
    grad_a, two_a, dn_b = lax.optimization_barrier((grad_a, two_a, dn_b))
    grad_b = lax.psum_scatter(dn_b, "tensor", scatter_dimension=0, tiled=True)
    in_grads_b, _ = weight_grad_scatter(
        d_gate_up, [x_a, x_b], eff, 4, "shared_in_grads", 2 * experts, 2 * shared_chunks
    )
    grad_two = jnp.concatenate([grad_a, grad_b], axis=0).astype(jnp.float32)
    grad_hidden = grad_out + norm_back(grad_two, unit_two, inv_two, gain_two)
    d_one_own, in_grads_b = lax.optimization_barrier(
        ((live_own * grad_hidden).astype(bf), in_grads_b)
    )
    d_one = lax.all_gather(d_one_own, "tensor", axis=0, tiled=True)
    d_gate_up, _ = lax.optimization_barrier((d_gate_up, d_one_own))
    in_grads_a, _ = weight_grad_scatter(
        d_gate_up, [x_a, x_b], eff, 3, "expert_in_grads", 0, 2 * experts
    )
    d_one, in_grads_a, bt_b = lax.optimization_barrier((d_one, in_grads_a, bt_b))
    two_b = lax.psum_scatter(bt_b, "tensor", scatter_dimension=0, tiled=True)
    d_mixed = lax.dot_general(d_one, out_weight, NT, preferred_element_type=jnp.float32).astype(bf)
    d_qkv, d_qkv_t, bias_part = attend_back(lengths, qkv, d_mixed, cos_table, sin_table)
    grad_one, norm_one_part = qkv_back(d_qkv, qkv_w, normed_one)
    grad_one, d_qkv_t, mixed_t, two_b = lax.optimization_barrier(
        (grad_one, d_qkv_t, mixed_t, two_b)
    )
    grad_one_own = lax.psum_scatter(grad_one, "tensor", scatter_dimension=0, tiled=True)
    part = jnp.concatenate(
        [
            router_part[: experts + 1],
            norm_one_part / gain_one[None],
            norm_two_part / gain_two[None],
            jnp.pad(bias_part.reshape(1, 3 * qkv_cols), ((0, 0), (0, model_width - 3 * qkv_cols))),
        ],
        axis=0,
    )
    sums = small_sums(part, experts + 3, 7)
    qkv_sum, _ = weight_grad_scatter(
        [d_qkv_t.reshape(3 * qkv_cols, slot_count)], [normed_one], 3 * qkv_cols // 4, 5, "qkv_grads"
    )
    out_sum, _ = weight_grad_scatter([mixed_t], [d_one], qkv_cols // 2, 6, "mix_grads")
    branch_two = jnp.concatenate([two_a, two_b], axis=0).astype(jnp.float32)
    output = (hidden + live_own * branch_two).astype(bf)
    grad_one = grad_one_own.astype(jnp.float32)
    input_grad = grad_hidden + norm_back(grad_one, unit_one, inv_one, gain_one)
    qkv_bias_grad = sums[experts + 3, : 3 * qkv_cols].reshape(3, qkv_cols)
    own_cols = out_grads.shape[1]
    expert_in_grad = in_grads_a.reshape(experts, 2, eff, own_cols).transpose(0, 3, 1, 2)
    shared_in_grad = (
        in_grads_b.reshape(shared_chunks, 2, eff, own_cols)
        .transpose(3, 1, 0, 2)
        .reshape(own_cols, 2, shared_chunks * eff)
    )
    return (
        output,
        input_grad,
        sums[experts + 1],
        qkv_sum.reshape(3, qkv_cols, own_cols).transpose(2, 0, 1),
        qkv_bias_grad,
        out_sum,
        sums[experts + 2],
        sums[:experts].T,
        expert_in_grad,
        out_grads.reshape(experts, eff, own_cols),
        shared_in_grad,
        shared_out_grad,
        sums[experts],
    )


def solution(mesh):
    in_specs = (
        P(("dp", "tensor"), None),
        P("dp"),
        P("dp", None),
        P(("dp", "tensor"), None),
        P(),
        P(None, None, "tensor"),
        P(None, "tensor"),
        P("tensor", None),
        P(),
        P(),
        P(None, None, None, "tensor"),
        P(None, "tensor", None),
        P(None, None, "tensor"),
        P("tensor", None),
        P(),
    )
    out_specs = (
        P(("dp", "tensor"), None),
        P(("dp", "tensor"), None),
        P(),
        P("dp", None, "tensor"),
        P(None, "tensor"),
        P("tensor", "dp"),
        P(),
        P(),
        P(None, "dp", None, "tensor"),
        P(None, "tensor", "dp"),
        P("dp", None, "tensor"),
        P("tensor", "dp"),
        P(),
    )
    return jax.shard_map(
        on_device, mesh=mesh, in_specs=in_specs, out_specs=out_specs, check_vma=False
    )
```

```python
import functools

import jax
import jax.numpy as jnp
from jax import lax
from jax.experimental import pallas as pl
from jax.experimental.pallas import tpu as pltpu
from jax.sharding import PartitionSpec as P

HEAD_DIM = 128
MESH = pl.DeviceIdType.MESH
LA, LB, LC = 1, 2, 2
FFN_LAGS = (1, 1, 1)
MIB = 2**20


epsilon = 1e-06
theta_base = 1000000.0
NT = (((1,), (1,)), ((), ()))
TN = (((0,), (0,)), ((), ()))


def rotary_tables(row_count, head_width):
    half_index = jnp.arange(head_width // 2).astype(jnp.float32)
    frequency = theta_base ** (-2.0 * half_index / head_width)
    angles = jnp.arange(row_count).astype(jnp.float32)[:, None] * frequency[None, :]
    sines = jnp.sin(angles)
    cosines = jnp.cos(angles)
    return (
        jnp.concatenate([cosines, cosines], axis=-1),
        jnp.concatenate([-sines, sines], axis=-1),
    )


def norm_back(d_normed, unit_rows, inverse, gain_vector):
    d_unit = d_normed * gain_vector
    return inverse * (d_unit - unit_rows * jnp.mean(d_unit * unit_rows, axis=-1, keepdims=True))


def scatter_scratch(r, w):
    f32, bf = jnp.float32, jnp.bfloat16
    dma = pltpu.SemaphoreType.DMA
    h = r // 2
    return [
        pltpu.VMEM((2, 4, r, w), f32), pltpu.VMEM((2, 4, r, w), bf), pltpu.VMEM((3, 4, r, w), bf),
        pltpu.VMEM((3, 2, 2, h, w), f32), pltpu.VMEM((3, 2, 2, h, w), bf), pltpu.VMEM((6, 2, 2, h, w), bf),
        pltpu.VMEM((3, 2, h, w), f32), pltpu.VMEM((2, 2, h, w), bf), pltpu.VMEM((6, 2, h, w), bf),
        dma((2,)), dma((3,)), dma((3, 2)), dma((6, 2)), dma((2, 2)), dma((6, 2)),
    ]


def scatter_steps(i, nc, lags, w, scratch, store, greet=None):
    own, sa, ra, kt, s1, r1, ku, s2, r2, sem_sa, sem_ra, sem_s1, sem_r1, sem_s2, sem_r2 = scratch
    la, lb, lc = lags
    keep_1 = min(3, lb + lc)
    hr = own.shape[2] // 2
    dp = lax.axis_index("dp")
    k = dp % 2
    x = (dp // 2) % 2
    y = dp // 4
    core_peer = y * 4 + x * 2 + (1 - k)
    x_peer = y * 4 + (1 - x) * 2 + k
    y_peer = (1 - y) * 4 + x * 2 + k

    def copy_a(c):
        return pltpu.make_async_remote_copy(
            src_ref=sa.at[c % 2], dst_ref=ra.at[c % 3], send_sem=sem_sa.at[c % 2], recv_sem=sem_ra.at[c % 3],
            device_id={"dp": core_peer}, device_id_type=MESH,
        )

    def copy_1(c, half):
        return pltpu.make_async_remote_copy(
            src_ref=s1.at[c % 3, half], dst_ref=r1.at[c % 6, half], send_sem=sem_s1.at[c % 3, half],
            recv_sem=sem_r1.at[c % 6, half], device_id={"dp": y_peer if half else x_peer}, device_id_type=MESH,
        )

    def copy_2(c, half):
        return pltpu.make_async_remote_copy(
            src_ref=s2.at[c % 2, half], dst_ref=r2.at[c % 6, half], send_sem=sem_s2.at[c % 2, half],
            recv_sem=sem_r2.at[c % 6, half], device_id={"dp": x_peer if half else y_peer}, device_id_type=MESH,
        )

    @pl.when(i == 0)
    def _():
        if greet is not None:
            greet()
            return
        barrier = pltpu.get_barrier_semaphore()
        for peer in (core_peer, x_peer, y_peer):
            pl.semaphore_signal(barrier, inc=1, device_id={"dp": peer}, device_id_type=MESH)
        pl.semaphore_wait(barrier, 3)

    @pl.when((i >= la + keep_1) & (i < nc + la + keep_1))
    def _():
        copy_1(i - la - keep_1, 0).wait_send()
        copy_1(i - la - keep_1, 1).wait_send()

    @pl.when((i >= la) & (i < nc + la))
    def _():
        c = i - la
        copy_a(c).wait_recv()
        for half in range(2):
            rows = slice(half * hr, half * hr + hr)
            keep, other = (1, 2) if half else (2, 1)

            def total(role):
                return own[c % 2, role, rows, :] + ra[c % 3, role, rows, :].astype(jnp.float32)

            s1[c % 3, half, 0] = total(other).astype(jnp.bfloat16)
            s1[c % 3, half, 1] = total(3).astype(jnp.bfloat16)
            copy_1(c, half).start()
            kt[c % 3, half, 0] = total(0)
            kt[c % 3, half, 1] = total(keep)

    @pl.when((i >= la + lb) & (i < nc + la + lb))
    def _():
        c = i - la - lb

        @pl.when(c >= 2)
        def _():
            copy_2(c - 2, 0).wait_send()
            copy_2(c - 2, 1).wait_send()

        for half in range(2):
            copy_1(c, half).wait_recv()
            s2[c % 2, half] = (kt[c % 3, half, 1] + r1[c % 6, half, 1].astype(jnp.float32)).astype(jnp.bfloat16)
            copy_2(c, half).start()
            ku[c % 3, half] = kt[c % 3, half, 0] + r1[c % 6, half, 0].astype(jnp.float32)

    @pl.when(i >= la + lb + lc)
    def _():
        c = i - la - lb - lc
        for half in range(2):
            copy_2(c, half).wait_recv()
            store(c, slice(half * hr, half * hr + hr), ku[c % 3, half] + r2[c % 6, half].astype(jnp.float32))

        @pl.when(c >= nc - 2)
        def _():
            copy_2(c, 0).wait_send()
            copy_2(c, 1).wait_send()

    @pl.when((i >= 2) & (i < nc + 2))
    def _():
        copy_a(i - 2).wait_send()

    def send(product):
        targets = (y * 4 + x * 2, y * 4 + (1 - x) * 2, (1 - y) * 4 + x * 2, (1 - y) * 4 + (1 - x) * 2)

        def cols(role, core):
            return pl.ds(pl.multiple_of((targets[role] + core) * w, w), w)

        for role in range(4):
            sa[i % 2, role] = product(cols(role, 1 - k)).astype(jnp.bfloat16)
        copy_a(i).start()
        for role in range(4):
            own[i % 2, role] = product(cols(role, k))

    return send


def rs_body(nc, cut, pairs, *refs):
    a_refs, b_refs = refs[:pairs], refs[pairs : 2 * pairs]
    o_ref, o2_ref = refs[2 * pairs : 2 * pairs + 2]
    i = pl.program_id(0)

    def store(c, rows, result):
        @pl.when(c < cut)
        def _():
            o_ref[rows, :] = result.astype(o_ref.dtype)

        @pl.when(c >= cut)
        def _():
            o2_ref[rows, :] = result.astype(o2_ref.dtype)

    send = scatter_steps(i, nc, (LA, LB, LC), o_ref.shape[1], refs[2 * pairs + 2 :], store)

    @pl.when(i < nc)
    def _():
        def product(cols):
            total = jnp.dot(a_refs[0][...], b_refs[0][:, cols], preferred_element_type=jnp.float32)
            for a_ref, b_ref in zip(a_refs[1:], b_refs[1:]):
                total += jnp.dot(a_ref[...], b_ref[:, cols], preferred_element_type=jnp.float32)
            return total

        send(product)


def scatter_outs(nc, cut, lag, r, w):
    rest = max(nc - cut, 1)
    specs = [
        pl.BlockSpec((r, w), lambda i: (jnp.clip(i - lag, 0, cut - 1), 0)),
        pl.BlockSpec((r, w), lambda i: (jnp.clip(i - lag - cut, 0, rest - 1), 0)),
    ]
    return specs, [jax.ShapeDtypeStruct((n * r, w), jnp.bfloat16) for n in (cut, rest)]


def weight_grad_scatter_kernel(a_list, b_list, r, cid, name, first, count, cut):
    D = b_list[0].shape[1]
    T = sum(b.shape[0] for b in b_list)
    w = D // 8
    lag = LA + LB + LC
    out_specs, out_shape = scatter_outs(count, cut, lag, r, w)
    return pl.pallas_call(
        functools.partial(rs_body, count, cut, len(a_list)),
        grid=(count + lag,),
        in_specs=[
            *[pl.BlockSpec((r, a.shape[1]), lambda i: (jnp.minimum(i, count - 1) + first, 0)) for a in a_list],
            *[pl.BlockSpec(b.shape, lambda i: (0, 0), pipeline_mode=pl.Buffered(1)) for b in b_list],
        ],
        out_specs=out_specs,
        out_shape=out_shape,
        scratch_shapes=scatter_scratch(r, w),
        compiler_params=pltpu.CompilerParams(vmem_limit_bytes=48 * MIB, collective_id=cid, has_side_effects=True),
        cost_estimate=pl.CostEstimate(
            flops=2 * count * r * T * D, bytes_accessed=2 * count * r * T + 2 * T * D + 4 * count * r * w, transcendentals=0
        ),
        name=name,
    )(*a_list, *b_list)


def ffn_body(
    experts, chunks, scatter,
    x_ref, d_ref, routes_ref, rw_ref, ei_ref, si_ref, eo_ref, so_ref, *refs,
):
    if scatter:
        s_other_ref, d_other_ref, dgu_ref, dn_ref, bt_ref, rg_ref, np_ref, og_ref, og2_ref, *refs = refs
    else:
        dgu_ref, dn_ref, bt_ref, rg_ref, np_ref, s_ref, *refs = refs
    dn_acc, bt_acc, probs_ref, w_ref, ds_ref, wi_buf, wd_buf, sem, *scratch = refs
    c = pl.program_id(0)
    h = eo_ref.shape[1]
    slots, width = x_ref.shape

    def fetch(step):
        slot = step % 2

        @pl.when(step < experts)
        def _():
            pltpu.make_async_copy(ei_ref.at[step], wi_buf.at[slot], sem.at[0, slot]).start()
            pltpu.make_async_copy(eo_ref.at[step], wd_buf.at[slot], sem.at[1, slot]).start()

        @pl.when(step >= experts)
        def _():
            pltpu.make_async_copy(si_ref.at[step - experts], wi_buf.at[slot], sem.at[0, slot]).start()
            pltpu.make_async_copy(so_ref.at[step - experts], wd_buf.at[slot], sem.at[1, slot]).start()

    @pl.when(c == 0)
    def _():
        fetch(c)

    @pl.when(c + 1 < chunks)
    def _():
        fetch(c + 1)

    def picked():
        expert = lax.broadcasted_iota(jnp.int32, (experts, slots), 0)
        hit = jnp.zeros((experts, slots), jnp.float32)
        for j in range(routes_ref.shape[0]):
            hit = hit + jnp.where(routes_ref[j : j + 1, :] == expert, 1.0, 0.0)
        return hit

    @pl.when(c == 0)
    def _():
        logits = lax.dot_general(rw_ref[...], x_ref[...], NT, preferred_element_type=jnp.float32)
        raised = jnp.exp(logits[:experts] - jnp.max(logits[:experts], axis=0, keepdims=True))
        probs = raised / jnp.sum(raised, axis=0, keepdims=True)
        gate = 1.0 / (1.0 + jnp.exp(-logits[experts:]))
        probs_ref[...] = probs
        w_ref[:experts, :] = probs * picked()
        w_ref[experts:, :] = gate
        ds_ref[...] = jnp.zeros_like(ds_ref)
        dn_acc[...] = jnp.zeros_like(dn_acc)
        bt_acc[...] = jnp.zeros_like(bt_acc)

    if scatter:
        def store(chunk, rows, result):
            @pl.when(chunk < experts)
            def _():
                og_ref[rows, :] = result.astype(og_ref.dtype)

            @pl.when(chunk >= experts)
            def _():
                og2_ref[rows, :] = result.astype(og2_ref.dtype)

        send = scatter_steps(c, chunks, FFN_LAGS, og_ref.shape[1], scratch, store)

    block = 512

    @pl.when(c < chunks)
    def _():
        row = pl.ds(jnp.minimum(c, experts), 1)
        slot = c % 2
        pltpu.make_async_copy(ei_ref.at[0], wi_buf.at[slot], sem.at[0, slot]).wait()
        pltpu.make_async_copy(eo_ref.at[0], wd_buf.at[slot], sem.at[1, slot]).wait()
        wi = wi_buf.at[slot]
        wd = wd_buf.at[slot]
        x = x_ref[...]
        g = lax.dot_general(wi[:h], x, NT, preferred_element_type=jnp.float32)
        u = lax.dot_general(wi[h:], x, NT, preferred_element_type=jnp.float32)
        p = lax.dot_general(wd[...], d_ref[...], NT, preferred_element_type=jnp.float32)
        w = w_ref[row, :]
        sg = 1.0 / (1.0 + jnp.exp(-g))
        si = g * sg
        inner = (si * u).astype(jnp.bfloat16).astype(jnp.float32)
        s = (w * inner).astype(jnp.bfloat16)
        ds_ref[row, :] += jnp.sum(p * inner, axis=0, keepdims=True)
        di = w * p
        dg = (di * u * sg * (1.0 + g * (1.0 - sg))).astype(jnp.bfloat16)
        du = (di * si).astype(jnp.bfloat16)
        dgu_ref[0, :h] = dg
        dgu_ref[0, h:] = du
        dgu = jnp.concatenate([dg, du], axis=0)
        if scatter:
            def product(cols):
                return jnp.dot(s, d_ref[:, cols], preferred_element_type=jnp.float32) + jnp.dot(
                    s_other_ref[0], d_other_ref[:, cols], preferred_element_type=jnp.float32
                )

            send(product)
        else:
            s_ref[0] = s
        for n in range(0, width, block):
            cols = slice(n, n + block)
            dn_acc[:, cols] += lax.dot_general(dgu, wi[:, cols], TN, preferred_element_type=jnp.float32)
            bt_acc[:, cols] += lax.dot_general(s, wd[:, cols], TN, preferred_element_type=jnp.float32)

    @pl.when(c == chunks - 1)
    def _():
        probs = probs_ref[...]
        d_probs = ds_ref[:experts, :] * picked()
        d_logits = probs * (d_probs - jnp.sum(probs * d_probs, axis=0, keepdims=True))
        gate = w_ref[experts:, :]
        d_gate = ds_ref[experts:, :] * gate * (1.0 - gate)
        small = jnp.concatenate([d_logits, d_gate], axis=0)
        high = small.astype(jnp.bfloat16)
        low = (small - high.astype(jnp.float32)).astype(jnp.bfloat16)
        rg_ref[...] = jnp.dot(high, x_ref[...], preferred_element_type=jnp.float32) + jnp.dot(
            low, x_ref[...], preferred_element_type=jnp.float32
        )
        for n in range(0, width, block):
            cols = slice(n, n + block)
            extra = lax.dot_general(high, rw_ref[:, cols], TN, preferred_element_type=jnp.float32)
            extra += lax.dot_general(low, rw_ref[:, cols], TN, preferred_element_type=jnp.float32)
            total = dn_acc[:, cols] + extra
            dn_ref[:, cols] = total.astype(dn_ref.dtype)
            np_ref[:, cols] = jnp.sum(total * x_ref[:, cols].astype(jnp.float32), axis=0, keepdims=True)
        bt_ref[...] = bt_acc[...].astype(bt_ref.dtype)


def ffn(x, d_two, routes_t, router_rows, ei, si, eo, so, other=None):
    experts, h2, width = ei.shape
    chunks = experts + si.shape[0]
    h = h2 // 2
    slots = x.shape[0]
    rows = router_rows.shape[0]
    bf, f32 = jnp.bfloat16, jnp.float32
    anywhere = pl.BlockSpec(memory_space=pl.ANY)
    scatter = other is not None

    def whole(shape):
        return pl.BlockSpec(shape, lambda c: (0,) * len(shape), pipeline_mode=pl.Buffered(1))

    def chunk(shape):
        return pl.BlockSpec((1, *shape), lambda c: (jnp.minimum(c, chunks - 1), 0, 0))

    in_specs = [
        whole((slots, width)), whole((slots, width)), whole(routes_t.shape), whole((rows, width)),
        anywhere, anywhere, anywhere, anywhere,
    ]
    out_specs = [chunk((h2, slots)), whole((slots, width)), whole((slots, width)), whole((rows, width)), whole((1, width))]
    out_shape = [
        jax.ShapeDtypeStruct((chunks, h2, slots), bf), jax.ShapeDtypeStruct((slots, width), bf),
        jax.ShapeDtypeStruct((slots, width), bf), jax.ShapeDtypeStruct((rows, width), f32),
        jax.ShapeDtypeStruct((1, width), f32),
    ]
    scratch = [
        pltpu.VMEM((slots, width), f32), pltpu.VMEM((slots, width), f32),
        pltpu.VMEM((experts, slots), f32), pltpu.VMEM((rows, slots), f32), pltpu.VMEM((rows, slots), f32),
        pltpu.VMEM((2, h2, width), bf), pltpu.VMEM((2, h, width), bf), pltpu.SemaphoreType.DMA((2, 2)),
    ]
    args = [x, d_two, routes_t, router_rows, ei, si, eo, so]
    if scatter:
        s_other, d_other = other
        in_specs += [chunk((h, s_other.shape[2])), whole(d_other.shape)]
        args += [s_other, d_other]
        w = width // 8
        lag = sum(FFN_LAGS)
        specs, shapes = scatter_outs(chunks, experts, lag, h, w)
        out_specs += specs
        out_shape += shapes
        scratch += scatter_scratch(h, w)
        grid = (chunks + lag,)
        params = pltpu.CompilerParams(vmem_limit_bytes=62 * MIB, collective_id=2, has_side_effects=True)
    else:
        out_specs.append(chunk((h, slots)))
        out_shape.append(jax.ShapeDtypeStruct((chunks, h, slots), bf))
        grid = (chunks,)
        params = pltpu.CompilerParams(vmem_limit_bytes=62 * MIB)
    return pl.pallas_call(
        functools.partial(ffn_body, experts, chunks, scatter),
        grid=grid,
        in_specs=in_specs,
        out_specs=out_specs,
        out_shape=out_shape,
        scratch_shapes=scratch,
        compiler_params=params,
        cost_estimate=pl.CostEstimate(
            flops=12 * chunks * h * slots * width, bytes_accessed=10 * chunks * h * width + 16 * slots * width,
            transcendentals=chunks * h * slots,
        ),
        name="ffn_scatter" if scatter else "ffn",
    )(*args)


def turn(v):
    half = v.shape[1] // 2
    return jnp.concatenate([v[:, half:], v[:, :half]], axis=1)


def qkv_body(x_ref, w_ref, bias_ref, cos_ref, sin_ref, out_ref):
    j = pl.program_id(0)
    cols = w_ref.shape[2]
    y = jnp.dot(x_ref[...], w_ref[0], preferred_element_type=jnp.float32)
    y = y + bias_ref[0].astype(jnp.float32)

    @pl.when(j < 2)
    def _():
        for head in range(cols // HEAD_DIM):
            place = slice(head * HEAD_DIM, (head + 1) * HEAD_DIM)
            v = y[:, place]
            out_ref[0, :, place] = (v * cos_ref[...] + turn(v) * sin_ref[...]).astype(out_ref.dtype)

    @pl.when(j == 2)
    def _():
        out_ref[0] = y.astype(out_ref.dtype)


def project_qkv(x, w, bias, cos_table, sin_table):
    slots, width = x.shape
    cols = w.shape[2]
    table = pl.BlockSpec((slots, HEAD_DIM), lambda j: (0, 0), pipeline_mode=pl.Buffered(1))
    return pl.pallas_call(
        qkv_body,
        grid=(3,),
        in_specs=[
            pl.BlockSpec((slots, width), lambda j: (0, 0), pipeline_mode=pl.Buffered(1)),
            pl.BlockSpec((1, width, cols), lambda j: (j, 0, 0)),
            pl.BlockSpec((1, 1, cols), lambda j: (j, 0, 0)),
            table, table,
        ],
        out_specs=pl.BlockSpec((1, slots, cols), lambda j: (j, 0, 0)),
        out_shape=jax.ShapeDtypeStruct((3, slots, cols), jnp.bfloat16),
        compiler_params=pltpu.CompilerParams(vmem_limit_bytes=48 * MIB),
        cost_estimate=pl.CostEstimate(
            flops=6 * slots * width * cols, bytes_accessed=2 * slots * width + 6 * width * cols, transcendentals=0
        ),
        name="project_qkv",
    )(x, w, bias, cos_table, sin_table)


def block_probs(length_ref, q, k, start):
    s = lax.dot_general(q, k, NT, preferred_element_type=jnp.float32) * (HEAD_DIM**-0.5)
    row = lax.broadcasted_iota(jnp.int32, s.shape, 0) + start
    col = lax.broadcasted_iota(jnp.int32, s.shape, 1)
    s = jnp.where((col <= row) & (col < length_ref[0]), s, -1000000000.0)
    e = jnp.exp(s - jnp.max(s, axis=1, keepdims=True))
    return e * (1.0 / jnp.sum(e, axis=1, keepdims=True))


def attend_body(rows, length_ref, q_ref, k_ref, v_ref, mixed_ref, mixed_t_ref):
    for start in range(0, q_ref.shape[1], rows):
        here, end = slice(start, start + rows), start + rows
        p = block_probs(length_ref, q_ref[0, here, :], k_ref[0, :end, :], start)
        mixed = jnp.dot(p.astype(jnp.bfloat16), v_ref[0, :end, :], preferred_element_type=jnp.float32)
        mixed_ref[here, :] = mixed.astype(mixed_ref.dtype)
        mixed_t_ref[:, here] = mixed.T.astype(mixed_ref.dtype)


def attend(lengths, qkv):
    _, slots, cols = qkv.shape
    rows = min(256, slots)

    def part(j):
        return pl.BlockSpec((1, slots, HEAD_DIM), lambda h: (j, 0, h))

    return pl.pallas_call(
        functools.partial(attend_body, rows),
        grid=(cols // HEAD_DIM,),
        in_specs=[pl.BlockSpec(memory_space=pltpu.SMEM), part(0), part(1), part(2)],
        out_specs=[
            pl.BlockSpec((slots, HEAD_DIM), lambda h: (0, h)), pl.BlockSpec((HEAD_DIM, slots), lambda h: (h, 0)),
        ],
        out_shape=[
            jax.ShapeDtypeStruct((slots, cols), jnp.bfloat16), jax.ShapeDtypeStruct((cols, slots), jnp.bfloat16),
        ],
        compiler_params=pltpu.CompilerParams(vmem_limit_bytes=32 * MIB),
        cost_estimate=pl.CostEstimate(
            flops=4 * slots * slots * cols, bytes_accessed=10 * slots * cols, transcendentals=slots * slots * cols // HEAD_DIM
        ),
        name="attend",
    )(lengths, qkv, qkv, qkv)


def attend_back_body(
    rows, length_ref, q_ref, k_ref, v_ref, dm_ref, cos_ref, sin_ref, out_ref, out_t_ref, bias_ref, dk_acc, dv_acc
):
    slots = q_ref.shape[1]
    scale = HEAD_DIM**-0.5
    bf, f32 = jnp.bfloat16, jnp.float32

    def finish(j, here, grad):
        if j < 2:
            grad = grad * cos_ref[here, :] - turn(grad) * sin_ref[here, :]
        low = grad.astype(bf)
        out_ref[j, here, :] = low
        out_t_ref[j, :, here] = grad.T.astype(bf)
        return jnp.sum(low.astype(f32), axis=0, keepdims=True)

    dq_sum = jnp.zeros((1, HEAD_DIM), f32)
    starts = list(range(0, slots, rows))[::-1]
    for start in starts:
        here, end = slice(start, start + rows), start + rows
        q, k, v, dm = q_ref[0, here, :], k_ref[0, :end, :], v_ref[0, :end, :], dm_ref[here, :]
        p = block_probs(length_ref, q, k, start)
        dp = lax.dot_general(dm, v, NT, preferred_element_type=f32)
        ds = (p * (dp - jnp.sum(p * dp, axis=1, keepdims=True))).astype(bf)
        dq_sum += finish(0, here, jnp.dot(ds, k, preferred_element_type=f32) * scale)
        dk = lax.dot_general(ds, q, TN, preferred_element_type=f32) * scale
        dv = lax.dot_general(p.astype(bf), dm, TN, preferred_element_type=f32)
        if start == starts[0]:
            dk_acc[...] = dk
            dv_acc[...] = dv
        else:
            dk_acc[:end, :] += dk
            dv_acc[:end, :] += dv
    every = slice(0, slots)
    bias_ref[0] = dq_sum
    bias_ref[1] = finish(1, every, dk_acc[...])
    bias_ref[2] = finish(2, every, dv_acc[...])


def attend_back(lengths, qkv, d_mixed, cos_table, sin_table):
    _, slots, cols = qkv.shape
    rows = min(256, slots)
    bf, f32 = jnp.bfloat16, jnp.float32

    def part(j):
        return pl.BlockSpec((1, slots, HEAD_DIM), lambda h: (j, 0, h))

    table = pl.BlockSpec((slots, HEAD_DIM), lambda h: (0, 0), pipeline_mode=pl.Buffered(1))
    return pl.pallas_call(
        functools.partial(attend_back_body, rows),
        grid=(cols // HEAD_DIM,),
        in_specs=[
            pl.BlockSpec(memory_space=pltpu.SMEM), part(0), part(1), part(2),
            pl.BlockSpec((slots, HEAD_DIM), lambda h: (0, h)), table, table,
        ],
        out_specs=[
            pl.BlockSpec((3, slots, HEAD_DIM), lambda h: (0, 0, h)), pl.BlockSpec((3, HEAD_DIM, slots), lambda h: (0, h, 0)),
            pl.BlockSpec((3, 1, HEAD_DIM), lambda h: (0, 0, h)),
        ],
        out_shape=[
            jax.ShapeDtypeStruct((3, slots, cols), bf), jax.ShapeDtypeStruct((3, cols, slots), bf),
            jax.ShapeDtypeStruct((3, 1, cols), f32),
        ],
        scratch_shapes=[pltpu.VMEM((slots, HEAD_DIM), f32), pltpu.VMEM((slots, HEAD_DIM), f32)],
        compiler_params=pltpu.CompilerParams(vmem_limit_bytes=40 * MIB),
        cost_estimate=pl.CostEstimate(
            flops=10 * slots * slots * cols, bytes_accessed=20 * slots * cols, transcendentals=slots * slots * cols // HEAD_DIM
        ),
        name="attend_back",
    )(lengths, qkv, qkv, qkv, d_mixed, cos_table, sin_table)


def qkv_back_body(d_ref, w_ref, x_ref, out_ref, np_ref):
    total = lax.dot_general(d_ref[0], w_ref[0], NT, preferred_element_type=jnp.float32)
    for j in range(1, 3):
        total += lax.dot_general(d_ref[j], w_ref[j], NT, preferred_element_type=jnp.float32)
    out_ref[...] = total.astype(out_ref.dtype)
    np_ref[...] = jnp.sum(total * x_ref[...].astype(jnp.float32), axis=0, keepdims=True)


def qkv_back(d_qkv, w, x):
    _, slots, cols = d_qkv.shape
    width = w.shape[1]
    block = 512
    return pl.pallas_call(
        qkv_back_body,
        grid=(width // block,),
        in_specs=[
            pl.BlockSpec((3, slots, cols), lambda n: (0, 0, 0), pipeline_mode=pl.Buffered(1)),
            pl.BlockSpec((3, block, cols), lambda n: (0, n, 0)),
            pl.BlockSpec((slots, block), lambda n: (0, n)),
        ],
        out_specs=[pl.BlockSpec((slots, block), lambda n: (0, n)), pl.BlockSpec((1, block), lambda n: (0, n))],
        out_shape=[
            jax.ShapeDtypeStruct((slots, width), jnp.bfloat16), jax.ShapeDtypeStruct((1, width), jnp.float32),
        ],
        compiler_params=pltpu.CompilerParams(vmem_limit_bytes=48 * MIB),
        cost_estimate=pl.CostEstimate(
            flops=6 * slots * width * cols, bytes_accessed=4 * slots * width + 6 * width * cols, transcendentals=0
        ),
        name="qkv_back",
    )(d_qkv, w, x)


def weight_grad_scatter(a_list, b_list, r, cid, name, first=0, count=None, cut=None):
    count = a_list[0].shape[0] // r if count is None else count
    cut = count if cut is None else cut
    if lax.axis_size("dp") == 8:
        return weight_grad_scatter_kernel(a_list, b_list, r, cid, name, first, count, cut)
    product = sum(
        jnp.dot(a[first * r : (first + count) * r], b, preferred_element_type=jnp.float32)
        for a, b in zip(a_list, b_list)
    )
    result = lax.psum_scatter(product.astype(jnp.bfloat16), "dp", scatter_dimension=1, tiled=True)
    return result[: cut * r], result[cut * r :]


def line_gather(me, size, own, block, local_sem, sems):
    send_left, recv_left, send_right, recv_right = sems
    has_left, has_right = me > 0, me < size - 1

    def remote(source, owner, send, recv, step, to):
        return pltpu.make_async_remote_copy(
            src_ref=source, dst_ref=block(owner), send_sem=send.at[step], recv_sem=recv.at[step],
            device_id={"tensor": to}, device_id_type=MESH,
        )

    def to_left(step):
        return remote(own if step == 0 else block(me + step), me + step, send_left, recv_left, step, me - 1)

    def to_right(step):
        return remote(own if step == 0 else block(me - step), me - step, send_right, recv_right, step, me + 1)

    def advance(step):
        if step == 0:
            pltpu.make_async_copy(own, block(me), local_sem).start()
        else:
            @pl.when(me + step < size)
            def _():
                remote(own, me + step, send_left, recv_left, step - 1, me + 1).wait_recv()

        @pl.when(has_left & (me + step < size))
        def _():
            to_left(step).start()

        if step > 0:
            @pl.when(me - step >= 0)
            def _():
                remote(own, me - step, send_right, recv_right, step - 1, me - 1).wait_recv()

        @pl.when(has_right & (me - step >= 0))
        def _():
            to_right(step).start()

    def finish():
        for step in range(size):
            @pl.when(has_left & (me + step < size))
            def _():
                to_left(step).wait_send()

            @pl.when(has_right & (me - step >= 0))
            def _():
                to_right(step).wait_send()

        pltpu.make_async_copy(own, block(me), local_sem).wait()

    return advance, finish


def line_barrier(me, size):
    barrier = pltpu.get_barrier_semaphore()
    has_left, has_right = me > 0, me < size - 1

    @pl.when(has_left)
    def _():
        pl.semaphore_signal(barrier, inc=1, device_id={"tensor": me - 1}, device_id_type=MESH)

    @pl.when(has_right)
    def _():
        pl.semaphore_signal(barrier, inc=1, device_id={"tensor": me + 1}, device_id_type=MESH)

    pl.semaphore_wait(barrier, has_left.astype(jnp.int32) + has_right.astype(jnp.int32))


def branch_body(
    length_ref, part_ref, tokens_ref, gain_ref, cot_ref, hidden_ref, second_ref, xa_ref, da_ref, db_ref,
    from_left, from_right, normed, local_sem, send_r, recv_r, send_l, recv_l, *sems,
):
    me = lax.axis_index("tensor")
    size = lax.axis_size("tensor")
    rows = tokens_ref.shape[0]
    half = rows // 2
    bf, f32 = jnp.bfloat16, jnp.float32
    has_left, has_right = me > 0, me < size - 1
    line_barrier(me, size)

    def place(ref, owner):
        return ref.at[pl.ds(pl.multiple_of(owner * half, half), half)]

    def own_cot(h):
        return cot_ref.at[pl.ds(h * half, half)]

    def part(ref, owner, h):
        return ref.at[owner, pl.ds(h * half, half)]

    def direction(right):
        slots, send, recv = (from_left, send_r, recv_r) if right else (from_right, send_l, recv_l)
        to = me + 1 if right else me - 1
        before = me if right else size - 1 - me
        has_to = has_right if right else has_left
        has_from = has_left if right else has_right

        def copy(source, target, t):
            return pltpu.make_async_remote_copy(
                src_ref=source, dst_ref=target, send_sem=send.at[t], recv_sem=recv.at[t],
                device_id={"tensor": to}, device_id_type=MESH,
            )

        def sent(t):
            copy(part(part_ref, 0, 0), part(slots, 0, 0), t).wait_send()

        def step(t):
            s, h = t // 2, t % 2
            gathered = (da_ref, db_ref)[h]
            if t >= 2:
                @pl.when(has_to)
                def _():
                    sent(t - 2)

            @pl.when(s <= before)
            def _():
                owner = me - s if right else me + s
                if s > 0:
                    copy(own_cot(h), place(gathered, owner), t - 2).wait_recv()

                @pl.when(has_to)
                def _():
                    copy(own_cot(h) if s == 0 else place(gathered, owner), place(gathered, owner), t).start()

            @pl.when(s > before)
            def _():
                owner = size + me - s if right else me + s - size

                @pl.when(has_from)
                def _():
                    copy(part(part_ref, owner, h), part(slots, owner, h), t - 2).wait_recv()
                    both = part(slots, owner, h)
                    both[...] = (both[...].astype(f32) + part(part_ref, owner, h)[...].astype(f32)).astype(bf)
                    copy(both, part(slots, owner, h), t).start()

                @pl.when(jnp.logical_not(has_from))
                def _():
                    copy(part(part_ref, owner, h), part(slots, owner, h), t).start()

        def last():
            @pl.when(has_to)
            def _():
                sent(2 * size - 2)
                sent(2 * size - 1)

            @pl.when(has_from)
            def _():
                for h in range(2):
                    copy(part(part_ref, me, h), part(slots, me, h), 2 * size - 2 + h).wait_recv()
                hidden_ref[...] += slots[me].astype(f32)

        return step, last

    local = [
        pltpu.make_async_copy(own_cot(h), place(ref, me), local_sem.at[h]) for h, ref in enumerate((da_ref, db_ref))
    ]
    for copy in local:
        copy.start()
    step_r, last_r = direction(True)
    step_l, last_l = direction(False)
    for t in range(2 * size):
        step_r(t)
        step_l(t)
    hidden_ref[...] = part_ref[me].astype(f32)
    last_r()
    last_l()
    row = lax.broadcasted_iota(jnp.int32, (rows, 1), 0) + me * rows
    live = jnp.where(row < length_ref[0], 1.0, 0.0)
    hidden = tokens_ref[...].astype(f32) + live * hidden_ref[...]
    hidden_ref[...] = hidden
    inverse = lax.rsqrt(jnp.mean(hidden * hidden, axis=1, keepdims=True) + epsilon)
    normed[...] = (hidden * inverse * gain_ref[...].astype(f32)).astype(bf)
    step_x, finish_x = line_gather(
        me, size, normed.at[:half], lambda owner: place(xa_ref, owner), local_sem.at[2], sems
    )
    for j in range(size):
        step_x(j)
    second_ref[...] = normed[half:, :]
    for copy in local:
        copy.wait()
    finish_x()


def finish_branch(lengths, part, tokens, gain, cot, cid):
    size = lax.axis_size("tensor")
    rows, width = tokens.shape
    half = rows // 2
    bf, f32 = jnp.bfloat16, jnp.float32
    vmem = pl.BlockSpec(memory_space=pltpu.VMEM)
    anywhere = pl.BlockSpec(memory_space=pl.ANY)
    dma = pltpu.SemaphoreType.DMA
    gathered = jax.ShapeDtypeStruct((size * half, width), bf)
    return pl.pallas_call(
        branch_body,
        in_specs=[pl.BlockSpec(memory_space=pltpu.SMEM), vmem, vmem, vmem, anywhere],
        out_specs=[vmem, vmem, anywhere, anywhere, anywhere],
        out_shape=[
            jax.ShapeDtypeStruct((rows, width), f32), jax.ShapeDtypeStruct((half, width), bf), gathered, gathered, gathered,
        ],
        scratch_shapes=[
            pltpu.VMEM((size, rows, width), bf), pltpu.VMEM((size, rows, width), bf), pltpu.VMEM((rows, width), bf),
            dma((3,)), *[dma((2 * size,))] * 4, *[dma((size,))] * 4,
        ],
        compiler_params=pltpu.CompilerParams(vmem_limit_bytes=48 * MIB, collective_id=cid, has_side_effects=True),
        cost_estimate=pl.CostEstimate(flops=0, bytes_accessed=24 * rows * size * width, transcendentals=0),
        name="finish_branch",
    )(lengths, part.reshape(size, rows, width), tokens, gain[None], cot)


def small_sum_phases(local_rows, part_ref, out_ref, scratch):
    staged, landed, from_dp, mine, from_tensor, send_dp, recv_dp, send_t, recv_t, send_out, recv_out = scratch
    size_dp, size_t = lax.axis_size("dp"), lax.axis_size("tensor")
    me_dp, me_t = lax.axis_index("dp"), lax.axis_index("tensor")
    width = mine.shape[1]

    def piece(ref, owner):
        return ref.at[:, pl.ds(pl.multiple_of(owner * width, width), width)]

    def greet():
        barrier = pltpu.get_barrier_semaphore()
        for step in range(1, size_dp):
            peer = lax.rem(me_dp + step, size_dp)
            pl.semaphore_signal(barrier, inc=1, device_id={"dp": peer}, device_id_type=MESH)
        for step in range(1, size_t):
            peer = lax.rem(me_t + step, size_t)
            pl.semaphore_signal(barrier, inc=1, device_id={"tensor": peer}, device_id_type=MESH)
        pl.semaphore_wait(barrier, size_dp + size_t - 2)

    def copy(source, target, axis, step, send_sem, recv_sem):
        me, size = (me_dp, size_dp) if axis == "dp" else (me_t, size_t)
        return pltpu.make_async_remote_copy(
            src_ref=source, dst_ref=target, send_sem=send_sem.at[step], recv_sem=recv_sem.at[step],
            device_id={axis: lax.rem(me + step, size)}, device_id_type=MESH,
        )

    def to_owner(step):
        return copy(piece(staged, lax.rem(me_dp + step, size_dp)), from_dp.at[step], "dp", step, send_dp, recv_dp)

    def to_tensor(step):
        return copy(mine, from_tensor.at[step], "tensor", step, send_t, recv_t)

    def to_all(step):
        here = piece(landed, me_dp)
        return copy(here, here, "dp", step, send_out, recv_out)

    def first():
        staged[...] = part_ref[...]
        for step in range(1, size_dp):
            to_owner(step).start()

    def second():
        total = piece(staged, me_dp)[...]
        for step in range(1, size_dp):
            to_owner(step).wait_recv()
            total = total + from_dp[step]
        mine[...] = total
        for step in range(1, size_t):
            to_tensor(step).start()

    def third():
        total = mine[...]
        for step in range(1, size_t):
            to_tensor(step).wait_recv()
            total = total + from_tensor[step]
        piece(landed, me_dp)[...] = total
        piece(landed.at[local_rows:], me_dp)[...] = mine[local_rows:, :]
        for step in range(1, size_dp):
            to_all(step).start()

    def last():
        for step in range(1, size_dp):
            to_all(step).wait_recv()
        out_ref[...] = landed[...]
        for step in range(1, size_dp):
            to_owner(step).wait_send()
            to_all(step).wait_send()
        for step in range(1, size_t):
            to_tensor(step).wait_send()

    return greet, first, second, third, last


def small_sum_scratch(shape):
    size_dp, size_t = lax.axis_size("dp"), lax.axis_size("tensor")
    rows, width = shape[0], shape[1] // size_dp
    dma = pltpu.SemaphoreType.DMA
    f32 = jnp.float32
    return [
        pltpu.VMEM(shape, f32), pltpu.VMEM(shape, f32),
        pltpu.VMEM((size_dp, rows, width), f32), pltpu.VMEM((rows, width), f32), pltpu.VMEM((size_t, rows, width), f32),
        dma((size_dp,)), dma((size_dp,)), dma((size_t,)), dma((size_t,)), dma((size_dp,)), dma((size_dp,)),
    ]


def sums_body(local_rows, part_ref, out_ref, *scratch):
    for phase in small_sum_phases(local_rows, part_ref, out_ref, scratch):
        phase()


def small_sums(part, local_rows, cid):
    vmem = pl.BlockSpec(memory_space=pltpu.VMEM)
    return pl.pallas_call(
        functools.partial(sums_body, local_rows),
        in_specs=[vmem],
        out_specs=vmem,
        out_shape=jax.ShapeDtypeStruct(part.shape, jnp.float32),
        scratch_shapes=small_sum_scratch(part.shape),
        compiler_params=pltpu.CompilerParams(collective_id=cid, has_side_effects=True),
        name="small_sums",
    )(part)


def attention_grads_body(nc, cut, local_rows, a_ref, a2_ref, b_ref, b2_ref, part_ref, o_ref, o2_ref, sums_ref, *scratch):
    i = pl.program_id(0)
    greet, *phases = small_sum_phases(local_rows, part_ref, sums_ref, scratch[:11])
    steps = nc + LA + LB + LC

    def store(c, rows, result):
        @pl.when(c < cut)
        def _():
            o_ref[rows, :] = result.astype(o_ref.dtype)

        @pl.when(c >= cut)
        def _():
            o2_ref[rows, :] = result.astype(o2_ref.dtype)

    send = scatter_steps(i, nc, (LA, LB, LC), o_ref.shape[1], scratch[11:], store, greet)
    for when, phase in zip((0, 4, 8, steps - 1), phases):
        pl.when(i == when)(phase)

    @pl.when(i < cut)
    def _():
        send(lambda cols: jnp.dot(a_ref[...], b_ref[:, cols], preferred_element_type=jnp.float32))

    @pl.when((i >= cut) & (i < nc))
    def _():
        send(lambda cols: jnp.dot(a2_ref[...], b2_ref[:, cols], preferred_element_type=jnp.float32))


def attention_grads(a, b, a2, b2, part, local_rows, r, cid):
    T, D = b.shape
    w = D // 8
    cut, rest = a.shape[0] // r, a2.shape[0] // r
    nc = cut + rest
    lag = LA + LB + LC
    out_specs, out_shape = scatter_outs(nc, cut, lag, r, w)

    def whole(shape):
        return pl.BlockSpec(shape, lambda i: (0, 0), pipeline_mode=pl.Buffered(1))

    return pl.pallas_call(
        functools.partial(attention_grads_body, nc, cut, local_rows),
        grid=(nc + lag,),
        in_specs=[
            pl.BlockSpec((r, T), lambda i: (jnp.minimum(i, cut - 1), 0)),
            pl.BlockSpec((r, T), lambda i: (jnp.clip(i - cut, 0, rest - 1), 0)),
            whole((T, D)), whole((T, D)), whole(part.shape),
        ],
        out_specs=[*out_specs, whole(part.shape)],
        out_shape=[*out_shape, jax.ShapeDtypeStruct(part.shape, jnp.float32)],
        scratch_shapes=[*small_sum_scratch(part.shape), *scatter_scratch(r, w)],
        compiler_params=pltpu.CompilerParams(vmem_limit_bytes=48 * MIB, collective_id=cid, has_side_effects=True),
        cost_estimate=pl.CostEstimate(flops=2 * nc * r * T * D, bytes_accessed=2 * nc * r * T + 4 * T * D, transcendentals=0),
        name="attention_grads",
    )(a, a2, b, b2, part)


def on_device(
    tokens,
    lengths,
    routes,
    cotangent,
    norm_one,
    qkv_weight,
    qkv_bias,
    out_weight,
    norm_two,
    router_weight,
    expert_in,
    expert_out,
    shared_in,
    shared_out,
    shared_gate,
):
    own_rows = tokens.shape[0]
    slot_count = routes.shape[0]
    model_width = tokens.shape[1]
    qkv_cols = qkv_weight.shape[2]
    local_heads = qkv_cols // HEAD_DIM
    experts = router_weight.shape[1]
    eff = expert_in.shape[3]
    shared_chunks = shared_out.shape[0] // eff
    chunks = experts + shared_chunks
    bf = jnp.bfloat16
    qkv_cols = qkv_weight.shape[2]
    length = lengths[0]
    tensor_index = lax.axis_index("tensor")
    first_row = tensor_index * own_rows
    live_own = (first_row + jnp.arange(own_rows) < length).astype(jnp.float32)[:, None]
    tokens_f = tokens.astype(jnp.float32)
    gain_one = norm_one.astype(jnp.float32)
    gain_two = norm_two.astype(jnp.float32)
    inv_one = lax.rsqrt(jnp.mean(tokens_f * tokens_f, axis=-1, keepdims=True) + epsilon)
    unit_one = tokens_f * inv_one
    normed_one = lax.all_gather((unit_one * gain_one).astype(bf), "tensor", axis=0, tiled=True)
    cos_table, sin_table = rotary_tables(slot_count, HEAD_DIM)
    qkv_w = qkv_weight.transpose(1, 0, 2)
    ei = expert_in.transpose(0, 2, 3, 1).reshape(experts, 2 * eff, model_width)
    eo = expert_out
    si = (
        shared_in.reshape(model_width, 2, shared_chunks, eff)
        .transpose(2, 1, 3, 0)
        .reshape(shared_chunks, 2 * eff, model_width)
    )
    so = shared_out.reshape(shared_chunks, eff, model_width)
    router_rows = jnp.concatenate(
        [
            router_weight.T,
            shared_gate[None],
            jnp.zeros((-(experts + 1) % 16, model_width), bf),
        ],
        axis=0,
    )
    grad_out = cotangent.astype(jnp.float32) * live_own
    d_two_own = (live_own * grad_out).astype(bf)
    normed_one, si, router_rows, cos_table, sin_table, d_two_own = lax.optimization_barrier(
        (normed_one, si, router_rows, cos_table, sin_table, d_two_own)
    )
    qkv = project_qkv(normed_one, qkv_w, qkv_bias[:, None, :], cos_table, sin_table)
    mixed, mixed_t = attend(lengths, qkv)
    branch_partial = jnp.dot(mixed, out_weight, preferred_element_type=jnp.float32).astype(bf)
    size_t = lax.axis_size("tensor")
    half = own_rows // 2
    hidden, second, x_a, d_a, d_b = finish_branch(
        lengths, branch_partial, tokens, norm_two, d_two_own, 1
    )
    inv_two = lax.rsqrt(jnp.mean(hidden * hidden, axis=-1, keepdims=True) + epsilon)
    unit_two = hidden * inv_two
    routes_a, routes_b = (
        routes.reshape(size_t, 2, half, -1).transpose(1, 0, 2, 3).reshape(2, size_t * half, -1)
    )
    x_b = lax.all_gather(second, "tensor", axis=0, tiled=True)
    weights = (router_rows, ei, si, eo, so)
    dgu_a, dn_a, bt_a, router_a, np_a, s_a = ffn(x_a, d_a, routes_a.T, *weights)
    x_b, dn_a, bt_a, s_a = lax.optimization_barrier((x_b, dn_a, bt_a, s_a))
    grad_a = lax.psum_scatter(dn_a, "tensor", scatter_dimension=0, tiled=True)
    two_a = lax.psum_scatter(bt_a, "tensor", scatter_dimension=0, tiled=True)
    if lax.axis_size("dp") == 8:
        dgu_b, dn_b, bt_b, router_b, np_b, out_grads, shared_out_grad = ffn(
            x_b, d_b, routes_b.T, *weights, other=(s_a, d_a)
        )
    else:
        dgu_b, dn_b, bt_b, router_b, np_b, s_b = ffn(x_b, d_b, routes_b.T, *weights)
        inner = [s.reshape(chunks * eff, -1) for s in (s_a, s_b)]
        out_grads, shared_out_grad = weight_grad_scatter(
            inner, [d_a, d_b], eff, 2, "down_grads", cut=experts
        )
    router_part = router_a + router_b
    norm_two_part = np_a + np_b
    d_gate_up = [d.reshape(chunks * 2 * eff, -1) for d in (dgu_a, dgu_b)]
    grad_a, two_a, dn_b = lax.optimization_barrier((grad_a, two_a, dn_b))
    grad_b = lax.psum_scatter(dn_b, "tensor", scatter_dimension=0, tiled=True)
    two_b = lax.psum_scatter(bt_b, "tensor", scatter_dimension=0, tiled=True)
    in_grads_b, _ = weight_grad_scatter(
        d_gate_up, [x_a, x_b], eff, 4, "shared_in_grads", 2 * experts, 2 * shared_chunks
    )
    grad_two = jnp.concatenate([grad_a, grad_b], axis=0).astype(jnp.float32)
    grad_hidden = grad_out + norm_back(grad_two, unit_two, inv_two, gain_two)
    d_one_own, in_grads_b = lax.optimization_barrier(
        ((live_own * grad_hidden).astype(bf), in_grads_b)
    )
    d_one = lax.all_gather(d_one_own, "tensor", axis=0, tiled=True)
    d_gate_up, _ = lax.optimization_barrier((d_gate_up, d_one_own))
    in_grads_a, _ = weight_grad_scatter(
        d_gate_up, [x_a, x_b], eff, 3, "expert_in_grads", 0, 2 * experts
    )
    d_one, in_grads_a = lax.optimization_barrier((d_one, in_grads_a))
    d_mixed = lax.dot_general(d_one, out_weight, NT, preferred_element_type=jnp.float32).astype(bf)
    d_qkv, d_qkv_t, bias_part = attend_back(lengths, qkv, d_mixed, cos_table, sin_table)
    grad_one, norm_one_part = qkv_back(d_qkv, qkv_w, normed_one)
    grad_one, d_qkv_t, mixed_t, two_b = lax.optimization_barrier(
        (grad_one, d_qkv_t, mixed_t, two_b)
    )
    grad_one_own = lax.psum_scatter(grad_one, "tensor", scatter_dimension=0, tiled=True)
    part = jnp.concatenate(
        [
            router_part[: experts + 1],
            norm_one_part / gain_one[None],
            norm_two_part / gain_two[None],
            jnp.pad(bias_part.reshape(1, 3 * qkv_cols), ((0, 0), (0, model_width - 3 * qkv_cols))),
        ],
        axis=0,
    )
    d_qkv_t = d_qkv_t.reshape(3 * qkv_cols, slot_count)
    if lax.axis_size("dp") == 8:
        qkv_sum, out_sum, sums = attention_grads(
            d_qkv_t, normed_one, mixed_t, d_one, part, experts + 3, qkv_cols // 2, 5
        )
    else:
        sums = small_sums(part, experts + 3, 7)
        qkv_sum, _ = weight_grad_scatter([d_qkv_t], [normed_one], qkv_cols, 5, "qkv_grads")
        out_sum, _ = weight_grad_scatter([mixed_t], [d_one], qkv_cols, 6, "mix_grads")
    branch_two = jnp.concatenate([two_a, two_b], axis=0).astype(jnp.float32)
    output = (hidden + live_own * branch_two).astype(bf)
    grad_one = grad_one_own.astype(jnp.float32)
    input_grad = grad_hidden + norm_back(grad_one, unit_one, inv_one, gain_one)
    qkv_bias_grad = sums[experts + 3, : 3 * qkv_cols].reshape(3, qkv_cols)
    own_cols = out_grads.shape[1]
    expert_in_grad = in_grads_a.astype(jnp.float32).reshape(experts, 2, eff, own_cols).transpose(0, 3, 1, 2)
    shared_in_grad = (
        in_grads_b.reshape(shared_chunks, 2, eff, own_cols)
        .transpose(3, 1, 0, 2)
        .reshape(own_cols, 2, shared_chunks * eff)
        .astype(jnp.float32)
    )
    return (
        output,
        input_grad,
        sums[experts + 1],
        qkv_sum.astype(jnp.float32).reshape(3, qkv_cols, own_cols).transpose(2, 0, 1),
        qkv_bias_grad,
        out_sum.astype(jnp.float32),
        sums[experts + 2],
        sums[:experts].T,
        expert_in_grad,
        out_grads.astype(jnp.float32).reshape(experts, eff, own_cols),
        shared_in_grad,
        shared_out_grad.astype(jnp.float32),
        sums[experts],
    )


def solution(mesh):
    in_specs = (
        P(("dp", "tensor"), None),
        P("dp"),
        P("dp", None),
        P(("dp", "tensor"), None),
        P(),
        P(None, None, "tensor"),
        P(None, "tensor"),
        P("tensor", None),
        P(),
        P(),
        P(None, None, None, "tensor"),
        P(None, "tensor", None),
        P(None, None, "tensor"),
        P("tensor", None),
        P(),
    )
    out_specs = (
        P(("dp", "tensor"), None),
        P(("dp", "tensor"), None),
        P(),
        P("dp", None, "tensor"),
        P(None, "tensor"),
        P("tensor", "dp"),
        P(),
        P(),
        P(None, "dp", None, "tensor"),
        P(None, "tensor", "dp"),
        P("dp", None, "tensor"),
        P("tensor", "dp"),
        P(),
    )
    return jax.shard_map(
        on_device, mesh=mesh, in_specs=in_specs, out_specs=out_specs, check_vma=False
    )
```

```python
import functools

import jax
import jax.numpy as jnp
from jax import lax
from jax.experimental import pallas as pl
from jax.experimental.pallas import tpu as pltpu
from jax.sharding import PartitionSpec as P

HEAD_DIM = 128
MESH = pl.DeviceIdType.MESH
LA, LB, LC = 1, 2, 2
FFN_LAGS = (1, 1, 1)
MIB = 2**20


epsilon = 1e-06
theta_base = 1000000.0
NT = (((1,), (1,)), ((), ()))
TN = (((0,), (0,)), ((), ()))


def rotary_tables(row_count, head_width):
    half_index = jnp.arange(head_width // 2).astype(jnp.float32)
    frequency = theta_base ** (-2.0 * half_index / head_width)
    angles = jnp.arange(row_count).astype(jnp.float32)[:, None] * frequency[None, :]
    sines = jnp.sin(angles)
    cosines = jnp.cos(angles)
    return (
        jnp.concatenate([cosines, cosines], axis=-1),
        jnp.concatenate([-sines, sines], axis=-1),
    )


def norm_back(d_normed, unit_rows, inverse, gain_vector):
    d_unit = d_normed * gain_vector
    return inverse * (d_unit - unit_rows * jnp.mean(d_unit * unit_rows, axis=-1, keepdims=True))


def scatter_scratch(r, w):
    f32, bf = jnp.float32, jnp.bfloat16
    dma = pltpu.SemaphoreType.DMA
    h = r // 2
    return [
        pltpu.VMEM((2, 4, r, w), f32), pltpu.VMEM((2, 4, r, w), bf), pltpu.VMEM((3, 4, r, w), bf),
        pltpu.VMEM((3, 2, 2, h, w), f32), pltpu.VMEM((3, 2, 2, h, w), bf), pltpu.VMEM((6, 2, 2, h, w), bf),
        pltpu.VMEM((3, 2, h, w), f32), pltpu.VMEM((2, 2, h, w), bf), pltpu.VMEM((6, 2, h, w), bf),
        dma((2,)), dma((3,)), dma((3, 2)), dma((6, 2)), dma((2, 2)), dma((6, 2)),
    ]


def scatter_steps(i, nc, lags, w, scratch, store, greet=None):
    own, sa, ra, kt, s1, r1, ku, s2, r2, sem_sa, sem_ra, sem_s1, sem_r1, sem_s2, sem_r2 = scratch
    la, lb, lc = lags
    keep_1 = min(3, lb + lc)
    hr = own.shape[2] // 2
    dp = lax.axis_index("dp")
    k = dp % 2
    x = (dp // 2) % 2
    y = dp // 4
    core_peer = y * 4 + x * 2 + (1 - k)
    x_peer = y * 4 + (1 - x) * 2 + k
    y_peer = (1 - y) * 4 + x * 2 + k

    def copy_a(c):
        return pltpu.make_async_remote_copy(
            src_ref=sa.at[c % 2], dst_ref=ra.at[c % 3], send_sem=sem_sa.at[c % 2], recv_sem=sem_ra.at[c % 3],
            device_id={"dp": core_peer}, device_id_type=MESH,
        )

    def copy_1(c, half):
        return pltpu.make_async_remote_copy(
            src_ref=s1.at[c % 3, half], dst_ref=r1.at[c % 6, half], send_sem=sem_s1.at[c % 3, half],
            recv_sem=sem_r1.at[c % 6, half], device_id={"dp": y_peer if half else x_peer}, device_id_type=MESH,
        )

    def copy_2(c, half):
        return pltpu.make_async_remote_copy(
            src_ref=s2.at[c % 2, half], dst_ref=r2.at[c % 6, half], send_sem=sem_s2.at[c % 2, half],
            recv_sem=sem_r2.at[c % 6, half], device_id={"dp": x_peer if half else y_peer}, device_id_type=MESH,
        )

    @pl.when(i == 0)
    def _():
        if greet is not None:
            greet()
            return
        barrier = pltpu.get_barrier_semaphore()
        for peer in (core_peer, x_peer, y_peer):
            pl.semaphore_signal(barrier, inc=1, device_id={"dp": peer}, device_id_type=MESH)
        pl.semaphore_wait(barrier, 3)

    @pl.when((i >= la + keep_1) & (i < nc + la + keep_1))
    def _():
        copy_1(i - la - keep_1, 0).wait_send()
        copy_1(i - la - keep_1, 1).wait_send()

    @pl.when((i >= la) & (i < nc + la))
    def _():
        c = i - la
        copy_a(c).wait_recv()
        for half in range(2):
            rows = slice(half * hr, half * hr + hr)
            keep, other = (1, 2) if half else (2, 1)

            def total(role):
                return own[c % 2, role, rows, :] + ra[c % 3, role, rows, :].astype(jnp.float32)

            s1[c % 3, half, 0] = total(other).astype(jnp.bfloat16)
            s1[c % 3, half, 1] = total(3).astype(jnp.bfloat16)
            copy_1(c, half).start()
            kt[c % 3, half, 0] = total(0)
            kt[c % 3, half, 1] = total(keep)

    @pl.when((i >= la + lb) & (i < nc + la + lb))
    def _():
        c = i - la - lb

        @pl.when(c >= 2)
        def _():
            copy_2(c - 2, 0).wait_send()
            copy_2(c - 2, 1).wait_send()

        for half in range(2):
            copy_1(c, half).wait_recv()
            s2[c % 2, half] = (kt[c % 3, half, 1] + r1[c % 6, half, 1].astype(jnp.float32)).astype(jnp.bfloat16)
            copy_2(c, half).start()
            ku[c % 3, half] = kt[c % 3, half, 0] + r1[c % 6, half, 0].astype(jnp.float32)

    @pl.when(i >= la + lb + lc)
    def _():
        c = i - la - lb - lc
        for half in range(2):
            copy_2(c, half).wait_recv()
            store(c, slice(half * hr, half * hr + hr), ku[c % 3, half] + r2[c % 6, half].astype(jnp.float32))

        @pl.when(c >= nc - 2)
        def _():
            copy_2(c, 0).wait_send()
            copy_2(c, 1).wait_send()

    @pl.when((i >= 2) & (i < nc + 2))
    def _():
        copy_a(i - 2).wait_send()

    def send(product):
        targets = (y * 4 + x * 2, y * 4 + (1 - x) * 2, (1 - y) * 4 + x * 2, (1 - y) * 4 + (1 - x) * 2)

        def cols(role, core):
            return pl.ds(pl.multiple_of((targets[role] + core) * w, w), w)

        for role in range(4):
            sa[i % 2, role] = product(cols(role, 1 - k)).astype(jnp.bfloat16)
        copy_a(i).start()
        for role in range(4):
            own[i % 2, role] = product(cols(role, k))

    return send


def rs_body(nc, cut, pairs, *refs):
    a_refs, b_refs = refs[:pairs], refs[pairs : 2 * pairs]
    o_ref, o2_ref = refs[2 * pairs : 2 * pairs + 2]
    i = pl.program_id(0)

    def store(c, rows, result):
        @pl.when(c < cut)
        def _():
            o_ref[rows, :] = result.astype(o_ref.dtype)

        @pl.when(c >= cut)
        def _():
            o2_ref[rows, :] = result.astype(o2_ref.dtype)

    send = scatter_steps(i, nc, (LA, LB, LC), o_ref.shape[1], refs[2 * pairs + 2 :], store)

    @pl.when(i < nc)
    def _():
        def product(cols):
            total = jnp.dot(a_refs[0][...], b_refs[0][:, cols], preferred_element_type=jnp.float32)
            for a_ref, b_ref in zip(a_refs[1:], b_refs[1:]):
                total += jnp.dot(a_ref[...], b_ref[:, cols], preferred_element_type=jnp.float32)
            return total

        send(product)


def scatter_outs(nc, cut, lag, r, w):
    rest = max(nc - cut, 1)
    specs = [
        pl.BlockSpec((r, w), lambda i: (jnp.clip(i - lag, 0, cut - 1), 0)),
        pl.BlockSpec((r, w), lambda i: (jnp.clip(i - lag - cut, 0, rest - 1), 0)),
    ]
    return specs, [jax.ShapeDtypeStruct((n * r, w), jnp.bfloat16) for n in (cut, rest)]


def weight_grad_scatter_kernel(a_list, b_list, r, cid, name, first, count, cut):
    D = b_list[0].shape[1]
    T = sum(b.shape[0] for b in b_list)
    w = D // 8
    lag = LA + LB + LC
    out_specs, out_shape = scatter_outs(count, cut, lag, r, w)
    return pl.pallas_call(
        functools.partial(rs_body, count, cut, len(a_list)),
        grid=(count + lag,),
        in_specs=[
            *[pl.BlockSpec((r, a.shape[1]), lambda i: (jnp.minimum(i, count - 1) + first, 0)) for a in a_list],
            *[pl.BlockSpec(b.shape, lambda i: (0, 0), pipeline_mode=pl.Buffered(1)) for b in b_list],
        ],
        out_specs=out_specs,
        out_shape=out_shape,
        scratch_shapes=scatter_scratch(r, w),
        compiler_params=pltpu.CompilerParams(vmem_limit_bytes=48 * MIB, collective_id=cid, has_side_effects=True),
        cost_estimate=pl.CostEstimate(
            flops=2 * count * r * T * D, bytes_accessed=2 * count * r * T + 2 * T * D + 4 * count * r * w, transcendentals=0
        ),
        name=name,
    )(*a_list, *b_list)


def ffn_body(
    experts, chunks, scatter, gather,
    x_ref, d_ref, routes_ref, rw_ref, ei_ref, si_ref, eo_ref, so_ref, *refs,
):
    if scatter:
        s_other_ref, d_other_ref, dgu_ref, dn_ref, bt_ref, rg_ref, np_ref, og_ref, og2_ref, *refs = refs
    else:
        if gather:
            own_x_ref, own_d_ref, *refs = refs
        dgu_ref, dn_ref, bt_ref, rg_ref, np_ref, s_ref, *refs = refs
        if gather:
            all_x_ref, all_d_ref, *refs = refs
    dn_acc, bt_acc, probs_ref, w_ref, ds_ref, wi_buf, wd_buf, sem, *scratch = refs
    c = pl.program_id(0)
    h = eo_ref.shape[1]
    slots, width = x_ref.shape
    if gather:
        me, size = lax.axis_index("tensor"), lax.axis_size("tensor")
        local_sem, *sems = scratch
        lines = []
        for number, (own, out) in enumerate(((own_x_ref, all_x_ref), (own_d_ref, all_d_ref))):
            def block(owner, out=out, rows=own.shape[0]):
                return out.at[pl.ds(pl.multiple_of(owner * rows, rows), rows)]

            lines.append(
                line_gather(me, size, own, block, local_sem.at[number], sems[4 * number : 4 * number + 4])
            )
        for hop in range(size - 1):
            @pl.when(c == -(-hop * (chunks - 1) // (size - 1)))
            def _():
                if hop == 0:
                    line_barrier(me, size)
                for advance, _ in lines:
                    advance(hop)

    def fetch(step):
        slot = step % 2

        @pl.when(step < experts)
        def _():
            pltpu.make_async_copy(ei_ref.at[step], wi_buf.at[slot], sem.at[0, slot]).start()
            pltpu.make_async_copy(eo_ref.at[step], wd_buf.at[slot], sem.at[1, slot]).start()

        @pl.when(step >= experts)
        def _():
            pltpu.make_async_copy(si_ref.at[step - experts], wi_buf.at[slot], sem.at[0, slot]).start()
            pltpu.make_async_copy(so_ref.at[step - experts], wd_buf.at[slot], sem.at[1, slot]).start()

    @pl.when(c == 0)
    def _():
        fetch(c)

    @pl.when(c + 1 < chunks)
    def _():
        fetch(c + 1)

    def picked():
        expert = lax.broadcasted_iota(jnp.int32, (experts, slots), 0)
        hit = jnp.zeros((experts, slots), jnp.float32)
        for j in range(routes_ref.shape[0]):
            hit = hit + jnp.where(routes_ref[j : j + 1, :] == expert, 1.0, 0.0)
        return hit

    @pl.when(c == 0)
    def _():
        logits = lax.dot_general(rw_ref[...], x_ref[...], NT, preferred_element_type=jnp.float32)
        raised = jnp.exp(logits[:experts] - jnp.max(logits[:experts], axis=0, keepdims=True))
        probs = raised / jnp.sum(raised, axis=0, keepdims=True)
        gate = 1.0 / (1.0 + jnp.exp(-logits[experts:]))
        probs_ref[...] = probs
        w_ref[:experts, :] = probs * picked()
        w_ref[experts:, :] = gate
        ds_ref[...] = jnp.zeros_like(ds_ref)
        dn_acc[...] = jnp.zeros_like(dn_acc)
        bt_acc[...] = jnp.zeros_like(bt_acc)

    if scatter:
        def store(chunk, rows, result):
            @pl.when(chunk < experts)
            def _():
                og_ref[rows, :] = result.astype(og_ref.dtype)

            @pl.when(chunk >= experts)
            def _():
                og2_ref[rows, :] = result.astype(og2_ref.dtype)

        send = scatter_steps(c, chunks, FFN_LAGS, og_ref.shape[1], scratch, store)

    block = 512

    @pl.when(c < chunks)
    def _():
        row = pl.ds(jnp.minimum(c, experts), 1)
        slot = c % 2
        pltpu.make_async_copy(ei_ref.at[0], wi_buf.at[slot], sem.at[0, slot]).wait()
        pltpu.make_async_copy(eo_ref.at[0], wd_buf.at[slot], sem.at[1, slot]).wait()
        wi = wi_buf.at[slot]
        wd = wd_buf.at[slot]
        x = x_ref[...]
        g = lax.dot_general(wi[:h], x, NT, preferred_element_type=jnp.float32)
        u = lax.dot_general(wi[h:], x, NT, preferred_element_type=jnp.float32)
        p = lax.dot_general(wd[...], d_ref[...], NT, preferred_element_type=jnp.float32)
        w = w_ref[row, :]
        sg = 1.0 / (1.0 + jnp.exp(-g))
        si = g * sg
        inner = (si * u).astype(jnp.bfloat16).astype(jnp.float32)
        s = (w * inner).astype(jnp.bfloat16)
        ds_ref[row, :] += jnp.sum(p * inner, axis=0, keepdims=True)
        di = w * p
        dg = (di * u * sg * (1.0 + g * (1.0 - sg))).astype(jnp.bfloat16)
        du = (di * si).astype(jnp.bfloat16)
        dgu_ref[0, :h] = dg
        dgu_ref[0, h:] = du
        dgu = jnp.concatenate([dg, du], axis=0)
        if scatter:
            def product(cols):
                return jnp.dot(s, d_ref[:, cols], preferred_element_type=jnp.float32) + jnp.dot(
                    s_other_ref[0], d_other_ref[:, cols], preferred_element_type=jnp.float32
                )

            send(product)
        else:
            s_ref[0] = s
        for n in range(0, width, block):
            cols = slice(n, n + block)
            dn_acc[:, cols] += lax.dot_general(dgu, wi[:, cols], TN, preferred_element_type=jnp.float32)
            bt_acc[:, cols] += lax.dot_general(s, wd[:, cols], TN, preferred_element_type=jnp.float32)

    @pl.when(c == (chunks if scatter else chunks - 1))
    def _():
        probs = probs_ref[...]
        d_probs = ds_ref[:experts, :] * picked()
        d_logits = probs * (d_probs - jnp.sum(probs * d_probs, axis=0, keepdims=True))
        gate = w_ref[experts:, :]
        d_gate = ds_ref[experts:, :] * gate * (1.0 - gate)
        small = jnp.concatenate([d_logits, d_gate], axis=0)
        high = small.astype(jnp.bfloat16)
        low = (small - high.astype(jnp.float32)).astype(jnp.bfloat16)
        rg_ref[...] = jnp.dot(high, x_ref[...], preferred_element_type=jnp.float32) + jnp.dot(
            low, x_ref[...], preferred_element_type=jnp.float32
        )
        for n in range(0, width, block):
            cols = slice(n, n + block)
            extra = lax.dot_general(high, rw_ref[:, cols], TN, preferred_element_type=jnp.float32)
            extra += lax.dot_general(low, rw_ref[:, cols], TN, preferred_element_type=jnp.float32)
            total = dn_acc[:, cols] + extra
            dn_ref[:, cols] = total.astype(dn_ref.dtype)
            np_ref[:, cols] = jnp.sum(total * x_ref[:, cols].astype(jnp.float32), axis=0, keepdims=True)
        bt_ref[...] = bt_acc[...].astype(bt_ref.dtype)
        if gather:
            for advance, finish in lines:
                advance(size - 1)
                finish()


def ffn(x, d_two, routes_t, router_rows, ei, si, eo, so, other=None, own=None):
    experts, h2, width = ei.shape
    chunks = experts + si.shape[0]
    h = h2 // 2
    slots = x.shape[0]
    rows = router_rows.shape[0]
    bf, f32 = jnp.bfloat16, jnp.float32
    anywhere = pl.BlockSpec(memory_space=pl.ANY)
    scatter = other is not None

    def whole(shape):
        return pl.BlockSpec(shape, lambda c: (0,) * len(shape), pipeline_mode=pl.Buffered(1))

    def chunk(shape):
        return pl.BlockSpec((1, *shape), lambda c: (jnp.minimum(c, chunks - 1), 0, 0))

    in_specs = [
        whole((slots, width)), whole((slots, width)), whole(routes_t.shape), whole((rows, width)),
        anywhere, anywhere, anywhere, anywhere,
    ]
    out_specs = [chunk((h2, slots)), whole((slots, width)), whole((slots, width)), whole((rows, width)), whole((1, width))]
    out_shape = [
        jax.ShapeDtypeStruct((chunks, h2, slots), bf), jax.ShapeDtypeStruct((slots, width), bf),
        jax.ShapeDtypeStruct((slots, width), bf), jax.ShapeDtypeStruct((rows, width), f32),
        jax.ShapeDtypeStruct((1, width), f32),
    ]
    scratch = [
        pltpu.VMEM((slots, width), f32), pltpu.VMEM((slots, width), f32),
        pltpu.VMEM((experts, slots), f32), pltpu.VMEM((rows, slots), f32), pltpu.VMEM((rows, slots), f32),
        pltpu.VMEM((2, h2, width), bf), pltpu.VMEM((2, h, width), bf), pltpu.SemaphoreType.DMA((2, 2)),
    ]
    args = [x, d_two, routes_t, router_rows, ei, si, eo, so]
    if scatter:
        s_other, d_other = other
        in_specs += [chunk((h, s_other.shape[2])), whole(d_other.shape)]
        args += [s_other, d_other]
        w = width // 8
        lag = sum(FFN_LAGS)
        specs, shapes = scatter_outs(chunks, experts, lag, h, w)
        out_specs += specs
        out_shape += shapes
        scratch += scatter_scratch(h, w)
        grid = (chunks + lag,)
        params = pltpu.CompilerParams(vmem_limit_bytes=62 * MIB, collective_id=2, has_side_effects=True)
    else:
        out_specs.append(chunk((h, slots)))
        out_shape.append(jax.ShapeDtypeStruct((chunks, h, slots), bf))
        grid = (chunks,)
        params = pltpu.CompilerParams(vmem_limit_bytes=62 * MIB)
        if own is not None:
            size = lax.axis_size("tensor")
            dma = pltpu.SemaphoreType.DMA
            in_specs += [anywhere, anywhere]
            args += own
            out_specs += [anywhere, anywhere]
            out_shape += [jax.ShapeDtypeStruct((size * a.shape[0], width), bf) for a in own]
            scratch += [dma((2,)), *[dma((size,))] * 8]
            params = pltpu.CompilerParams(vmem_limit_bytes=62 * MIB, collective_id=8, has_side_effects=True)
    return pl.pallas_call(
        functools.partial(ffn_body, experts, chunks, scatter, own is not None),
        grid=grid,
        in_specs=in_specs,
        out_specs=out_specs,
        out_shape=out_shape,
        scratch_shapes=scratch,
        compiler_params=params,
        cost_estimate=pl.CostEstimate(
            flops=12 * chunks * h * slots * width, bytes_accessed=10 * chunks * h * width + 16 * slots * width,
            transcendentals=chunks * h * slots,
        ),
        name="ffn_scatter" if scatter else "ffn",
    )(*args)


def turn(v):
    half = v.shape[1] // 2
    return jnp.concatenate([v[:, half:], v[:, :half]], axis=1)


def qkv_body(x_ref, w_ref, bias_ref, cos_ref, sin_ref, out_ref):
    j = pl.program_id(0)
    cols = w_ref.shape[2]
    y = jnp.dot(x_ref[...], w_ref[0], preferred_element_type=jnp.float32)
    y = y + bias_ref[0].astype(jnp.float32)

    @pl.when(j < 2)
    def _():
        for head in range(cols // HEAD_DIM):
            place = slice(head * HEAD_DIM, (head + 1) * HEAD_DIM)
            v = y[:, place]
            out_ref[0, :, place] = (v * cos_ref[...] + turn(v) * sin_ref[...]).astype(out_ref.dtype)

    @pl.when(j == 2)
    def _():
        out_ref[0] = y.astype(out_ref.dtype)


def project_qkv(x, w, bias, cos_table, sin_table):
    slots, width = x.shape
    cols = w.shape[2]
    table = pl.BlockSpec((slots, HEAD_DIM), lambda j: (0, 0), pipeline_mode=pl.Buffered(1))
    return pl.pallas_call(
        qkv_body,
        grid=(3,),
        in_specs=[
            pl.BlockSpec((slots, width), lambda j: (0, 0), pipeline_mode=pl.Buffered(1)),
            pl.BlockSpec((1, width, cols), lambda j: (j, 0, 0)),
            pl.BlockSpec((1, 1, cols), lambda j: (j, 0, 0)),
            table, table,
        ],
        out_specs=pl.BlockSpec((1, slots, cols), lambda j: (j, 0, 0)),
        out_shape=jax.ShapeDtypeStruct((3, slots, cols), jnp.bfloat16),
        compiler_params=pltpu.CompilerParams(vmem_limit_bytes=48 * MIB),
        cost_estimate=pl.CostEstimate(
            flops=6 * slots * width * cols, bytes_accessed=2 * slots * width + 6 * width * cols, transcendentals=0
        ),
        name="project_qkv",
    )(x, w, bias, cos_table, sin_table)


def block_probs(length_ref, q, k, start):
    s = lax.dot_general(q, k, NT, preferred_element_type=jnp.float32) * (HEAD_DIM**-0.5)
    row = lax.broadcasted_iota(jnp.int32, s.shape, 0) + start
    col = lax.broadcasted_iota(jnp.int32, s.shape, 1)
    s = jnp.where((col <= row) & (col < length_ref[0]), s, -1000000000.0)
    e = jnp.exp(s - jnp.max(s, axis=1, keepdims=True))
    return e * (1.0 / jnp.sum(e, axis=1, keepdims=True))


def attend_body(rows, length_ref, q_ref, k_ref, v_ref, mixed_ref, mixed_t_ref):
    for start in range(0, q_ref.shape[1], rows):
        here, end = slice(start, start + rows), start + rows
        p = block_probs(length_ref, q_ref[0, here, :], k_ref[0, :end, :], start)
        mixed = jnp.dot(p.astype(jnp.bfloat16), v_ref[0, :end, :], preferred_element_type=jnp.float32)
        mixed_ref[here, :] = mixed.astype(mixed_ref.dtype)
        mixed_t_ref[:, here] = mixed.T.astype(mixed_ref.dtype)


def attend(lengths, qkv):
    _, slots, cols = qkv.shape
    rows = min(256, slots)

    def part(j):
        return pl.BlockSpec((1, slots, HEAD_DIM), lambda h: (j, 0, h))

    return pl.pallas_call(
        functools.partial(attend_body, rows),
        grid=(cols // HEAD_DIM,),
        in_specs=[pl.BlockSpec(memory_space=pltpu.SMEM), part(0), part(1), part(2)],
        out_specs=[
            pl.BlockSpec((slots, HEAD_DIM), lambda h: (0, h)), pl.BlockSpec((HEAD_DIM, slots), lambda h: (h, 0)),
        ],
        out_shape=[
            jax.ShapeDtypeStruct((slots, cols), jnp.bfloat16), jax.ShapeDtypeStruct((cols, slots), jnp.bfloat16),
        ],
        compiler_params=pltpu.CompilerParams(vmem_limit_bytes=32 * MIB),
        cost_estimate=pl.CostEstimate(
            flops=4 * slots * slots * cols, bytes_accessed=10 * slots * cols, transcendentals=slots * slots * cols // HEAD_DIM
        ),
        name="attend",
    )(lengths, qkv, qkv, qkv)


def attend_back_body(
    rows, length_ref, q_ref, k_ref, v_ref, dm_ref, cos_ref, sin_ref, out_ref, out_t_ref, bias_ref, dk_acc, dv_acc
):
    slots = q_ref.shape[1]
    scale = HEAD_DIM**-0.5
    bf, f32 = jnp.bfloat16, jnp.float32

    def finish(j, here, grad):
        if j < 2:
            grad = grad * cos_ref[here, :] - turn(grad) * sin_ref[here, :]
        low = grad.astype(bf)
        out_ref[j, here, :] = low
        out_t_ref[j, :, here] = grad.T.astype(bf)
        return jnp.sum(low.astype(f32), axis=0, keepdims=True)

    dq_sum = jnp.zeros((1, HEAD_DIM), f32)
    starts = list(range(0, slots, rows))[::-1]
    for start in starts:
        here, end = slice(start, start + rows), start + rows
        q, k, v, dm = q_ref[0, here, :], k_ref[0, :end, :], v_ref[0, :end, :], dm_ref[here, :]
        p = block_probs(length_ref, q, k, start)
        dp = lax.dot_general(dm, v, NT, preferred_element_type=f32)
        ds = (p * (dp - jnp.sum(p * dp, axis=1, keepdims=True))).astype(bf)
        dq_sum += finish(0, here, jnp.dot(ds, k, preferred_element_type=f32) * scale)
        dk = lax.dot_general(ds, q, TN, preferred_element_type=f32) * scale
        dv = lax.dot_general(p.astype(bf), dm, TN, preferred_element_type=f32)
        if start == starts[0]:
            dk_acc[...] = dk
            dv_acc[...] = dv
        else:
            dk_acc[:end, :] += dk
            dv_acc[:end, :] += dv
    every = slice(0, slots)
    bias_ref[0] = dq_sum
    bias_ref[1] = finish(1, every, dk_acc[...])
    bias_ref[2] = finish(2, every, dv_acc[...])


def attend_back(lengths, qkv, d_mixed, cos_table, sin_table):
    _, slots, cols = qkv.shape
    rows = min(256, slots)
    bf, f32 = jnp.bfloat16, jnp.float32

    def part(j):
        return pl.BlockSpec((1, slots, HEAD_DIM), lambda h: (j, 0, h))

    table = pl.BlockSpec((slots, HEAD_DIM), lambda h: (0, 0), pipeline_mode=pl.Buffered(1))
    return pl.pallas_call(
        functools.partial(attend_back_body, rows),
        grid=(cols // HEAD_DIM,),
        in_specs=[
            pl.BlockSpec(memory_space=pltpu.SMEM), part(0), part(1), part(2),
            pl.BlockSpec((slots, HEAD_DIM), lambda h: (0, h)), table, table,
        ],
        out_specs=[
            pl.BlockSpec((3, slots, HEAD_DIM), lambda h: (0, 0, h)), pl.BlockSpec((3, HEAD_DIM, slots), lambda h: (0, h, 0)),
            pl.BlockSpec((3, 1, HEAD_DIM), lambda h: (0, 0, h)),
        ],
        out_shape=[
            jax.ShapeDtypeStruct((3, slots, cols), bf), jax.ShapeDtypeStruct((3, cols, slots), bf),
            jax.ShapeDtypeStruct((3, 1, cols), f32),
        ],
        scratch_shapes=[pltpu.VMEM((slots, HEAD_DIM), f32), pltpu.VMEM((slots, HEAD_DIM), f32)],
        compiler_params=pltpu.CompilerParams(vmem_limit_bytes=40 * MIB),
        cost_estimate=pl.CostEstimate(
            flops=10 * slots * slots * cols, bytes_accessed=20 * slots * cols, transcendentals=slots * slots * cols // HEAD_DIM
        ),
        name="attend_back",
    )(lengths, qkv, qkv, qkv, d_mixed, cos_table, sin_table)


def qkv_back_body(d_ref, w_ref, x_ref, out_ref, np_ref):
    total = lax.dot_general(d_ref[0], w_ref[0], NT, preferred_element_type=jnp.float32)
    for j in range(1, 3):
        total += lax.dot_general(d_ref[j], w_ref[j], NT, preferred_element_type=jnp.float32)
    out_ref[...] = total.astype(out_ref.dtype)
    np_ref[...] = jnp.sum(total * x_ref[...].astype(jnp.float32), axis=0, keepdims=True)


def qkv_back(d_qkv, w, x):
    _, slots, cols = d_qkv.shape
    width = w.shape[1]
    block = 512
    return pl.pallas_call(
        qkv_back_body,
        grid=(width // block,),
        in_specs=[
            pl.BlockSpec((3, slots, cols), lambda n: (0, 0, 0), pipeline_mode=pl.Buffered(1)),
            pl.BlockSpec((3, block, cols), lambda n: (0, n, 0)),
            pl.BlockSpec((slots, block), lambda n: (0, n)),
        ],
        out_specs=[pl.BlockSpec((slots, block), lambda n: (0, n)), pl.BlockSpec((1, block), lambda n: (0, n))],
        out_shape=[
            jax.ShapeDtypeStruct((slots, width), jnp.bfloat16), jax.ShapeDtypeStruct((1, width), jnp.float32),
        ],
        compiler_params=pltpu.CompilerParams(vmem_limit_bytes=48 * MIB),
        cost_estimate=pl.CostEstimate(
            flops=6 * slots * width * cols, bytes_accessed=4 * slots * width + 6 * width * cols, transcendentals=0
        ),
        name="qkv_back",
    )(d_qkv, w, x)


def weight_grad_scatter(a_list, b_list, r, cid, name, first=0, count=None, cut=None):
    count = a_list[0].shape[0] // r if count is None else count
    cut = count if cut is None else cut
    if lax.axis_size("dp") == 8:
        return weight_grad_scatter_kernel(a_list, b_list, r, cid, name, first, count, cut)
    product = sum(
        jnp.dot(a[first * r : (first + count) * r], b, preferred_element_type=jnp.float32)
        for a, b in zip(a_list, b_list)
    )
    result = lax.psum_scatter(product.astype(jnp.bfloat16), "dp", scatter_dimension=1, tiled=True)
    return result[: cut * r], result[cut * r :]


def line_gather(me, size, own, block, local_sem, sems):
    send_left, recv_left, send_right, recv_right = sems
    has_left, has_right = me > 0, me < size - 1

    def remote(source, owner, send, recv, step, to):
        return pltpu.make_async_remote_copy(
            src_ref=source, dst_ref=block(owner), send_sem=send.at[step], recv_sem=recv.at[step],
            device_id={"tensor": to}, device_id_type=MESH,
        )

    def to_left(step):
        return remote(own if step == 0 else block(me + step), me + step, send_left, recv_left, step, me - 1)

    def to_right(step):
        return remote(own if step == 0 else block(me - step), me - step, send_right, recv_right, step, me + 1)

    def advance(step):
        if step == 0:
            pltpu.make_async_copy(own, block(me), local_sem).start()
        else:
            @pl.when(me + step < size)
            def _():
                remote(own, me + step, send_left, recv_left, step - 1, me + 1).wait_recv()

        @pl.when(has_left & (me + step < size))
        def _():
            to_left(step).start()

        if step > 0:
            @pl.when(me - step >= 0)
            def _():
                remote(own, me - step, send_right, recv_right, step - 1, me - 1).wait_recv()

        @pl.when(has_right & (me - step >= 0))
        def _():
            to_right(step).start()

    def finish():
        for step in range(size):
            @pl.when(has_left & (me + step < size))
            def _():
                to_left(step).wait_send()

            @pl.when(has_right & (me - step >= 0))
            def _():
                to_right(step).wait_send()

        pltpu.make_async_copy(own, block(me), local_sem).wait()

    return advance, finish


def line_barrier(me, size):
    barrier = pltpu.get_barrier_semaphore()
    has_left, has_right = me > 0, me < size - 1

    @pl.when(has_left)
    def _():
        pl.semaphore_signal(barrier, inc=1, device_id={"tensor": me - 1}, device_id_type=MESH)

    @pl.when(has_right)
    def _():
        pl.semaphore_signal(barrier, inc=1, device_id={"tensor": me + 1}, device_id_type=MESH)

    pl.semaphore_wait(barrier, has_left.astype(jnp.int32) + has_right.astype(jnp.int32))


def branch_body(
    length_ref, part_ref, tokens_ref, gain_ref, cot_ref, hidden_ref, second_ref, xa_ref, da_ref,
    from_left, from_right, normed, local_sem, send_r, recv_r, send_l, recv_l, *sems,
):
    me = lax.axis_index("tensor")
    size = lax.axis_size("tensor")
    rows = tokens_ref.shape[0]
    half, quarter = rows // 2, rows // 4
    bf, f32 = jnp.bfloat16, jnp.float32
    has_left, has_right = me > 0, me < size - 1
    line_barrier(me, size)

    def gathered(owner, h):
        return da_ref.at[pl.ds(pl.multiple_of(owner * half + h * quarter, quarter), quarter)]

    def own_cot(h):
        return cot_ref.at[pl.ds(h * quarter, quarter)]

    def part(ref, owner, which):
        return ref.at[owner, pl.ds(pl.multiple_of(which * quarter, quarter), quarter)]

    def direction(right):
        slots, send, recv = (from_left, send_r, recv_r) if right else (from_right, send_l, recv_l)
        to = me + 1 if right else me - 1
        before = me if right else size - 1 - me
        has_to = has_right if right else has_left
        has_from = has_left if right else has_right

        def copy(source, target, t):
            return pltpu.make_async_remote_copy(
                src_ref=source, dst_ref=target, send_sem=send.at[t], recv_sem=recv.at[t],
                device_id={"tensor": to}, device_id_type=MESH,
            )

        def sends(s):
            return has_to & (s - before - 1 < 2 * (size - 1 - before))

        def step(t):
            s, h = t // 2, t % 2
            if t >= 2:
                @pl.when(sends(s - 1))
                def _():
                    copy(part(part_ref, 0, 0), part(slots, 0, 0), t - 2).wait_send()

            if s < size:
                @pl.when(s <= before)
                def _():
                    owner = me - s if right else me + s
                    if s > 0:
                        copy(own_cot(h), gathered(owner, h), t - 2).wait_recv()

                    @pl.when(has_to)
                    def _():
                        copy(own_cot(h) if s == 0 else gathered(owner, h), gathered(owner, h), t).start()

            @pl.when((s > before) & sends(s))
            def _():
                r = s - before - 1
                owner = size - 1 - r // 2 if right else r // 2
                which = 2 * (r % 2) + h

                @pl.when(has_from)
                def _():
                    both = part(slots, owner, which)
                    copy(part(part_ref, owner, which), both, t - 2).wait_recv()
                    both[...] = (both[...].astype(f32) + part(part_ref, owner, which)[...].astype(f32)).astype(bf)
                    copy(both, both, t).start()

                @pl.when(jnp.logical_not(has_from))
                def _():
                    copy(part(part_ref, owner, which), part(slots, owner, which), t).start()

        def last():
            @pl.when(has_from)
            def _():
                for which in range(4):
                    t = 2 * (before + 2 * (size - 1 - before)) + which
                    copy(part(part_ref, me, which), part(slots, me, which), t).wait_recv()
                hidden_ref[...] += slots[me].astype(f32)

        return step, last

    local = [pltpu.make_async_copy(own_cot(h), gathered(me, h), local_sem.at[h]) for h in range(2)]
    for copy in local:
        copy.start()
    step_r, last_r = direction(True)
    step_l, last_l = direction(False)
    for t in range(2 * (2 * size - 1) + 2):
        step_r(t)
        step_l(t)
    hidden_ref[...] = part_ref[me].astype(f32)
    last_r()
    last_l()
    row = lax.broadcasted_iota(jnp.int32, (rows, 1), 0) + me * rows
    live = jnp.where(row < length_ref[0], 1.0, 0.0)
    hidden = tokens_ref[...].astype(f32) + live * hidden_ref[...]
    hidden_ref[...] = hidden
    inverse = lax.rsqrt(jnp.mean(hidden * hidden, axis=1, keepdims=True) + epsilon)
    normed[...] = (hidden * inverse * gain_ref[...].astype(f32)).astype(bf)
    step_x, finish_x = line_gather(
        me, size, normed.at[:half], lambda owner: xa_ref.at[pl.ds(pl.multiple_of(owner * half, half), half)],
        local_sem.at[2], sems,
    )
    for j in range(size):
        step_x(j)
    second_ref[...] = normed[half:, :]
    for copy in local:
        copy.wait()
    finish_x()


def finish_branch(lengths, part, tokens, gain, cot, cid):
    size = lax.axis_size("tensor")
    rows, width = tokens.shape
    half = rows // 2
    bf, f32 = jnp.bfloat16, jnp.float32
    vmem = pl.BlockSpec(memory_space=pltpu.VMEM)
    anywhere = pl.BlockSpec(memory_space=pl.ANY)
    dma = pltpu.SemaphoreType.DMA
    gathered = jax.ShapeDtypeStruct((size * half, width), bf)
    return pl.pallas_call(
        branch_body,
        in_specs=[pl.BlockSpec(memory_space=pltpu.SMEM), vmem, vmem, vmem, anywhere],
        out_specs=[vmem, vmem, anywhere, anywhere],
        out_shape=[
            jax.ShapeDtypeStruct((rows, width), f32), jax.ShapeDtypeStruct((half, width), bf), gathered, gathered,
        ],
        scratch_shapes=[
            pltpu.VMEM((size, rows, width), bf), pltpu.VMEM((size, rows, width), bf), pltpu.VMEM((rows, width), bf),
            dma((3,)), *[dma((4 * size,))] * 4, *[dma((size,))] * 4,
        ],
        compiler_params=pltpu.CompilerParams(vmem_limit_bytes=48 * MIB, collective_id=cid, has_side_effects=True),
        cost_estimate=pl.CostEstimate(flops=0, bytes_accessed=24 * rows * size * width, transcendentals=0),
        name="finish_branch",
    )(lengths, part.reshape(size, rows, width), tokens, gain[None], cot)


def small_sum_phases(local_rows, part_ref, out_ref, scratch):
    staged, landed, from_dp, mine, from_tensor, send_dp, recv_dp, send_t, recv_t, send_out, recv_out = scratch
    size_dp, size_t = lax.axis_size("dp"), lax.axis_size("tensor")
    me_dp, me_t = lax.axis_index("dp"), lax.axis_index("tensor")
    width = mine.shape[1]

    def piece(ref, owner):
        return ref.at[:, pl.ds(pl.multiple_of(owner * width, width), width)]

    def greet():
        barrier = pltpu.get_barrier_semaphore()
        for step in range(1, size_dp):
            peer = lax.rem(me_dp + step, size_dp)
            pl.semaphore_signal(barrier, inc=1, device_id={"dp": peer}, device_id_type=MESH)
        for step in range(1, size_t):
            peer = lax.rem(me_t + step, size_t)
            pl.semaphore_signal(barrier, inc=1, device_id={"tensor": peer}, device_id_type=MESH)
        pl.semaphore_wait(barrier, size_dp + size_t - 2)

    def copy(source, target, axis, step, send_sem, recv_sem):
        me, size = (me_dp, size_dp) if axis == "dp" else (me_t, size_t)
        return pltpu.make_async_remote_copy(
            src_ref=source, dst_ref=target, send_sem=send_sem.at[step], recv_sem=recv_sem.at[step],
            device_id={axis: lax.rem(me + step, size)}, device_id_type=MESH,
        )

    def to_owner(step):
        return copy(piece(staged, lax.rem(me_dp + step, size_dp)), from_dp.at[step], "dp", step, send_dp, recv_dp)

    def to_tensor(step):
        return copy(mine, from_tensor.at[step], "tensor", step, send_t, recv_t)

    def to_all(step):
        here = piece(landed, me_dp)
        return copy(here, here, "dp", step, send_out, recv_out)

    def first():
        staged[...] = part_ref[...]
        for step in range(1, size_dp):
            to_owner(step).start()

    def second():
        total = piece(staged, me_dp)[...]
        for step in range(1, size_dp):
            to_owner(step).wait_recv()
            total = total + from_dp[step]
        mine[...] = total
        for step in range(1, size_t):
            to_tensor(step).start()

    def third():
        total = mine[...]
        for step in range(1, size_t):
            to_tensor(step).wait_recv()
            total = total + from_tensor[step]
        piece(landed, me_dp)[...] = total
        piece(landed.at[local_rows:], me_dp)[...] = mine[local_rows:, :]
        for step in range(1, size_dp):
            to_all(step).start()

    def last():
        for step in range(1, size_dp):
            to_all(step).wait_recv()
        out_ref[...] = landed[...]
        for step in range(1, size_dp):
            to_owner(step).wait_send()
            to_all(step).wait_send()
        for step in range(1, size_t):
            to_tensor(step).wait_send()

    return greet, first, second, third, last


def small_sum_scratch(shape):
    size_dp, size_t = lax.axis_size("dp"), lax.axis_size("tensor")
    rows, width = shape[0], shape[1] // size_dp
    dma = pltpu.SemaphoreType.DMA
    f32 = jnp.float32
    return [
        pltpu.VMEM(shape, f32), pltpu.VMEM(shape, f32),
        pltpu.VMEM((size_dp, rows, width), f32), pltpu.VMEM((rows, width), f32), pltpu.VMEM((size_t, rows, width), f32),
        dma((size_dp,)), dma((size_dp,)), dma((size_t,)), dma((size_t,)), dma((size_dp,)), dma((size_dp,)),
    ]


def sums_body(local_rows, part_ref, out_ref, *scratch):
    for phase in small_sum_phases(local_rows, part_ref, out_ref, scratch):
        phase()


def small_sums(part, local_rows, cid):
    vmem = pl.BlockSpec(memory_space=pltpu.VMEM)
    return pl.pallas_call(
        functools.partial(sums_body, local_rows),
        in_specs=[vmem],
        out_specs=vmem,
        out_shape=jax.ShapeDtypeStruct(part.shape, jnp.float32),
        scratch_shapes=small_sum_scratch(part.shape),
        compiler_params=pltpu.CompilerParams(collective_id=cid, has_side_effects=True),
        name="small_sums",
    )(part)


def attention_grads_body(nc, cut, local_rows, a_ref, a2_ref, b_ref, b2_ref, part_ref, o_ref, o2_ref, sums_ref, *scratch):
    i = pl.program_id(0)
    greet, *phases = small_sum_phases(local_rows, part_ref, sums_ref, scratch[:11])
    steps = nc + LA + LB + LC

    def store(c, rows, result):
        @pl.when(c < cut)
        def _():
            o_ref[rows, :] = result.astype(o_ref.dtype)

        @pl.when(c >= cut)
        def _():
            o2_ref[rows, :] = result.astype(o2_ref.dtype)

    send = scatter_steps(i, nc, (LA, LB, LC), o_ref.shape[1], scratch[11:], store, greet)
    for when, phase in zip((0, 4, 8, steps - 1), phases):
        pl.when(i == when)(phase)

    @pl.when(i < cut)
    def _():
        send(lambda cols: jnp.dot(a_ref[...], b_ref[:, cols], preferred_element_type=jnp.float32))

    @pl.when((i >= cut) & (i < nc))
    def _():
        send(lambda cols: jnp.dot(a2_ref[...], b2_ref[:, cols], preferred_element_type=jnp.float32))


def attention_grads(a, b, a2, b2, part, local_rows, r, cid):
    T, D = b.shape
    w = D // 8
    cut, rest = a.shape[0] // r, a2.shape[0] // r
    nc = cut + rest
    lag = LA + LB + LC
    out_specs, out_shape = scatter_outs(nc, cut, lag, r, w)

    def whole(shape):
        return pl.BlockSpec(shape, lambda i: (0, 0), pipeline_mode=pl.Buffered(1))

    return pl.pallas_call(
        functools.partial(attention_grads_body, nc, cut, local_rows),
        grid=(nc + lag,),
        in_specs=[
            pl.BlockSpec((r, T), lambda i: (jnp.minimum(i, cut - 1), 0)),
            pl.BlockSpec((r, T), lambda i: (jnp.clip(i - cut, 0, rest - 1), 0)),
            whole((T, D)), whole((T, D)), whole(part.shape),
        ],
        out_specs=[*out_specs, whole(part.shape)],
        out_shape=[*out_shape, jax.ShapeDtypeStruct(part.shape, jnp.float32)],
        scratch_shapes=[*small_sum_scratch(part.shape), *scatter_scratch(r, w)],
        compiler_params=pltpu.CompilerParams(vmem_limit_bytes=48 * MIB, collective_id=cid, has_side_effects=True),
        cost_estimate=pl.CostEstimate(flops=2 * nc * r * T * D, bytes_accessed=2 * nc * r * T + 4 * T * D, transcendentals=0),
        name="attention_grads",
    )(a, a2, b, b2, part)


def on_device(
    tokens,
    lengths,
    routes,
    cotangent,
    norm_one,
    qkv_weight,
    qkv_bias,
    out_weight,
    norm_two,
    router_weight,
    expert_in,
    expert_out,
    shared_in,
    shared_out,
    shared_gate,
):
    own_rows = tokens.shape[0]
    slot_count = routes.shape[0]
    model_width = tokens.shape[1]
    qkv_cols = qkv_weight.shape[2]
    local_heads = qkv_cols // HEAD_DIM
    experts = router_weight.shape[1]
    eff = expert_in.shape[3]
    shared_chunks = shared_out.shape[0] // eff
    chunks = experts + shared_chunks
    bf = jnp.bfloat16
    qkv_cols = qkv_weight.shape[2]
    length = lengths[0]
    tensor_index = lax.axis_index("tensor")
    first_row = tensor_index * own_rows
    live_own = (first_row + jnp.arange(own_rows) < length).astype(jnp.float32)[:, None]
    tokens_f = tokens.astype(jnp.float32)
    gain_one = norm_one.astype(jnp.float32)
    gain_two = norm_two.astype(jnp.float32)
    inv_one = lax.rsqrt(jnp.mean(tokens_f * tokens_f, axis=-1, keepdims=True) + epsilon)
    unit_one = tokens_f * inv_one
    normed_one = lax.all_gather((unit_one * gain_one).astype(bf), "tensor", axis=0, tiled=True)
    cos_table, sin_table = rotary_tables(slot_count, HEAD_DIM)
    qkv_w = qkv_weight.transpose(1, 0, 2)
    ei = expert_in.transpose(0, 2, 3, 1).reshape(experts, 2 * eff, model_width)
    eo = expert_out
    si = (
        shared_in.reshape(model_width, 2, shared_chunks, eff)
        .transpose(2, 1, 3, 0)
        .reshape(shared_chunks, 2 * eff, model_width)
    )
    so = shared_out.reshape(shared_chunks, eff, model_width)
    router_rows = jnp.concatenate(
        [
            router_weight.T,
            shared_gate[None],
            jnp.zeros((-(experts + 1) % 16, model_width), bf),
        ],
        axis=0,
    )
    grad_out = cotangent.astype(jnp.float32) * live_own
    d_two_own = (live_own * grad_out).astype(bf)
    normed_one, si, router_rows, cos_table, sin_table, d_two_own = lax.optimization_barrier(
        (normed_one, si, router_rows, cos_table, sin_table, d_two_own)
    )
    qkv = project_qkv(normed_one, qkv_w, qkv_bias[:, None, :], cos_table, sin_table)
    mixed, mixed_t = attend(lengths, qkv)
    branch_partial = jnp.dot(mixed, out_weight, preferred_element_type=jnp.float32).astype(bf)
    size_t = lax.axis_size("tensor")
    half = own_rows // 2
    hidden, second, x_a, d_a = finish_branch(
        lengths, branch_partial, tokens, norm_two, d_two_own, 1
    )
    inv_two = lax.rsqrt(jnp.mean(hidden * hidden, axis=-1, keepdims=True) + epsilon)
    unit_two = hidden * inv_two
    routes_a, routes_b = (
        routes.reshape(size_t, 2, half, -1).transpose(1, 0, 2, 3).reshape(2, size_t * half, -1)
    )
    weights = (router_rows, ei, si, eo, so)
    dgu_a, dn_a, bt_a, router_a, np_a, s_a, x_b, d_b = ffn(
        x_a, d_a, routes_a.T, *weights, own=[second, d_two_own[half:]]
    )
    grad_a = lax.psum_scatter(dn_a, "tensor", scatter_dimension=0, tiled=True)
    two_a = lax.psum_scatter(bt_a, "tensor", scatter_dimension=0, tiled=True)
    if lax.axis_size("dp") == 8:
        dgu_b, dn_b, bt_b, router_b, np_b, out_grads, shared_out_grad = ffn(
            x_b, d_b, routes_b.T, *weights, other=(s_a, d_a)
        )
    else:
        dgu_b, dn_b, bt_b, router_b, np_b, s_b = ffn(x_b, d_b, routes_b.T, *weights)
        inner = [s.reshape(chunks * eff, -1) for s in (s_a, s_b)]
        out_grads, shared_out_grad = weight_grad_scatter(
            inner, [d_a, d_b], eff, 2, "down_grads", cut=experts
        )
    router_part = router_a + router_b
    norm_two_part = np_a + np_b
    d_gate_up = [d.reshape(chunks * 2 * eff, -1) for d in (dgu_a, dgu_b)]
    grad_a, two_a, dn_b = lax.optimization_barrier((grad_a, two_a, dn_b))
    grad_b = lax.psum_scatter(dn_b, "tensor", scatter_dimension=0, tiled=True)
    two_b = lax.psum_scatter(bt_b, "tensor", scatter_dimension=0, tiled=True)
    in_grads_b, _ = weight_grad_scatter(
        d_gate_up, [x_a, x_b], eff, 4, "shared_in_grads", 2 * experts, 2 * shared_chunks
    )
    grad_two = jnp.concatenate([grad_a, grad_b], axis=0).astype(jnp.float32)
    grad_hidden = grad_out + norm_back(grad_two, unit_two, inv_two, gain_two)
    d_one_own, in_grads_b = lax.optimization_barrier(
        ((live_own * grad_hidden).astype(bf), in_grads_b)
    )
    d_one = lax.all_gather(d_one_own, "tensor", axis=0, tiled=True)
    d_gate_up, _ = lax.optimization_barrier((d_gate_up, d_one_own))
    in_grads_a, _ = weight_grad_scatter(
        d_gate_up, [x_a, x_b], eff, 3, "expert_in_grads", 0, 2 * experts
    )
    d_one, in_grads_a = lax.optimization_barrier((d_one, in_grads_a))
    d_mixed = lax.dot_general(d_one, out_weight, NT, preferred_element_type=jnp.float32).astype(bf)
    d_qkv, d_qkv_t, bias_part = attend_back(lengths, qkv, d_mixed, cos_table, sin_table)
    grad_one, norm_one_part = qkv_back(d_qkv, qkv_w, normed_one)
    grad_one, d_qkv_t, mixed_t, two_b = lax.optimization_barrier(
        (grad_one, d_qkv_t, mixed_t, two_b)
    )
    grad_one_own = lax.psum_scatter(grad_one, "tensor", scatter_dimension=0, tiled=True)
    part = jnp.concatenate(
        [
            router_part[: experts + 1],
            norm_one_part / gain_one[None],
            norm_two_part / gain_two[None],
            jnp.pad(bias_part.reshape(1, 3 * qkv_cols), ((0, 0), (0, model_width - 3 * qkv_cols))),
        ],
        axis=0,
    )
    d_qkv_t = d_qkv_t.reshape(3 * qkv_cols, slot_count)
    if lax.axis_size("dp") == 8:
        qkv_sum, out_sum, sums = attention_grads(
            d_qkv_t, normed_one, mixed_t, d_one, part, experts + 3, qkv_cols // 2, 5
        )
    else:
        sums = small_sums(part, experts + 3, 7)
        qkv_sum, _ = weight_grad_scatter([d_qkv_t], [normed_one], qkv_cols, 5, "qkv_grads")
        out_sum, _ = weight_grad_scatter([mixed_t], [d_one], qkv_cols, 6, "mix_grads")
    branch_two = jnp.concatenate([two_a, two_b], axis=0).astype(jnp.float32)
    output = (hidden + live_own * branch_two).astype(bf)
    grad_one = grad_one_own.astype(jnp.float32)
    input_grad = grad_hidden + norm_back(grad_one, unit_one, inv_one, gain_one)
    qkv_bias_grad = sums[experts + 3, : 3 * qkv_cols].reshape(3, qkv_cols)
    own_cols = out_grads.shape[1]
    expert_in_grad = in_grads_a.astype(jnp.float32).reshape(experts, 2, eff, own_cols).transpose(0, 3, 1, 2)
    shared_in_grad = (
        in_grads_b.reshape(shared_chunks, 2, eff, own_cols)
        .transpose(3, 1, 0, 2)
        .reshape(own_cols, 2, shared_chunks * eff)
        .astype(jnp.float32)
    )
    return (
        output,
        input_grad,
        sums[experts + 1],
        qkv_sum.astype(jnp.float32).reshape(3, qkv_cols, own_cols).transpose(2, 0, 1),
        qkv_bias_grad,
        out_sum.astype(jnp.float32),
        sums[experts + 2],
        sums[:experts].T,
        expert_in_grad,
        out_grads.astype(jnp.float32).reshape(experts, eff, own_cols),
        shared_in_grad,
        shared_out_grad.astype(jnp.float32),
        sums[experts],
    )


def solution(mesh):
    in_specs = (
        P(("dp", "tensor"), None),
        P("dp"),
        P("dp", None),
        P(("dp", "tensor"), None),
        P(),
        P(None, None, "tensor"),
        P(None, "tensor"),
        P("tensor", None),
        P(),
        P(),
        P(None, None, None, "tensor"),
        P(None, "tensor", None),
        P(None, None, "tensor"),
        P("tensor", None),
        P(),
    )
    out_specs = (
        P(("dp", "tensor"), None),
        P(("dp", "tensor"), None),
        P(),
        P("dp", None, "tensor"),
        P(None, "tensor"),
        P("tensor", "dp"),
        P(),
        P(),
        P(None, "dp", None, "tensor"),
        P(None, "tensor", "dp"),
        P("dp", None, "tensor"),
        P("tensor", "dp"),
        P(),
    )
    return jax.shard_map(
        on_device, mesh=mesh, in_specs=in_specs, out_specs=out_specs, check_vma=False
    )
```

```python
import functools

import jax
import jax.numpy as jnp
from jax import lax
from jax.experimental import pallas as pl
from jax.experimental.pallas import tpu as pltpu
from jax.sharding import PartitionSpec as P

HEAD_DIM = 128
MESH = pl.DeviceIdType.MESH
LA, LB, LC = 1, 2, 2
FFN_LAGS = (1, 1, 1)
MIB = 2**20
ATTEND_HEADS = 1


epsilon = 1e-06
theta_base = 1000000.0
NT = (((1,), (1,)), ((), ()))
TN = (((0,), (0,)), ((), ()))


def rotary_tables(row_count, head_width):
    half_index = jnp.arange(head_width // 2).astype(jnp.float32)
    frequency = theta_base ** (-2.0 * half_index / head_width)
    angles = jnp.arange(row_count).astype(jnp.float32)[:, None] * frequency[None, :]
    sines = jnp.sin(angles)
    cosines = jnp.cos(angles)
    return (
        jnp.concatenate([cosines, cosines], axis=-1),
        jnp.concatenate([-sines, sines], axis=-1),
    )


def norm_back(d_normed, unit_rows, inverse, gain_vector):
    d_unit = d_normed * gain_vector
    return inverse * (d_unit - unit_rows * jnp.mean(d_unit * unit_rows, axis=-1, keepdims=True))


def scatter_scratch(r, w):
    f32, bf = jnp.float32, jnp.bfloat16
    dma = pltpu.SemaphoreType.DMA
    h = r // 2
    return [
        pltpu.VMEM((2, 4, r, w), f32), pltpu.VMEM((2, 4, r, w), bf), pltpu.VMEM((3, 4, r, w), bf),
        pltpu.VMEM((3, 2, 2, h, w), f32), pltpu.VMEM((3, 2, 2, h, w), bf), pltpu.VMEM((6, 2, 2, h, w), bf),
        pltpu.VMEM((3, 2, h, w), f32), pltpu.VMEM((2, 2, h, w), bf), pltpu.VMEM((6, 2, h, w), bf),
        dma((2,)), dma((3,)), dma((3, 2)), dma((6, 2)), dma((2, 2)), dma((6, 2)),
    ]


def scatter_steps(i, nc, lags, w, scratch, store, greet=None):
    own, sa, ra, kt, s1, r1, ku, s2, r2, sem_sa, sem_ra, sem_s1, sem_r1, sem_s2, sem_r2 = scratch
    la, lb, lc = lags
    keep_1 = min(3, lb + lc)
    hr = own.shape[2] // 2
    dp = lax.axis_index("dp")
    k = dp % 2
    x = (dp // 2) % 2
    y = dp // 4
    core_peer = y * 4 + x * 2 + (1 - k)
    x_peer = y * 4 + (1 - x) * 2 + k
    y_peer = (1 - y) * 4 + x * 2 + k

    def copy_a(c):
        return pltpu.make_async_remote_copy(
            src_ref=sa.at[c % 2], dst_ref=ra.at[c % 3], send_sem=sem_sa.at[c % 2], recv_sem=sem_ra.at[c % 3],
            device_id={"dp": core_peer}, device_id_type=MESH,
        )

    def copy_1(c, half):
        return pltpu.make_async_remote_copy(
            src_ref=s1.at[c % 3, half], dst_ref=r1.at[c % 6, half], send_sem=sem_s1.at[c % 3, half],
            recv_sem=sem_r1.at[c % 6, half], device_id={"dp": y_peer if half else x_peer}, device_id_type=MESH,
        )

    def copy_2(c, half):
        return pltpu.make_async_remote_copy(
            src_ref=s2.at[c % 2, half], dst_ref=r2.at[c % 6, half], send_sem=sem_s2.at[c % 2, half],
            recv_sem=sem_r2.at[c % 6, half], device_id={"dp": x_peer if half else y_peer}, device_id_type=MESH,
        )

    @pl.when(i == 0)
    def _():
        if greet is not None:
            greet()
            return
        barrier = pltpu.get_barrier_semaphore()
        for peer in (core_peer, x_peer, y_peer):
            pl.semaphore_signal(barrier, inc=1, device_id={"dp": peer}, device_id_type=MESH)
        pl.semaphore_wait(barrier, 3)

    @pl.when((i >= la + keep_1) & (i < nc + la + keep_1))
    def _():
        copy_1(i - la - keep_1, 0).wait_send()
        copy_1(i - la - keep_1, 1).wait_send()

    @pl.when((i >= la) & (i < nc + la))
    def _():
        c = i - la
        copy_a(c).wait_recv()
        for half in range(2):
            rows = slice(half * hr, half * hr + hr)
            keep, other = (1, 2) if half else (2, 1)

            def total(role):
                return own[c % 2, role, rows, :] + ra[c % 3, role, rows, :].astype(jnp.float32)

            s1[c % 3, half, 0] = total(other).astype(jnp.bfloat16)
            s1[c % 3, half, 1] = total(3).astype(jnp.bfloat16)
            copy_1(c, half).start()
            kt[c % 3, half, 0] = total(0)
            kt[c % 3, half, 1] = total(keep)

    @pl.when((i >= la + lb) & (i < nc + la + lb))
    def _():
        c = i - la - lb

        @pl.when(c >= 2)
        def _():
            copy_2(c - 2, 0).wait_send()
            copy_2(c - 2, 1).wait_send()

        for half in range(2):
            copy_1(c, half).wait_recv()
            s2[c % 2, half] = (kt[c % 3, half, 1] + r1[c % 6, half, 1].astype(jnp.float32)).astype(jnp.bfloat16)
            copy_2(c, half).start()
            ku[c % 3, half] = kt[c % 3, half, 0] + r1[c % 6, half, 0].astype(jnp.float32)

    @pl.when(i >= la + lb + lc)
    def _():
        c = i - la - lb - lc
        for half in range(2):
            copy_2(c, half).wait_recv()
            store(c, slice(half * hr, half * hr + hr), ku[c % 3, half] + r2[c % 6, half].astype(jnp.float32))

        @pl.when(c >= nc - 2)
        def _():
            copy_2(c, 0).wait_send()
            copy_2(c, 1).wait_send()

    @pl.when((i >= 2) & (i < nc + 2))
    def _():
        copy_a(i - 2).wait_send()

    def send(product):
        targets = (y * 4 + x * 2, y * 4 + (1 - x) * 2, (1 - y) * 4 + x * 2, (1 - y) * 4 + (1 - x) * 2)

        def cols(role, core):
            return pl.ds(pl.multiple_of((targets[role] + core) * w, w), w)

        for role in range(4):
            sa[i % 2, role] = product(cols(role, 1 - k)).astype(jnp.bfloat16)
        copy_a(i).start()
        for role in range(4):
            own[i % 2, role] = product(cols(role, k))

    return send


def rs_body(nc, cut, pairs, *refs):
    a_refs, b_refs = refs[:pairs], refs[pairs : 2 * pairs]
    o_ref, o2_ref = refs[2 * pairs : 2 * pairs + 2]
    i = pl.program_id(0)

    def store(c, rows, result):
        @pl.when(c < cut)
        def _():
            o_ref[rows, :] = result.astype(o_ref.dtype)

        @pl.when(c >= cut)
        def _():
            o2_ref[rows, :] = result.astype(o2_ref.dtype)

    send = scatter_steps(i, nc, (LA, LB, LC), o_ref.shape[1], refs[2 * pairs + 2 :], store)

    @pl.when(i < nc)
    def _():
        def product(cols):
            total = jnp.dot(a_refs[0][...], b_refs[0][:, cols], preferred_element_type=jnp.float32)
            for a_ref, b_ref in zip(a_refs[1:], b_refs[1:]):
                total += jnp.dot(a_ref[...], b_ref[:, cols], preferred_element_type=jnp.float32)
            return total

        send(product)


def scatter_outs(nc, cut, lag, r, w):
    rest = max(nc - cut, 1)
    specs = [
        pl.BlockSpec((r, w), lambda i: (jnp.clip(i - lag, 0, cut - 1), 0)),
        pl.BlockSpec((r, w), lambda i: (jnp.clip(i - lag - cut, 0, rest - 1), 0)),
    ]
    return specs, [jax.ShapeDtypeStruct((n * r, w), jnp.bfloat16) for n in (cut, rest)]


def weight_grad_scatter_kernel(a_list, b_list, r, cid, name, first, count, cut):
    D = b_list[0].shape[1]
    T = sum(b.shape[0] for b in b_list)
    w = D // 8
    lag = LA + LB + LC
    out_specs, out_shape = scatter_outs(count, cut, lag, r, w)
    return pl.pallas_call(
        functools.partial(rs_body, count, cut, len(a_list)),
        grid=(count + lag,),
        in_specs=[
            *[pl.BlockSpec((r, a.shape[1]), lambda i: (jnp.minimum(i, count - 1) + first, 0)) for a in a_list],
            *[pl.BlockSpec(b.shape, lambda i: (0, 0), pipeline_mode=pl.Buffered(1)) for b in b_list],
        ],
        out_specs=out_specs,
        out_shape=out_shape,
        scratch_shapes=scatter_scratch(r, w),
        compiler_params=pltpu.CompilerParams(vmem_limit_bytes=48 * MIB, collective_id=cid, has_side_effects=True),
        cost_estimate=pl.CostEstimate(
            flops=2 * count * r * T * D, bytes_accessed=2 * count * r * T + 2 * T * D + 4 * count * r * w, transcendentals=0
        ),
        name=name,
    )(*a_list, *b_list)


def ffn_body(
    experts, chunks, scatter, gather,
    x_ref, d_ref, routes_ref, rw_ref, ei_ref, si_ref, eo_ref, so_ref, *refs,
):
    if scatter:
        s_other_ref, d_other_ref, dgu_ref, dn_ref, bt_ref, rg_ref, np_ref, og_ref, og2_ref, *refs = refs
    else:
        if gather:
            own_x_ref, own_d_ref, *refs = refs
        dgu_ref, dn_ref, bt_ref, rg_ref, np_ref, s_ref, *refs = refs
        if gather:
            all_x_ref, all_d_ref, *refs = refs
    dn_acc, bt_acc, probs_ref, w_ref, ds_ref, wi_buf, wd_buf, sem, *scratch = refs
    c = pl.program_id(0)
    h = eo_ref.shape[1]
    slots, width = x_ref.shape
    if gather:
        me, size = lax.axis_index("tensor"), lax.axis_size("tensor")
        local_sem, *sems = scratch
        lines = []
        for number, (own, out) in enumerate(((own_x_ref, all_x_ref), (own_d_ref, all_d_ref))):
            def block(owner, out=out, rows=own.shape[0]):
                return out.at[pl.ds(pl.multiple_of(owner * rows, rows), rows)]

            lines.append(
                line_gather(me, size, own, block, local_sem.at[number], sems[4 * number : 4 * number + 4])
            )
        for hop in range(size - 1):
            @pl.when(c == -(-hop * (chunks - 1) // (size - 1)))
            def _():
                if hop == 0:
                    line_barrier(me, size)
                for advance, _ in lines:
                    advance(hop)

    def fetch(step):
        slot = step % 2

        @pl.when(step < experts)
        def _():
            pltpu.make_async_copy(ei_ref.at[step], wi_buf.at[slot], sem.at[0, slot]).start()
            pltpu.make_async_copy(eo_ref.at[step], wd_buf.at[slot], sem.at[1, slot]).start()

        @pl.when(step >= experts)
        def _():
            pltpu.make_async_copy(si_ref.at[step - experts], wi_buf.at[slot], sem.at[0, slot]).start()
            pltpu.make_async_copy(so_ref.at[step - experts], wd_buf.at[slot], sem.at[1, slot]).start()

    @pl.when(c == 0)
    def _():
        fetch(c)

    @pl.when(c + 1 < chunks)
    def _():
        fetch(c + 1)

    def picked():
        expert = lax.broadcasted_iota(jnp.int32, (experts, slots), 0)
        hit = jnp.zeros((experts, slots), jnp.float32)
        for j in range(routes_ref.shape[0]):
            hit = hit + jnp.where(routes_ref[j : j + 1, :] == expert, 1.0, 0.0)
        return hit

    @pl.when(c == 0)
    def _():
        logits = lax.dot_general(rw_ref[...], x_ref[...], NT, preferred_element_type=jnp.float32)
        raised = jnp.exp(logits[:experts] - jnp.max(logits[:experts], axis=0, keepdims=True))
        probs = raised / jnp.sum(raised, axis=0, keepdims=True)
        gate = 1.0 / (1.0 + jnp.exp(-logits[experts:]))
        probs_ref[...] = probs
        w_ref[:experts, :] = probs * picked()
        w_ref[experts:, :] = gate
        ds_ref[...] = jnp.zeros_like(ds_ref)
        dn_acc[...] = jnp.zeros_like(dn_acc)
        bt_acc[...] = jnp.zeros_like(bt_acc)

    if scatter:
        def store(chunk, rows, result):
            @pl.when(chunk < experts)
            def _():
                og_ref[rows, :] = result.astype(og_ref.dtype)

            @pl.when(chunk >= experts)
            def _():
                og2_ref[rows, :] = result.astype(og2_ref.dtype)

        send = scatter_steps(c, chunks, FFN_LAGS, og_ref.shape[1], scratch, store)

    block = 512

    @pl.when(c < chunks)
    def _():
        row = pl.ds(jnp.minimum(c, experts), 1)
        slot = c % 2
        pltpu.make_async_copy(ei_ref.at[0], wi_buf.at[slot], sem.at[0, slot]).wait()
        pltpu.make_async_copy(eo_ref.at[0], wd_buf.at[slot], sem.at[1, slot]).wait()
        wi = wi_buf.at[slot]
        wd = wd_buf.at[slot]
        x = x_ref[...]
        g = lax.dot_general(wi[:h], x, NT, preferred_element_type=jnp.float32)
        u = lax.dot_general(wi[h:], x, NT, preferred_element_type=jnp.float32)
        p = lax.dot_general(wd[...], d_ref[...], NT, preferred_element_type=jnp.float32)
        w = w_ref[row, :]
        sg = 1.0 / (1.0 + jnp.exp(-g))
        si = g * sg
        inner = (si * u).astype(jnp.bfloat16).astype(jnp.float32)
        s = (w * inner).astype(jnp.bfloat16)
        ds_ref[row, :] += jnp.sum(p * inner, axis=0, keepdims=True)
        di = w * p
        dg = (di * u * sg * (1.0 + g * (1.0 - sg))).astype(jnp.bfloat16)
        du = (di * si).astype(jnp.bfloat16)
        dgu_ref[0, :h] = dg
        dgu_ref[0, h:] = du
        dgu = jnp.concatenate([dg, du], axis=0)
        if scatter:
            def product(cols):
                return jnp.dot(s, d_ref[:, cols], preferred_element_type=jnp.float32) + jnp.dot(
                    s_other_ref[0], d_other_ref[:, cols], preferred_element_type=jnp.float32
                )

            send(product)
        else:
            s_ref[0] = s
        for n in range(0, width, block):
            cols = slice(n, n + block)
            dn_acc[:, cols] += lax.dot_general(dgu, wi[:, cols], TN, preferred_element_type=jnp.float32)
            bt_acc[:, cols] += lax.dot_general(s, wd[:, cols], TN, preferred_element_type=jnp.float32)

    @pl.when(c == (chunks if scatter else chunks - 1))
    def _():
        probs = probs_ref[...]
        d_probs = ds_ref[:experts, :] * picked()
        d_logits = probs * (d_probs - jnp.sum(probs * d_probs, axis=0, keepdims=True))
        gate = w_ref[experts:, :]
        d_gate = ds_ref[experts:, :] * gate * (1.0 - gate)
        small = jnp.concatenate([d_logits, d_gate], axis=0)
        high = small.astype(jnp.bfloat16)
        low = (small - high.astype(jnp.float32)).astype(jnp.bfloat16)
        rg_ref[...] = jnp.dot(high, x_ref[...], preferred_element_type=jnp.float32) + jnp.dot(
            low, x_ref[...], preferred_element_type=jnp.float32
        )
        for n in range(0, width, block):
            cols = slice(n, n + block)
            extra = lax.dot_general(high, rw_ref[:, cols], TN, preferred_element_type=jnp.float32)
            extra += lax.dot_general(low, rw_ref[:, cols], TN, preferred_element_type=jnp.float32)
            total = dn_acc[:, cols] + extra
            dn_ref[:, cols] = total.astype(dn_ref.dtype)
            np_ref[:, cols] = jnp.sum(total * x_ref[:, cols].astype(jnp.float32), axis=0, keepdims=True)
        bt_ref[...] = bt_acc[...].astype(bt_ref.dtype)
        if gather:
            for advance, finish in lines:
                advance(size - 1)
                finish()


def ffn(x, d_two, routes_t, router_rows, ei, si, eo, so, other=None, own=None):
    experts, h2, width = ei.shape
    chunks = experts + si.shape[0]
    h = h2 // 2
    slots = x.shape[0]
    rows = router_rows.shape[0]
    bf, f32 = jnp.bfloat16, jnp.float32
    anywhere = pl.BlockSpec(memory_space=pl.ANY)
    scatter = other is not None

    def whole(shape):
        return pl.BlockSpec(shape, lambda c: (0,) * len(shape), pipeline_mode=pl.Buffered(1))

    def chunk(shape):
        return pl.BlockSpec((1, *shape), lambda c: (jnp.minimum(c, chunks - 1), 0, 0))

    in_specs = [
        whole((slots, width)), whole((slots, width)), whole(routes_t.shape), whole((rows, width)),
        anywhere, anywhere, anywhere, anywhere,
    ]
    out_specs = [chunk((h2, slots)), whole((slots, width)), whole((slots, width)), whole((rows, width)), whole((1, width))]
    out_shape = [
        jax.ShapeDtypeStruct((chunks, h2, slots), bf), jax.ShapeDtypeStruct((slots, width), bf),
        jax.ShapeDtypeStruct((slots, width), bf), jax.ShapeDtypeStruct((rows, width), f32),
        jax.ShapeDtypeStruct((1, width), f32),
    ]
    scratch = [
        pltpu.VMEM((slots, width), f32), pltpu.VMEM((slots, width), f32),
        pltpu.VMEM((experts, slots), f32), pltpu.VMEM((rows, slots), f32), pltpu.VMEM((rows, slots), f32),
        pltpu.VMEM((2, h2, width), bf), pltpu.VMEM((2, h, width), bf), pltpu.SemaphoreType.DMA((2, 2)),
    ]
    args = [x, d_two, routes_t, router_rows, ei, si, eo, so]
    if scatter:
        s_other, d_other = other
        in_specs += [chunk((h, s_other.shape[2])), whole(d_other.shape)]
        args += [s_other, d_other]
        w = width // 8
        lag = sum(FFN_LAGS)
        specs, shapes = scatter_outs(chunks, experts, lag, h, w)
        out_specs += specs
        out_shape += shapes
        scratch += scatter_scratch(h, w)
        grid = (chunks + lag,)
        params = pltpu.CompilerParams(vmem_limit_bytes=62 * MIB, collective_id=2, has_side_effects=True)
    else:
        out_specs.append(chunk((h, slots)))
        out_shape.append(jax.ShapeDtypeStruct((chunks, h, slots), bf))
        grid = (chunks,)
        params = pltpu.CompilerParams(vmem_limit_bytes=62 * MIB)
        if own is not None:
            size = lax.axis_size("tensor")
            dma = pltpu.SemaphoreType.DMA
            in_specs += [anywhere, anywhere]
            args += own
            out_specs += [anywhere, anywhere]
            out_shape += [jax.ShapeDtypeStruct((size * a.shape[0], width), bf) for a in own]
            scratch += [dma((2,)), *[dma((size,))] * 8]
            params = pltpu.CompilerParams(vmem_limit_bytes=62 * MIB, collective_id=8, has_side_effects=True)
    return pl.pallas_call(
        functools.partial(ffn_body, experts, chunks, scatter, own is not None),
        grid=grid,
        in_specs=in_specs,
        out_specs=out_specs,
        out_shape=out_shape,
        scratch_shapes=scratch,
        compiler_params=params,
        cost_estimate=pl.CostEstimate(
            flops=12 * chunks * h * slots * width, bytes_accessed=10 * chunks * h * width + 16 * slots * width,
            transcendentals=chunks * h * slots,
        ),
        name="ffn_scatter" if scatter else "ffn",
    )(*args)


def turn(v):
    half = v.shape[1] // 2
    return jnp.concatenate([v[:, half:], v[:, :half]], axis=1)


def qkv_body(x_ref, w_ref, bias_ref, cos_ref, sin_ref, out_ref):
    j = pl.program_id(0)
    cols = w_ref.shape[2]
    y = jnp.dot(x_ref[...], w_ref[0], preferred_element_type=jnp.float32)
    y = y + bias_ref[0].astype(jnp.float32)

    @pl.when(j < 2)
    def _():
        for head in range(cols // HEAD_DIM):
            place = slice(head * HEAD_DIM, (head + 1) * HEAD_DIM)
            v = y[:, place]
            out_ref[0, :, place] = (v * cos_ref[...] + turn(v) * sin_ref[...]).astype(out_ref.dtype)

    @pl.when(j == 2)
    def _():
        out_ref[0] = y.astype(out_ref.dtype)


def project_qkv(x, w, bias, cos_table, sin_table):
    slots, width = x.shape
    cols = w.shape[2]
    table = pl.BlockSpec((slots, HEAD_DIM), lambda j: (0, 0), pipeline_mode=pl.Buffered(1))
    return pl.pallas_call(
        qkv_body,
        grid=(3,),
        in_specs=[
            pl.BlockSpec((slots, width), lambda j: (0, 0), pipeline_mode=pl.Buffered(1)),
            pl.BlockSpec((1, width, cols), lambda j: (j, 0, 0)),
            pl.BlockSpec((1, 1, cols), lambda j: (j, 0, 0)),
            table, table,
        ],
        out_specs=pl.BlockSpec((1, slots, cols), lambda j: (j, 0, 0)),
        out_shape=jax.ShapeDtypeStruct((3, slots, cols), jnp.bfloat16),
        compiler_params=pltpu.CompilerParams(vmem_limit_bytes=48 * MIB),
        cost_estimate=pl.CostEstimate(
            flops=6 * slots * width * cols, bytes_accessed=2 * slots * width + 6 * width * cols, transcendentals=0
        ),
        name="project_qkv",
    )(x, w, bias, cos_table, sin_table)


def block_probs(length_ref, q, k, start):
    s = lax.dot_general(q, k, NT, preferred_element_type=jnp.float32) * (HEAD_DIM**-0.5)
    row = lax.broadcasted_iota(jnp.int32, s.shape, 0) + start
    col = lax.broadcasted_iota(jnp.int32, s.shape, 1)
    s = jnp.where((col <= row) & (col < length_ref[0]), s, -1000000000.0)
    e = jnp.exp(s - jnp.max(s, axis=1, keepdims=True))
    return e * (1.0 / jnp.sum(e, axis=1, keepdims=True))


def attend_body(rows, length_ref, q_ref, k_ref, v_ref, mixed_ref, mixed_t_ref):
    for start in range(0, q_ref.shape[1], rows):
        here, end = slice(start, start + rows), start + rows
        p = block_probs(length_ref, q_ref[0, here, :], k_ref[0, :end, :], start)
        mixed = jnp.dot(p.astype(jnp.bfloat16), v_ref[0, :end, :], preferred_element_type=jnp.float32)
        mixed_ref[here, :] = mixed.astype(mixed_ref.dtype)
        mixed_t_ref[:, here] = mixed.T.astype(mixed_ref.dtype)


def attend(lengths, qkv):
    _, slots, cols = qkv.shape
    rows = min(512, slots)

    def part(j):
        return pl.BlockSpec((1, slots, HEAD_DIM), lambda h: (j, 0, h))

    return pl.pallas_call(
        functools.partial(attend_body, rows),
        grid=(cols // HEAD_DIM,),
        in_specs=[pl.BlockSpec(memory_space=pltpu.SMEM), part(0), part(1), part(2)],
        out_specs=[
            pl.BlockSpec((slots, HEAD_DIM), lambda h: (0, h)), pl.BlockSpec((HEAD_DIM, slots), lambda h: (h, 0)),
        ],
        out_shape=[
            jax.ShapeDtypeStruct((slots, cols), jnp.bfloat16), jax.ShapeDtypeStruct((cols, slots), jnp.bfloat16),
        ],
        compiler_params=pltpu.CompilerParams(vmem_limit_bytes=32 * MIB),
        cost_estimate=pl.CostEstimate(
            flops=4 * slots * slots * cols, bytes_accessed=10 * slots * cols, transcendentals=slots * slots * cols // HEAD_DIM
        ),
        name="attend",
    )(lengths, qkv, qkv, qkv)


def attend_back_body(
    rows, length_ref, q_ref, k_ref, v_ref, dm_ref, cos_ref, sin_ref, out_ref, out_t_ref, bias_ref, dk_acc, dv_acc
):
    slots = q_ref.shape[1]
    heads = [slice(n, n + HEAD_DIM) for n in range(0, q_ref.shape[2], HEAD_DIM)]
    scale = HEAD_DIM**-0.5
    bf, f32 = jnp.bfloat16, jnp.float32

    def finish(j, here, head, grad):
        if j < 2:
            grad = grad * cos_ref[here, :] - turn(grad) * sin_ref[here, :]
        low = grad.astype(bf)
        out_ref[j, here, head] = low
        out_t_ref[j, head, here] = grad.T.astype(bf)
        return jnp.sum(low.astype(f32), axis=0, keepdims=True)

    dq_sums = [jnp.zeros((1, HEAD_DIM), f32) for _ in heads]
    starts = list(range(0, slots, rows))[::-1]
    for start in starts:
        here, end = slice(start, start + rows), start + rows
        for n, head in enumerate(heads):
            q, k, v = q_ref[0, here, head], k_ref[0, :end, head], v_ref[0, :end, head]
            dm = dm_ref[here, head]
            p = block_probs(length_ref, q, k, start)
            dp = lax.dot_general(dm, v, NT, preferred_element_type=f32)
            ds = (p * (dp - jnp.sum(p * dp, axis=1, keepdims=True))).astype(bf)
            dq_sums[n] += finish(0, here, head, jnp.dot(ds, k, preferred_element_type=f32) * scale)
            dk = lax.dot_general(ds, q, TN, preferred_element_type=f32) * scale
            dv = lax.dot_general(p.astype(bf), dm, TN, preferred_element_type=f32)
            if start == starts[0]:
                dk_acc[n] = dk
                dv_acc[n] = dv
            else:
                dk_acc[n, :end, :] += dk
                dv_acc[n, :end, :] += dv
    every = slice(0, slots)
    for n, head in enumerate(heads):
        bias_ref[0, :, head] = dq_sums[n]
        bias_ref[1, :, head] = finish(1, every, head, dk_acc[n])
        bias_ref[2, :, head] = finish(2, every, head, dv_acc[n])


def attend_back(lengths, qkv, d_mixed, cos_table, sin_table):
    _, slots, cols = qkv.shape
    rows = min(512, slots)
    bf, f32 = jnp.bfloat16, jnp.float32
    together = ATTEND_HEADS
    wide = together * HEAD_DIM

    def part(j):
        return pl.BlockSpec((1, slots, wide), lambda h: (j, 0, h))

    table = pl.BlockSpec((slots, HEAD_DIM), lambda h: (0, 0), pipeline_mode=pl.Buffered(1))
    return pl.pallas_call(
        functools.partial(attend_back_body, rows),
        grid=(cols // wide,),
        in_specs=[
            pl.BlockSpec(memory_space=pltpu.SMEM), part(0), part(1), part(2),
            pl.BlockSpec((slots, wide), lambda h: (0, h)), table, table,
        ],
        out_specs=[
            pl.BlockSpec((3, slots, wide), lambda h: (0, 0, h)), pl.BlockSpec((3, wide, slots), lambda h: (0, h, 0)),
            pl.BlockSpec((3, 1, wide), lambda h: (0, 0, h)),
        ],
        out_shape=[
            jax.ShapeDtypeStruct((3, slots, cols), bf), jax.ShapeDtypeStruct((3, cols, slots), bf),
            jax.ShapeDtypeStruct((3, 1, cols), f32),
        ],
        scratch_shapes=[pltpu.VMEM((together, slots, HEAD_DIM), f32)] * 2,
        compiler_params=pltpu.CompilerParams(vmem_limit_bytes=56 * MIB),
        cost_estimate=pl.CostEstimate(
            flops=10 * slots * slots * cols, bytes_accessed=20 * slots * cols, transcendentals=slots * slots * cols // HEAD_DIM
        ),
        name="attend_back",
    )(lengths, qkv, qkv, qkv, d_mixed, cos_table, sin_table)


def qkv_back_body(d_ref, w_ref, x_ref, out_ref, np_ref):
    total = lax.dot_general(d_ref[0], w_ref[0], NT, preferred_element_type=jnp.float32)
    for j in range(1, 3):
        total += lax.dot_general(d_ref[j], w_ref[j], NT, preferred_element_type=jnp.float32)
    out_ref[...] = total.astype(out_ref.dtype)
    np_ref[...] = jnp.sum(total * x_ref[...].astype(jnp.float32), axis=0, keepdims=True)


def qkv_back(d_qkv, w, x):
    _, slots, cols = d_qkv.shape
    width = w.shape[1]
    block = 512
    return pl.pallas_call(
        qkv_back_body,
        grid=(width // block,),
        in_specs=[
            pl.BlockSpec((3, slots, cols), lambda n: (0, 0, 0), pipeline_mode=pl.Buffered(1)),
            pl.BlockSpec((3, block, cols), lambda n: (0, n, 0)),
            pl.BlockSpec((slots, block), lambda n: (0, n)),
        ],
        out_specs=[pl.BlockSpec((slots, block), lambda n: (0, n)), pl.BlockSpec((1, block), lambda n: (0, n))],
        out_shape=[
            jax.ShapeDtypeStruct((slots, width), jnp.bfloat16), jax.ShapeDtypeStruct((1, width), jnp.float32),
        ],
        compiler_params=pltpu.CompilerParams(vmem_limit_bytes=48 * MIB),
        cost_estimate=pl.CostEstimate(
            flops=6 * slots * width * cols, bytes_accessed=4 * slots * width + 6 * width * cols, transcendentals=0
        ),
        name="qkv_back",
    )(d_qkv, w, x)


def weight_grad_scatter(a_list, b_list, r, cid, name, first=0, count=None, cut=None):
    count = a_list[0].shape[0] // r if count is None else count
    cut = count if cut is None else cut
    if lax.axis_size("dp") == 8:
        return weight_grad_scatter_kernel(a_list, b_list, r, cid, name, first, count, cut)
    product = sum(
        jnp.dot(a[first * r : (first + count) * r], b, preferred_element_type=jnp.float32)
        for a, b in zip(a_list, b_list)
    )
    result = lax.psum_scatter(product.astype(jnp.bfloat16), "dp", scatter_dimension=1, tiled=True)
    return result[: cut * r], result[cut * r :]


def line_gather(me, size, own, block, local_sem, sems):
    send_left, recv_left, send_right, recv_right = sems
    has_left, has_right = me > 0, me < size - 1

    def remote(source, owner, send, recv, step, to):
        return pltpu.make_async_remote_copy(
            src_ref=source, dst_ref=block(owner), send_sem=send.at[step], recv_sem=recv.at[step],
            device_id={"tensor": to}, device_id_type=MESH,
        )

    def to_left(step):
        return remote(own if step == 0 else block(me + step), me + step, send_left, recv_left, step, me - 1)

    def to_right(step):
        return remote(own if step == 0 else block(me - step), me - step, send_right, recv_right, step, me + 1)

    def advance(step):
        if step == 0:
            pltpu.make_async_copy(own, block(me), local_sem).start()
        else:
            @pl.when(me + step < size)
            def _():
                remote(own, me + step, send_left, recv_left, step - 1, me + 1).wait_recv()

        @pl.when(has_left & (me + step < size))
        def _():
            to_left(step).start()

        if step > 0:
            @pl.when(me - step >= 0)
            def _():
                remote(own, me - step, send_right, recv_right, step - 1, me - 1).wait_recv()

        @pl.when(has_right & (me - step >= 0))
        def _():
            to_right(step).start()

    def finish():
        for step in range(size):
            @pl.when(has_left & (me + step < size))
            def _():
                to_left(step).wait_send()

            @pl.when(has_right & (me - step >= 0))
            def _():
                to_right(step).wait_send()

        pltpu.make_async_copy(own, block(me), local_sem).wait()

    return advance, finish


def line_barrier(me, size):
    barrier = pltpu.get_barrier_semaphore()
    has_left, has_right = me > 0, me < size - 1

    @pl.when(has_left)
    def _():
        pl.semaphore_signal(barrier, inc=1, device_id={"tensor": me - 1}, device_id_type=MESH)

    @pl.when(has_right)
    def _():
        pl.semaphore_signal(barrier, inc=1, device_id={"tensor": me + 1}, device_id_type=MESH)

    pl.semaphore_wait(barrier, has_left.astype(jnp.int32) + has_right.astype(jnp.int32))


def branch_body(
    length_ref, part_ref, tokens_ref, gain_ref, cot_ref, hidden_ref, second_ref, xa_ref, da_ref,
    from_left, from_right, normed, local_sem, send_r, recv_r, send_l, recv_l, *sems,
):
    me = lax.axis_index("tensor")
    size = lax.axis_size("tensor")
    rows = tokens_ref.shape[0]
    half, quarter = rows // 2, rows // 4
    bf, f32 = jnp.bfloat16, jnp.float32
    has_left, has_right = me > 0, me < size - 1
    line_barrier(me, size)

    def gathered(owner, h):
        return da_ref.at[pl.ds(pl.multiple_of(owner * half + h * quarter, quarter), quarter)]

    def own_cot(h):
        return cot_ref.at[pl.ds(h * quarter, quarter)]

    def part(ref, owner, which):
        return ref.at[owner, pl.ds(pl.multiple_of(which * quarter, quarter), quarter)]

    def direction(right):
        slots, send, recv = (from_left, send_r, recv_r) if right else (from_right, send_l, recv_l)
        to = me + 1 if right else me - 1
        before = me if right else size - 1 - me
        has_to = has_right if right else has_left
        has_from = has_left if right else has_right

        def copy(source, target, t):
            return pltpu.make_async_remote_copy(
                src_ref=source, dst_ref=target, send_sem=send.at[t], recv_sem=recv.at[t],
                device_id={"tensor": to}, device_id_type=MESH,
            )

        def sends(s):
            return has_to & (s - before - 1 < 2 * (size - 1 - before))

        def step(t):
            s, h = t // 2, t % 2
            if t >= 2:
                @pl.when(sends(s - 1))
                def _():
                    copy(part(part_ref, 0, 0), part(slots, 0, 0), t - 2).wait_send()

            if s < size:
                @pl.when(s <= before)
                def _():
                    owner = me - s if right else me + s
                    if s > 0:
                        copy(own_cot(h), gathered(owner, h), t - 2).wait_recv()

                    @pl.when(has_to)
                    def _():
                        copy(own_cot(h) if s == 0 else gathered(owner, h), gathered(owner, h), t).start()

            @pl.when((s > before) & sends(s))
            def _():
                r = s - before - 1
                owner = size - 1 - r // 2 if right else r // 2
                which = 2 * (r % 2) + h

                @pl.when(has_from)
                def _():
                    both = part(slots, owner, which)
                    copy(part(part_ref, owner, which), both, t - 2).wait_recv()
                    both[...] = (both[...].astype(f32) + part(part_ref, owner, which)[...].astype(f32)).astype(bf)
                    copy(both, both, t).start()

                @pl.when(jnp.logical_not(has_from))
                def _():
                    copy(part(part_ref, owner, which), part(slots, owner, which), t).start()

        def last():
            @pl.when(has_from)
            def _():
                for which in range(4):
                    t = 2 * (before + 2 * (size - 1 - before)) + which
                    copy(part(part_ref, me, which), part(slots, me, which), t).wait_recv()
                hidden_ref[...] += slots[me].astype(f32)

        return step, last

    local = [pltpu.make_async_copy(own_cot(h), gathered(me, h), local_sem.at[h]) for h in range(2)]
    for copy in local:
        copy.start()
    step_r, last_r = direction(True)
    step_l, last_l = direction(False)
    for t in range(2 * (2 * size - 1) + 2):
        step_r(t)
        step_l(t)
    hidden_ref[...] = part_ref[me].astype(f32)
    last_r()
    last_l()
    row = lax.broadcasted_iota(jnp.int32, (rows, 1), 0) + me * rows
    live = jnp.where(row < length_ref[0], 1.0, 0.0)
    hidden = tokens_ref[...].astype(f32) + live * hidden_ref[...]
    hidden_ref[...] = hidden
    inverse = lax.rsqrt(jnp.mean(hidden * hidden, axis=1, keepdims=True) + epsilon)
    normed[...] = (hidden * inverse * gain_ref[...].astype(f32)).astype(bf)
    step_x, finish_x = line_gather(
        me, size, normed.at[:half], lambda owner: xa_ref.at[pl.ds(pl.multiple_of(owner * half, half), half)],
        local_sem.at[2], sems,
    )
    for j in range(size):
        step_x(j)
    second_ref[...] = normed[half:, :]
    for copy in local:
        copy.wait()
    finish_x()


def finish_branch(lengths, part, tokens, gain, cot, cid):
    size = lax.axis_size("tensor")
    rows, width = tokens.shape
    half = rows // 2
    bf, f32 = jnp.bfloat16, jnp.float32
    vmem = pl.BlockSpec(memory_space=pltpu.VMEM)
    anywhere = pl.BlockSpec(memory_space=pl.ANY)
    dma = pltpu.SemaphoreType.DMA
    gathered = jax.ShapeDtypeStruct((size * half, width), bf)
    return pl.pallas_call(
        branch_body,
        in_specs=[pl.BlockSpec(memory_space=pltpu.SMEM), vmem, vmem, vmem, anywhere],
        out_specs=[vmem, vmem, anywhere, anywhere],
        out_shape=[
            jax.ShapeDtypeStruct((rows, width), f32), jax.ShapeDtypeStruct((half, width), bf), gathered, gathered,
        ],
        scratch_shapes=[
            pltpu.VMEM((size, rows, width), bf), pltpu.VMEM((size, rows, width), bf), pltpu.VMEM((rows, width), bf),
            dma((3,)), *[dma((4 * size,))] * 4, *[dma((size,))] * 4,
        ],
        compiler_params=pltpu.CompilerParams(vmem_limit_bytes=48 * MIB, collective_id=cid, has_side_effects=True),
        cost_estimate=pl.CostEstimate(flops=0, bytes_accessed=24 * rows * size * width, transcendentals=0),
        name="finish_branch",
    )(lengths, part.reshape(size, rows, width), tokens, gain[None], cot)


def small_sum_phases(local_rows, part_ref, out_ref, scratch):
    staged, landed, from_dp, mine, from_tensor, send_dp, recv_dp, send_t, recv_t, send_out, recv_out = scratch
    size_dp, size_t = lax.axis_size("dp"), lax.axis_size("tensor")
    me_dp, me_t = lax.axis_index("dp"), lax.axis_index("tensor")
    width = mine.shape[1]

    def piece(ref, owner):
        return ref.at[:, pl.ds(pl.multiple_of(owner * width, width), width)]

    def greet():
        barrier = pltpu.get_barrier_semaphore()
        for step in range(1, size_dp):
            peer = lax.rem(me_dp + step, size_dp)
            pl.semaphore_signal(barrier, inc=1, device_id={"dp": peer}, device_id_type=MESH)
        for step in range(1, size_t):
            peer = lax.rem(me_t + step, size_t)
            pl.semaphore_signal(barrier, inc=1, device_id={"tensor": peer}, device_id_type=MESH)
        pl.semaphore_wait(barrier, size_dp + size_t - 2)

    def copy(source, target, axis, step, send_sem, recv_sem):
        me, size = (me_dp, size_dp) if axis == "dp" else (me_t, size_t)
        return pltpu.make_async_remote_copy(
            src_ref=source, dst_ref=target, send_sem=send_sem.at[step], recv_sem=recv_sem.at[step],
            device_id={axis: lax.rem(me + step, size)}, device_id_type=MESH,
        )

    def to_owner(step):
        return copy(piece(staged, lax.rem(me_dp + step, size_dp)), from_dp.at[step], "dp", step, send_dp, recv_dp)

    def to_tensor(step):
        return copy(mine, from_tensor.at[step], "tensor", step, send_t, recv_t)

    def to_all(step):
        here = piece(landed, me_dp)
        return copy(here, here, "dp", step, send_out, recv_out)

    def first():
        staged[...] = part_ref[...]
        for step in range(1, size_dp):
            to_owner(step).start()

    def second():
        total = piece(staged, me_dp)[...]
        for step in range(1, size_dp):
            to_owner(step).wait_recv()
            total = total + from_dp[step]
        mine[...] = total
        for step in range(1, size_t):
            to_tensor(step).start()

    def third():
        total = mine[...]
        for step in range(1, size_t):
            to_tensor(step).wait_recv()
            total = total + from_tensor[step]
        piece(landed, me_dp)[...] = total
        piece(landed.at[local_rows:], me_dp)[...] = mine[local_rows:, :]
        for step in range(1, size_dp):
            to_all(step).start()

    def last():
        for step in range(1, size_dp):
            to_all(step).wait_recv()
        out_ref[...] = landed[...]
        for step in range(1, size_dp):
            to_owner(step).wait_send()
            to_all(step).wait_send()
        for step in range(1, size_t):
            to_tensor(step).wait_send()

    return greet, first, second, third, last


def small_sum_scratch(shape):
    size_dp, size_t = lax.axis_size("dp"), lax.axis_size("tensor")
    rows, width = shape[0], shape[1] // size_dp
    dma = pltpu.SemaphoreType.DMA
    f32 = jnp.float32
    return [
        pltpu.VMEM(shape, f32), pltpu.VMEM(shape, f32),
        pltpu.VMEM((size_dp, rows, width), f32), pltpu.VMEM((rows, width), f32), pltpu.VMEM((size_t, rows, width), f32),
        dma((size_dp,)), dma((size_dp,)), dma((size_t,)), dma((size_t,)), dma((size_dp,)), dma((size_dp,)),
    ]


def sums_body(local_rows, part_ref, out_ref, *scratch):
    for phase in small_sum_phases(local_rows, part_ref, out_ref, scratch):
        phase()


def small_sums(part, local_rows, cid):
    vmem = pl.BlockSpec(memory_space=pltpu.VMEM)
    return pl.pallas_call(
        functools.partial(sums_body, local_rows),
        in_specs=[vmem],
        out_specs=vmem,
        out_shape=jax.ShapeDtypeStruct(part.shape, jnp.float32),
        scratch_shapes=small_sum_scratch(part.shape),
        compiler_params=pltpu.CompilerParams(collective_id=cid, has_side_effects=True),
        name="small_sums",
    )(part)


def attention_grads_body(nc, cut, local_rows, a_ref, a2_ref, b_ref, b2_ref, part_ref, o_ref, o2_ref, sums_ref, *scratch):
    i = pl.program_id(0)
    greet, *phases = small_sum_phases(local_rows, part_ref, sums_ref, scratch[:11])
    steps = nc + LA + LB + LC

    def store(c, rows, result):
        @pl.when(c < cut)
        def _():
            o_ref[rows, :] = result.astype(o_ref.dtype)

        @pl.when(c >= cut)
        def _():
            o2_ref[rows, :] = result.astype(o2_ref.dtype)

    send = scatter_steps(i, nc, (LA, LB, LC), o_ref.shape[1], scratch[11:], store, greet)
    for when, phase in zip((0, 4, 8, steps - 1), phases):
        pl.when(i == when)(phase)

    @pl.when(i < cut)
    def _():
        send(lambda cols: jnp.dot(a_ref[...], b_ref[:, cols], preferred_element_type=jnp.float32))

    @pl.when((i >= cut) & (i < nc))
    def _():
        send(lambda cols: jnp.dot(a2_ref[...], b2_ref[:, cols], preferred_element_type=jnp.float32))


def attention_grads(a, b, a2, b2, part, local_rows, r, cid):
    T, D = b.shape
    w = D // 8
    cut, rest = a.shape[0] // r, a2.shape[0] // r
    nc = cut + rest
    lag = LA + LB + LC
    out_specs, out_shape = scatter_outs(nc, cut, lag, r, w)

    def whole(shape):
        return pl.BlockSpec(shape, lambda i: (0, 0), pipeline_mode=pl.Buffered(1))

    return pl.pallas_call(
        functools.partial(attention_grads_body, nc, cut, local_rows),
        grid=(nc + lag,),
        in_specs=[
            pl.BlockSpec((r, T), lambda i: (jnp.minimum(i, cut - 1), 0)),
            pl.BlockSpec((r, T), lambda i: (jnp.clip(i - cut, 0, rest - 1), 0)),
            whole((T, D)), whole((T, D)), whole(part.shape),
        ],
        out_specs=[*out_specs, whole(part.shape)],
        out_shape=[*out_shape, jax.ShapeDtypeStruct(part.shape, jnp.float32)],
        scratch_shapes=[*small_sum_scratch(part.shape), *scatter_scratch(r, w)],
        compiler_params=pltpu.CompilerParams(vmem_limit_bytes=48 * MIB, collective_id=cid, has_side_effects=True),
        cost_estimate=pl.CostEstimate(flops=2 * nc * r * T * D, bytes_accessed=2 * nc * r * T + 4 * T * D, transcendentals=0),
        name="attention_grads",
    )(a, a2, b, b2, part)


def on_device(
    tokens,
    lengths,
    routes,
    cotangent,
    norm_one,
    qkv_weight,
    qkv_bias,
    out_weight,
    norm_two,
    router_weight,
    expert_in,
    expert_out,
    shared_in,
    shared_out,
    shared_gate,
):
    own_rows = tokens.shape[0]
    slot_count = routes.shape[0]
    model_width = tokens.shape[1]
    qkv_cols = qkv_weight.shape[2]
    local_heads = qkv_cols // HEAD_DIM
    experts = router_weight.shape[1]
    eff = expert_in.shape[3]
    shared_chunks = shared_out.shape[0] // eff
    chunks = experts + shared_chunks
    bf = jnp.bfloat16
    qkv_cols = qkv_weight.shape[2]
    length = lengths[0]
    tensor_index = lax.axis_index("tensor")
    first_row = tensor_index * own_rows
    live_own = (first_row + jnp.arange(own_rows) < length).astype(jnp.float32)[:, None]
    tokens_f = tokens.astype(jnp.float32)
    gain_one = norm_one.astype(jnp.float32)
    gain_two = norm_two.astype(jnp.float32)
    inv_one = lax.rsqrt(jnp.mean(tokens_f * tokens_f, axis=-1, keepdims=True) + epsilon)
    unit_one = tokens_f * inv_one
    normed_one = lax.all_gather((unit_one * gain_one).astype(bf), "tensor", axis=0, tiled=True)
    cos_table, sin_table = rotary_tables(slot_count, HEAD_DIM)
    qkv_w = qkv_weight.transpose(1, 0, 2)
    ei = expert_in.transpose(0, 2, 3, 1).reshape(experts, 2 * eff, model_width)
    eo = expert_out
    si = (
        shared_in.reshape(model_width, 2, shared_chunks, eff)
        .transpose(2, 1, 3, 0)
        .reshape(shared_chunks, 2 * eff, model_width)
    )
    so = shared_out.reshape(shared_chunks, eff, model_width)
    router_rows = jnp.concatenate(
        [
            router_weight.T,
            shared_gate[None],
            jnp.zeros((-(experts + 1) % 16, model_width), bf),
        ],
        axis=0,
    )
    grad_out = cotangent.astype(jnp.float32) * live_own
    d_two_own = (live_own * grad_out).astype(bf)
    normed_one, si, router_rows, cos_table, sin_table, d_two_own = lax.optimization_barrier(
        (normed_one, si, router_rows, cos_table, sin_table, d_two_own)
    )
    qkv = project_qkv(normed_one, qkv_w, qkv_bias[:, None, :], cos_table, sin_table)
    mixed, mixed_t = attend(lengths, qkv)
    branch_partial = jnp.dot(mixed, out_weight, preferred_element_type=jnp.float32).astype(bf)
    size_t = lax.axis_size("tensor")
    half = own_rows // 2
    hidden, second, x_a, d_a = finish_branch(
        lengths, branch_partial, tokens, norm_two, d_two_own, 1
    )
    inv_two = lax.rsqrt(jnp.mean(hidden * hidden, axis=-1, keepdims=True) + epsilon)
    unit_two = hidden * inv_two
    routes_a, routes_b = (
        routes.reshape(size_t, 2, half, -1).transpose(1, 0, 2, 3).reshape(2, size_t * half, -1)
    )
    weights = (router_rows, ei, si, eo, so)
    dgu_a, dn_a, bt_a, router_a, np_a, s_a, x_b, d_b = ffn(
        x_a, d_a, routes_a.T, *weights, own=[second, d_two_own[half:]]
    )
    grad_a = lax.psum_scatter(dn_a, "tensor", scatter_dimension=0, tiled=True)
    two_a = lax.psum_scatter(bt_a, "tensor", scatter_dimension=0, tiled=True)
    if lax.axis_size("dp") == 8:
        dgu_b, dn_b, bt_b, router_b, np_b, out_grads, shared_out_grad = ffn(
            x_b, d_b, routes_b.T, *weights, other=(s_a, d_a)
        )
    else:
        dgu_b, dn_b, bt_b, router_b, np_b, s_b = ffn(x_b, d_b, routes_b.T, *weights)
        inner = [s.reshape(chunks * eff, -1) for s in (s_a, s_b)]
        out_grads, shared_out_grad = weight_grad_scatter(
            inner, [d_a, d_b], eff, 2, "down_grads", cut=experts
        )
    router_part = router_a + router_b
    norm_two_part = np_a + np_b
    d_gate_up = [d.reshape(chunks * 2 * eff, -1) for d in (dgu_a, dgu_b)]
    grad_a, two_a, dn_b = lax.optimization_barrier((grad_a, two_a, dn_b))
    grad_b = lax.psum_scatter(dn_b, "tensor", scatter_dimension=0, tiled=True)
    two_b = lax.psum_scatter(bt_b, "tensor", scatter_dimension=0, tiled=True)
    in_grads_b, _ = weight_grad_scatter(
        d_gate_up, [x_a, x_b], eff, 4, "shared_in_grads", 2 * experts, 2 * shared_chunks
    )
    grad_two = jnp.concatenate([grad_a, grad_b], axis=0).astype(jnp.float32)
    grad_hidden = grad_out + norm_back(grad_two, unit_two, inv_two, gain_two)
    d_one_own, in_grads_b = lax.optimization_barrier(
        ((live_own * grad_hidden).astype(bf), in_grads_b)
    )
    d_one = lax.all_gather(d_one_own, "tensor", axis=0, tiled=True)
    d_gate_up, _ = lax.optimization_barrier((d_gate_up, d_one_own))
    in_grads_a, _ = weight_grad_scatter(
        d_gate_up, [x_a, x_b], eff, 3, "expert_in_grads", 0, 2 * experts
    )
    d_one, in_grads_a = lax.optimization_barrier((d_one, in_grads_a))
    d_mixed = lax.dot_general(d_one, out_weight, NT, preferred_element_type=jnp.float32).astype(bf)
    d_qkv, d_qkv_t, bias_part = attend_back(lengths, qkv, d_mixed, cos_table, sin_table)
    grad_one, norm_one_part = qkv_back(d_qkv, qkv_w, normed_one)
    grad_one, d_qkv_t, mixed_t, two_b = lax.optimization_barrier(
        (grad_one, d_qkv_t, mixed_t, two_b)
    )
    grad_one_own = lax.psum_scatter(grad_one, "tensor", scatter_dimension=0, tiled=True)
    part = jnp.concatenate(
        [
            router_part[: experts + 1],
            norm_one_part / gain_one[None],
            norm_two_part / gain_two[None],
            jnp.pad(bias_part.reshape(1, 3 * qkv_cols), ((0, 0), (0, model_width - 3 * qkv_cols))),
        ],
        axis=0,
    )
    d_qkv_t = d_qkv_t.reshape(3 * qkv_cols, slot_count)
    if lax.axis_size("dp") == 8:
        qkv_sum, out_sum, sums = attention_grads(
            d_qkv_t, normed_one, mixed_t, d_one, part, experts + 3, qkv_cols // 2, 5
        )
    else:
        sums = small_sums(part, experts + 3, 7)
        qkv_sum, _ = weight_grad_scatter([d_qkv_t], [normed_one], qkv_cols, 5, "qkv_grads")
        out_sum, _ = weight_grad_scatter([mixed_t], [d_one], qkv_cols, 6, "mix_grads")
    branch_two = jnp.concatenate([two_a, two_b], axis=0).astype(jnp.float32)
    output = (hidden + live_own * branch_two).astype(bf)
    grad_one = grad_one_own.astype(jnp.float32)
    input_grad = grad_hidden + norm_back(grad_one, unit_one, inv_one, gain_one)
    qkv_bias_grad = sums[experts + 3, : 3 * qkv_cols].reshape(3, qkv_cols)
    own_cols = out_grads.shape[1]
    expert_in_grad = in_grads_a.astype(jnp.float32).reshape(experts, 2, eff, own_cols).transpose(0, 3, 1, 2)
    shared_in_grad = (
        in_grads_b.reshape(shared_chunks, 2, eff, own_cols)
        .transpose(3, 1, 0, 2)
        .reshape(own_cols, 2, shared_chunks * eff)
        .astype(jnp.float32)
    )
    return (
        output,
        input_grad,
        sums[experts + 1],
        qkv_sum.astype(jnp.float32).reshape(3, qkv_cols, own_cols).transpose(2, 0, 1),
        qkv_bias_grad,
        out_sum.astype(jnp.float32),
        sums[experts + 2],
        sums[:experts].T,
        expert_in_grad,
        out_grads.astype(jnp.float32).reshape(experts, eff, own_cols),
        shared_in_grad,
        shared_out_grad.astype(jnp.float32),
        sums[experts],
    )


def solution(mesh):
    in_specs = (
        P(("dp", "tensor"), None),
        P("dp"),
        P("dp", None),
        P(("dp", "tensor"), None),
        P(),
        P(None, None, "tensor"),
        P(None, "tensor"),
        P("tensor", None),
        P(),
        P(),
        P(None, None, None, "tensor"),
        P(None, "tensor", None),
        P(None, None, "tensor"),
        P("tensor", None),
        P(),
    )
    out_specs = (
        P(("dp", "tensor"), None),
        P(("dp", "tensor"), None),
        P(),
        P("dp", None, "tensor"),
        P(None, "tensor"),
        P("tensor", "dp"),
        P(),
        P(),
        P(None, "dp", None, "tensor"),
        P(None, "tensor", "dp"),
        P("dp", None, "tensor"),
        P("tensor", "dp"),
        P(),
    )
    return jax.shard_map(
        on_device, mesh=mesh, in_specs=in_specs, out_specs=out_specs, check_vma=False
    )
```

```python
import functools

import jax
import jax.numpy as jnp
from jax import lax
from jax.experimental import pallas as pl
from jax.experimental.pallas import tpu as pltpu
from jax.sharding import PartitionSpec as P

HEAD_DIM = 128
MESH = pl.DeviceIdType.MESH
LA, LB, LC = 1, 2, 2
FFN_LAGS = (1, 1, 1)
MIB = 2**20
ATTEND_HEADS = 1


epsilon = 1e-06
theta_base = 1000000.0
NT = (((1,), (1,)), ((), ()))
TN = (((0,), (0,)), ((), ()))


def rotary_tables(row_count, head_width):
    half_index = jnp.arange(head_width // 2).astype(jnp.float32)
    frequency = theta_base ** (-2.0 * half_index / head_width)
    angles = jnp.arange(row_count).astype(jnp.float32)[:, None] * frequency[None, :]
    sines = jnp.sin(angles)
    cosines = jnp.cos(angles)
    return (
        jnp.concatenate([cosines, cosines], axis=-1),
        jnp.concatenate([-sines, sines], axis=-1),
    )


def norm_back(d_normed, unit_rows, inverse, gain_vector):
    d_unit = d_normed * gain_vector
    return inverse * (d_unit - unit_rows * jnp.mean(d_unit * unit_rows, axis=-1, keepdims=True))


def scatter_scratch(r, w):
    f32, bf = jnp.float32, jnp.bfloat16
    dma = pltpu.SemaphoreType.DMA
    h = r // 2
    return [
        pltpu.VMEM((2, 4, r, w), f32), pltpu.VMEM((2, 4, r, w), bf), pltpu.VMEM((3, 4, r, w), bf),
        pltpu.VMEM((3, 2, 2, h, w), f32), pltpu.VMEM((3, 2, 2, h, w), bf), pltpu.VMEM((6, 2, 2, h, w), bf),
        pltpu.VMEM((3, 2, h, w), f32), pltpu.VMEM((2, 2, h, w), bf), pltpu.VMEM((6, 2, h, w), bf),
        dma((2,)), dma((3,)), dma((3, 2)), dma((6, 2)), dma((2, 2)), dma((6, 2)),
    ]


def scatter_steps(i, nc, lags, w, scratch, store, greet=None):
    own, sa, ra, kt, s1, r1, ku, s2, r2, sem_sa, sem_ra, sem_s1, sem_r1, sem_s2, sem_r2 = scratch
    la, lb, lc = lags
    keep_1 = min(3, lb + lc)
    hr = own.shape[2] // 2
    dp = lax.axis_index("dp")
    k = dp % 2
    x = (dp // 2) % 2
    y = dp // 4
    core_peer = y * 4 + x * 2 + (1 - k)
    x_peer = y * 4 + (1 - x) * 2 + k
    y_peer = (1 - y) * 4 + x * 2 + k

    def copy_a(c):
        return pltpu.make_async_remote_copy(
            src_ref=sa.at[c % 2], dst_ref=ra.at[c % 3], send_sem=sem_sa.at[c % 2], recv_sem=sem_ra.at[c % 3],
            device_id={"dp": core_peer}, device_id_type=MESH,
        )

    def copy_1(c, half):
        return pltpu.make_async_remote_copy(
            src_ref=s1.at[c % 3, half], dst_ref=r1.at[c % 6, half], send_sem=sem_s1.at[c % 3, half],
            recv_sem=sem_r1.at[c % 6, half], device_id={"dp": y_peer if half else x_peer}, device_id_type=MESH,
        )

    def copy_2(c, half):
        return pltpu.make_async_remote_copy(
            src_ref=s2.at[c % 2, half], dst_ref=r2.at[c % 6, half], send_sem=sem_s2.at[c % 2, half],
            recv_sem=sem_r2.at[c % 6, half], device_id={"dp": x_peer if half else y_peer}, device_id_type=MESH,
        )

    @pl.when(i == 0)
    def _():
        if greet is not None:
            greet()
            return
        barrier = pltpu.get_barrier_semaphore()
        for peer in (core_peer, x_peer, y_peer):
            pl.semaphore_signal(barrier, inc=1, device_id={"dp": peer}, device_id_type=MESH)
        pl.semaphore_wait(barrier, 3)

    @pl.when((i >= la + keep_1) & (i < nc + la + keep_1))
    def _():
        copy_1(i - la - keep_1, 0).wait_send()
        copy_1(i - la - keep_1, 1).wait_send()

    @pl.when((i >= la) & (i < nc + la))
    def _():
        c = i - la
        copy_a(c).wait_recv()
        for half in range(2):
            rows = slice(half * hr, half * hr + hr)
            keep, other = (1, 2) if half else (2, 1)

            def total(role):
                return own[c % 2, role, rows, :] + ra[c % 3, role, rows, :].astype(jnp.float32)

            s1[c % 3, half, 0] = total(other).astype(jnp.bfloat16)
            s1[c % 3, half, 1] = total(3).astype(jnp.bfloat16)
            copy_1(c, half).start()
            kt[c % 3, half, 0] = total(0)
            kt[c % 3, half, 1] = total(keep)

    @pl.when((i >= la + lb) & (i < nc + la + lb))
    def _():
        c = i - la - lb

        @pl.when(c >= 2)
        def _():
            copy_2(c - 2, 0).wait_send()
            copy_2(c - 2, 1).wait_send()

        for half in range(2):
            copy_1(c, half).wait_recv()
            s2[c % 2, half] = (kt[c % 3, half, 1] + r1[c % 6, half, 1].astype(jnp.float32)).astype(jnp.bfloat16)
            copy_2(c, half).start()
            ku[c % 3, half] = kt[c % 3, half, 0] + r1[c % 6, half, 0].astype(jnp.float32)

    @pl.when(i >= la + lb + lc)
    def _():
        c = i - la - lb - lc
        for half in range(2):
            copy_2(c, half).wait_recv()
            store(c, slice(half * hr, half * hr + hr), ku[c % 3, half] + r2[c % 6, half].astype(jnp.float32))

        @pl.when(c >= nc - 2)
        def _():
            copy_2(c, 0).wait_send()
            copy_2(c, 1).wait_send()

    @pl.when((i >= 2) & (i < nc + 2))
    def _():
        copy_a(i - 2).wait_send()

    def send(product):
        targets = (y * 4 + x * 2, y * 4 + (1 - x) * 2, (1 - y) * 4 + x * 2, (1 - y) * 4 + (1 - x) * 2)

        def cols(role, core):
            return pl.ds(pl.multiple_of((targets[role] + core) * w, w), w)

        for role in range(4):
            sa[i % 2, role] = product(cols(role, 1 - k)).astype(jnp.bfloat16)
        copy_a(i).start()
        for role in range(4):
            own[i % 2, role] = product(cols(role, k))

    return send


def rs_body(nc, cut, pairs, *refs):
    a_refs, b_refs = refs[:pairs], refs[pairs : 2 * pairs]
    o_ref, o2_ref = refs[2 * pairs : 2 * pairs + 2]
    i = pl.program_id(0)

    def store(c, rows, result):
        @pl.when(c < cut)
        def _():
            o_ref[rows, :] = result.astype(o_ref.dtype)

        @pl.when(c >= cut)
        def _():
            o2_ref[rows, :] = result.astype(o2_ref.dtype)

    send = scatter_steps(i, nc, (LA, LB, LC), o_ref.shape[1], refs[2 * pairs + 2 :], store)

    @pl.when(i < nc)
    def _():
        def product(cols):
            total = jnp.dot(a_refs[0][...], b_refs[0][:, cols], preferred_element_type=jnp.float32)
            for a_ref, b_ref in zip(a_refs[1:], b_refs[1:]):
                total += jnp.dot(a_ref[...], b_ref[:, cols], preferred_element_type=jnp.float32)
            return total

        send(product)


def scatter_outs(nc, cut, lag, r, w):
    rest = max(nc - cut, 1)
    specs = [
        pl.BlockSpec((r, w), lambda i: (jnp.clip(i - lag, 0, cut - 1), 0)),
        pl.BlockSpec((r, w), lambda i: (jnp.clip(i - lag - cut, 0, rest - 1), 0)),
    ]
    return specs, [jax.ShapeDtypeStruct((n * r, w), jnp.bfloat16) for n in (cut, rest)]


def weight_grad_scatter_kernel(a_list, b_list, r, cid, name, first, count, cut):
    D = b_list[0].shape[1]
    T = sum(b.shape[0] for b in b_list)
    w = D // 8
    lag = LA + LB + LC
    out_specs, out_shape = scatter_outs(count, cut, lag, r, w)
    return pl.pallas_call(
        functools.partial(rs_body, count, cut, len(a_list)),
        grid=(count + lag,),
        in_specs=[
            *[pl.BlockSpec((r, a.shape[1]), lambda i: (jnp.minimum(i, count - 1) + first, 0)) for a in a_list],
            *[pl.BlockSpec(b.shape, lambda i: (0, 0), pipeline_mode=pl.Buffered(1)) for b in b_list],
        ],
        out_specs=out_specs,
        out_shape=out_shape,
        scratch_shapes=scatter_scratch(r, w),
        compiler_params=pltpu.CompilerParams(vmem_limit_bytes=48 * MIB, collective_id=cid, has_side_effects=True),
        cost_estimate=pl.CostEstimate(
            flops=2 * count * r * T * D, bytes_accessed=2 * count * r * T + 2 * T * D + 4 * count * r * w, transcendentals=0
        ),
        name=name,
    )(*a_list, *b_list)


def ffn_body(
    experts, chunks, scatter, gather,
    x_ref, d_ref, routes_ref, rw_ref, ei_ref, si_ref, eo_ref, so_ref, *refs,
):
    if scatter:
        s_other_ref, d_other_ref, dgu_ref, dn_ref, bt_ref, rg_ref, np_ref, og_ref, og2_ref, *refs = refs
    else:
        if gather:
            own_x_ref, own_d_ref, *refs = refs
        dgu_ref, dn_ref, bt_ref, rg_ref, np_ref, s_ref, *refs = refs
        if gather:
            all_x_ref, all_d_ref, *refs = refs
    dn_acc, bt_acc, probs_ref, w_ref, ds_ref, wi_buf, wd_buf, sem, *scratch = refs
    c = pl.program_id(0)
    h = eo_ref.shape[1]
    slots, width = x_ref.shape
    if gather:
        me, size = lax.axis_index("tensor"), lax.axis_size("tensor")
        local_sem, *sems = scratch
        lines = []
        for number, (own, out) in enumerate(((own_x_ref, all_x_ref), (own_d_ref, all_d_ref))):
            def block(owner, out=out, rows=own.shape[0]):
                return out.at[pl.ds(pl.multiple_of(owner * rows, rows), rows)]

            lines.append(
                line_gather(me, size, own, block, local_sem.at[number], sems[4 * number : 4 * number + 4])
            )
        for hop in range(size - 1):
            @pl.when(c == -(-hop * (chunks - 1) // (size - 1)))
            def _():
                if hop == 0:
                    line_barrier(me, size)
                for advance, _ in lines:
                    advance(hop)

    def fetch(step):
        slot = step % 2

        @pl.when(step < experts)
        def _():
            pltpu.make_async_copy(ei_ref.at[step], wi_buf.at[slot], sem.at[0, slot]).start()
            pltpu.make_async_copy(eo_ref.at[step], wd_buf.at[slot], sem.at[1, slot]).start()

        @pl.when(step >= experts)
        def _():
            pltpu.make_async_copy(si_ref.at[step - experts], wi_buf.at[slot], sem.at[0, slot]).start()
            pltpu.make_async_copy(so_ref.at[step - experts], wd_buf.at[slot], sem.at[1, slot]).start()

    @pl.when(c == 0)
    def _():
        fetch(c)

    @pl.when(c + 1 < chunks)
    def _():
        fetch(c + 1)

    def picked():
        expert = lax.broadcasted_iota(jnp.int32, (experts, slots), 0)
        hit = jnp.zeros((experts, slots), jnp.float32)
        for j in range(routes_ref.shape[0]):
            hit = hit + jnp.where(routes_ref[j : j + 1, :] == expert, 1.0, 0.0)
        return hit

    @pl.when(c == 0)
    def _():
        logits = lax.dot_general(rw_ref[...], x_ref[...], NT, preferred_element_type=jnp.float32)
        raised = jnp.exp(logits[:experts] - jnp.max(logits[:experts], axis=0, keepdims=True))
        probs = raised / jnp.sum(raised, axis=0, keepdims=True)
        gate = 1.0 / (1.0 + jnp.exp(-logits[experts:]))
        probs_ref[...] = probs
        w_ref[:experts, :] = probs * picked()
        w_ref[experts:, :] = gate
        ds_ref[...] = jnp.zeros_like(ds_ref)
        dn_acc[...] = jnp.zeros_like(dn_acc)
        bt_acc[...] = jnp.zeros_like(bt_acc)

    if scatter:
        def store(chunk, rows, result):
            @pl.when(chunk < experts)
            def _():
                og_ref[rows, :] = result.astype(og_ref.dtype)

            @pl.when(chunk >= experts)
            def _():
                og2_ref[rows, :] = result.astype(og2_ref.dtype)

        send = scatter_steps(c, chunks, FFN_LAGS, og_ref.shape[1], scratch, store)

    block = 512

    @pl.when(c < chunks)
    def _():
        row = pl.ds(jnp.minimum(c, experts), 1)
        slot = c % 2
        pltpu.make_async_copy(ei_ref.at[0], wi_buf.at[slot], sem.at[0, slot]).wait()
        pltpu.make_async_copy(eo_ref.at[0], wd_buf.at[slot], sem.at[1, slot]).wait()
        wi = wi_buf.at[slot]
        wd = wd_buf.at[slot]
        x = x_ref[...]
        g = lax.dot_general(wi[:h], x, NT, preferred_element_type=jnp.float32)
        u = lax.dot_general(wi[h:], x, NT, preferred_element_type=jnp.float32)
        p = lax.dot_general(wd[...], d_ref[...], NT, preferred_element_type=jnp.float32)
        w = w_ref[row, :]
        sg = 1.0 / (1.0 + jnp.exp(-g))
        si = g * sg
        inner = (si * u).astype(jnp.bfloat16).astype(jnp.float32)
        s = (w * inner).astype(jnp.bfloat16)
        ds_ref[row, :] += jnp.sum(p * inner, axis=0, keepdims=True)
        di = w * p
        dg = (di * u * sg * (1.0 + g * (1.0 - sg))).astype(jnp.bfloat16)
        du = (di * si).astype(jnp.bfloat16)
        dgu_ref[0, :h] = dg
        dgu_ref[0, h:] = du
        dgu = jnp.concatenate([dg, du], axis=0)
        if scatter:
            def product(cols):
                return jnp.dot(s, d_ref[:, cols], preferred_element_type=jnp.float32) + jnp.dot(
                    s_other_ref[0], d_other_ref[:, cols], preferred_element_type=jnp.float32
                )

            send(product)
        else:
            s_ref[0] = s
        for n in range(0, width, block):
            cols = slice(n, n + block)
            dn_acc[:, cols] += lax.dot_general(dgu, wi[:, cols], TN, preferred_element_type=jnp.float32)
            bt_acc[:, cols] += lax.dot_general(s, wd[:, cols], TN, preferred_element_type=jnp.float32)

    @pl.when(c == (chunks if scatter else chunks - 1))
    def _():
        probs = probs_ref[...]
        d_probs = ds_ref[:experts, :] * picked()
        d_logits = probs * (d_probs - jnp.sum(probs * d_probs, axis=0, keepdims=True))
        gate = w_ref[experts:, :]
        d_gate = ds_ref[experts:, :] * gate * (1.0 - gate)
        small = jnp.concatenate([d_logits, d_gate], axis=0)
        high = small.astype(jnp.bfloat16)
        low = (small - high.astype(jnp.float32)).astype(jnp.bfloat16)
        rg_ref[...] = jnp.dot(high, x_ref[...], preferred_element_type=jnp.float32) + jnp.dot(
            low, x_ref[...], preferred_element_type=jnp.float32
        )
        for n in range(0, width, block):
            cols = slice(n, n + block)
            extra = lax.dot_general(high, rw_ref[:, cols], TN, preferred_element_type=jnp.float32)
            extra += lax.dot_general(low, rw_ref[:, cols], TN, preferred_element_type=jnp.float32)
            total = dn_acc[:, cols] + extra
            dn_ref[:, cols] = total.astype(dn_ref.dtype)
            np_ref[:, cols] = jnp.sum(total * x_ref[:, cols].astype(jnp.float32), axis=0, keepdims=True)
        bt_ref[...] = bt_acc[...].astype(bt_ref.dtype)
        if gather:
            for advance, finish in lines:
                advance(size - 1)
                finish()


def ffn(x, d_two, routes_t, router_rows, ei, si, eo, so, other=None, own=None):
    experts, h2, width = ei.shape
    chunks = experts + si.shape[0]
    h = h2 // 2
    slots = x.shape[0]
    rows = router_rows.shape[0]
    bf, f32 = jnp.bfloat16, jnp.float32
    anywhere = pl.BlockSpec(memory_space=pl.ANY)
    scatter = other is not None

    def whole(shape):
        return pl.BlockSpec(shape, lambda c: (0,) * len(shape), pipeline_mode=pl.Buffered(1))

    def chunk(shape):
        return pl.BlockSpec((1, *shape), lambda c: (jnp.minimum(c, chunks - 1), 0, 0))

    in_specs = [
        whole((slots, width)), whole((slots, width)), whole(routes_t.shape), whole((rows, width)),
        anywhere, anywhere, anywhere, anywhere,
    ]
    out_specs = [chunk((h2, slots)), whole((slots, width)), whole((slots, width)), whole((rows, width)), whole((1, width))]
    out_shape = [
        jax.ShapeDtypeStruct((chunks, h2, slots), bf), jax.ShapeDtypeStruct((slots, width), bf),
        jax.ShapeDtypeStruct((slots, width), bf), jax.ShapeDtypeStruct((rows, width), f32),
        jax.ShapeDtypeStruct((1, width), f32),
    ]
    scratch = [
        pltpu.VMEM((slots, width), f32), pltpu.VMEM((slots, width), f32),
        pltpu.VMEM((experts, slots), f32), pltpu.VMEM((rows, slots), f32), pltpu.VMEM((rows, slots), f32),
        pltpu.VMEM((2, h2, width), bf), pltpu.VMEM((2, h, width), bf), pltpu.SemaphoreType.DMA((2, 2)),
    ]
    args = [x, d_two, routes_t, router_rows, ei, si, eo, so]
    if scatter:
        s_other, d_other = other
        in_specs += [chunk((h, s_other.shape[2])), whole(d_other.shape)]
        args += [s_other, d_other]
        w = width // 8
        lag = sum(FFN_LAGS)
        specs, shapes = scatter_outs(chunks, experts, lag, h, w)
        out_specs += specs
        out_shape += shapes
        scratch += scatter_scratch(h, w)
        grid = (chunks + lag,)
        params = pltpu.CompilerParams(vmem_limit_bytes=62 * MIB, collective_id=2, has_side_effects=True)
    else:
        out_specs.append(chunk((h, slots)))
        out_shape.append(jax.ShapeDtypeStruct((chunks, h, slots), bf))
        grid = (chunks,)
        params = pltpu.CompilerParams(vmem_limit_bytes=62 * MIB)
        if own is not None:
            size = lax.axis_size("tensor")
            dma = pltpu.SemaphoreType.DMA
            in_specs += [anywhere, anywhere]
            args += own
            out_specs += [anywhere, anywhere]
            out_shape += [jax.ShapeDtypeStruct((size * a.shape[0], width), bf) for a in own]
            scratch += [dma((2,)), *[dma((size,))] * 8]
            params = pltpu.CompilerParams(vmem_limit_bytes=62 * MIB, collective_id=8, has_side_effects=True)
    return pl.pallas_call(
        functools.partial(ffn_body, experts, chunks, scatter, own is not None),
        grid=grid,
        in_specs=in_specs,
        out_specs=out_specs,
        out_shape=out_shape,
        scratch_shapes=scratch,
        compiler_params=params,
        cost_estimate=pl.CostEstimate(
            flops=12 * chunks * h * slots * width, bytes_accessed=10 * chunks * h * width + 16 * slots * width,
            transcendentals=chunks * h * slots,
        ),
        name="ffn_scatter" if scatter else "ffn",
    )(*args)


def turn(v):
    half = v.shape[1] // 2
    return jnp.concatenate([v[:, half:], v[:, :half]], axis=1)


def qkv_body(x_ref, w_ref, bias_ref, cos_ref, sin_ref, out_ref):
    j = pl.program_id(0)
    cols = w_ref.shape[2]
    y = jnp.dot(x_ref[...], w_ref[0], preferred_element_type=jnp.float32)
    y = y + bias_ref[0].astype(jnp.float32)

    @pl.when(j < 2)
    def _():
        for head in range(cols // HEAD_DIM):
            place = slice(head * HEAD_DIM, (head + 1) * HEAD_DIM)
            v = y[:, place]
            out_ref[0, :, place] = (v * cos_ref[...] + turn(v) * sin_ref[...]).astype(out_ref.dtype)

    @pl.when(j == 2)
    def _():
        out_ref[0] = y.astype(out_ref.dtype)


def project_qkv(x, w, bias, cos_table, sin_table):
    slots, width = x.shape
    cols = w.shape[2]
    table = pl.BlockSpec((slots, HEAD_DIM), lambda j: (0, 0), pipeline_mode=pl.Buffered(1))
    return pl.pallas_call(
        qkv_body,
        grid=(3,),
        in_specs=[
            pl.BlockSpec((slots, width), lambda j: (0, 0), pipeline_mode=pl.Buffered(1)),
            pl.BlockSpec((1, width, cols), lambda j: (j, 0, 0)),
            pl.BlockSpec((1, 1, cols), lambda j: (j, 0, 0)),
            table, table,
        ],
        out_specs=pl.BlockSpec((1, slots, cols), lambda j: (j, 0, 0)),
        out_shape=jax.ShapeDtypeStruct((3, slots, cols), jnp.bfloat16),
        compiler_params=pltpu.CompilerParams(vmem_limit_bytes=48 * MIB),
        cost_estimate=pl.CostEstimate(
            flops=6 * slots * width * cols, bytes_accessed=2 * slots * width + 6 * width * cols, transcendentals=0
        ),
        name="project_qkv",
    )(x, w, bias, cos_table, sin_table)


def block_probs(length_ref, q, k, start):
    s = lax.dot_general(q, k, NT, preferred_element_type=jnp.float32) * (HEAD_DIM**-0.5)
    row = lax.broadcasted_iota(jnp.int32, s.shape, 0) + start
    col = lax.broadcasted_iota(jnp.int32, s.shape, 1)
    s = jnp.where((col <= row) & (col < length_ref[0]), s, -1000000000.0)
    e = jnp.exp(s - jnp.max(s, axis=1, keepdims=True))
    return e * (1.0 / jnp.sum(e, axis=1, keepdims=True))


def attend_body(rows, length_ref, q_ref, k_ref, v_ref, mixed_ref, mixed_t_ref):
    for start in range(0, q_ref.shape[1], rows):
        here, end = slice(start, start + rows), start + rows
        p = block_probs(length_ref, q_ref[0, here, :], k_ref[0, :end, :], start)
        mixed = jnp.dot(p.astype(jnp.bfloat16), v_ref[0, :end, :], preferred_element_type=jnp.float32)
        mixed_ref[here, :] = mixed.astype(mixed_ref.dtype)
        mixed_t_ref[:, here] = mixed.T.astype(mixed_ref.dtype)


def attend(lengths, qkv):
    _, slots, cols = qkv.shape
    rows = min(512, slots)

    def part(j):
        return pl.BlockSpec((1, slots, HEAD_DIM), lambda h: (j, 0, h))

    return pl.pallas_call(
        functools.partial(attend_body, rows),
        grid=(cols // HEAD_DIM,),
        in_specs=[pl.BlockSpec(memory_space=pltpu.SMEM), part(0), part(1), part(2)],
        out_specs=[
            pl.BlockSpec((slots, HEAD_DIM), lambda h: (0, h)), pl.BlockSpec((HEAD_DIM, slots), lambda h: (h, 0)),
        ],
        out_shape=[
            jax.ShapeDtypeStruct((slots, cols), jnp.bfloat16), jax.ShapeDtypeStruct((cols, slots), jnp.bfloat16),
        ],
        compiler_params=pltpu.CompilerParams(vmem_limit_bytes=32 * MIB),
        cost_estimate=pl.CostEstimate(
            flops=4 * slots * slots * cols, bytes_accessed=10 * slots * cols, transcendentals=slots * slots * cols // HEAD_DIM
        ),
        name="attend",
    )(lengths, qkv, qkv, qkv)


def attend_back_body(
    rows, length_ref, q_ref, k_ref, v_ref, dm_ref, cos_ref, sin_ref, out_ref, out_t_ref, bias_ref, dk_acc, dv_acc
):
    slots = q_ref.shape[1]
    heads = [slice(n, n + HEAD_DIM) for n in range(0, q_ref.shape[2], HEAD_DIM)]
    scale = HEAD_DIM**-0.5
    bf, f32 = jnp.bfloat16, jnp.float32

    def finish(j, here, head, grad):
        if j < 2:
            grad = grad * cos_ref[here, :] - turn(grad) * sin_ref[here, :]
        low = grad.astype(bf)
        out_ref[j, here, head] = low
        out_t_ref[j, head, here] = grad.T.astype(bf)
        return jnp.sum(low.astype(f32), axis=0, keepdims=True)

    dq_sums = [jnp.zeros((1, HEAD_DIM), f32) for _ in heads]
    starts = list(range(0, slots, rows))[::-1]
    for start in starts:
        here, end = slice(start, start + rows), start + rows
        for n, head in enumerate(heads):
            q, k, v = q_ref[0, here, head], k_ref[0, :end, head], v_ref[0, :end, head]
            dm = dm_ref[here, head]
            p = block_probs(length_ref, q, k, start)
            dp = lax.dot_general(dm, v, NT, preferred_element_type=f32)
            ds = (p * (dp - jnp.sum(p * dp, axis=1, keepdims=True))).astype(bf)
            dq_sums[n] += finish(0, here, head, jnp.dot(ds, k, preferred_element_type=f32) * scale)
            dk = lax.dot_general(ds, q, TN, preferred_element_type=f32) * scale
            dv = lax.dot_general(p.astype(bf), dm, TN, preferred_element_type=f32)
            if start == starts[0]:
                dk_acc[n] = dk
                dv_acc[n] = dv
            else:
                dk_acc[n, :end, :] += dk
                dv_acc[n, :end, :] += dv
    every = slice(0, slots)
    for n, head in enumerate(heads):
        bias_ref[0, :, head] = dq_sums[n]
        bias_ref[1, :, head] = finish(1, every, head, dk_acc[n])
        bias_ref[2, :, head] = finish(2, every, head, dv_acc[n])


def attend_back(lengths, qkv, d_mixed, cos_table, sin_table):
    _, slots, cols = qkv.shape
    rows = min(512, slots)
    bf, f32 = jnp.bfloat16, jnp.float32
    together = ATTEND_HEADS
    wide = together * HEAD_DIM

    def part(j):
        return pl.BlockSpec((1, slots, wide), lambda h: (j, 0, h))

    table = pl.BlockSpec((slots, HEAD_DIM), lambda h: (0, 0), pipeline_mode=pl.Buffered(1))
    return pl.pallas_call(
        functools.partial(attend_back_body, rows),
        grid=(cols // wide,),
        in_specs=[
            pl.BlockSpec(memory_space=pltpu.SMEM), part(0), part(1), part(2),
            pl.BlockSpec((slots, wide), lambda h: (0, h)), table, table,
        ],
        out_specs=[
            pl.BlockSpec((3, slots, wide), lambda h: (0, 0, h)), pl.BlockSpec((3, wide, slots), lambda h: (0, h, 0)),
            pl.BlockSpec((3, 1, wide), lambda h: (0, 0, h)),
        ],
        out_shape=[
            jax.ShapeDtypeStruct((3, slots, cols), bf), jax.ShapeDtypeStruct((3, cols, slots), bf),
            jax.ShapeDtypeStruct((3, 1, cols), f32),
        ],
        scratch_shapes=[pltpu.VMEM((together, slots, HEAD_DIM), f32)] * 2,
        compiler_params=pltpu.CompilerParams(vmem_limit_bytes=56 * MIB),
        cost_estimate=pl.CostEstimate(
            flops=10 * slots * slots * cols, bytes_accessed=20 * slots * cols, transcendentals=slots * slots * cols // HEAD_DIM
        ),
        name="attend_back",
    )(lengths, qkv, qkv, qkv, d_mixed, cos_table, sin_table)


def rows_times_body(dims, x_ref, w_ref, out_ref):
    product = lax.dot_general(x_ref[...], w_ref[...], dims, preferred_element_type=jnp.float32)
    out_ref[...] = product.astype(out_ref.dtype)


def rows_times(x, w, dims, name):
    slots, depth = x.shape
    cols = w.shape[0] if dims == NT else w.shape[1]
    rows = min(256, slots)
    return pl.pallas_call(
        functools.partial(rows_times_body, dims),
        grid=(slots // rows,),
        in_specs=[
            pl.BlockSpec((rows, depth), lambda i: (i, 0)),
            pl.BlockSpec(w.shape, lambda i: (0, 0), pipeline_mode=pl.Buffered(1)),
        ],
        out_specs=pl.BlockSpec((rows, cols), lambda i: (i, 0)),
        out_shape=jax.ShapeDtypeStruct((slots, cols), jnp.bfloat16),
        compiler_params=pltpu.CompilerParams(vmem_limit_bytes=32 * MIB),
        cost_estimate=pl.CostEstimate(
            flops=2 * slots * depth * cols, bytes_accessed=2 * (slots * depth + slots * cols + depth * cols), transcendentals=0
        ),
        name=name,
    )(x, w)


def qkv_back_body(d_ref, w_ref, x_ref, out_ref, np_ref):
    total = lax.dot_general(d_ref[0], w_ref[0], NT, preferred_element_type=jnp.float32)
    for j in range(1, 3):
        total += lax.dot_general(d_ref[j], w_ref[j], NT, preferred_element_type=jnp.float32)
    out_ref[...] = total.astype(out_ref.dtype)
    np_ref[...] = jnp.sum(total * x_ref[...].astype(jnp.float32), axis=0, keepdims=True)


def qkv_back(d_qkv, w, x):
    _, slots, cols = d_qkv.shape
    width = w.shape[1]
    block = 512
    return pl.pallas_call(
        qkv_back_body,
        grid=(width // block,),
        in_specs=[
            pl.BlockSpec((3, slots, cols), lambda n: (0, 0, 0), pipeline_mode=pl.Buffered(1)),
            pl.BlockSpec((3, block, cols), lambda n: (0, n, 0)),
            pl.BlockSpec((slots, block), lambda n: (0, n)),
        ],
        out_specs=[pl.BlockSpec((slots, block), lambda n: (0, n)), pl.BlockSpec((1, block), lambda n: (0, n))],
        out_shape=[
            jax.ShapeDtypeStruct((slots, width), jnp.bfloat16), jax.ShapeDtypeStruct((1, width), jnp.float32),
        ],
        compiler_params=pltpu.CompilerParams(vmem_limit_bytes=48 * MIB),
        cost_estimate=pl.CostEstimate(
            flops=6 * slots * width * cols, bytes_accessed=4 * slots * width + 6 * width * cols, transcendentals=0
        ),
        name="qkv_back",
    )(d_qkv, w, x)


def weight_grad_scatter(a_list, b_list, r, cid, name, first=0, count=None, cut=None):
    count = a_list[0].shape[0] // r if count is None else count
    cut = count if cut is None else cut
    if lax.axis_size("dp") == 8:
        return weight_grad_scatter_kernel(a_list, b_list, r, cid, name, first, count, cut)
    product = sum(
        jnp.dot(a[first * r : (first + count) * r], b, preferred_element_type=jnp.float32)
        for a, b in zip(a_list, b_list)
    )
    result = lax.psum_scatter(product.astype(jnp.bfloat16), "dp", scatter_dimension=1, tiled=True)
    return result[: cut * r], result[cut * r :]


def line_gather(me, size, own, block, local_sem, sems):
    send_left, recv_left, send_right, recv_right = sems
    has_left, has_right = me > 0, me < size - 1

    def remote(source, owner, send, recv, step, to):
        return pltpu.make_async_remote_copy(
            src_ref=source, dst_ref=block(owner), send_sem=send.at[step], recv_sem=recv.at[step],
            device_id={"tensor": to}, device_id_type=MESH,
        )

    def to_left(step):
        return remote(own if step == 0 else block(me + step), me + step, send_left, recv_left, step, me - 1)

    def to_right(step):
        return remote(own if step == 0 else block(me - step), me - step, send_right, recv_right, step, me + 1)

    def advance(step):
        if step == 0:
            pltpu.make_async_copy(own, block(me), local_sem).start()
        else:
            @pl.when(me + step < size)
            def _():
                remote(own, me + step, send_left, recv_left, step - 1, me + 1).wait_recv()

        @pl.when(has_left & (me + step < size))
        def _():
            to_left(step).start()

        if step > 0:
            @pl.when(me - step >= 0)
            def _():
                remote(own, me - step, send_right, recv_right, step - 1, me - 1).wait_recv()

        @pl.when(has_right & (me - step >= 0))
        def _():
            to_right(step).start()

    def finish():
        for step in range(size):
            @pl.when(has_left & (me + step < size))
            def _():
                to_left(step).wait_send()

            @pl.when(has_right & (me - step >= 0))
            def _():
                to_right(step).wait_send()

        pltpu.make_async_copy(own, block(me), local_sem).wait()

    return advance, finish


def line_barrier(me, size):
    barrier = pltpu.get_barrier_semaphore()
    has_left, has_right = me > 0, me < size - 1

    @pl.when(has_left)
    def _():
        pl.semaphore_signal(barrier, inc=1, device_id={"tensor": me - 1}, device_id_type=MESH)

    @pl.when(has_right)
    def _():
        pl.semaphore_signal(barrier, inc=1, device_id={"tensor": me + 1}, device_id_type=MESH)

    pl.semaphore_wait(barrier, has_left.astype(jnp.int32) + has_right.astype(jnp.int32))


def branch_body(
    length_ref, part_ref, tokens_ref, gain_ref, cot_ref, hidden_ref, second_ref, xa_ref, da_ref,
    from_left, from_right, normed, local_sem, send_r, recv_r, send_l, recv_l, *sems,
):
    me = lax.axis_index("tensor")
    size = lax.axis_size("tensor")
    rows = tokens_ref.shape[0]
    half, quarter = rows // 2, rows // 4
    bf, f32 = jnp.bfloat16, jnp.float32
    has_left, has_right = me > 0, me < size - 1
    line_barrier(me, size)

    def gathered(owner, h):
        return da_ref.at[pl.ds(pl.multiple_of(owner * half + h * quarter, quarter), quarter)]

    def own_cot(h):
        return cot_ref.at[pl.ds(h * quarter, quarter)]

    def part(ref, owner, which):
        return ref.at[owner, pl.ds(pl.multiple_of(which * quarter, quarter), quarter)]

    def direction(right):
        slots, send, recv = (from_left, send_r, recv_r) if right else (from_right, send_l, recv_l)
        to = me + 1 if right else me - 1
        before = me if right else size - 1 - me
        has_to = has_right if right else has_left
        has_from = has_left if right else has_right

        def copy(source, target, t):
            return pltpu.make_async_remote_copy(
                src_ref=source, dst_ref=target, send_sem=send.at[t], recv_sem=recv.at[t],
                device_id={"tensor": to}, device_id_type=MESH,
            )

        def sends(s):
            return has_to & (s - before - 1 < 2 * (size - 1 - before))

        def step(t):
            s, h = t // 2, t % 2
            if t >= 2:
                @pl.when(sends(s - 1))
                def _():
                    copy(part(part_ref, 0, 0), part(slots, 0, 0), t - 2).wait_send()

            if s < size:
                @pl.when(s <= before)
                def _():
                    owner = me - s if right else me + s
                    if s > 0:
                        copy(own_cot(h), gathered(owner, h), t - 2).wait_recv()

                    @pl.when(has_to)
                    def _():
                        copy(own_cot(h) if s == 0 else gathered(owner, h), gathered(owner, h), t).start()

            @pl.when((s > before) & sends(s))
            def _():
                r = s - before - 1
                owner = size - 1 - r // 2 if right else r // 2
                which = 2 * (r % 2) + h

                @pl.when(has_from)
                def _():
                    both = part(slots, owner, which)
                    copy(part(part_ref, owner, which), both, t - 2).wait_recv()
                    both[...] = (both[...].astype(f32) + part(part_ref, owner, which)[...].astype(f32)).astype(bf)
                    copy(both, both, t).start()

                @pl.when(jnp.logical_not(has_from))
                def _():
                    copy(part(part_ref, owner, which), part(slots, owner, which), t).start()

        def last():
            @pl.when(has_from)
            def _():
                for which in range(4):
                    t = 2 * (before + 2 * (size - 1 - before)) + which
                    copy(part(part_ref, me, which), part(slots, me, which), t).wait_recv()
                hidden_ref[...] += slots[me].astype(f32)

        return step, last

    local = [pltpu.make_async_copy(own_cot(h), gathered(me, h), local_sem.at[h]) for h in range(2)]
    for copy in local:
        copy.start()
    step_r, last_r = direction(True)
    step_l, last_l = direction(False)
    for t in range(2 * (2 * size - 1) + 2):
        step_r(t)
        step_l(t)
    hidden_ref[...] = part_ref[me].astype(f32)
    last_r()
    last_l()
    row = lax.broadcasted_iota(jnp.int32, (rows, 1), 0) + me * rows
    live = jnp.where(row < length_ref[0], 1.0, 0.0)
    hidden = tokens_ref[...].astype(f32) + live * hidden_ref[...]
    hidden_ref[...] = hidden
    inverse = lax.rsqrt(jnp.mean(hidden * hidden, axis=1, keepdims=True) + epsilon)
    normed[...] = (hidden * inverse * gain_ref[...].astype(f32)).astype(bf)
    step_x, finish_x = line_gather(
        me, size, normed.at[:half], lambda owner: xa_ref.at[pl.ds(pl.multiple_of(owner * half, half), half)],
        local_sem.at[2], sems,
    )
    for j in range(size):
        step_x(j)
    second_ref[...] = normed[half:, :]
    for copy in local:
        copy.wait()
    finish_x()


def finish_branch(lengths, part, tokens, gain, cot, cid):
    size = lax.axis_size("tensor")
    rows, width = tokens.shape
    half = rows // 2
    bf, f32 = jnp.bfloat16, jnp.float32
    vmem = pl.BlockSpec(memory_space=pltpu.VMEM)
    anywhere = pl.BlockSpec(memory_space=pl.ANY)
    dma = pltpu.SemaphoreType.DMA
    gathered = jax.ShapeDtypeStruct((size * half, width), bf)
    return pl.pallas_call(
        branch_body,
        in_specs=[pl.BlockSpec(memory_space=pltpu.SMEM), vmem, vmem, vmem, anywhere],
        out_specs=[vmem, vmem, anywhere, anywhere],
        out_shape=[
            jax.ShapeDtypeStruct((rows, width), f32), jax.ShapeDtypeStruct((half, width), bf), gathered, gathered,
        ],
        scratch_shapes=[
            pltpu.VMEM((size, rows, width), bf), pltpu.VMEM((size, rows, width), bf), pltpu.VMEM((rows, width), bf),
            dma((3,)), *[dma((4 * size,))] * 4, *[dma((size,))] * 4,
        ],
        compiler_params=pltpu.CompilerParams(vmem_limit_bytes=48 * MIB, collective_id=cid, has_side_effects=True),
        cost_estimate=pl.CostEstimate(flops=0, bytes_accessed=24 * rows * size * width, transcendentals=0),
        name="finish_branch",
    )(lengths, part.reshape(size, rows, width), tokens, gain[None], cot)


def small_sum_phases(local_rows, part_ref, out_ref, scratch):
    staged, landed, from_dp, mine, from_tensor, send_dp, recv_dp, send_t, recv_t, send_out, recv_out = scratch
    size_dp, size_t = lax.axis_size("dp"), lax.axis_size("tensor")
    me_dp, me_t = lax.axis_index("dp"), lax.axis_index("tensor")
    width = mine.shape[1]

    def piece(ref, owner):
        return ref.at[:, pl.ds(pl.multiple_of(owner * width, width), width)]

    def greet():
        barrier = pltpu.get_barrier_semaphore()
        for step in range(1, size_dp):
            peer = lax.rem(me_dp + step, size_dp)
            pl.semaphore_signal(barrier, inc=1, device_id={"dp": peer}, device_id_type=MESH)
        for step in range(1, size_t):
            peer = lax.rem(me_t + step, size_t)
            pl.semaphore_signal(barrier, inc=1, device_id={"tensor": peer}, device_id_type=MESH)
        pl.semaphore_wait(barrier, size_dp + size_t - 2)

    def copy(source, target, axis, step, send_sem, recv_sem):
        me, size = (me_dp, size_dp) if axis == "dp" else (me_t, size_t)
        return pltpu.make_async_remote_copy(
            src_ref=source, dst_ref=target, send_sem=send_sem.at[step], recv_sem=recv_sem.at[step],
            device_id={axis: lax.rem(me + step, size)}, device_id_type=MESH,
        )

    def to_owner(step):
        return copy(piece(staged, lax.rem(me_dp + step, size_dp)), from_dp.at[step], "dp", step, send_dp, recv_dp)

    def to_tensor(step):
        return copy(mine, from_tensor.at[step], "tensor", step, send_t, recv_t)

    def to_all(step):
        here = piece(landed, me_dp)
        return copy(here, here, "dp", step, send_out, recv_out)

    def first():
        staged[...] = part_ref[...]
        for step in range(1, size_dp):
            to_owner(step).start()

    def second():
        total = piece(staged, me_dp)[...]
        for step in range(1, size_dp):
            to_owner(step).wait_recv()
            total = total + from_dp[step]
        mine[...] = total
        for step in range(1, size_t):
            to_tensor(step).start()

    def third():
        total = mine[...]
        for step in range(1, size_t):
            to_tensor(step).wait_recv()
            total = total + from_tensor[step]
        piece(landed, me_dp)[...] = total
        piece(landed.at[local_rows:], me_dp)[...] = mine[local_rows:, :]
        for step in range(1, size_dp):
            to_all(step).start()

    def last():
        for step in range(1, size_dp):
            to_all(step).wait_recv()
        out_ref[...] = landed[...]
        for step in range(1, size_dp):
            to_owner(step).wait_send()
            to_all(step).wait_send()
        for step in range(1, size_t):
            to_tensor(step).wait_send()

    return greet, first, second, third, last


def small_sum_scratch(shape):
    size_dp, size_t = lax.axis_size("dp"), lax.axis_size("tensor")
    rows, width = shape[0], shape[1] // size_dp
    dma = pltpu.SemaphoreType.DMA
    f32 = jnp.float32
    return [
        pltpu.VMEM(shape, f32), pltpu.VMEM(shape, f32),
        pltpu.VMEM((size_dp, rows, width), f32), pltpu.VMEM((rows, width), f32), pltpu.VMEM((size_t, rows, width), f32),
        dma((size_dp,)), dma((size_dp,)), dma((size_t,)), dma((size_t,)), dma((size_dp,)), dma((size_dp,)),
    ]


def sums_body(local_rows, part_ref, out_ref, *scratch):
    for phase in small_sum_phases(local_rows, part_ref, out_ref, scratch):
        phase()


def small_sums(part, local_rows, cid):
    vmem = pl.BlockSpec(memory_space=pltpu.VMEM)
    return pl.pallas_call(
        functools.partial(sums_body, local_rows),
        in_specs=[vmem],
        out_specs=vmem,
        out_shape=jax.ShapeDtypeStruct(part.shape, jnp.float32),
        scratch_shapes=small_sum_scratch(part.shape),
        compiler_params=pltpu.CompilerParams(collective_id=cid, has_side_effects=True),
        name="small_sums",
    )(part)


def attention_grads_body(nc, cut, local_rows, a_ref, a2_ref, b_ref, b2_ref, part_ref, o_ref, o2_ref, sums_ref, *scratch):
    i = pl.program_id(0)
    greet, *phases = small_sum_phases(local_rows, part_ref, sums_ref, scratch[:11])
    steps = nc + LA + LB + LC

    def store(c, rows, result):
        @pl.when(c < cut)
        def _():
            o_ref[rows, :] = result.astype(o_ref.dtype)

        @pl.when(c >= cut)
        def _():
            o2_ref[rows, :] = result.astype(o2_ref.dtype)

    send = scatter_steps(i, nc, (LA, LB, LC), o_ref.shape[1], scratch[11:], store, greet)
    for when, phase in zip((0, 4, 8, steps - 1), phases):
        pl.when(i == when)(phase)

    @pl.when(i < cut)
    def _():
        send(lambda cols: jnp.dot(a_ref[...], b_ref[:, cols], preferred_element_type=jnp.float32))

    @pl.when((i >= cut) & (i < nc))
    def _():
        send(lambda cols: jnp.dot(a2_ref[...], b2_ref[:, cols], preferred_element_type=jnp.float32))


def attention_grads(a, b, a2, b2, part, local_rows, r, cid):
    T, D = b.shape
    w = D // 8
    cut, rest = a.shape[0] // r, a2.shape[0] // r
    nc = cut + rest
    lag = LA + LB + LC
    out_specs, out_shape = scatter_outs(nc, cut, lag, r, w)

    def whole(shape):
        return pl.BlockSpec(shape, lambda i: (0, 0), pipeline_mode=pl.Buffered(1))

    return pl.pallas_call(
        functools.partial(attention_grads_body, nc, cut, local_rows),
        grid=(nc + lag,),
        in_specs=[
            pl.BlockSpec((r, T), lambda i: (jnp.minimum(i, cut - 1), 0)),
            pl.BlockSpec((r, T), lambda i: (jnp.clip(i - cut, 0, rest - 1), 0)),
            whole((T, D)), whole((T, D)), whole(part.shape),
        ],
        out_specs=[*out_specs, whole(part.shape)],
        out_shape=[*out_shape, jax.ShapeDtypeStruct(part.shape, jnp.float32)],
        scratch_shapes=[*small_sum_scratch(part.shape), *scatter_scratch(r, w)],
        compiler_params=pltpu.CompilerParams(vmem_limit_bytes=48 * MIB, collective_id=cid, has_side_effects=True),
        cost_estimate=pl.CostEstimate(flops=2 * nc * r * T * D, bytes_accessed=2 * nc * r * T + 4 * T * D, transcendentals=0),
        name="attention_grads",
    )(a, a2, b, b2, part)


def on_device(
    tokens,
    lengths,
    routes,
    cotangent,
    norm_one,
    qkv_weight,
    qkv_bias,
    out_weight,
    norm_two,
    router_weight,
    expert_in,
    expert_out,
    shared_in,
    shared_out,
    shared_gate,
):
    own_rows = tokens.shape[0]
    slot_count = routes.shape[0]
    model_width = tokens.shape[1]
    qkv_cols = qkv_weight.shape[2]
    local_heads = qkv_cols // HEAD_DIM
    experts = router_weight.shape[1]
    eff = expert_in.shape[3]
    shared_chunks = shared_out.shape[0] // eff
    chunks = experts + shared_chunks
    bf = jnp.bfloat16
    qkv_cols = qkv_weight.shape[2]
    length = lengths[0]
    tensor_index = lax.axis_index("tensor")
    first_row = tensor_index * own_rows
    live_own = (first_row + jnp.arange(own_rows) < length).astype(jnp.float32)[:, None]
    tokens_f = tokens.astype(jnp.float32)
    gain_one = norm_one.astype(jnp.float32)
    gain_two = norm_two.astype(jnp.float32)
    inv_one = lax.rsqrt(jnp.mean(tokens_f * tokens_f, axis=-1, keepdims=True) + epsilon)
    unit_one = tokens_f * inv_one
    normed_one = lax.all_gather((unit_one * gain_one).astype(bf), "tensor", axis=0, tiled=True)
    cos_table, sin_table = rotary_tables(slot_count, HEAD_DIM)
    qkv_w = qkv_weight.transpose(1, 0, 2)
    ei = expert_in.transpose(0, 2, 3, 1).reshape(experts, 2 * eff, model_width)
    eo = expert_out
    si = (
        shared_in.reshape(model_width, 2, shared_chunks, eff)
        .transpose(2, 1, 3, 0)
        .reshape(shared_chunks, 2 * eff, model_width)
    )
    so = shared_out.reshape(shared_chunks, eff, model_width)
    router_rows = jnp.concatenate(
        [
            router_weight.T,
            shared_gate[None],
            jnp.zeros((-(experts + 1) % 16, model_width), bf),
        ],
        axis=0,
    )
    grad_out = cotangent.astype(jnp.float32) * live_own
    d_two_own = (live_own * grad_out).astype(bf)
    normed_one, si, router_rows, cos_table, sin_table, d_two_own = lax.optimization_barrier(
        (normed_one, si, router_rows, cos_table, sin_table, d_two_own)
    )
    qkv = project_qkv(normed_one, qkv_w, qkv_bias[:, None, :], cos_table, sin_table)
    mixed, mixed_t = attend(lengths, qkv)
    branch_partial = jnp.dot(mixed, out_weight, preferred_element_type=jnp.float32).astype(bf)
    size_t = lax.axis_size("tensor")
    half = own_rows // 2
    hidden, second, x_a, d_a = finish_branch(
        lengths, branch_partial, tokens, norm_two, d_two_own, 1
    )
    inv_two = lax.rsqrt(jnp.mean(hidden * hidden, axis=-1, keepdims=True) + epsilon)
    unit_two = hidden * inv_two
    routes_a, routes_b = (
        routes.reshape(size_t, 2, half, -1).transpose(1, 0, 2, 3).reshape(2, size_t * half, -1)
    )
    weights = (router_rows, ei, si, eo, so)
    dgu_a, dn_a, bt_a, router_a, np_a, s_a, x_b, d_b = ffn(
        x_a, d_a, routes_a.T, *weights, own=[second, d_two_own[half:]]
    )
    grad_a = lax.psum_scatter(dn_a, "tensor", scatter_dimension=0, tiled=True)
    two_a = lax.psum_scatter(bt_a, "tensor", scatter_dimension=0, tiled=True)
    if lax.axis_size("dp") == 8:
        dgu_b, dn_b, bt_b, router_b, np_b, out_grads, shared_out_grad = ffn(
            x_b, d_b, routes_b.T, *weights, other=(s_a, d_a)
        )
    else:
        dgu_b, dn_b, bt_b, router_b, np_b, s_b = ffn(x_b, d_b, routes_b.T, *weights)
        inner = [s.reshape(chunks * eff, -1) for s in (s_a, s_b)]
        out_grads, shared_out_grad = weight_grad_scatter(
            inner, [d_a, d_b], eff, 2, "down_grads", cut=experts
        )
    router_part = router_a + router_b
    norm_two_part = np_a + np_b
    d_gate_up = [d.reshape(chunks * 2 * eff, -1) for d in (dgu_a, dgu_b)]
    grad_a, two_a, dn_b = lax.optimization_barrier((grad_a, two_a, dn_b))
    grad_b = lax.psum_scatter(dn_b, "tensor", scatter_dimension=0, tiled=True)
    two_b = lax.psum_scatter(bt_b, "tensor", scatter_dimension=0, tiled=True)
    in_grads_b, _ = weight_grad_scatter(
        d_gate_up, [x_a, x_b], eff, 4, "shared_in_grads", 2 * experts, 2 * shared_chunks
    )
    grad_two = jnp.concatenate([grad_a, grad_b], axis=0).astype(jnp.float32)
    grad_hidden = grad_out + norm_back(grad_two, unit_two, inv_two, gain_two)
    d_one_own, in_grads_b = lax.optimization_barrier(
        ((live_own * grad_hidden).astype(bf), in_grads_b)
    )
    d_one = lax.all_gather(d_one_own, "tensor", axis=0, tiled=True)
    d_gate_up, _ = lax.optimization_barrier((d_gate_up, d_one_own))
    in_grads_a, _ = weight_grad_scatter(
        d_gate_up, [x_a, x_b], eff, 3, "expert_in_grads", 0, 2 * experts
    )
    d_one, in_grads_a = lax.optimization_barrier((d_one, in_grads_a))
    d_mixed = rows_times(d_one, out_weight, NT, "mixed_back")
    d_qkv, d_qkv_t, bias_part = attend_back(lengths, qkv, d_mixed, cos_table, sin_table)
    grad_one, norm_one_part = qkv_back(d_qkv, qkv_w, normed_one)
    grad_one, d_qkv_t, mixed_t, two_b = lax.optimization_barrier(
        (grad_one, d_qkv_t, mixed_t, two_b)
    )
    grad_one_own = lax.psum_scatter(grad_one, "tensor", scatter_dimension=0, tiled=True)
    part = jnp.concatenate(
        [
            router_part[: experts + 1],
            norm_one_part / gain_one[None],
            norm_two_part / gain_two[None],
            jnp.pad(bias_part.reshape(1, 3 * qkv_cols), ((0, 0), (0, model_width - 3 * qkv_cols))),
        ],
        axis=0,
    )
    d_qkv_t = d_qkv_t.reshape(3 * qkv_cols, slot_count)
    if lax.axis_size("dp") == 8:
        qkv_sum, out_sum, sums = attention_grads(
            d_qkv_t, normed_one, mixed_t, d_one, part, experts + 3, qkv_cols // 2, 5
        )
    else:
        sums = small_sums(part, experts + 3, 7)
        qkv_sum, _ = weight_grad_scatter([d_qkv_t], [normed_one], qkv_cols, 5, "qkv_grads")
        out_sum, _ = weight_grad_scatter([mixed_t], [d_one], qkv_cols, 6, "mix_grads")
    branch_two = jnp.concatenate([two_a, two_b], axis=0).astype(jnp.float32)
    output = (hidden + live_own * branch_two).astype(bf)
    grad_one = grad_one_own.astype(jnp.float32)
    input_grad = grad_hidden + norm_back(grad_one, unit_one, inv_one, gain_one)
    qkv_bias_grad = sums[experts + 3, : 3 * qkv_cols].reshape(3, qkv_cols)
    own_cols = out_grads.shape[1]
    expert_in_grad = in_grads_a.astype(jnp.float32).reshape(experts, 2, eff, own_cols).transpose(0, 3, 1, 2)
    shared_in_grad = (
        in_grads_b.reshape(shared_chunks, 2, eff, own_cols)
        .transpose(3, 1, 0, 2)
        .reshape(own_cols, 2, shared_chunks * eff)
        .astype(jnp.float32)
    )
    return (
        output,
        input_grad,
        sums[experts + 1],
        qkv_sum.astype(jnp.float32).reshape(3, qkv_cols, own_cols).transpose(2, 0, 1),
        qkv_bias_grad,
        out_sum.astype(jnp.float32),
        sums[experts + 2],
        sums[:experts].T,
        expert_in_grad,
        out_grads.astype(jnp.float32).reshape(experts, eff, own_cols),
        shared_in_grad,
        shared_out_grad.astype(jnp.float32),
        sums[experts],
    )


def solution(mesh):
    in_specs = (
        P(("dp", "tensor"), None),
        P("dp"),
        P("dp", None),
        P(("dp", "tensor"), None),
        P(),
        P(None, None, "tensor"),
        P(None, "tensor"),
        P("tensor", None),
        P(),
        P(),
        P(None, None, None, "tensor"),
        P(None, "tensor", None),
        P(None, None, "tensor"),
        P("tensor", None),
        P(),
    )
    out_specs = (
        P(("dp", "tensor"), None),
        P(("dp", "tensor"), None),
        P(),
        P("dp", None, "tensor"),
        P(None, "tensor"),
        P("tensor", "dp"),
        P(),
        P(),
        P(None, "dp", None, "tensor"),
        P(None, "tensor", "dp"),
        P("dp", None, "tensor"),
        P("tensor", "dp"),
        P(),
    )
    return jax.shard_map(
        on_device, mesh=mesh, in_specs=in_specs, out_specs=out_specs, check_vma=False
    )
```

```python
import functools

import jax
import jax.numpy as jnp
from jax import lax
from jax.experimental import pallas as pl
from jax.experimental.pallas import tpu as pltpu
from jax.sharding import PartitionSpec as P

HEAD_DIM = 128
MESH = pl.DeviceIdType.MESH
LA, LB, LC = 1, 2, 2
FFN_LAGS = (1, 1, 1)
MIB = 2**20
ATTEND_HEADS = 1


epsilon = 1e-06
theta_base = 1000000.0
NT = (((1,), (1,)), ((), ()))
TN = (((0,), (0,)), ((), ()))


def rotary_tables(row_count, head_width):
    half_index = jnp.arange(head_width // 2).astype(jnp.float32)
    frequency = theta_base ** (-2.0 * half_index / head_width)
    angles = jnp.arange(row_count).astype(jnp.float32)[:, None] * frequency[None, :]
    sines = jnp.sin(angles)
    cosines = jnp.cos(angles)
    return (
        jnp.concatenate([cosines, cosines], axis=-1),
        jnp.concatenate([-sines, sines], axis=-1),
    )


def norm_back(d_normed, unit_rows, inverse, gain_vector):
    d_unit = d_normed * gain_vector
    return inverse * (d_unit - unit_rows * jnp.mean(d_unit * unit_rows, axis=-1, keepdims=True))


def scatter_scratch(r, w):
    f32, bf = jnp.float32, jnp.bfloat16
    dma = pltpu.SemaphoreType.DMA
    h = r // 2
    return [
        pltpu.VMEM((2, 4, r, w), f32), pltpu.VMEM((2, 4, r, w), bf), pltpu.VMEM((3, 4, r, w), bf),
        pltpu.VMEM((3, 2, 2, h, w), f32), pltpu.VMEM((3, 2, 2, h, w), bf), pltpu.VMEM((6, 2, 2, h, w), bf),
        pltpu.VMEM((3, 2, h, w), f32), pltpu.VMEM((2, 2, h, w), bf), pltpu.VMEM((6, 2, h, w), bf),
        dma((2,)), dma((3,)), dma((3, 2)), dma((6, 2)), dma((2, 2)), dma((6, 2)),
    ]


def scatter_steps(i, nc, lags, w, scratch, store, greet=None):
    own, sa, ra, kt, s1, r1, ku, s2, r2, sem_sa, sem_ra, sem_s1, sem_r1, sem_s2, sem_r2 = scratch
    la, lb, lc = lags
    keep_1 = min(3, lb + lc)
    hr = own.shape[2] // 2
    dp = lax.axis_index("dp")
    k = dp % 2
    x = (dp // 2) % 2
    y = dp // 4
    core_peer = y * 4 + x * 2 + (1 - k)
    x_peer = y * 4 + (1 - x) * 2 + k
    y_peer = (1 - y) * 4 + x * 2 + k

    def copy_a(c):
        return pltpu.make_async_remote_copy(
            src_ref=sa.at[c % 2], dst_ref=ra.at[c % 3], send_sem=sem_sa.at[c % 2], recv_sem=sem_ra.at[c % 3],
            device_id={"dp": core_peer}, device_id_type=MESH,
        )

    def copy_1(c, half):
        return pltpu.make_async_remote_copy(
            src_ref=s1.at[c % 3, half], dst_ref=r1.at[c % 6, half], send_sem=sem_s1.at[c % 3, half],
            recv_sem=sem_r1.at[c % 6, half], device_id={"dp": y_peer if half else x_peer}, device_id_type=MESH,
        )

    def copy_2(c, half):
        return pltpu.make_async_remote_copy(
            src_ref=s2.at[c % 2, half], dst_ref=r2.at[c % 6, half], send_sem=sem_s2.at[c % 2, half],
            recv_sem=sem_r2.at[c % 6, half], device_id={"dp": x_peer if half else y_peer}, device_id_type=MESH,
        )

    @pl.when(i == 0)
    def _():
        if greet is not None:
            greet()
            return
        barrier = pltpu.get_barrier_semaphore()
        for peer in (core_peer, x_peer, y_peer):
            pl.semaphore_signal(barrier, inc=1, device_id={"dp": peer}, device_id_type=MESH)
        pl.semaphore_wait(barrier, 3)

    @pl.when((i >= la + keep_1) & (i < nc + la + keep_1))
    def _():
        copy_1(i - la - keep_1, 0).wait_send()
        copy_1(i - la - keep_1, 1).wait_send()

    @pl.when((i >= la) & (i < nc + la))
    def _():
        c = i - la
        copy_a(c).wait_recv()
        for half in range(2):
            rows = slice(half * hr, half * hr + hr)
            keep, other = (1, 2) if half else (2, 1)

            def total(role):
                return own[c % 2, role, rows, :] + ra[c % 3, role, rows, :].astype(jnp.float32)

            s1[c % 3, half, 0] = total(other).astype(jnp.bfloat16)
            s1[c % 3, half, 1] = total(3).astype(jnp.bfloat16)
            copy_1(c, half).start()
            kt[c % 3, half, 0] = total(0)
            kt[c % 3, half, 1] = total(keep)

    @pl.when((i >= la + lb) & (i < nc + la + lb))
    def _():
        c = i - la - lb

        @pl.when(c >= 2)
        def _():
            copy_2(c - 2, 0).wait_send()
            copy_2(c - 2, 1).wait_send()

        for half in range(2):
            copy_1(c, half).wait_recv()
            s2[c % 2, half] = (kt[c % 3, half, 1] + r1[c % 6, half, 1].astype(jnp.float32)).astype(jnp.bfloat16)
            copy_2(c, half).start()
            ku[c % 3, half] = kt[c % 3, half, 0] + r1[c % 6, half, 0].astype(jnp.float32)

    @pl.when(i >= la + lb + lc)
    def _():
        c = i - la - lb - lc
        for half in range(2):
            copy_2(c, half).wait_recv()
            store(c, slice(half * hr, half * hr + hr), ku[c % 3, half] + r2[c % 6, half].astype(jnp.float32))

        @pl.when(c >= nc - 2)
        def _():
            copy_2(c, 0).wait_send()
            copy_2(c, 1).wait_send()

    @pl.when((i >= 2) & (i < nc + 2))
    def _():
        copy_a(i - 2).wait_send()

    def send(product):
        targets = (y * 4 + x * 2, y * 4 + (1 - x) * 2, (1 - y) * 4 + x * 2, (1 - y) * 4 + (1 - x) * 2)

        def cols(role, core):
            return pl.ds(pl.multiple_of((targets[role] + core) * w, w), w)

        for role in range(4):
            sa[i % 2, role] = product(cols(role, 1 - k)).astype(jnp.bfloat16)
        copy_a(i).start()
        for role in range(4):
            own[i % 2, role] = product(cols(role, k))

    return send


def rs_body(nc, cut, pairs, *refs):
    a_refs, b_refs = refs[:pairs], refs[pairs : 2 * pairs]
    o_ref, o2_ref = refs[2 * pairs : 2 * pairs + 2]
    i = pl.program_id(0)

    def store(c, rows, result):
        @pl.when(c < cut)
        def _():
            o_ref[rows, :] = result.astype(o_ref.dtype)

        @pl.when(c >= cut)
        def _():
            o2_ref[rows, :] = result.astype(o2_ref.dtype)

    send = scatter_steps(i, nc, (LA, LB, LC), o_ref.shape[1], refs[2 * pairs + 2 :], store)

    @pl.when(i < nc)
    def _():
        def product(cols):
            total = jnp.dot(a_refs[0][...], b_refs[0][:, cols], preferred_element_type=jnp.float32)
            for a_ref, b_ref in zip(a_refs[1:], b_refs[1:]):
                total += jnp.dot(a_ref[...], b_ref[:, cols], preferred_element_type=jnp.float32)
            return total

        send(product)


def scatter_outs(nc, cut, lag, r, w):
    rest = max(nc - cut, 1)
    specs = [
        pl.BlockSpec((r, w), lambda i: (jnp.clip(i - lag, 0, cut - 1), 0)),
        pl.BlockSpec((r, w), lambda i: (jnp.clip(i - lag - cut, 0, rest - 1), 0)),
    ]
    return specs, [jax.ShapeDtypeStruct((n * r, w), jnp.bfloat16) for n in (cut, rest)]


def weight_grad_scatter_kernel(a_list, b_list, r, cid, name, first, count, cut):
    D = b_list[0].shape[1]
    T = sum(b.shape[0] for b in b_list)
    w = D // 8
    lag = LA + LB + LC
    out_specs, out_shape = scatter_outs(count, cut, lag, r, w)
    return pl.pallas_call(
        functools.partial(rs_body, count, cut, len(a_list)),
        grid=(count + lag,),
        in_specs=[
            *[pl.BlockSpec((r, a.shape[1]), lambda i: (jnp.minimum(i, count - 1) + first, 0)) for a in a_list],
            *[pl.BlockSpec(b.shape, lambda i: (0, 0), pipeline_mode=pl.Buffered(1)) for b in b_list],
        ],
        out_specs=out_specs,
        out_shape=out_shape,
        scratch_shapes=scatter_scratch(r, w),
        compiler_params=pltpu.CompilerParams(vmem_limit_bytes=48 * MIB, collective_id=cid, has_side_effects=True),
        cost_estimate=pl.CostEstimate(
            flops=2 * count * r * T * D, bytes_accessed=2 * count * r * T + 2 * T * D + 4 * count * r * w, transcendentals=0
        ),
        name=name,
    )(*a_list, *b_list)


def ffn_body(
    experts, chunks, scatter, gather,
    x_ref, d_ref, routes_ref, rw_ref, ei_ref, si_ref, eo_ref, so_ref, *refs,
):
    if scatter:
        s_other_ref, d_other_ref, dgu_ref, dn_ref, bt_ref, rg_ref, np_ref, og_ref, og2_ref, *refs = refs
    else:
        if gather:
            own_x_ref, own_d_ref, *refs = refs
        dgu_ref, dn_ref, bt_ref, rg_ref, np_ref, s_ref, *refs = refs
        if gather:
            all_x_ref, all_d_ref, *refs = refs
    dn_acc, bt_acc, probs_ref, w_ref, ds_ref, wi_buf, wd_buf, sem, *scratch = refs
    c = pl.program_id(0)
    h = eo_ref.shape[1]
    slots, width = x_ref.shape
    if gather:
        me, size = lax.axis_index("tensor"), lax.axis_size("tensor")
        local_sem, *sems = scratch
        lines = []
        for number, (own, out) in enumerate(((own_x_ref, all_x_ref), (own_d_ref, all_d_ref))):
            def block(owner, out=out, rows=own.shape[0]):
                return out.at[pl.ds(pl.multiple_of(owner * rows, rows), rows)]

            lines.append(
                line_gather(me, size, own, block, local_sem.at[number], sems[4 * number : 4 * number + 4])
            )
        for hop in range(size - 1):
            @pl.when(c == -(-hop * (chunks - 1) // (size - 1)))
            def _():
                if hop == 0:
                    line_barrier(me, size)
                for advance, _ in lines:
                    advance(hop)

    def fetch(step):
        slot = step % 2

        @pl.when(step < experts)
        def _():
            pltpu.make_async_copy(ei_ref.at[step], wi_buf.at[slot], sem.at[0, slot]).start()
            pltpu.make_async_copy(eo_ref.at[step], wd_buf.at[slot], sem.at[1, slot]).start()

        @pl.when(step >= experts)
        def _():
            pltpu.make_async_copy(si_ref.at[step - experts], wi_buf.at[slot], sem.at[0, slot]).start()
            pltpu.make_async_copy(so_ref.at[step - experts], wd_buf.at[slot], sem.at[1, slot]).start()

    @pl.when(c == 0)
    def _():
        fetch(c)

    @pl.when(c + 1 < chunks)
    def _():
        fetch(c + 1)

    def picked():
        expert = lax.broadcasted_iota(jnp.int32, (experts, slots), 0)
        hit = jnp.zeros((experts, slots), jnp.float32)
        for j in range(routes_ref.shape[0]):
            hit = hit + jnp.where(routes_ref[j : j + 1, :] == expert, 1.0, 0.0)
        return hit

    @pl.when(c == 0)
    def _():
        logits = lax.dot_general(rw_ref[...], x_ref[...], NT, preferred_element_type=jnp.float32)
        raised = jnp.exp(logits[:experts] - jnp.max(logits[:experts], axis=0, keepdims=True))
        probs = raised / jnp.sum(raised, axis=0, keepdims=True)
        gate = 1.0 / (1.0 + jnp.exp(-logits[experts:]))
        probs_ref[...] = probs
        w_ref[:experts, :] = probs * picked()
        w_ref[experts:, :] = gate
        ds_ref[...] = jnp.zeros_like(ds_ref)
        dn_acc[...] = jnp.zeros_like(dn_acc)
        bt_acc[...] = jnp.zeros_like(bt_acc)

    if scatter:
        def store(chunk, rows, result):
            @pl.when(chunk < experts)
            def _():
                og_ref[rows, :] = result.astype(og_ref.dtype)

            @pl.when(chunk >= experts)
            def _():
                og2_ref[rows, :] = result.astype(og2_ref.dtype)

        send = scatter_steps(c, chunks, FFN_LAGS, og_ref.shape[1], scratch, store)

    block = 512

    @pl.when(c < chunks)
    def _():
        row = pl.ds(jnp.minimum(c, experts), 1)
        slot = c % 2
        pltpu.make_async_copy(ei_ref.at[0], wi_buf.at[slot], sem.at[0, slot]).wait()
        pltpu.make_async_copy(eo_ref.at[0], wd_buf.at[slot], sem.at[1, slot]).wait()
        wi = wi_buf.at[slot]
        wd = wd_buf.at[slot]
        x = x_ref[...]
        g = lax.dot_general(wi[:h], x, NT, preferred_element_type=jnp.float32)
        u = lax.dot_general(wi[h:], x, NT, preferred_element_type=jnp.float32)
        p = lax.dot_general(wd[...], d_ref[...], NT, preferred_element_type=jnp.float32)
        w = w_ref[row, :]
        sg = 1.0 / (1.0 + jnp.exp(-g))
        si = g * sg
        inner = (si * u).astype(jnp.bfloat16).astype(jnp.float32)
        s = (w * inner).astype(jnp.bfloat16)
        ds_ref[row, :] += jnp.sum(p * inner, axis=0, keepdims=True)
        di = w * p
        dg = (di * u * sg * (1.0 + g * (1.0 - sg))).astype(jnp.bfloat16)
        du = (di * si).astype(jnp.bfloat16)
        dgu_ref[0, :h] = dg
        dgu_ref[0, h:] = du
        dgu = jnp.concatenate([dg, du], axis=0)
        if scatter:
            def product(cols):
                return jnp.dot(s, d_ref[:, cols], preferred_element_type=jnp.float32) + jnp.dot(
                    s_other_ref[0], d_other_ref[:, cols], preferred_element_type=jnp.float32
                )

            send(product)
        else:
            s_ref[0] = s
        for n in range(0, width, block):
            cols = slice(n, n + block)
            dn_acc[:, cols] += lax.dot_general(dgu, wi[:, cols], TN, preferred_element_type=jnp.float32)
            bt_acc[:, cols] += lax.dot_general(s, wd[:, cols], TN, preferred_element_type=jnp.float32)

    @pl.when(c == (chunks if scatter else chunks - 1))
    def _():
        probs = probs_ref[...]
        d_probs = ds_ref[:experts, :] * picked()
        d_logits = probs * (d_probs - jnp.sum(probs * d_probs, axis=0, keepdims=True))
        gate = w_ref[experts:, :]
        d_gate = ds_ref[experts:, :] * gate * (1.0 - gate)
        small = jnp.concatenate([d_logits, d_gate], axis=0)
        high = small.astype(jnp.bfloat16)
        low = (small - high.astype(jnp.float32)).astype(jnp.bfloat16)
        rg_ref[...] = jnp.dot(high, x_ref[...], preferred_element_type=jnp.float32) + jnp.dot(
            low, x_ref[...], preferred_element_type=jnp.float32
        )
        for n in range(0, width, block):
            cols = slice(n, n + block)
            extra = lax.dot_general(high, rw_ref[:, cols], TN, preferred_element_type=jnp.float32)
            extra += lax.dot_general(low, rw_ref[:, cols], TN, preferred_element_type=jnp.float32)
            total = dn_acc[:, cols] + extra
            dn_ref[:, cols] = total.astype(dn_ref.dtype)
            np_ref[:, cols] = jnp.sum(total * x_ref[:, cols].astype(jnp.float32), axis=0, keepdims=True)
        bt_ref[...] = bt_acc[...].astype(bt_ref.dtype)
        if gather:
            for advance, finish in lines:
                advance(size - 1)
                finish()


def ffn(x, d_two, routes_t, router_rows, ei, si, eo, so, other=None, own=None):
    experts, h2, width = ei.shape
    chunks = experts + si.shape[0]
    h = h2 // 2
    slots = x.shape[0]
    rows = router_rows.shape[0]
    bf, f32 = jnp.bfloat16, jnp.float32
    anywhere = pl.BlockSpec(memory_space=pl.ANY)
    scatter = other is not None

    def whole(shape):
        return pl.BlockSpec(shape, lambda c: (0,) * len(shape), pipeline_mode=pl.Buffered(1))

    def chunk(shape):
        return pl.BlockSpec((1, *shape), lambda c: (jnp.minimum(c, chunks - 1), 0, 0))

    in_specs = [
        whole((slots, width)), whole((slots, width)), whole(routes_t.shape), whole((rows, width)),
        anywhere, anywhere, anywhere, anywhere,
    ]
    out_specs = [chunk((h2, slots)), whole((slots, width)), whole((slots, width)), whole((rows, width)), whole((1, width))]
    out_shape = [
        jax.ShapeDtypeStruct((chunks, h2, slots), bf), jax.ShapeDtypeStruct((slots, width), bf),
        jax.ShapeDtypeStruct((slots, width), bf), jax.ShapeDtypeStruct((rows, width), f32),
        jax.ShapeDtypeStruct((1, width), f32),
    ]
    scratch = [
        pltpu.VMEM((slots, width), f32), pltpu.VMEM((slots, width), f32),
        pltpu.VMEM((experts, slots), f32), pltpu.VMEM((rows, slots), f32), pltpu.VMEM((rows, slots), f32),
        pltpu.VMEM((2, h2, width), bf), pltpu.VMEM((2, h, width), bf), pltpu.SemaphoreType.DMA((2, 2)),
    ]
    args = [x, d_two, routes_t, router_rows, ei, si, eo, so]
    if scatter:
        s_other, d_other = other
        in_specs += [chunk((h, s_other.shape[2])), whole(d_other.shape)]
        args += [s_other, d_other]
        w = width // 8
        lag = sum(FFN_LAGS)
        specs, shapes = scatter_outs(chunks, experts, lag, h, w)
        out_specs += specs
        out_shape += shapes
        scratch += scatter_scratch(h, w)
        grid = (chunks + lag,)
        params = pltpu.CompilerParams(vmem_limit_bytes=62 * MIB, collective_id=2, has_side_effects=True)
    else:
        out_specs.append(chunk((h, slots)))
        out_shape.append(jax.ShapeDtypeStruct((chunks, h, slots), bf))
        grid = (chunks,)
        params = pltpu.CompilerParams(vmem_limit_bytes=62 * MIB)
        if own is not None:
            size = lax.axis_size("tensor")
            dma = pltpu.SemaphoreType.DMA
            in_specs += [anywhere, anywhere]
            args += own
            out_specs += [anywhere, anywhere]
            out_shape += [jax.ShapeDtypeStruct((size * a.shape[0], width), bf) for a in own]
            scratch += [dma((2,)), *[dma((size,))] * 8]
            params = pltpu.CompilerParams(vmem_limit_bytes=62 * MIB, collective_id=8, has_side_effects=True)
    return pl.pallas_call(
        functools.partial(ffn_body, experts, chunks, scatter, own is not None),
        grid=grid,
        in_specs=in_specs,
        out_specs=out_specs,
        out_shape=out_shape,
        scratch_shapes=scratch,
        compiler_params=params,
        cost_estimate=pl.CostEstimate(
            flops=12 * chunks * h * slots * width, bytes_accessed=10 * chunks * h * width + 16 * slots * width,
            transcendentals=chunks * h * slots,
        ),
        name="ffn_scatter" if scatter else "ffn",
    )(*args)


def turn(v):
    half = v.shape[1] // 2
    return jnp.concatenate([v[:, half:], v[:, :half]], axis=1)


def qkv_body(x_ref, w_ref, bias_ref, cos_ref, sin_ref, out_ref):
    j = pl.program_id(0)
    cols = w_ref.shape[2]
    y = jnp.dot(x_ref[...], w_ref[0], preferred_element_type=jnp.float32)
    y = y + bias_ref[0].astype(jnp.float32)

    @pl.when(j < 2)
    def _():
        for head in range(cols // HEAD_DIM):
            place = slice(head * HEAD_DIM, (head + 1) * HEAD_DIM)
            v = y[:, place]
            out_ref[0, :, place] = (v * cos_ref[...] + turn(v) * sin_ref[...]).astype(out_ref.dtype)

    @pl.when(j == 2)
    def _():
        out_ref[0] = y.astype(out_ref.dtype)


def project_qkv(x, w, bias, cos_table, sin_table):
    slots, width = x.shape
    cols = w.shape[2]
    table = pl.BlockSpec((slots, HEAD_DIM), lambda j: (0, 0), pipeline_mode=pl.Buffered(1))
    return pl.pallas_call(
        qkv_body,
        grid=(3,),
        in_specs=[
            pl.BlockSpec((slots, width), lambda j: (0, 0), pipeline_mode=pl.Buffered(1)),
            pl.BlockSpec((1, width, cols), lambda j: (j, 0, 0)),
            pl.BlockSpec((1, 1, cols), lambda j: (j, 0, 0)),
            table, table,
        ],
        out_specs=pl.BlockSpec((1, slots, cols), lambda j: (j, 0, 0)),
        out_shape=jax.ShapeDtypeStruct((3, slots, cols), jnp.bfloat16),
        compiler_params=pltpu.CompilerParams(vmem_limit_bytes=48 * MIB),
        cost_estimate=pl.CostEstimate(
            flops=6 * slots * width * cols, bytes_accessed=2 * slots * width + 6 * width * cols, transcendentals=0
        ),
        name="project_qkv",
    )(x, w, bias, cos_table, sin_table)


def block_probs(length_ref, q, k, start):
    s = lax.dot_general(q, k, NT, preferred_element_type=jnp.float32) * (HEAD_DIM**-0.5)
    row = lax.broadcasted_iota(jnp.int32, s.shape, 0) + start
    col = lax.broadcasted_iota(jnp.int32, s.shape, 1)
    s = jnp.where((col <= row) & (col < length_ref[0]), s, -1000000000.0)
    e = jnp.exp(s - jnp.max(s, axis=1, keepdims=True))
    return e * (1.0 / jnp.sum(e, axis=1, keepdims=True))


def attend_body(rows, length_ref, q_ref, k_ref, v_ref, mixed_ref, mixed_t_ref):
    for start in range(0, q_ref.shape[1], rows):
        here, end = slice(start, start + rows), start + rows
        p = block_probs(length_ref, q_ref[0, here, :], k_ref[0, :end, :], start)
        mixed = jnp.dot(p.astype(jnp.bfloat16), v_ref[0, :end, :], preferred_element_type=jnp.float32)
        mixed_ref[here, :] = mixed.astype(mixed_ref.dtype)
        mixed_t_ref[:, here] = mixed.T.astype(mixed_ref.dtype)


def attend(lengths, qkv):
    _, slots, cols = qkv.shape
    rows = min(512, slots)

    def part(j):
        return pl.BlockSpec((1, slots, HEAD_DIM), lambda h: (j, 0, h))

    return pl.pallas_call(
        functools.partial(attend_body, rows),
        grid=(cols // HEAD_DIM,),
        in_specs=[pl.BlockSpec(memory_space=pltpu.SMEM), part(0), part(1), part(2)],
        out_specs=[
            pl.BlockSpec((slots, HEAD_DIM), lambda h: (0, h)), pl.BlockSpec((HEAD_DIM, slots), lambda h: (h, 0)),
        ],
        out_shape=[
            jax.ShapeDtypeStruct((slots, cols), jnp.bfloat16), jax.ShapeDtypeStruct((cols, slots), jnp.bfloat16),
        ],
        compiler_params=pltpu.CompilerParams(vmem_limit_bytes=32 * MIB),
        cost_estimate=pl.CostEstimate(
            flops=4 * slots * slots * cols, bytes_accessed=10 * slots * cols, transcendentals=slots * slots * cols // HEAD_DIM
        ),
        name="attend",
    )(lengths, qkv, qkv, qkv)


def attend_back_body(
    rows, length_ref, q_ref, k_ref, v_ref, dm_ref, cos_ref, sin_ref, out_ref, out_t_ref, bias_ref, dk_acc, dv_acc
):
    slots = q_ref.shape[1]
    heads = [slice(n, n + HEAD_DIM) for n in range(0, q_ref.shape[2], HEAD_DIM)]
    scale = HEAD_DIM**-0.5
    bf, f32 = jnp.bfloat16, jnp.float32

    def finish(j, here, head, grad):
        if j < 2:
            grad = grad * cos_ref[here, :] - turn(grad) * sin_ref[here, :]
        low = grad.astype(bf)
        out_ref[j, here, head] = low
        out_t_ref[j, head, here] = grad.T.astype(bf)
        return jnp.sum(low.astype(f32), axis=0, keepdims=True)

    dq_sums = [jnp.zeros((1, HEAD_DIM), f32) for _ in heads]
    starts = list(range(0, slots, rows))[::-1]
    for start in starts:
        here, end = slice(start, start + rows), start + rows
        for n, head in enumerate(heads):
            q, k, v = q_ref[0, here, head], k_ref[0, :end, head], v_ref[0, :end, head]
            dm = dm_ref[here, head]
            p = block_probs(length_ref, q, k, start)
            dp = lax.dot_general(dm, v, NT, preferred_element_type=f32)
            ds = (p * (dp - jnp.sum(p * dp, axis=1, keepdims=True))).astype(bf)
            dq_sums[n] += finish(0, here, head, jnp.dot(ds, k, preferred_element_type=f32) * scale)
            dk = lax.dot_general(ds, q, TN, preferred_element_type=f32) * scale
            dv = lax.dot_general(p.astype(bf), dm, TN, preferred_element_type=f32)
            if start == starts[0]:
                dk_acc[n] = dk
                dv_acc[n] = dv
            else:
                dk_acc[n, :end, :] += dk
                dv_acc[n, :end, :] += dv
    every = slice(0, slots)
    for n, head in enumerate(heads):
        bias_ref[0, :, head] = dq_sums[n]
        bias_ref[1, :, head] = finish(1, every, head, dk_acc[n])
        bias_ref[2, :, head] = finish(2, every, head, dv_acc[n])


def attend_back(lengths, qkv, d_mixed, cos_table, sin_table):
    _, slots, cols = qkv.shape
    rows = min(512, slots)
    bf, f32 = jnp.bfloat16, jnp.float32
    together = ATTEND_HEADS
    wide = together * HEAD_DIM

    def part(j):
        return pl.BlockSpec((1, slots, wide), lambda h: (j, 0, h))

    table = pl.BlockSpec((slots, HEAD_DIM), lambda h: (0, 0), pipeline_mode=pl.Buffered(1))
    return pl.pallas_call(
        functools.partial(attend_back_body, rows),
        grid=(cols // wide,),
        in_specs=[
            pl.BlockSpec(memory_space=pltpu.SMEM), part(0), part(1), part(2),
            pl.BlockSpec((slots, wide), lambda h: (0, h)), table, table,
        ],
        out_specs=[
            pl.BlockSpec((3, slots, wide), lambda h: (0, 0, h)), pl.BlockSpec((3, wide, slots), lambda h: (0, h, 0)),
            pl.BlockSpec((3, 1, wide), lambda h: (0, 0, h)),
        ],
        out_shape=[
            jax.ShapeDtypeStruct((3, slots, cols), bf), jax.ShapeDtypeStruct((3, cols, slots), bf),
            jax.ShapeDtypeStruct((3, 1, cols), f32),
        ],
        scratch_shapes=[pltpu.VMEM((together, slots, HEAD_DIM), f32)] * 2,
        compiler_params=pltpu.CompilerParams(vmem_limit_bytes=56 * MIB),
        cost_estimate=pl.CostEstimate(
            flops=10 * slots * slots * cols, bytes_accessed=20 * slots * cols, transcendentals=slots * slots * cols // HEAD_DIM
        ),
        name="attend_back",
    )(lengths, qkv, qkv, qkv, d_mixed, cos_table, sin_table)


def rows_times_body(dims, x_ref, w_ref, out_ref):
    product = lax.dot_general(x_ref[...], w_ref[...], dims, preferred_element_type=jnp.float32)
    out_ref[...] = product.astype(out_ref.dtype)


def rows_times(x, w, dims, name):
    slots, depth = x.shape
    cols = w.shape[0] if dims == NT else w.shape[1]
    rows = min(256, slots)
    return pl.pallas_call(
        functools.partial(rows_times_body, dims),
        grid=(slots // rows,),
        in_specs=[
            pl.BlockSpec((rows, depth), lambda i: (i, 0)),
            pl.BlockSpec(w.shape, lambda i: (0, 0), pipeline_mode=pl.Buffered(1)),
        ],
        out_specs=pl.BlockSpec((rows, cols), lambda i: (i, 0)),
        out_shape=jax.ShapeDtypeStruct((slots, cols), jnp.bfloat16),
        compiler_params=pltpu.CompilerParams(vmem_limit_bytes=62 * MIB),
        cost_estimate=pl.CostEstimate(
            flops=2 * slots * depth * cols, bytes_accessed=2 * (slots * depth + slots * cols + depth * cols), transcendentals=0
        ),
        name=name,
    )(x, w)


def qkv_back_body(d_ref, w_ref, x_ref, out_ref, np_ref):
    total = lax.dot_general(d_ref[0], w_ref[0], NT, preferred_element_type=jnp.float32)
    for j in range(1, 3):
        total += lax.dot_general(d_ref[j], w_ref[j], NT, preferred_element_type=jnp.float32)
    out_ref[...] = total.astype(out_ref.dtype)
    np_ref[...] = jnp.sum(total * x_ref[...].astype(jnp.float32), axis=0, keepdims=True)


def qkv_back(d_qkv, w, x):
    _, slots, cols = d_qkv.shape
    width = w.shape[1]
    block = 512
    return pl.pallas_call(
        qkv_back_body,
        grid=(width // block,),
        in_specs=[
            pl.BlockSpec((3, slots, cols), lambda n: (0, 0, 0), pipeline_mode=pl.Buffered(1)),
            pl.BlockSpec((3, block, cols), lambda n: (0, n, 0)),
            pl.BlockSpec((slots, block), lambda n: (0, n)),
        ],
        out_specs=[pl.BlockSpec((slots, block), lambda n: (0, n)), pl.BlockSpec((1, block), lambda n: (0, n))],
        out_shape=[
            jax.ShapeDtypeStruct((slots, width), jnp.bfloat16), jax.ShapeDtypeStruct((1, width), jnp.float32),
        ],
        compiler_params=pltpu.CompilerParams(vmem_limit_bytes=48 * MIB),
        cost_estimate=pl.CostEstimate(
            flops=6 * slots * width * cols, bytes_accessed=4 * slots * width + 6 * width * cols, transcendentals=0
        ),
        name="qkv_back",
    )(d_qkv, w, x)


def weight_grad_scatter(a_list, b_list, r, cid, name, first=0, count=None, cut=None):
    count = a_list[0].shape[0] // r if count is None else count
    cut = count if cut is None else cut
    if lax.axis_size("dp") == 8:
        return weight_grad_scatter_kernel(a_list, b_list, r, cid, name, first, count, cut)
    product = sum(
        jnp.dot(a[first * r : (first + count) * r], b, preferred_element_type=jnp.float32)
        for a, b in zip(a_list, b_list)
    )
    result = lax.psum_scatter(product.astype(jnp.bfloat16), "dp", scatter_dimension=1, tiled=True)
    return result[: cut * r], result[cut * r :]


def line_gather(me, size, own, block, local_sem, sems):
    send_left, recv_left, send_right, recv_right = sems
    has_left, has_right = me > 0, me < size - 1

    def remote(source, owner, send, recv, step, to):
        return pltpu.make_async_remote_copy(
            src_ref=source, dst_ref=block(owner), send_sem=send.at[step], recv_sem=recv.at[step],
            device_id={"tensor": to}, device_id_type=MESH,
        )

    def to_left(step):
        return remote(own if step == 0 else block(me + step), me + step, send_left, recv_left, step, me - 1)

    def to_right(step):
        return remote(own if step == 0 else block(me - step), me - step, send_right, recv_right, step, me + 1)

    def advance(step):
        if step == 0:
            pltpu.make_async_copy(own, block(me), local_sem).start()
        else:
            @pl.when(me + step < size)
            def _():
                remote(own, me + step, send_left, recv_left, step - 1, me + 1).wait_recv()

        @pl.when(has_left & (me + step < size))
        def _():
            to_left(step).start()

        if step > 0:
            @pl.when(me - step >= 0)
            def _():
                remote(own, me - step, send_right, recv_right, step - 1, me - 1).wait_recv()

        @pl.when(has_right & (me - step >= 0))
        def _():
            to_right(step).start()

    def finish():
        for step in range(size):
            @pl.when(has_left & (me + step < size))
            def _():
                to_left(step).wait_send()

            @pl.when(has_right & (me - step >= 0))
            def _():
                to_right(step).wait_send()

        pltpu.make_async_copy(own, block(me), local_sem).wait()

    return advance, finish


def line_barrier(me, size):
    barrier = pltpu.get_barrier_semaphore()
    has_left, has_right = me > 0, me < size - 1

    @pl.when(has_left)
    def _():
        pl.semaphore_signal(barrier, inc=1, device_id={"tensor": me - 1}, device_id_type=MESH)

    @pl.when(has_right)
    def _():
        pl.semaphore_signal(barrier, inc=1, device_id={"tensor": me + 1}, device_id_type=MESH)

    pl.semaphore_wait(barrier, has_left.astype(jnp.int32) + has_right.astype(jnp.int32))


def branch_body(
    length_ref, part_ref, tokens_ref, gain_ref, cot_ref, hidden_ref, second_ref, xa_ref, da_ref,
    from_left, from_right, normed, local_sem, send_r, recv_r, send_l, recv_l, *sems,
):
    me = lax.axis_index("tensor")
    size = lax.axis_size("tensor")
    rows = tokens_ref.shape[0]
    half, quarter = rows // 2, rows // 4
    bf, f32 = jnp.bfloat16, jnp.float32
    has_left, has_right = me > 0, me < size - 1
    line_barrier(me, size)

    def gathered(owner, h):
        return da_ref.at[pl.ds(pl.multiple_of(owner * half + h * quarter, quarter), quarter)]

    def own_cot(h):
        return cot_ref.at[pl.ds(h * quarter, quarter)]

    def part(ref, owner, which):
        return ref.at[owner, pl.ds(pl.multiple_of(which * quarter, quarter), quarter)]

    def direction(right):
        slots, send, recv = (from_left, send_r, recv_r) if right else (from_right, send_l, recv_l)
        to = me + 1 if right else me - 1
        before = me if right else size - 1 - me
        has_to = has_right if right else has_left
        has_from = has_left if right else has_right

        def copy(source, target, t):
            return pltpu.make_async_remote_copy(
                src_ref=source, dst_ref=target, send_sem=send.at[t], recv_sem=recv.at[t],
                device_id={"tensor": to}, device_id_type=MESH,
            )

        def sends(s):
            return has_to & (s - before - 1 < 2 * (size - 1 - before))

        def step(t):
            s, h = t // 2, t % 2
            if t >= 2:
                @pl.when(sends(s - 1))
                def _():
                    copy(part(part_ref, 0, 0), part(slots, 0, 0), t - 2).wait_send()

            if s < size:
                @pl.when(s <= before)
                def _():
                    owner = me - s if right else me + s
                    if s > 0:
                        copy(own_cot(h), gathered(owner, h), t - 2).wait_recv()

                    @pl.when(has_to)
                    def _():
                        copy(own_cot(h) if s == 0 else gathered(owner, h), gathered(owner, h), t).start()

            @pl.when((s > before) & sends(s))
            def _():
                r = s - before - 1
                owner = size - 1 - r // 2 if right else r // 2
                which = 2 * (r % 2) + h

                @pl.when(has_from)
                def _():
                    both = part(slots, owner, which)
                    copy(part(part_ref, owner, which), both, t - 2).wait_recv()
                    both[...] = (both[...].astype(f32) + part(part_ref, owner, which)[...].astype(f32)).astype(bf)
                    copy(both, both, t).start()

                @pl.when(jnp.logical_not(has_from))
                def _():
                    copy(part(part_ref, owner, which), part(slots, owner, which), t).start()

        def last():
            @pl.when(has_from)
            def _():
                for which in range(4):
                    t = 2 * (before + 2 * (size - 1 - before)) + which
                    copy(part(part_ref, me, which), part(slots, me, which), t).wait_recv()
                hidden_ref[...] += slots[me].astype(f32)

        return step, last

    local = [pltpu.make_async_copy(own_cot(h), gathered(me, h), local_sem.at[h]) for h in range(2)]
    for copy in local:
        copy.start()
    step_r, last_r = direction(True)
    step_l, last_l = direction(False)
    for t in range(2 * (2 * size - 1) + 2):
        step_r(t)
        step_l(t)
    hidden_ref[...] = part_ref[me].astype(f32)
    last_r()
    last_l()
    row = lax.broadcasted_iota(jnp.int32, (rows, 1), 0) + me * rows
    live = jnp.where(row < length_ref[0], 1.0, 0.0)
    hidden = tokens_ref[...].astype(f32) + live * hidden_ref[...]
    hidden_ref[...] = hidden
    inverse = lax.rsqrt(jnp.mean(hidden * hidden, axis=1, keepdims=True) + epsilon)
    normed[...] = (hidden * inverse * gain_ref[...].astype(f32)).astype(bf)
    step_x, finish_x = line_gather(
        me, size, normed.at[:half], lambda owner: xa_ref.at[pl.ds(pl.multiple_of(owner * half, half), half)],
        local_sem.at[2], sems,
    )
    for j in range(size):
        step_x(j)
    second_ref[...] = normed[half:, :]
    for copy in local:
        copy.wait()
    finish_x()


def finish_branch(lengths, part, tokens, gain, cot, cid):
    size = lax.axis_size("tensor")
    rows, width = tokens.shape
    half = rows // 2
    bf, f32 = jnp.bfloat16, jnp.float32
    vmem = pl.BlockSpec(memory_space=pltpu.VMEM)
    anywhere = pl.BlockSpec(memory_space=pl.ANY)
    dma = pltpu.SemaphoreType.DMA
    gathered = jax.ShapeDtypeStruct((size * half, width), bf)
    return pl.pallas_call(
        branch_body,
        in_specs=[pl.BlockSpec(memory_space=pltpu.SMEM), vmem, vmem, vmem, anywhere],
        out_specs=[vmem, vmem, anywhere, anywhere],
        out_shape=[
            jax.ShapeDtypeStruct((rows, width), f32), jax.ShapeDtypeStruct((half, width), bf), gathered, gathered,
        ],
        scratch_shapes=[
            pltpu.VMEM((size, rows, width), bf), pltpu.VMEM((size, rows, width), bf), pltpu.VMEM((rows, width), bf),
            dma((3,)), *[dma((4 * size,))] * 4, *[dma((size,))] * 4,
        ],
        compiler_params=pltpu.CompilerParams(vmem_limit_bytes=48 * MIB, collective_id=cid, has_side_effects=True),
        cost_estimate=pl.CostEstimate(flops=0, bytes_accessed=24 * rows * size * width, transcendentals=0),
        name="finish_branch",
    )(lengths, part.reshape(size, rows, width), tokens, gain[None], cot)


def small_sum_phases(local_rows, part_ref, out_ref, scratch):
    staged, landed, from_dp, mine, from_tensor, send_dp, recv_dp, send_t, recv_t, send_out, recv_out = scratch
    size_dp, size_t = lax.axis_size("dp"), lax.axis_size("tensor")
    me_dp, me_t = lax.axis_index("dp"), lax.axis_index("tensor")
    width = mine.shape[1]

    def piece(ref, owner):
        return ref.at[:, pl.ds(pl.multiple_of(owner * width, width), width)]

    def greet():
        barrier = pltpu.get_barrier_semaphore()
        for step in range(1, size_dp):
            peer = lax.rem(me_dp + step, size_dp)
            pl.semaphore_signal(barrier, inc=1, device_id={"dp": peer}, device_id_type=MESH)
        for step in range(1, size_t):
            peer = lax.rem(me_t + step, size_t)
            pl.semaphore_signal(barrier, inc=1, device_id={"tensor": peer}, device_id_type=MESH)
        pl.semaphore_wait(barrier, size_dp + size_t - 2)

    def copy(source, target, axis, step, send_sem, recv_sem):
        me, size = (me_dp, size_dp) if axis == "dp" else (me_t, size_t)
        return pltpu.make_async_remote_copy(
            src_ref=source, dst_ref=target, send_sem=send_sem.at[step], recv_sem=recv_sem.at[step],
            device_id={axis: lax.rem(me + step, size)}, device_id_type=MESH,
        )

    def to_owner(step):
        return copy(piece(staged, lax.rem(me_dp + step, size_dp)), from_dp.at[step], "dp", step, send_dp, recv_dp)

    def to_tensor(step):
        return copy(mine, from_tensor.at[step], "tensor", step, send_t, recv_t)

    def to_all(step):
        here = piece(landed, me_dp)
        return copy(here, here, "dp", step, send_out, recv_out)

    def first():
        staged[...] = part_ref[...]
        for step in range(1, size_dp):
            to_owner(step).start()

    def second():
        total = piece(staged, me_dp)[...]
        for step in range(1, size_dp):
            to_owner(step).wait_recv()
            total = total + from_dp[step]
        mine[...] = total
        for step in range(1, size_t):
            to_tensor(step).start()

    def third():
        total = mine[...]
        for step in range(1, size_t):
            to_tensor(step).wait_recv()
            total = total + from_tensor[step]
        piece(landed, me_dp)[...] = total
        piece(landed.at[local_rows:], me_dp)[...] = mine[local_rows:, :]
        for step in range(1, size_dp):
            to_all(step).start()

    def last():
        for step in range(1, size_dp):
            to_all(step).wait_recv()
        out_ref[...] = landed[...]
        for step in range(1, size_dp):
            to_owner(step).wait_send()
            to_all(step).wait_send()
        for step in range(1, size_t):
            to_tensor(step).wait_send()

    return greet, first, second, third, last


def small_sum_scratch(shape):
    size_dp, size_t = lax.axis_size("dp"), lax.axis_size("tensor")
    rows, width = shape[0], shape[1] // size_dp
    dma = pltpu.SemaphoreType.DMA
    f32 = jnp.float32
    return [
        pltpu.VMEM(shape, f32), pltpu.VMEM(shape, f32),
        pltpu.VMEM((size_dp, rows, width), f32), pltpu.VMEM((rows, width), f32), pltpu.VMEM((size_t, rows, width), f32),
        dma((size_dp,)), dma((size_dp,)), dma((size_t,)), dma((size_t,)), dma((size_dp,)), dma((size_dp,)),
    ]


def sums_body(local_rows, part_ref, out_ref, *scratch):
    for phase in small_sum_phases(local_rows, part_ref, out_ref, scratch):
        phase()


def small_sums(part, local_rows, cid):
    vmem = pl.BlockSpec(memory_space=pltpu.VMEM)
    return pl.pallas_call(
        functools.partial(sums_body, local_rows),
        in_specs=[vmem],
        out_specs=vmem,
        out_shape=jax.ShapeDtypeStruct(part.shape, jnp.float32),
        scratch_shapes=small_sum_scratch(part.shape),
        compiler_params=pltpu.CompilerParams(collective_id=cid, has_side_effects=True),
        name="small_sums",
    )(part)


def attention_grads_body(nc, cut, local_rows, a_ref, a2_ref, b_ref, b2_ref, part_ref, o_ref, o2_ref, sums_ref, *scratch):
    i = pl.program_id(0)
    greet, *phases = small_sum_phases(local_rows, part_ref, sums_ref, scratch[:11])
    steps = nc + LA + LB + LC

    def store(c, rows, result):
        @pl.when(c < cut)
        def _():
            o_ref[rows, :] = result.astype(o_ref.dtype)

        @pl.when(c >= cut)
        def _():
            o2_ref[rows, :] = result.astype(o2_ref.dtype)

    send = scatter_steps(i, nc, (LA, LB, LC), o_ref.shape[1], scratch[11:], store, greet)
    for when, phase in zip((0, 4, 8, steps - 1), phases):
        pl.when(i == when)(phase)

    @pl.when(i < cut)
    def _():
        send(lambda cols: jnp.dot(a_ref[...], b_ref[:, cols], preferred_element_type=jnp.float32))

    @pl.when((i >= cut) & (i < nc))
    def _():
        send(lambda cols: jnp.dot(a2_ref[...], b2_ref[:, cols], preferred_element_type=jnp.float32))


def attention_grads(a, b, a2, b2, part, local_rows, r, cid):
    T, D = b.shape
    w = D // 8
    cut, rest = a.shape[0] // r, a2.shape[0] // r
    nc = cut + rest
    lag = LA + LB + LC
    out_specs, out_shape = scatter_outs(nc, cut, lag, r, w)

    def whole(shape):
        return pl.BlockSpec(shape, lambda i: (0, 0), pipeline_mode=pl.Buffered(1))

    return pl.pallas_call(
        functools.partial(attention_grads_body, nc, cut, local_rows),
        grid=(nc + lag,),
        in_specs=[
            pl.BlockSpec((r, T), lambda i: (jnp.minimum(i, cut - 1), 0)),
            pl.BlockSpec((r, T), lambda i: (jnp.clip(i - cut, 0, rest - 1), 0)),
            whole((T, D)), whole((T, D)), whole(part.shape),
        ],
        out_specs=[*out_specs, whole(part.shape)],
        out_shape=[*out_shape, jax.ShapeDtypeStruct(part.shape, jnp.float32)],
        scratch_shapes=[*small_sum_scratch(part.shape), *scatter_scratch(r, w)],
        compiler_params=pltpu.CompilerParams(vmem_limit_bytes=48 * MIB, collective_id=cid, has_side_effects=True),
        cost_estimate=pl.CostEstimate(flops=2 * nc * r * T * D, bytes_accessed=2 * nc * r * T + 4 * T * D, transcendentals=0),
        name="attention_grads",
    )(a, a2, b, b2, part)


def on_device(
    tokens,
    lengths,
    routes,
    cotangent,
    norm_one,
    qkv_weight,
    qkv_bias,
    out_weight,
    norm_two,
    router_weight,
    expert_in,
    expert_out,
    shared_in,
    shared_out,
    shared_gate,
):
    own_rows = tokens.shape[0]
    slot_count = routes.shape[0]
    model_width = tokens.shape[1]
    qkv_cols = qkv_weight.shape[2]
    local_heads = qkv_cols // HEAD_DIM
    experts = router_weight.shape[1]
    eff = expert_in.shape[3]
    shared_chunks = shared_out.shape[0] // eff
    chunks = experts + shared_chunks
    bf = jnp.bfloat16
    qkv_cols = qkv_weight.shape[2]
    length = lengths[0]
    tensor_index = lax.axis_index("tensor")
    first_row = tensor_index * own_rows
    live_own = (first_row + jnp.arange(own_rows) < length).astype(jnp.float32)[:, None]
    tokens_f = tokens.astype(jnp.float32)
    gain_one = norm_one.astype(jnp.float32)
    gain_two = norm_two.astype(jnp.float32)
    inv_one = lax.rsqrt(jnp.mean(tokens_f * tokens_f, axis=-1, keepdims=True) + epsilon)
    unit_one = tokens_f * inv_one
    normed_one = lax.all_gather((unit_one * gain_one).astype(bf), "tensor", axis=0, tiled=True)
    cos_table, sin_table = rotary_tables(slot_count, HEAD_DIM)
    qkv_w = qkv_weight.transpose(1, 0, 2)
    ei = expert_in.transpose(0, 2, 3, 1).reshape(experts, 2 * eff, model_width)
    eo = expert_out
    si = (
        shared_in.reshape(model_width, 2, shared_chunks, eff)
        .transpose(2, 1, 3, 0)
        .reshape(shared_chunks, 2 * eff, model_width)
    )
    so = shared_out.reshape(shared_chunks, eff, model_width)
    router_rows = jnp.concatenate(
        [
            router_weight.T,
            shared_gate[None],
            jnp.zeros((-(experts + 1) % 16, model_width), bf),
        ],
        axis=0,
    )
    grad_out = cotangent.astype(jnp.float32) * live_own
    d_two_own = (live_own * grad_out).astype(bf)
    normed_one, si, router_rows, cos_table, sin_table, d_two_own = lax.optimization_barrier(
        (normed_one, si, router_rows, cos_table, sin_table, d_two_own)
    )
    qkv = project_qkv(normed_one, qkv_w, qkv_bias[:, None, :], cos_table, sin_table)
    mixed, mixed_t = attend(lengths, qkv)
    branch_partial = jnp.dot(mixed, out_weight, preferred_element_type=jnp.float32).astype(bf)
    size_t = lax.axis_size("tensor")
    half = own_rows // 2
    hidden, second, x_a, d_a = finish_branch(
        lengths, branch_partial, tokens, norm_two, d_two_own, 1
    )
    inv_two = lax.rsqrt(jnp.mean(hidden * hidden, axis=-1, keepdims=True) + epsilon)
    unit_two = hidden * inv_two
    routes_a, routes_b = (
        routes.reshape(size_t, 2, half, -1).transpose(1, 0, 2, 3).reshape(2, size_t * half, -1)
    )
    weights = (router_rows, ei, si, eo, so)
    dgu_a, dn_a, bt_a, router_a, np_a, s_a, x_b, d_b = ffn(
        x_a, d_a, routes_a.T, *weights, own=[second, d_two_own[half:]]
    )
    grad_a = lax.psum_scatter(dn_a, "tensor", scatter_dimension=0, tiled=True)
    two_a = lax.psum_scatter(bt_a, "tensor", scatter_dimension=0, tiled=True)
    if lax.axis_size("dp") == 8:
        dgu_b, dn_b, bt_b, router_b, np_b, out_grads, shared_out_grad = ffn(
            x_b, d_b, routes_b.T, *weights, other=(s_a, d_a)
        )
    else:
        dgu_b, dn_b, bt_b, router_b, np_b, s_b = ffn(x_b, d_b, routes_b.T, *weights)
        inner = [s.reshape(chunks * eff, -1) for s in (s_a, s_b)]
        out_grads, shared_out_grad = weight_grad_scatter(
            inner, [d_a, d_b], eff, 2, "down_grads", cut=experts
        )
    router_part = router_a + router_b
    norm_two_part = np_a + np_b
    d_gate_up = [d.reshape(chunks * 2 * eff, -1) for d in (dgu_a, dgu_b)]
    grad_a, two_a, dn_b = lax.optimization_barrier((grad_a, two_a, dn_b))
    grad_b = lax.psum_scatter(dn_b, "tensor", scatter_dimension=0, tiled=True)
    two_b = lax.psum_scatter(bt_b, "tensor", scatter_dimension=0, tiled=True)
    in_grads_b, _ = weight_grad_scatter(
        d_gate_up, [x_a, x_b], eff, 4, "shared_in_grads", 2 * experts, 2 * shared_chunks
    )
    grad_two = jnp.concatenate([grad_a, grad_b], axis=0).astype(jnp.float32)
    grad_hidden = grad_out + norm_back(grad_two, unit_two, inv_two, gain_two)
    d_one_own, in_grads_b = lax.optimization_barrier(
        ((live_own * grad_hidden).astype(bf), in_grads_b)
    )
    d_one = lax.all_gather(d_one_own, "tensor", axis=0, tiled=True)
    d_gate_up, _ = lax.optimization_barrier((d_gate_up, d_one_own))
    in_grads_a, _ = weight_grad_scatter(
        d_gate_up, [x_a, x_b], eff, 3, "expert_in_grads", 0, 2 * experts
    )
    d_one, in_grads_a = lax.optimization_barrier((d_one, in_grads_a))
    d_mixed = rows_times(d_one, out_weight, NT, "mixed_back")
    d_qkv, d_qkv_t, bias_part = attend_back(lengths, qkv, d_mixed, cos_table, sin_table)
    grad_one, norm_one_part = qkv_back(d_qkv, qkv_w, normed_one)
    grad_one, d_qkv_t, mixed_t, two_b = lax.optimization_barrier(
        (grad_one, d_qkv_t, mixed_t, two_b)
    )
    grad_one_own = lax.psum_scatter(grad_one, "tensor", scatter_dimension=0, tiled=True)
    part = jnp.concatenate(
        [
            router_part[: experts + 1],
            norm_one_part / gain_one[None],
            norm_two_part / gain_two[None],
            jnp.pad(bias_part.reshape(1, 3 * qkv_cols), ((0, 0), (0, model_width - 3 * qkv_cols))),
        ],
        axis=0,
    )
    d_qkv_t = d_qkv_t.reshape(3 * qkv_cols, slot_count)
    if lax.axis_size("dp") == 8:
        qkv_sum, out_sum, sums = attention_grads(
            d_qkv_t, normed_one, mixed_t, d_one, part, experts + 3, qkv_cols // 2, 5
        )
    else:
        sums = small_sums(part, experts + 3, 7)
        qkv_sum, _ = weight_grad_scatter([d_qkv_t], [normed_one], qkv_cols, 5, "qkv_grads")
        out_sum, _ = weight_grad_scatter([mixed_t], [d_one], qkv_cols, 6, "mix_grads")
    branch_two = jnp.concatenate([two_a, two_b], axis=0).astype(jnp.float32)
    output = (hidden + live_own * branch_two).astype(bf)
    grad_one = grad_one_own.astype(jnp.float32)
    input_grad = grad_hidden + norm_back(grad_one, unit_one, inv_one, gain_one)
    qkv_bias_grad = sums[experts + 3, : 3 * qkv_cols].reshape(3, qkv_cols)
    own_cols = out_grads.shape[1]
    expert_in_grad = in_grads_a.astype(jnp.float32).reshape(experts, 2, eff, own_cols).transpose(0, 3, 1, 2)
    shared_in_grad = (
        in_grads_b.reshape(shared_chunks, 2, eff, own_cols)
        .transpose(3, 1, 0, 2)
        .reshape(own_cols, 2, shared_chunks * eff)
        .astype(jnp.float32)
    )
    return (
        output,
        input_grad,
        sums[experts + 1],
        qkv_sum.astype(jnp.float32).reshape(3, qkv_cols, own_cols).transpose(2, 0, 1),
        qkv_bias_grad,
        out_sum.astype(jnp.float32),
        sums[experts + 2],
        sums[:experts].T,
        expert_in_grad,
        out_grads.astype(jnp.float32).reshape(experts, eff, own_cols),
        shared_in_grad,
        shared_out_grad.astype(jnp.float32),
        sums[experts],
    )


def solution(mesh):
    in_specs = (
        P(("dp", "tensor"), None),
        P("dp"),
        P("dp", None),
        P(("dp", "tensor"), None),
        P(),
        P(None, None, "tensor"),
        P(None, "tensor"),
        P("tensor", None),
        P(),
        P(),
        P(None, None, None, "tensor"),
        P(None, "tensor", None),
        P(None, None, "tensor"),
        P("tensor", None),
        P(),
    )
    out_specs = (
        P(("dp", "tensor"), None),
        P(("dp", "tensor"), None),
        P(),
        P("dp", None, "tensor"),
        P(None, "tensor"),
        P("tensor", "dp"),
        P(),
        P(),
        P(None, "dp", None, "tensor"),
        P(None, "tensor", "dp"),
        P("dp", None, "tensor"),
        P("tensor", "dp"),
        P(),
    )
    return jax.shard_map(
        on_device, mesh=mesh, in_specs=in_specs, out_specs=out_specs, check_vma=False
    )
```
